32 devices in a mesh: dp: 16 (over z, x, core), tensor: 2 (over y).
Axes of the slice: x: 2, y: 2, z: 4, core: 2. Of those that a mesh axis runs over, the one named last changes fastest.
Arguments:
- images: bfloat16 [32, 578, 1024], P('dp', 'tensor'), may hold values from -6 to 6
- cotangent: bfloat16 [32, 578, 1024], P('dp', 'tensor'), may hold values from -6 to 6
- slot_live: int32 [32], P('dp'), may hold values from 0 to 1, as said below
- first_gain: bfloat16 [1024], replicated, may hold values from 0.099609375 to 1.8984375
- first_shift: bfloat16 [1024], replicated, may hold values from -2 to 2
- query_weight: bfloat16 [1024, 1024], P('dp', 'tensor'), may hold values from -0.1875 to 0.1875
- query_bias: bfloat16 [1024], replicated, may hold values from -3 to 3
- key_weight: bfloat16 [1024, 1024], P('dp', 'tensor'), may hold values from -0.1875 to 0.1875
- value_weight: bfloat16 [1024, 1024], P('dp', 'tensor'), may hold values from -0.1875 to 0.1875
- value_bias: bfloat16 [1024], replicated, may hold values from -2 to 2
- output_weight: bfloat16 [1024, 1024], P('tensor', 'dp'), may hold values from -3 to 3
- output_bias: bfloat16 [1024], replicated, may hold values from -2 to 2
- second_gain: bfloat16 [1024], replicated, may hold values from 0.099609375 to 1.8984375
- second_shift: bfloat16 [1024], replicated, may hold values from -2 to 2
- up_weight: bfloat16 [1024, 4096], P('dp', 'tensor'), may hold values from -0.1875 to 0.1875
- up_bias: bfloat16 [4096], replicated, may hold values from -3 to 3
- down_weight: bfloat16 [4096, 1024], P('tensor', 'dp'), may hold values from -0.09375 to 0.09375
- down_bias: bfloat16 [1024], replicated, may hold values from -2 to 2
Outputs:
- layer_out: bfloat16 [32, 578, 1024], P('dp', 'tensor')
- images_grad: float32 [32, 578, 1024], P('dp', 'tensor')
- first_gain_grad: float32 [1024], replicated
- first_shift_grad: float32 [1024], replicated
- query_weight_grad: float32 [1024, 1024], P('dp', 'tensor')
- query_bias_grad: float32 [1024], replicated
- key_weight_grad: float32 [1024, 1024], P('dp', 'tensor')
- value_weight_grad: float32 [1024, 1024], P('dp', 'tensor')
- value_bias_grad: float32 [1024], replicated
- output_weight_grad: float32 [1024, 1024], P('tensor', 'dp')
- output_bias_grad: float32 [1024], replicated
- second_gain_grad: float32 [1024], replicated
- second_shift_grad: float32 [1024], replicated
- up_weight_grad: float32 [1024, 4096], P('dp', 'tensor')
- up_bias_grad: float32 [4096], replicated
- down_weight_grad: float32 [4096, 1024], P('tensor', 'dp')
- down_bias_grad: float32 [1024], replicated
The draws below stay inside these ranges and needn't reach their ends.
Inputs may be any that keep to these rules, and one draw needn't show every extreme that they name: `slot_live`: in every group of 2 consecutive slots the first holds an image, and in some group every slot does.
All inputs are finite; a program needn't handle non-finite values.
Results may differ from the reference program's by a relative error of at most 0.017.
Values may be sent and summed in bfloat16 or wider, within the bound.
No kernel may reach another device: no remote copies, remote signals or barrier semaphores. Data moves between devices by JAX's collectives and lax.ppermute only.
A program may use at most 128 MiB of HBM per device.

```python
import jax
import jax.numpy as jnp
from jax import lax

D = 1024
HEADS = 16
HDIM = 64
FF = 4096
VALID = 577
SLOTS = 2
IMAGES = 32
PADDED = 578


def draw_slot_live(key, part):
    groups = IMAGES // SLOTS
    first_key = jax.random.fold_in(key, 11)
    second_key = jax.random.fold_in(key, 12)
    picks = jax.random.randint(first_key, (groups, SLOTS), 0, 4)
    live = (picks >= 1).astype(jnp.int32)
    live = live.at[:, 0].set(1)
    chosen = jax.random.randint(second_key, (), 0, groups)
    live = jnp.where(jnp.arange(groups)[:, None] == chosen, 1, live)
    return live.reshape(IMAGES).astype(jnp.int32)


def block_scale(own_key, dims, pieces, least, top_value):
    loudness, own = 1.0, jax.random.fold_in(own_key, 6)
    for axis_at, shards_of in pieces:
        heights = jnp.exp(jax.random.uniform(jax.random.fold_in(own, axis_at), (shards_of,), jnp.float32, least / len(pieces), top_value / len(pieces)))
        loudness = loudness * jnp.repeat(heights, dims[axis_at] // shards_of).reshape([-1 if axis == axis_at else 1 for axis in range(len(dims))])
    return loudness


def centred(own_key, dims, scale, limit, shards=(), held_as=jnp.bfloat16):
    array = scale * jax.random.normal(own_key, dims, jnp.float32)
    if shards:
        array = array * block_scale(own_key, dims, shards, -0.22, 0.18)
    return jnp.clip(array, -limit, limit).astype(held_as)


def setup_inputs(seed: int = 0) -> dict:
    key_list = jax.random.split(jax.random.key(seed), 19)
    images = centred(key_list[0], (IMAGES, PADDED, D), 1.0, 6.0, ((0, 16), (1, 2)))
    cotangent = centred(key_list[1], (IMAGES, PADDED, D), 1.0, 6.0, ((0, 16), (1, 2)))
    slot_live = draw_slot_live(jax.random.fold_in(key_list[18], 71), 0)
    first_gain = jnp.clip(1.0 + 0.18 * jax.random.normal(key_list[3], (D,), jnp.float32), 0.099609375, 1.8984375).astype(jnp.bfloat16)
    first_shift = centred(key_list[4], (D,), 0.3, 2.0)
    query_weight = centred(key_list[5], (D, D), D ** -0.5, 0.1875, ((0, 16), (1, 2)))
    query_bias = centred(key_list[6], (D,), 0.5, 3.0)
    key_weight = centred(key_list[7], (D, D), D ** -0.5, 0.1875, ((0, 16), (1, 2)))
    value_weight = centred(key_list[8], (D, D), D ** -0.5, 0.1875, ((0, 16), (1, 2)))
    value_bias = centred(key_list[9], (D,), 0.3, 2.0)
    output_weight = centred(key_list[10], (D, D), 4 ** -0.5, 3.0, ((0, 2), (1, 16)))
    output_bias = centred(key_list[11], (D,), 0.3, 2.0)
    second_gain = jnp.clip(1.0 + 0.18 * jax.random.normal(key_list[12], (D,), jnp.float32), 0.099609375, 1.8984375).astype(jnp.bfloat16)
    second_shift = centred(key_list[13], (D,), 0.3, 2.0)
    up_weight = centred(key_list[14], (D, FF), D ** -0.5, 0.1875, ((0, 16), (1, 2)))
    up_bias = centred(key_list[15], (FF,), 0.5, 3.0)
    down_weight = centred(key_list[16], (FF, D), FF ** -0.5, 0.09375, ((0, 2), (1, 16)))
    down_bias = centred(key_list[17], (D,), 0.3, 2.0)
    return {"images": images, "cotangent": cotangent, "slot_live": slot_live, "first_gain": first_gain, "first_shift": first_shift, "query_weight": query_weight, "query_bias": query_bias, "key_weight": key_weight, "value_weight": value_weight, "value_bias": value_bias, "output_weight": output_weight, "output_bias": output_bias, "second_gain": second_gain, "second_shift": second_shift, "up_weight": up_weight, "up_bias": up_bias, "down_weight": down_weight, "down_bias": down_bias}


@jax.custom_vjp
def low(v):
    return lax.optimization_barrier(v.astype(jnp.bfloat16)).astype(jnp.float32)

@jax.custom_vjp
def low_back(v):
    return v

def low_keep(v):
    return (low(v), None)

def low_pass(kept, grad):
    return (grad,)

def back_keep(v):
    return (v, None)

def back_low(kept, grad):
    return (low(grad),)
low.defvjp(low_keep, low_pass)
low_back.defvjp(back_keep, back_low)
EPS = 1e-05
HIGH = lax.Precision.HIGHEST

def layer_norm(values, gain, shift):
    center = values - lax.optimization_barrier(jnp.mean(values, axis=-1, keepdims=True))
    spread = lax.rsqrt(lax.optimization_barrier(jnp.mean(center * center, axis=-1, keepdims=True)) + EPS)
    return center * spread * gain + shift

def matmul(left, right):
    return jnp.dot(left, right, precision=HIGH, preferred_element_type=jnp.float32)

def layer(resid, live, params):
    first_gain, first_shift, query_weight, query_bias, key_weight, value_weight, value_bias, output_weight, output_bias, second_gain, second_shift, up_weight, up_bias, down_weight, down_bias = params
    positions = jnp.arange(PADDED)
    row_mask = (live * (positions < VALID).astype(jnp.float32))[:, None]
    key_ok = positions < VALID
    normed = low(layer_norm(resid, first_gain, first_shift))
    queries = low(low_back(matmul(normed, query_weight) + query_bias)).reshape(PADDED, HEADS, HDIM)
    keys = low(low_back(matmul(normed, key_weight))).reshape(PADDED, HEADS, HDIM)
    values = low(low_back(matmul(normed, value_weight) + value_bias)).reshape(PADDED, HEADS, HDIM)
    scores = low_back(jnp.einsum('qhe,khe->hqk', queries, keys, precision=HIGH) * HDIM ** (-0.5))
    scores = jnp.where(key_ok[None, None, :], scores, -1e+30)
    total = jax.nn.logsumexp(scores, axis=-1, keepdims=True)
    probs = low(jnp.exp(scores - total))
    mixed = low(low_back(jnp.einsum('hqk,khe->qhe', probs, values, precision=HIGH).reshape(PADDED, D)))
    attended = low_back(matmul(mixed, output_weight) + output_bias)
    middle = row_mask * (resid + attended)
    second = low(layer_norm(middle, second_gain, second_shift))
    hidden = low_back(matmul(second, up_weight) + up_bias)
    active = low(hidden * jax.nn.sigmoid(1.702 * hidden))
    fed = low_back(matmul(active, down_weight) + down_bias)
    return row_mask * (middle + fed)

def reference(images, cotangent, slot_live, first_gain, first_shift, query_weight, query_bias, key_weight, value_weight, value_bias, output_weight, output_bias, second_gain, second_shift, up_weight, up_bias, down_weight, down_bias):
    params = tuple((p.astype(jnp.float32) for p in (first_gain, first_shift, query_weight, query_bias, key_weight, value_weight, value_bias, output_weight, output_bias, second_gain, second_shift, up_weight, up_bias, down_weight, down_bias)))
    zeros = tuple((jnp.zeros(p.shape, jnp.float32) for p in params))

    def one_image(carry, items):
        image, grad_out, live = items
        resid = image.astype(jnp.float32)
        live_f = live.astype(jnp.float32)
        result, pullback = jax.vjp(lambda r, p: layer(r, live_f, p), resid, params)
        grad_resid, grad_params = pullback(grad_out.astype(jnp.float32))
        carry = tuple((c + g for c, g in zip(carry, grad_params)))
        return (carry, (result.astype(jnp.bfloat16), grad_resid))
    sums, (layer_out, images_grad) = lax.scan(one_image, zeros, (images, cotangent, slot_live))
    g_fg, g_fs, g_qw, g_qb, g_kw, g_vw, g_vb, g_ow, g_ob, g_sg, g_ss, g_uw, g_ub, g_dw, g_db = sums
    return (layer_out, images_grad, g_fg, g_fs, g_qw, g_qb, g_kw, g_vw, g_vb, g_ow, g_ob, g_sg, g_ss, g_uw, g_ub, g_dw, g_db)
```

```python
import jax
import jax.numpy as jnp
from jax import lax
from jax.experimental import pallas as pl
from jax.experimental.pallas import tpu as pltpu
from jax.sharding import PartitionSpec as P

HDIM = 64
VALID = 577


EPS = 1e-05
NEGATIVE = -1e30
SLOPE = 1.702


def layer_norm(values, gain, shift):
    center = values - jnp.mean(values, axis=-1, keepdims=True)
    spread = lax.rsqrt(jnp.mean(center * center, axis=-1, keepdims=True) + EPS)
    unit = center * spread
    return (unit * gain + shift, unit, spread)


def norm_back(upstream, unit, spread, gain):
    scaled = upstream * gain
    inner = (
        scaled
        - jnp.mean(scaled, axis=-1, keepdims=True)
        - unit * jnp.mean(scaled * unit, axis=-1, keepdims=True)
    )
    return (spread * inner, jnp.sum(upstream * unit, axis=(0, 1)), jnp.sum(upstream, axis=(0, 1)))


def dense(left, right):
    return jnp.einsum("spa,ab->spb", left, right, preferred_element_type=jnp.float32)


def project_back(left, right):
    return jnp.einsum("spa,ba->spb", left, right, preferred_element_type=jnp.float32)


def outer(left, right):
    return jnp.einsum("spa,spb->ab", left, right, preferred_element_type=jnp.float32)


def column_sum(values):
    return jnp.sum(values.astype(jnp.float32), axis=(0, 1))


def widen(piece, length, start):
    return lax.dynamic_update_slice_in_dim(jnp.zeros((length,), jnp.float32), piece, start, 0)


def split_heads(block):
    return block.reshape(block.shape[0], -1, HDIM)


def scores_of(query, key, key_ok):
    raw = jnp.einsum(
        "qhe,khe->hqk", split_heads(query), split_heads(key), preferred_element_type=jnp.float32
    )
    return jnp.where(key_ok[None, None, :], raw * HDIM ** (-0.5), NEGATIVE)


def attend(query, key, value, key_ok):
    scores = scores_of(query, key, key_ok)
    top = jnp.max(scores, axis=-1, keepdims=True)
    total = top + jnp.log(jnp.sum(jnp.exp(scores - top), axis=-1, keepdims=True))
    probs = jnp.exp(scores - total).astype(jnp.bfloat16)
    mixed = jnp.einsum(
        "hqk,khe->qhe", probs, split_heads(value), preferred_element_type=jnp.float32
    )
    return (mixed.reshape(query.shape[0], -1).astype(jnp.bfloat16), total)


def attend_back(query, key, value, grad_mixed, total, key_ok):
    scores = scores_of(query, key, key_ok)
    probs = jnp.exp(scores - total)
    grad_heads = split_heads(grad_mixed)
    grad_probs = jnp.einsum(
        "qhe,khe->hqk", grad_heads, split_heads(value), preferred_element_type=jnp.float32
    )
    grad_value = jnp.einsum(
        "hqk,qhe->khe", probs.astype(jnp.bfloat16), grad_heads, preferred_element_type=jnp.float32
    )
    grad_scores = (
        probs * (grad_probs - jnp.sum(probs * grad_probs, axis=-1, keepdims=True))
    ).astype(jnp.bfloat16)
    grad_query = jnp.einsum(
        "hqk,khe->qhe", grad_scores, split_heads(key), preferred_element_type=jnp.float32
    ) * HDIM ** (-0.5)
    grad_key = jnp.einsum(
        "hqk,qhe->khe", grad_scores, split_heads(query), preferred_element_type=jnp.float32
    ) * HDIM ** (-0.5)
    length = query.shape[0]
    return (
        grad_query.reshape(length, -1).astype(jnp.bfloat16),
        grad_key.reshape(length, -1).astype(jnp.bfloat16),
        grad_value.reshape(length, -1).astype(jnp.bfloat16),
    )


def local(
    images,
    cotangent,
    slot_live,
    first_gain,
    first_shift,
    query_weight,
    query_bias,
    key_weight,
    value_weight,
    value_bias,
    output_weight,
    output_bias,
    second_gain,
    second_shift,
    up_weight,
    up_bias,
    down_weight,
    down_bias,
):
    slots, strip, width = images.shape
    tensor_count = lax.axis_size("tensor")
    tensor_place = lax.axis_index("tensor")
    seq_len = strip * tensor_count
    positions = tensor_place * strip + jnp.arange(strip)
    row_mask = (
        slot_live.astype(jnp.float32)[:, None, None]
        * (positions < VALID).astype(jnp.float32)[None, :, None]
    )
    key_ok = jnp.arange(seq_len) < VALID
    query_full, key_full, value_full, upper_full, output_full, lower_full = (
        lax.all_gather(query_weight, "dp", axis=0, tiled=True),
        lax.all_gather(key_weight, "dp", axis=0, tiled=True),
        lax.all_gather(value_weight, "dp", axis=0, tiled=True),
        lax.all_gather(up_weight, "dp", axis=0, tiled=True),
        lax.all_gather(output_weight, "dp", axis=1, tiled=True),
        lax.all_gather(down_weight, "dp", axis=1, tiled=True),
    )
    head_cols = query_full.shape[1]
    head_start = tensor_place * head_cols
    gain_one = first_gain.astype(jnp.float32)
    shift_one = first_shift.astype(jnp.float32)
    gain_two = second_gain.astype(jnp.float32)
    shift_two = second_shift.astype(jnp.float32)
    query_shift = lax.dynamic_slice_in_dim(query_bias.astype(jnp.float32), head_start, head_cols)
    value_shift = lax.dynamic_slice_in_dim(value_bias.astype(jnp.float32), head_start, head_cols)
    resid = images.astype(jnp.float32)
    normed, unit_one, spread_one = layer_norm(resid, gain_one, shift_one)
    normed_rows = lax.all_gather(normed.astype(jnp.bfloat16), "tensor", axis=1, tiled=True)
    queries = (dense(normed_rows, query_full) + query_shift).astype(jnp.bfloat16)
    keys_low = dense(normed_rows, key_full).astype(jnp.bfloat16)
    values_low = (dense(normed_rows, value_full) + value_shift).astype(jnp.bfloat16)
    mixed, totals = lax.map(
        lambda items: attend(items[0], items[1], items[2], key_ok), (queries, keys_low, values_low)
    )
    attended = lax.psum_scatter(
        dense(mixed, output_full), "tensor", scatter_dimension=1, tiled=True
    ) + output_bias.astype(jnp.float32)
    middle = row_mask * (resid + attended)
    second, unit_two, spread_two = layer_norm(middle, gain_two, shift_two)
    second_low = second.astype(jnp.bfloat16)
    grad_top = row_mask * cotangent.astype(jnp.float32)
    fed_grad = grad_top.astype(jnp.bfloat16)
    down_shift = down_bias.astype(jnp.float32)
    units = upper_full.shape[1]
    second_rows = lax.all_gather(second_low, "tensor", axis=1, tiled=True)
    up_shift = lax.dynamic_slice_in_dim(up_bias.astype(jnp.float32), tensor_place * units, units)
    hidden = dense(second_rows, upper_full) + up_shift
    sigma = jax.nn.sigmoid(SLOPE * hidden)
    active = (hidden * sigma).astype(jnp.bfloat16)
    fed = (
        lax.psum_scatter(
            dense(active, lower_full).astype(jnp.bfloat16),
            "tensor",
            scatter_dimension=1,
            tiled=True,
        ).astype(jnp.float32)
        + down_shift
    )
    fed_rows = lax.all_gather(fed_grad, "tensor", axis=1, tiled=True)
    grad_active = project_back(fed_rows, lower_full)
    lower_grad = outer(active, fed_rows)
    hidden_grad = (grad_active * (sigma + SLOPE * hidden * sigma * (1.0 - sigma))).astype(
        jnp.bfloat16
    )
    upper_grad = outer(second_rows, hidden_grad)
    up_bias_grad = widen(column_sum(hidden_grad), up_bias.shape[0], tensor_place * units)
    second_grad = lax.psum_scatter(
        project_back(hidden_grad, upper_full), "tensor", scatter_dimension=1, tiled=True
    )
    layer_out = (row_mask * (middle + fed)).astype(jnp.bfloat16)
    down_bias_grad = column_sum(fed_grad)
    middle_back, gain_two_grad, shift_two_grad = norm_back(
        second_grad, unit_two, spread_two, gain_two
    )
    middle_grad = row_mask * (grad_top + middle_back)
    attended_grad = middle_grad.astype(jnp.bfloat16)
    output_bias_grad = column_sum(attended_grad)
    attended_rows = lax.all_gather(attended_grad, "tensor", axis=1, tiled=True)
    grad_mixed = project_back(attended_rows, output_full).astype(jnp.bfloat16)
    output_grad = outer(mixed, attended_rows)
    grad_query, grad_key, grad_value = lax.map(
        lambda items: attend_back(items[0], items[1], items[2], items[3], items[4], key_ok),
        (queries, keys_low, values_low, grad_mixed, totals),
    )
    query_grad = outer(normed_rows, grad_query)
    key_grad = outer(normed_rows, grad_key)
    value_grad = outer(normed_rows, grad_value)
    query_bias_grad = widen(column_sum(grad_query), width, head_start)
    value_bias_grad = widen(column_sum(grad_value), width, head_start)
    normed_terms = (
        project_back(grad_query, query_full)
        + project_back(grad_key, key_full)
        + project_back(grad_value, value_full)
    )
    normed_grad = lax.psum_scatter(
        normed_terms.astype(jnp.bfloat16), "tensor", scatter_dimension=1, tiled=True
    ).astype(jnp.float32)
    first_back, gain_one_grad, shift_one_grad = norm_back(
        normed_grad, unit_one, spread_one, gain_one
    )
    images_grad = middle_grad + first_back
    query_owned, key_owned, value_owned, upper_owned, output_owned, lower_owned = (
        lax.psum_scatter(
            query_grad.astype(jnp.bfloat16), "dp", scatter_dimension=0, tiled=True
        ).astype(jnp.float32),
        lax.psum_scatter(
            key_grad.astype(jnp.bfloat16), "dp", scatter_dimension=0, tiled=True
        ).astype(jnp.float32),
        lax.psum_scatter(
            value_grad.astype(jnp.bfloat16), "dp", scatter_dimension=0, tiled=True
        ).astype(jnp.float32),
        lax.psum_scatter(
            upper_grad.astype(jnp.bfloat16), "dp", scatter_dimension=0, tiled=True
        ).astype(jnp.float32),
        lax.psum_scatter(
            output_grad.astype(jnp.bfloat16), "dp", scatter_dimension=1, tiled=True
        ).astype(jnp.float32),
        lax.psum_scatter(
            lower_grad.astype(jnp.bfloat16), "dp", scatter_dimension=1, tiled=True
        ).astype(jnp.float32),
    )
    vector_sums = lax.psum(
        (
            gain_one_grad,
            shift_one_grad,
            query_bias_grad,
            value_bias_grad,
            output_bias_grad,
            gain_two_grad,
            shift_two_grad,
            up_bias_grad,
            down_bias_grad,
        ),
        ("dp", "tensor"),
    )
    (
        gain_one_total,
        shift_one_total,
        query_bias_total,
        value_bias_total,
        output_bias_total,
        gain_two_total,
        shift_two_total,
        up_bias_total,
        down_bias_total,
    ) = vector_sums
    return (
        layer_out,
        images_grad,
        gain_one_total,
        shift_one_total,
        query_owned,
        query_bias_total,
        key_owned,
        value_owned,
        value_bias_total,
        output_owned,
        output_bias_total,
        gain_two_total,
        shift_two_total,
        upper_owned,
        up_bias_total,
        lower_owned,
        down_bias_total,
    )


BOTH = ("dp", "tensor")
HALF_PAD = 8
LANES = 128


def exchange(value, far_z=0, far_x=0, far_core=0, far_y=0):
    pairs = []
    for place in range(32):
        other = place ^ (far_z * 8 + far_x * 4 + far_core * 2 + far_y)
        pairs.append((place, other))
    return lax.ppermute(value, BOTH, pairs)


def pick_two(bit, own, other, axis):
    first = jnp.where(bit == 0, own, other)
    last = jnp.where(bit == 0, other, own)
    return jnp.stack([first, last], axis)


def after(value, *others):
    return lax.optimization_barrier((value, *others))[0]


def gather_start(shard, core):
    keep = jnp.where(core == 0, shard[0], shard[1])
    send = jnp.where(core == 0, shard[1], shard[0])
    return pick_two(core, keep, exchange(send, far_core=1), 1)


def gather_z(piece, place_z):
    found = [piece] + [exchange(piece, far_z=step) for step in (1, 2, 3)]
    ordered = [lax.select_n(place_z ^ spot, *found) for spot in range(4)]
    return jnp.stack(ordered, 1)


def gather_plane_one(ordered):
    return exchange(ordered[0], far_x=1), exchange(ordered[1], far_y=1)


def gather_plane_two(ordered, crossed, place_x):
    one = pick_two(place_x, ordered[0], crossed[0], 1)
    two = jnp.stack([ordered[1], crossed[1]])
    return one, two, exchange(one, far_y=1), exchange(two, far_x=1)


def gather_finish(parts, place_x):
    one, two, one_far, two_far = parts
    wide = one.shape[-1]
    two_all = pick_two(place_x, two, two_far, 2)
    pieces = [one, one_far, two_all[0], two_all[1]]
    return jnp.concatenate([piece.reshape(-1, wide) for piece in pieces], 1)


def scatter_sum(pieces, place_x, place_z, core):
    rows, wide = pieces[0].shape
    pieces = [piece.reshape(4, 2, 2, rows // 16, wide) for piece in pieces]

    def low_sum(left, right):
        return (left.astype(jnp.float32) + right.astype(jnp.float32)).astype(jnp.bfloat16)

    def split_x(value, axis):
        keep = lax.dynamic_index_in_dim(value, place_x, axis, keepdims=False)
        send = lax.dynamic_index_in_dim(value, 1 - place_x, axis, keepdims=False)
        return keep, send

    two_keep, two_send = split_x(jnp.stack(pieces[2:]), 2)
    one_far = exchange(pieces[1], far_y=1)
    two_far = exchange(two_send, far_x=1)
    one_keep, one_send = split_x(low_sum(pieces[0], one_far), 1)
    two = low_sum(two_keep, two_far)
    one_far = exchange(one_send, far_x=1)
    two_far = exchange(two[1], far_y=1)
    both = jnp.stack([low_sum(one_keep, one_far), low_sum(two[0], two_far)], 1)
    total = lax.dynamic_index_in_dim(both, place_z, 0, keepdims=False).astype(jnp.float32)
    for step in (1, 2, 3):
        piece = lax.dynamic_index_in_dim(both, place_z ^ step, 0, keepdims=False)
        total = total + exchange(piece, far_z=step).astype(jnp.float32)
    total = total.astype(jnp.bfloat16)
    keep = lax.dynamic_index_in_dim(total, core, 1, keepdims=False)
    send = lax.dynamic_index_in_dim(total, 1 - core, 1, keepdims=False)
    owned = pick_two(core, keep, exchange(send, far_core=1), 0)
    return owned.astype(jnp.float32).transpose(2, 0, 1, 3)


def lane_of(shape):
    return lax.broadcasted_iota(jnp.int32, shape, 1)


def dot_lanes(left, right):
    return lax.dot_general(
        left, right, (((1,), (1,)), ((), ())), preferred_element_type=jnp.float32
    )


def head_views(query, key, bias, head):
    lane = lane_of(query.shape)
    mine = (lane >= HDIM) if head else (lane < HDIM)
    spot = 0 if head else HDIM
    zero = jnp.zeros_like(query)
    query_view = jnp.where(mine, query, jnp.where(lane == spot, zero + 1, zero))
    key_view = jnp.where(lane == spot, bias, key)
    return mine, query_view, key_view


def attend_kernel(qkv_ref, bias_ref, mixed_ref, total_ref):
    query = qkv_ref[:, 0:LANES] * jnp.bfloat16(HDIM ** (-0.5))
    key = qkv_ref[:, LANES : 2 * LANES]
    value = qkv_ref[:, 2 * LANES : 3 * LANES]
    bias = bias_ref[...]
    sums, tops = [], []
    for head in range(2):
        mine, query_view, key_view = head_views(query, key, bias, head)
        scores = dot_lanes(query_view, key_view)
        top = jnp.max(scores, axis=1, keepdims=True)
        weight = jnp.exp(scores - top).astype(jnp.bfloat16)
        value_view = jnp.where(mine, value, jnp.ones_like(value))
        sums.append(jnp.dot(weight, value_view, preferred_element_type=jnp.float32))
        tops.append(top)
    low = lane_of(sums[0].shape) < HDIM
    upper = jnp.where(low, sums[0], sums[1])
    lower = jnp.where(low, sums[1], sums[0])
    lower = pltpu.roll(lower, HDIM, 1)
    mixed_ref[...] = (upper / lower).astype(jnp.bfloat16)
    total = jnp.where(low, tops[0], tops[1]) + jnp.log(lower)
    total = jnp.transpose(total)
    total_ref[0, 0:1, :] = total[0:1]
    total_ref[0, 1:2, :] = total[HDIM : HDIM + 1]


def attend_back_kernel(qkv_ref, bias_ref, grad_ref, mixed_ref, total_ref, out_ref):
    scale = HDIM ** (-0.5)
    query = qkv_ref[:, 0:LANES] * jnp.bfloat16(scale)
    key = qkv_ref[:, LANES : 2 * LANES]
    value = qkv_ref[:, 2 * LANES : 3 * LANES]
    bias = bias_ref[...]
    grad = grad_ref[...]
    product = grad.astype(jnp.float32) * mixed_ref[...].astype(jnp.float32)
    grad_query = grad_key = grad_value = None
    for head in range(2):
        mine, query_view, key_view = head_views(query, key, bias, head)
        zero = jnp.zeros_like(query)
        scores = dot_lanes(key_view, query_view)
        probs = jnp.exp(scores - total_ref[0, head : head + 1, :])
        grad_view = jnp.where(mine, grad, zero)
        grad_probs = dot_lanes(value, grad_view)
        ones = jnp.where(mine[0:8], 1.0, 0.0)
        inner = lax.dot_general(
            ones,
            product,
            (((1,), (1,)), ((), ())),
            precision=lax.Precision.HIGHEST,
            preferred_element_type=jnp.float32,
        )
        grad_scores = (probs * (grad_probs - inner[0:1])).astype(jnp.bfloat16)
        one_value = jnp.dot(
            probs.astype(jnp.bfloat16), grad_view, preferred_element_type=jnp.float32
        )
        one_key = jnp.dot(
            grad_scores, jnp.where(mine, query, zero), preferred_element_type=jnp.float32
        )
        one_query = lax.dot_general(
            grad_scores,
            jnp.where(mine, key, zero),
            (((0,), (0,)), ((), ())),
            preferred_element_type=jnp.float32,
        )
        grad_query = one_query if head == 0 else grad_query + one_query
        grad_key = one_key if head == 0 else grad_key + one_key
        grad_value = one_value if head == 0 else grad_value + one_value
    out_ref[:, 0:LANES] = (grad_query * scale).astype(jnp.bfloat16)
    out_ref[:, LANES : 2 * LANES] = grad_key.astype(jnp.bfloat16)
    out_ref[:, 2 * LANES : 3 * LANES] = grad_value.astype(jnp.bfloat16)


def attend_all(qkv, bias, rows):
    images = qkv.shape[0] // rows
    blocks = qkv.shape[1] // (3 * LANES)
    return pl.pallas_call(
        attend_kernel,
        grid=(images, blocks),
        in_specs=[
            pl.BlockSpec((rows, 3 * LANES), lambda i, j: (i, j)),
            pl.BlockSpec((rows, LANES), lambda i, j: (0, 0)),
        ],
        out_specs=[
            pl.BlockSpec((rows, LANES), lambda i, j: (i, j)),
            pl.BlockSpec((1, 8, rows), lambda i, j: (i * blocks + j, 0, 0)),
        ],
        out_shape=[
            jax.ShapeDtypeStruct((images * rows, blocks * LANES), jnp.bfloat16),
            jax.ShapeDtypeStruct((images * blocks, 8, rows), jnp.float32),
        ],
        compiler_params=pltpu.CompilerParams(vmem_limit_bytes=32 * 2**20),
        cost_estimate=pl.CostEstimate(
            flops=images * blocks * 2 * 2 * 2 * rows * rows * LANES * 2,
            transcendentals=images * blocks * 2 * rows * rows,
            bytes_accessed=images * rows * blocks * LANES * 8,
        ),
    )(qkv, bias)


def attend_back_all(qkv, bias, grad, mixed, total, rows):
    images = qkv.shape[0] // rows
    blocks = qkv.shape[1] // (3 * LANES)
    return pl.pallas_call(
        attend_back_kernel,
        grid=(images, blocks),
        in_specs=[
            pl.BlockSpec((rows, 3 * LANES), lambda i, j: (i, j)),
            pl.BlockSpec((rows, LANES), lambda i, j: (0, 0)),
            pl.BlockSpec((rows, LANES), lambda i, j: (i, j)),
            pl.BlockSpec((rows, LANES), lambda i, j: (i, j)),
            pl.BlockSpec((1, 8, rows), lambda i, j: (i * blocks + j, 0, 0)),
        ],
        out_specs=pl.BlockSpec((rows, 3 * LANES), lambda i, j: (i, j)),
        out_shape=jax.ShapeDtypeStruct(qkv.shape, jnp.bfloat16),
        compiler_params=pltpu.CompilerParams(vmem_limit_bytes=48 * 2**20),
        cost_estimate=pl.CostEstimate(
            flops=images * blocks * 2 * 5 * 2 * rows * rows * LANES * 2,
            transcendentals=images * blocks * 2 * rows * rows,
            bytes_accessed=images * rows * blocks * LANES * 16,
        ),
    )(qkv, bias, grad, mixed, total)


def mat(left, right):
    return jnp.dot(left, right, preferred_element_type=jnp.float32)


def mat_far(left, right):
    return lax.dot_general(
        left, right, (((1,), (1,)), ((), ())), preferred_element_type=jnp.float32
    )


def mat_rows(left, right):
    return lax.dot_general(
        left, right, (((0,), (0,)), ((), ())), preferred_element_type=jnp.float32
    )


def flat_norm(values, gain, shift):
    center = values - jnp.mean(values, axis=-1, keepdims=True)
    spread = lax.rsqrt(jnp.mean(center * center, axis=-1, keepdims=True) + EPS)
    unit = center * spread
    return unit * gain + shift, unit, spread


def flat_norm_back(upstream, unit, spread, gain):
    scaled = upstream * gain
    inner = (
        scaled
        - jnp.mean(scaled, axis=-1, keepdims=True)
        - unit * jnp.mean(scaled * unit, axis=-1, keepdims=True)
    )
    return spread * inner, jnp.sum(upstream * unit, axis=0), jnp.sum(upstream, axis=0)


def whole_images(
    images,
    cotangent,
    slot_live,
    first_gain,
    first_shift,
    query_weight,
    query_bias,
    key_weight,
    value_weight,
    value_bias,
    output_weight,
    output_bias,
    second_gain,
    second_shift,
    up_weight,
    up_bias,
    down_weight,
    down_bias,
):
    low = jnp.bfloat16
    dp_place = lax.axis_index("dp")
    place_y = lax.axis_index("tensor")
    core, place_x, place_z = dp_place % 2, (dp_place // 2) % 2, dp_place // 4
    strip, width = images.shape[1:]
    half = -(-strip // HALF_PAD) * HALF_PAD
    rows = 2 * half
    depth, head_cols = query_weight.shape
    units = up_weight.shape[1]
    head_part, unit_part = head_cols // 4, units // 4

    stacked = jnp.stack([images, cotangent])
    stacked = jnp.pad(stacked, ((0, 0), (0, 0), (0, half - strip), (0, 0)))
    mine = lax.dynamic_index_in_dim(stacked, place_y, 1, keepdims=False)
    theirs = lax.dynamic_index_in_dim(stacked, 1 - place_y, 1, keepdims=False)
    arrived = exchange(theirs, far_y=1)
    whole = jnp.stack([mine, arrived], 1).reshape(2, rows, width)

    def four(weight):
        return weight.reshape(depth, 2, 2, -1)

    def by_core(parts):
        return jnp.concatenate(parts, 3).transpose(1, 2, 0, 3)

    shard_one = by_core([four(query_weight), four(key_weight), four(value_weight)])
    shard_two = by_core([four(output_weight.T), four(up_weight)])
    shard_three = by_core([four(down_weight.T)])

    start_one = gather_start(shard_one, core)
    line_one = gather_z(start_one, place_z)
    cross_one = gather_plane_one(line_one)
    parts_one = gather_plane_two(line_one, cross_one, place_x)
    qkv_full = gather_finish(parts_one, place_x)

    start_two = after(gather_start(shard_two, core), line_one)
    line_two = gather_z(start_two, place_z)
    cross_two = gather_plane_one(after(line_two, *parts_one))
    parts_two = gather_plane_two(line_two, cross_two, place_x)
    pair_full = gather_finish(parts_two, place_x)
    pair_full = pair_full.reshape(width, 4, head_part + unit_part)
    output_full = pair_full[:, :, :head_part].reshape(width, 4 * head_part)
    upper_full = pair_full[:, :, head_part:].reshape(width, 4 * unit_part)

    start_three = after(gather_start(shard_three, core), line_two)
    line_three = gather_z(start_three, place_z)
    cross_three = gather_plane_one(after(line_three, *parts_two))
    parts_three = gather_plane_two(line_three, cross_three, place_x)
    lower_full = gather_finish(parts_three, place_x)

    def local_columns(vector):
        wide = vector.shape[0] // 8
        table = vector.astype(jnp.float32).reshape(2, 2, 2, wide)
        table = lax.dynamic_index_in_dim(table, core, 1, keepdims=False)
        table = jnp.where(place_y == 0, table, table[::-1])
        return table.transpose(1, 0, 2)

    def spread_columns(vector):
        wide = vector.shape[0] // 4
        table = vector.reshape(2, 2, wide).transpose(1, 0, 2)
        table = jnp.where(place_y == 0, table, table[::-1])
        table = jnp.stack(
            [jnp.where(core == 0, table, 0.0), jnp.where(core == 1, table, 0.0)], 1
        )
        return table.reshape(-1)

    gain_one, shift_one = first_gain.astype(jnp.float32), first_shift.astype(jnp.float32)
    gain_two, shift_two = second_gain.astype(jnp.float32), second_shift.astype(jnp.float32)
    query_shift = local_columns(query_bias).reshape(4, 1, head_part)
    value_shift = local_columns(value_bias).reshape(4, 1, head_part)
    qkv_shift = jnp.concatenate(
        [query_shift, jnp.zeros_like(query_shift), value_shift], 1
    ).reshape(-1)
    up_shift = local_columns(up_bias).reshape(-1)

    row = jnp.arange(rows)
    in_half = row % half
    spot = jnp.where(row < half, place_y, 1 - place_y) * strip + in_half
    ok = (in_half < strip) & (spot < VALID)
    live = lax.dynamic_index_in_dim(slot_live, place_y, 0, keepdims=False).astype(jnp.float32)
    row_mask = (live * ok.astype(jnp.float32))[:, None]
    key_bias = jnp.broadcast_to(
        jnp.where(ok, 0.0, NEGATIVE).astype(low)[:, None], (rows, LANES)
    )

    def pair_up(own):
        return jnp.concatenate([own, exchange(own, far_core=1)], 0)

    def pair_sum(partial):
        other = exchange(partial[rows:].astype(low), far_core=1)
        return partial[:rows] + other.astype(jnp.float32)

    resid = whole[0].astype(jnp.float32)
    grad_top = row_mask * whole[1].astype(jnp.float32)
    fed_grad = grad_top.astype(low)
    fed_rows = pair_up(fed_grad)
    normed, unit_one, spread_one = flat_norm(resid, gain_one, shift_one)
    normed_rows = pair_up(normed.astype(low))
    qkv = (mat(normed_rows, qkv_full) + qkv_shift).astype(low)
    mixed, totals = attend_all(qkv, key_bias, rows)
    attended = pair_sum(mat_far(mixed, output_full)) + output_bias.astype(jnp.float32)
    middle = row_mask * (resid + attended)
    second, unit_two, spread_two = flat_norm(middle, gain_two, shift_two)
    second_rows = pair_up(second.astype(low))
    hidden = mat(second_rows, upper_full) + up_shift
    sigma = jax.nn.sigmoid(SLOPE * hidden)
    active = (hidden * sigma).astype(low)
    slope = (sigma + SLOPE * hidden * sigma * (1.0 - sigma)).astype(low)

    def weight_pieces(left, right):
        wide = right.shape[1] // 4
        return [
            mat_rows(left, right[:, at * wide : (at + 1) * wide]).astype(low) for at in range(4)
        ]

    lower_owned = scatter_sum(weight_pieces(fed_rows, active), place_x, place_z, core)
    hidden_grad = (mat(fed_rows, lower_full) * slope.astype(jnp.float32)).astype(low)
    upper_owned = scatter_sum(weight_pieces(second_rows, hidden_grad), place_x, place_z, core)
    second_grad = pair_sum(mat_far(hidden_grad, upper_full))
    fed = pair_sum(mat_far(active, lower_full)) + down_bias.astype(jnp.float32)
    layer_own = (row_mask * (middle + fed)).astype(low)
    middle_back, gain_two_grad, shift_two_grad = flat_norm_back(
        second_grad, unit_two, spread_two, gain_two
    )
    middle_grad = row_mask * (grad_top + middle_back)
    attended_grad = middle_grad.astype(low)
    attended_rows = pair_up(attended_grad)
    grad_mixed = mat(attended_rows, output_full).astype(low)
    output_pieces = weight_pieces(attended_rows, mixed)
    grad_qkv = attend_back_all(qkv, key_bias, grad_mixed, mixed, totals, rows)
    early = jnp.concatenate(
        [
            column_flat(attended_grad),
            gain_two_grad,
            shift_two_grad,
            column_flat(fed_grad),
            spread_columns(column_flat(hidden_grad)),
        ]
    )
    qkv_pieces = weight_pieces(normed_rows, grad_qkv)
    last_pieces = [
        jnp.concatenate([left, right], 1) for left, right in zip(qkv_pieces, output_pieces)
    ]
    last_owned = scatter_sum(last_pieces, place_x, place_z, core)
    normed_grad = pair_sum(mat_far(grad_qkv, qkv_full))
    first_back, gain_one_grad, shift_one_grad = flat_norm_back(
        normed_grad, unit_one, spread_one, gain_one
    )
    images_own = middle_grad + first_back
    qkv_sums = column_flat(grad_qkv).reshape(4, 3, head_part)
    late = jnp.concatenate(
        [
            gain_one_grad,
            shift_one_grad,
            spread_columns(qkv_sums[:, 0].reshape(-1)),
            spread_columns(qkv_sums[:, 2].reshape(-1)),
        ]
    )

    def to_strips(own):
        send = own[half : half + strip]
        return pick_two(place_y, own[:strip], exchange(send, far_y=1), 0)

    layer_out = to_strips(layer_own)
    images_grad = to_strips(images_own.astype(low)).astype(jnp.float32)
    early = lax.psum(early, BOTH)
    late = lax.psum(late, BOTH)
    owned = last_owned.reshape(depth, 2, 2, 4, head_part)

    def full_columns(at):
        return owned[:, :, :, at].reshape(depth, head_cols)

    return (
        layer_out,
        images_grad,
        late[:width],
        late[width : 2 * width],
        full_columns(0),
        late[2 * width : 3 * width],
        full_columns(1),
        full_columns(2),
        late[3 * width :],
        full_columns(3).T,
        early[:width],
        early[width : 2 * width],
        early[2 * width : 3 * width],
        upper_owned.reshape(depth, units),
        early[4 * width :],
        lower_owned.reshape(depth, units).T,
        early[3 * width : 4 * width],
    )


def column_flat(values):
    return jnp.sum(values.astype(jnp.float32), axis=0)


def pick(mesh):
    sizes = dict(mesh.shape)
    if sizes["dp"] == 16 and sizes["tensor"] == 2:
        return whole_images
    return local


def solution(mesh):
    in_specs = (
        P("dp", "tensor", None),
        P("dp", "tensor", None),
        P("dp"),
        P(),
        P(),
        P("dp", "tensor"),
        P(),
        P("dp", "tensor"),
        P("dp", "tensor"),
        P(),
        P("tensor", "dp"),
        P(),
        P(),
        P(),
        P("dp", "tensor"),
        P(),
        P("tensor", "dp"),
        P(),
    )
    out_specs = (
        P("dp", "tensor", None),
        P("dp", "tensor", None),
        P(),
        P(),
        P("dp", "tensor"),
        P(),
        P("dp", "tensor"),
        P("dp", "tensor"),
        P(),
        P("tensor", "dp"),
        P(),
        P(),
        P(),
        P("dp", "tensor"),
        P(),
        P("tensor", "dp"),
        P(),
    )
    return jax.shard_map(pick(mesh), mesh=mesh, in_specs=in_specs, out_specs=out_specs, check_vma=False)
```

```python
import jax
import jax.numpy as jnp
from jax import lax
from jax.experimental import pallas as pl
from jax.experimental.pallas import tpu as pltpu
from jax.sharding import PartitionSpec as P

HDIM = 64
VALID = 577


EPS = 1e-05
NEGATIVE = -1e30
SLOPE = 1.702


def layer_norm(values, gain, shift):
    center = values - jnp.mean(values, axis=-1, keepdims=True)
    spread = lax.rsqrt(jnp.mean(center * center, axis=-1, keepdims=True) + EPS)
    unit = center * spread
    return (unit * gain + shift, unit, spread)


def norm_back(upstream, unit, spread, gain):
    scaled = upstream * gain
    inner = (
        scaled
        - jnp.mean(scaled, axis=-1, keepdims=True)
        - unit * jnp.mean(scaled * unit, axis=-1, keepdims=True)
    )
    return (spread * inner, jnp.sum(upstream * unit, axis=(0, 1)), jnp.sum(upstream, axis=(0, 1)))


def dense(left, right):
    return jnp.einsum("spa,ab->spb", left, right, preferred_element_type=jnp.float32)


def project_back(left, right):
    return jnp.einsum("spa,ba->spb", left, right, preferred_element_type=jnp.float32)


def outer(left, right):
    return jnp.einsum("spa,spb->ab", left, right, preferred_element_type=jnp.float32)


def column_sum(values):
    return jnp.sum(values.astype(jnp.float32), axis=(0, 1))


def widen(piece, length, start):
    return lax.dynamic_update_slice_in_dim(jnp.zeros((length,), jnp.float32), piece, start, 0)


def split_heads(block):
    return block.reshape(block.shape[0], -1, HDIM)


def scores_of(query, key, key_ok):
    raw = jnp.einsum(
        "qhe,khe->hqk", split_heads(query), split_heads(key), preferred_element_type=jnp.float32
    )
    return jnp.where(key_ok[None, None, :], raw * HDIM ** (-0.5), NEGATIVE)


def attend(query, key, value, key_ok):
    scores = scores_of(query, key, key_ok)
    top = jnp.max(scores, axis=-1, keepdims=True)
    total = top + jnp.log(jnp.sum(jnp.exp(scores - top), axis=-1, keepdims=True))
    probs = jnp.exp(scores - total).astype(jnp.bfloat16)
    mixed = jnp.einsum(
        "hqk,khe->qhe", probs, split_heads(value), preferred_element_type=jnp.float32
    )
    return (mixed.reshape(query.shape[0], -1).astype(jnp.bfloat16), total)


def attend_back(query, key, value, grad_mixed, total, key_ok):
    scores = scores_of(query, key, key_ok)
    probs = jnp.exp(scores - total)
    grad_heads = split_heads(grad_mixed)
    grad_probs = jnp.einsum(
        "qhe,khe->hqk", grad_heads, split_heads(value), preferred_element_type=jnp.float32
    )
    grad_value = jnp.einsum(
        "hqk,qhe->khe", probs.astype(jnp.bfloat16), grad_heads, preferred_element_type=jnp.float32
    )
    grad_scores = (
        probs * (grad_probs - jnp.sum(probs * grad_probs, axis=-1, keepdims=True))
    ).astype(jnp.bfloat16)
    grad_query = jnp.einsum(
        "hqk,khe->qhe", grad_scores, split_heads(key), preferred_element_type=jnp.float32
    ) * HDIM ** (-0.5)
    grad_key = jnp.einsum(
        "hqk,qhe->khe", grad_scores, split_heads(query), preferred_element_type=jnp.float32
    ) * HDIM ** (-0.5)
    length = query.shape[0]
    return (
        grad_query.reshape(length, -1).astype(jnp.bfloat16),
        grad_key.reshape(length, -1).astype(jnp.bfloat16),
        grad_value.reshape(length, -1).astype(jnp.bfloat16),
    )


def local(
    images,
    cotangent,
    slot_live,
    first_gain,
    first_shift,
    query_weight,
    query_bias,
    key_weight,
    value_weight,
    value_bias,
    output_weight,
    output_bias,
    second_gain,
    second_shift,
    up_weight,
    up_bias,
    down_weight,
    down_bias,
):
    slots, strip, width = images.shape
    tensor_count = lax.axis_size("tensor")
    tensor_place = lax.axis_index("tensor")
    seq_len = strip * tensor_count
    positions = tensor_place * strip + jnp.arange(strip)
    row_mask = (
        slot_live.astype(jnp.float32)[:, None, None]
        * (positions < VALID).astype(jnp.float32)[None, :, None]
    )
    key_ok = jnp.arange(seq_len) < VALID
    query_full, key_full, value_full, upper_full, output_full, lower_full = (
        lax.all_gather(query_weight, "dp", axis=0, tiled=True),
        lax.all_gather(key_weight, "dp", axis=0, tiled=True),
        lax.all_gather(value_weight, "dp", axis=0, tiled=True),
        lax.all_gather(up_weight, "dp", axis=0, tiled=True),
        lax.all_gather(output_weight, "dp", axis=1, tiled=True),
        lax.all_gather(down_weight, "dp", axis=1, tiled=True),
    )
    head_cols = query_full.shape[1]
    head_start = tensor_place * head_cols
    gain_one = first_gain.astype(jnp.float32)
    shift_one = first_shift.astype(jnp.float32)
    gain_two = second_gain.astype(jnp.float32)
    shift_two = second_shift.astype(jnp.float32)
    query_shift = lax.dynamic_slice_in_dim(query_bias.astype(jnp.float32), head_start, head_cols)
    value_shift = lax.dynamic_slice_in_dim(value_bias.astype(jnp.float32), head_start, head_cols)
    resid = images.astype(jnp.float32)
    normed, unit_one, spread_one = layer_norm(resid, gain_one, shift_one)
    normed_rows = lax.all_gather(normed.astype(jnp.bfloat16), "tensor", axis=1, tiled=True)
    queries = (dense(normed_rows, query_full) + query_shift).astype(jnp.bfloat16)
    keys_low = dense(normed_rows, key_full).astype(jnp.bfloat16)
    values_low = (dense(normed_rows, value_full) + value_shift).astype(jnp.bfloat16)
    mixed, totals = lax.map(
        lambda items: attend(items[0], items[1], items[2], key_ok), (queries, keys_low, values_low)
    )
    attended = lax.psum_scatter(
        dense(mixed, output_full), "tensor", scatter_dimension=1, tiled=True
    ) + output_bias.astype(jnp.float32)
    middle = row_mask * (resid + attended)
    second, unit_two, spread_two = layer_norm(middle, gain_two, shift_two)
    second_low = second.astype(jnp.bfloat16)
    grad_top = row_mask * cotangent.astype(jnp.float32)
    fed_grad = grad_top.astype(jnp.bfloat16)
    down_shift = down_bias.astype(jnp.float32)
    units = upper_full.shape[1]
    second_rows = lax.all_gather(second_low, "tensor", axis=1, tiled=True)
    up_shift = lax.dynamic_slice_in_dim(up_bias.astype(jnp.float32), tensor_place * units, units)
    hidden = dense(second_rows, upper_full) + up_shift
    sigma = jax.nn.sigmoid(SLOPE * hidden)
    active = (hidden * sigma).astype(jnp.bfloat16)
    fed = (
        lax.psum_scatter(
            dense(active, lower_full).astype(jnp.bfloat16),
            "tensor",
            scatter_dimension=1,
            tiled=True,
        ).astype(jnp.float32)
        + down_shift
    )
    fed_rows = lax.all_gather(fed_grad, "tensor", axis=1, tiled=True)
    grad_active = project_back(fed_rows, lower_full)
    lower_grad = outer(active, fed_rows)
    hidden_grad = (grad_active * (sigma + SLOPE * hidden * sigma * (1.0 - sigma))).astype(
        jnp.bfloat16
    )
    upper_grad = outer(second_rows, hidden_grad)
    up_bias_grad = widen(column_sum(hidden_grad), up_bias.shape[0], tensor_place * units)
    second_grad = lax.psum_scatter(
        project_back(hidden_grad, upper_full), "tensor", scatter_dimension=1, tiled=True
    )
    layer_out = (row_mask * (middle + fed)).astype(jnp.bfloat16)
    down_bias_grad = column_sum(fed_grad)
    middle_back, gain_two_grad, shift_two_grad = norm_back(
        second_grad, unit_two, spread_two, gain_two
    )
    middle_grad = row_mask * (grad_top + middle_back)
    attended_grad = middle_grad.astype(jnp.bfloat16)
    output_bias_grad = column_sum(attended_grad)
    attended_rows = lax.all_gather(attended_grad, "tensor", axis=1, tiled=True)
    grad_mixed = project_back(attended_rows, output_full).astype(jnp.bfloat16)
    output_grad = outer(mixed, attended_rows)
    grad_query, grad_key, grad_value = lax.map(
        lambda items: attend_back(items[0], items[1], items[2], items[3], items[4], key_ok),
        (queries, keys_low, values_low, grad_mixed, totals),
    )
    query_grad = outer(normed_rows, grad_query)
    key_grad = outer(normed_rows, grad_key)
    value_grad = outer(normed_rows, grad_value)
    query_bias_grad = widen(column_sum(grad_query), width, head_start)
    value_bias_grad = widen(column_sum(grad_value), width, head_start)
    normed_terms = (
        project_back(grad_query, query_full)
        + project_back(grad_key, key_full)
        + project_back(grad_value, value_full)
    )
    normed_grad = lax.psum_scatter(
        normed_terms.astype(jnp.bfloat16), "tensor", scatter_dimension=1, tiled=True
    ).astype(jnp.float32)
    first_back, gain_one_grad, shift_one_grad = norm_back(
        normed_grad, unit_one, spread_one, gain_one
    )
    images_grad = middle_grad + first_back
    query_owned, key_owned, value_owned, upper_owned, output_owned, lower_owned = (
        lax.psum_scatter(
            query_grad.astype(jnp.bfloat16), "dp", scatter_dimension=0, tiled=True
        ).astype(jnp.float32),
        lax.psum_scatter(
            key_grad.astype(jnp.bfloat16), "dp", scatter_dimension=0, tiled=True
        ).astype(jnp.float32),
        lax.psum_scatter(
            value_grad.astype(jnp.bfloat16), "dp", scatter_dimension=0, tiled=True
        ).astype(jnp.float32),
        lax.psum_scatter(
            upper_grad.astype(jnp.bfloat16), "dp", scatter_dimension=0, tiled=True
        ).astype(jnp.float32),
        lax.psum_scatter(
            output_grad.astype(jnp.bfloat16), "dp", scatter_dimension=1, tiled=True
        ).astype(jnp.float32),
        lax.psum_scatter(
            lower_grad.astype(jnp.bfloat16), "dp", scatter_dimension=1, tiled=True
        ).astype(jnp.float32),
    )
    vector_sums = lax.psum(
        (
            gain_one_grad,
            shift_one_grad,
            query_bias_grad,
            value_bias_grad,
            output_bias_grad,
            gain_two_grad,
            shift_two_grad,
            up_bias_grad,
            down_bias_grad,
        ),
        ("dp", "tensor"),
    )
    (
        gain_one_total,
        shift_one_total,
        query_bias_total,
        value_bias_total,
        output_bias_total,
        gain_two_total,
        shift_two_total,
        up_bias_total,
        down_bias_total,
    ) = vector_sums
    return (
        layer_out,
        images_grad,
        gain_one_total,
        shift_one_total,
        query_owned,
        query_bias_total,
        key_owned,
        value_owned,
        value_bias_total,
        output_owned,
        output_bias_total,
        gain_two_total,
        shift_two_total,
        upper_owned,
        up_bias_total,
        lower_owned,
        down_bias_total,
    )


BOTH = ("dp", "tensor")
HALF_PAD = 8
LANES = 128
LOW = jnp.bfloat16
VMEM_ROOM = 56 * 2**20


def exchange(value, far_z=0, far_x=0, far_core=0, far_y=0):
    pairs = []
    for place in range(32):
        other = place ^ (far_z * 8 + far_x * 4 + far_core * 2 + far_y)
        pairs.append((place, other))
    return lax.ppermute(value, BOTH, pairs)


def pick_two(bit, own, other, axis):
    first = jnp.where(bit == 0, own, other)
    last = jnp.where(bit == 0, other, own)
    return jnp.stack([first, last], axis)


def after(value, *others):
    return lax.optimization_barrier((value, *others))[0]


def pack(places, sources, shapes, plan):
    def kernel(places_ref, *refs):
        ins, outs = refs[: len(sources)], refs[len(sources) :]
        spots = [places_ref[at] for at in range(4)]
        for at, take, to, put in plan:
            outs[to][put(*spots)] = ins[at][take(*spots)]

    return pl.pallas_call(
        kernel,
        in_specs=[pl.BlockSpec(memory_space=pltpu.SMEM)]
        + [pl.BlockSpec(memory_space=pltpu.VMEM)] * len(sources),
        out_specs=[pl.BlockSpec(memory_space=pltpu.VMEM)] * len(shapes),
        out_shape=[jax.ShapeDtypeStruct(shape, LOW) for shape in shapes],
        compiler_params=pltpu.CompilerParams(vmem_limit_bytes=VMEM_ROOM),
        cost_estimate=pl.CostEstimate(
            flops=0,
            transcendentals=0,
            bytes_accessed=sum(2 * source.size * 2 for source in sources),
        ),
    )(places, *sources)


def gather_weights(keep, send, places, core):
    deep, wide = keep.shape[1:]
    every = slice(None)
    piece = pick_two(core, keep, exchange(send, far_core=1), 1).reshape(2, 2 * deep, wide)
    line = [piece] + [exchange(piece, far_z=step) for step in (1, 2, 3)]
    rows = 2 * deep
    plan = []
    for step in range(4):
        for part in range(2):
            plan.append(
                (
                    step,
                    lambda z, x, c, y, part=part: part,
                    part,
                    lambda z, x, c, y, step=step: z ^ step,
                )
            )
    one, two = pack(places, line, [(4, rows, wide)] * 2, plan)
    one_x, two_y = exchange(one, far_x=1), exchange(two, far_y=1)
    plan = [
        (0, lambda z, x, c, y: every, 0, lambda z, x, c, y: x),
        (1, lambda z, x, c, y: every, 0, lambda z, x, c, y: 1 - x),
        (2, lambda z, x, c, y: every, 1, lambda z, x, c, y: 0),
        (3, lambda z, x, c, y: every, 1, lambda z, x, c, y: 1),
    ]
    one_pair, two_pair = pack(places, [one, one_x, two, two_y], [(2, 4, rows, wide)] * 2, plan)
    one_y, two_x = exchange(one_pair, far_y=1), exchange(two_pair, far_x=1)
    most = 3 * wide // 4
    plan = []
    for to, low, high in ((0, 0, most), (1, most, wide)):
        span = high - low
        for place_z in range(4):
            for far in range(2):
                for number in range(2):
                    plan.append(
                        (
                            number,
                            lambda z, x, c, y, a=far, p=place_z, lo=low, hi=high: (
                                a,
                                p,
                                every,
                                slice(lo, hi),
                            ),
                            to,
                            lambda z, x, c, y, a=far, p=place_z, s=span, n=number: (
                                p,
                                a,
                                every,
                                slice(n * s, n * s + s),
                            ),
                        )
                    )
                    plan.append(
                        (
                            2 + far,
                            lambda z, x, c, y, n=number, p=place_z, lo=low, hi=high: (
                                n,
                                p,
                                every,
                                slice(lo, hi),
                            ),
                            to,
                            lambda z, x, c, y, f=far, p=place_z, s=span, n=number: (
                                p,
                                x ^ f,
                                every,
                                slice((2 + n) * s, (3 + n) * s),
                            ),
                        )
                    )
    shapes = [(4, 2, rows, 4 * most), (4, 2, rows, 4 * (wide - most))]
    full, rest = pack(places, [one_pair, one_y, two_pair, two_x], shapes, plan)
    return full.reshape(8 * rows, -1), rest.reshape(8 * rows, -1)


def low_add(*values):
    total = values[0].astype(jnp.float32)
    for value in values[1:]:
        total = total + value.astype(jnp.float32)
    return total


def line_kernel(one_ref, one_a, one_b, two_ref, two_a, two_b, own_ref, *send_refs):
    tall = own_ref.shape[1]
    for step in range(4):
        rows = slice(step * tall, (step + 1) * tall)
        one = low_add(one_ref[0, rows], one_a[0, rows], one_b[rows])
        two = low_add(two_ref[0, rows], two_a[0, rows], two_b[rows])
        if step == 0:
            own_ref[0] = one
            own_ref[1] = two
        else:
            send_refs[step - 1][0] = one.astype(LOW)
            send_refs[step - 1][1] = two.astype(LOW)


def scatter_sum(send_one, send_two, keep_one, keep_two, core):
    lines, wide = send_one.shape[1:]
    tall = lines // 4
    one_y, two_x = exchange(send_one, far_y=1), exchange(send_two, far_x=1)
    one_x = exchange(low_add(keep_one[1], one_y[1]).astype(LOW), far_x=1)
    two_y = exchange(low_add(keep_two[1], two_x[1]).astype(LOW), far_y=1)
    first = pl.BlockSpec((1, lines, wide), lambda i: (0, 0, 0))
    flat = pl.BlockSpec((lines, wide), lambda i: (0, 0))
    piece = pl.BlockSpec((2, tall, wide), lambda i: (0, 0, 0))
    sends = pl.pallas_call(
        line_kernel,
        grid=(1,),
        in_specs=[first, first, flat, first, first, flat],
        out_specs=[piece] * 4,
        out_shape=[jax.ShapeDtypeStruct((2, tall, wide), jnp.float32)]
        + [jax.ShapeDtypeStruct((2, tall, wide), LOW)] * 3,
        compiler_params=pltpu.CompilerParams(vmem_limit_bytes=VMEM_ROOM),
        cost_estimate=pl.CostEstimate(
            flops=lines * wide * 4, transcendentals=0, bytes_accessed=lines * wide * 18
        ),
    )(keep_one, one_y, one_x, keep_two, two_x, two_y)
    total = low_add(
        sends[0], *[exchange(sends[step], far_z=step) for step in (1, 2, 3)]
    ).reshape(2, 2, tall // 2, wide)
    keep = lax.dynamic_index_in_dim(total, core, 1, keepdims=False)
    send = lax.dynamic_index_in_dim(total, 1 - core, 1, keepdims=False)
    far = exchange(send.astype(LOW), far_core=1).astype(jnp.float32)
    return pick_two(core, keep, far, 0)


def vector_sum(vector):
    for step in ({"far_core": 1}, {"far_y": 1}, {"far_x": 1}):
        vector = vector + exchange(vector, **step)
    others = [exchange(vector, far_z=step) for step in (1, 2, 3)]
    return vector + others[0] + others[1] + others[2]


def mat_far(left, right):
    return lax.dot_general(
        left, right, (((1,), (1,)), ((), ())), preferred_element_type=jnp.float32
    )


def mat_rows(left, right):
    return lax.dot_general(
        left, right, (((0,), (0,)), ((), ())), preferred_element_type=jnp.float32
    )


def pair_kernel(places_ref, own_ref, far_ref, rows_ref, turned_ref):
    spots = [places_ref[0] ^ (block % 4) for block in range(8)]
    for block in range(8):
        at = spots[block] * 2 + (places_ref[1] ^ (block // 4))
        start = pl.multiple_of(at * LANES, LANES)
        for half, ref in enumerate((own_ref, far_ref)):
            turned_ref[half, :, block * LANES : (block + 1) * LANES] = ref[:, pl.ds(start, LANES)]
    rows_ref[0] = own_ref[...]
    rows_ref[1] = far_ref[...]


def pair_up(places, own):
    rows, width = own.shape
    made = pl.pallas_call(
        pair_kernel,
        in_specs=[pl.BlockSpec(memory_space=pltpu.SMEM)]
        + [pl.BlockSpec(memory_space=pltpu.VMEM)] * 2,
        out_specs=[pl.BlockSpec(memory_space=pltpu.VMEM)] * 2,
        out_shape=[jax.ShapeDtypeStruct((2, rows, width), LOW)] * 2,
        compiler_params=pltpu.CompilerParams(vmem_limit_bytes=VMEM_ROOM),
        cost_estimate=pl.CostEstimate(
            flops=0, transcendentals=0, bytes_accessed=own.size * 12
        ),
    )(places, own, exchange(own, far_core=1))
    return [array.reshape(2 * rows, width) for array in made]


def half_sums(left, right, rows):
    send = mat_far(left[rows:], right).astype(LOW)
    far = exchange(send, far_core=1)
    return mat_far(left[:rows], right) + far.astype(jnp.float32)


def scatter_grads(pairs, core):
    lines = pairs[0][0].shape[1] // 2

    def grads(row_far, part, y_far):
        made = []
        for left, cut in pairs:
            left = left if row_far is None else left[:, row_far * lines : (row_far + 1) * lines]
            made.append(mat_rows(left, cut(part, y_far)).astype(LOW))
        return made[0] if len(made) == 1 else jnp.concatenate(made, 1)

    send_one = grads(None, 0, 1).reshape(2, lines, -1)
    send_two = jnp.stack([grads(1, 1, 0), grads(1, 1, 1)])
    keep_one = grads(None, 0, 0).reshape(2, lines, -1)
    keep_two = jnp.stack([grads(0, 1, 0), grads(0, 1, 1)])
    return scatter_sum(send_one, send_two, keep_one, keep_two, core)


def lane_of(shape):
    return lax.broadcasted_iota(jnp.int32, shape, 1)


def head_views(query, key, bias, head):
    lane = lane_of(query.shape)
    mine = (lane >= HDIM) if head else (lane < HDIM)
    spot = 0 if head else HDIM
    zero = jnp.zeros_like(query)
    query_view = jnp.where(mine, query, jnp.where(lane == spot, zero + 1, zero))
    key_view = jnp.where(lane == spot, bias, key)
    return mine, query_view, key_view


def attend_kernel(qkv_ref, bias_ref, mixed_ref, total_ref):
    query = qkv_ref[:, 0:LANES] * jnp.bfloat16(HDIM ** (-0.5))
    key = qkv_ref[:, LANES : 2 * LANES]
    value = qkv_ref[:, 2 * LANES : 3 * LANES]
    bias = bias_ref[...]
    sums, tops = [], []
    for head in range(2):
        mine, query_view, key_view = head_views(query, key, bias, head)
        scores = mat_far(query_view, key_view)
        top = jnp.max(scores, axis=1, keepdims=True)
        weight = jnp.exp(scores - top).astype(LOW)
        value_view = jnp.where(mine, value, jnp.ones_like(value))
        sums.append(jnp.dot(weight, value_view, preferred_element_type=jnp.float32))
        tops.append(top)
    low = lane_of(sums[0].shape) < HDIM
    upper = jnp.where(low, sums[0], sums[1])
    lower = jnp.where(low, sums[1], sums[0])
    lower = pltpu.roll(lower, HDIM, 1)
    mixed_ref[...] = (upper / lower).astype(LOW)
    total = jnp.where(low, tops[0], tops[1]) + jnp.log(lower)
    total = jnp.transpose(total)
    total_ref[0, 0:1, :] = total[0:1]
    total_ref[0, 1:2, :] = total[HDIM : HDIM + 1]


def attend_back_kernel(qkv_ref, bias_ref, grad_ref, mixed_ref, total_ref, out_ref):
    scale = HDIM ** (-0.5)
    query = qkv_ref[:, 0:LANES] * jnp.bfloat16(scale)
    key = qkv_ref[:, LANES : 2 * LANES]
    value = qkv_ref[:, 2 * LANES : 3 * LANES]
    bias = bias_ref[...]
    grad = grad_ref[...]
    product = grad.astype(jnp.float32) * mixed_ref[...].astype(jnp.float32)
    grad_query = grad_key = grad_value = None
    for head in range(2):
        mine, query_view, key_view = head_views(query, key, bias, head)
        zero = jnp.zeros_like(query)
        scores = mat_far(key_view, query_view)
        probs = jnp.exp(scores - total_ref[0, head : head + 1, :])
        grad_view = jnp.where(mine, grad, zero)
        grad_probs = mat_far(value, grad_view)
        ones = jnp.where(mine[0:8], 1.0, 0.0)
        inner = lax.dot_general(
            ones,
            product,
            (((1,), (1,)), ((), ())),
            precision=lax.Precision.HIGHEST,
            preferred_element_type=jnp.float32,
        )
        grad_scores = (probs * (grad_probs - inner[0:1])).astype(LOW)
        one_value = jnp.dot(probs.astype(LOW), grad_view, preferred_element_type=jnp.float32)
        one_key = jnp.dot(
            grad_scores, jnp.where(mine, query, zero), preferred_element_type=jnp.float32
        )
        one_query = mat_rows(grad_scores, jnp.where(mine, key, zero))
        grad_query = one_query if head == 0 else grad_query + one_query
        grad_key = one_key if head == 0 else grad_key + one_key
        grad_value = one_value if head == 0 else grad_value + one_value
    out_ref[:, 0:LANES] = (grad_query * scale).astype(LOW)
    out_ref[:, LANES : 2 * LANES] = grad_key.astype(LOW)
    out_ref[:, 2 * LANES : 3 * LANES] = grad_value.astype(LOW)


def attend_all(qkv, bias, rows):
    images = qkv.shape[0] // rows
    blocks = qkv.shape[1] // (3 * LANES)
    return pl.pallas_call(
        attend_kernel,
        grid=(images, blocks),
        in_specs=[
            pl.BlockSpec((rows, 3 * LANES), lambda i, j: (i, j)),
            pl.BlockSpec((rows, LANES), lambda i, j: (0, 0)),
        ],
        out_specs=[
            pl.BlockSpec((rows, LANES), lambda i, j: (i, j)),
            pl.BlockSpec((1, 8, rows), lambda i, j: (i * blocks + j, 0, 0)),
        ],
        out_shape=[
            jax.ShapeDtypeStruct((images * rows, blocks * LANES), LOW),
            jax.ShapeDtypeStruct((images * blocks, 8, rows), jnp.float32),
        ],
        compiler_params=pltpu.CompilerParams(vmem_limit_bytes=VMEM_ROOM),
        cost_estimate=pl.CostEstimate(
            flops=images * blocks * 2 * 2 * 2 * rows * rows * LANES * 2,
            transcendentals=images * blocks * 2 * rows * rows,
            bytes_accessed=images * rows * blocks * LANES * 8,
        ),
    )(qkv, bias)


def attend_back_all(qkv, bias, grad, mixed, total, rows):
    images = qkv.shape[0] // rows
    blocks = qkv.shape[1] // (3 * LANES)
    return pl.pallas_call(
        attend_back_kernel,
        grid=(images, blocks),
        in_specs=[
            pl.BlockSpec((rows, 3 * LANES), lambda i, j: (i, j)),
            pl.BlockSpec((rows, LANES), lambda i, j: (0, 0)),
            pl.BlockSpec((rows, LANES), lambda i, j: (i, j)),
            pl.BlockSpec((rows, LANES), lambda i, j: (i, j)),
            pl.BlockSpec((1, 8, rows), lambda i, j: (i * blocks + j, 0, 0)),
        ],
        out_specs=pl.BlockSpec((rows, 3 * LANES), lambda i, j: (i, j)),
        out_shape=jax.ShapeDtypeStruct(qkv.shape, LOW),
        compiler_params=pltpu.CompilerParams(vmem_limit_bytes=VMEM_ROOM),
        cost_estimate=pl.CostEstimate(
            flops=images * blocks * 2 * 5 * 2 * rows * rows * LANES * 2,
            transcendentals=images * blocks * 2 * rows * rows,
            bytes_accessed=images * rows * blocks * LANES * 16,
        ),
    )(qkv, bias, grad, mixed, total)


def mat(left, right):
    return jnp.dot(left, right, preferred_element_type=jnp.float32)


def flat_norm(values, gain, shift):
    center = values - jnp.mean(values, axis=-1, keepdims=True)
    spread = lax.rsqrt(jnp.mean(center * center, axis=-1, keepdims=True) + EPS)
    unit = center * spread
    return unit * gain + shift, unit, spread


def flat_norm_back(upstream, unit, spread, gain):
    scaled = upstream * gain
    inner = (
        scaled
        - jnp.mean(scaled, axis=-1, keepdims=True)
        - unit * jnp.mean(scaled * unit, axis=-1, keepdims=True)
    )
    return spread * inner, jnp.sum(upstream * unit, axis=0), jnp.sum(upstream, axis=0)


def column_flat(values):
    return jnp.sum(values.astype(jnp.float32), axis=0)


def whole_images(
    images,
    cotangent,
    slot_live,
    first_gain,
    first_shift,
    query_weight,
    query_bias,
    key_weight,
    value_weight,
    value_bias,
    output_weight,
    output_bias,
    second_gain,
    second_shift,
    up_weight,
    up_bias,
    down_weight,
    down_bias,
):
    dp_place = lax.axis_index("dp")
    place_y = lax.axis_index("tensor")
    core, place_x, place_z = dp_place % 2, (dp_place // 2) % 2, dp_place // 4
    places = jnp.stack([place_z, place_x, core, place_y]).astype(jnp.int32)
    strip, width = images.shape[1:]
    half = -(-strip // HALF_PAD) * HALF_PAD
    rows = 2 * half
    depth, head_cols = query_weight.shape
    units = up_weight.shape[1]

    def feed_part(place):
        wide = units // 2
        return jnp.concatenate(
            [
                lax.dynamic_slice_in_dim(up_weight, place * wide, wide, 1),
                lax.dynamic_slice_in_dim(down_weight, place * wide, wide, 0).T,
            ],
            1,
        )

    feed = pick_two(core, feed_part(core), exchange(feed_part(1 - core), far_core=1), 0)
    groups = [
        [place for place in range(32) if (place // 2) % 2 == at] for at in range(2)
    ]
    feed_full = lax.all_gather(
        feed.reshape(2 * depth, units),
        BOTH,
        axis=0,
        tiled=True,
        axis_index_groups=groups,
    ).reshape(8, 2, 2 * depth, units)
    upper_full = feed_full[..., : units // 2].transpose(0, 2, 1, 3).reshape(width, units)
    lower_full = feed_full[..., units // 2 :].transpose(0, 2, 1, 3).reshape(width, units)

    def core_parts(place):
        cuts = [
            lax.dynamic_slice_in_dim(weight, place * (head_cols // 2), head_cols // 2, 1)
            for weight in (query_weight, key_weight, value_weight, output_weight.T)
        ]
        spans = [slice(0, head_cols // 4), slice(head_cols // 4, head_cols // 2)]
        return jnp.stack([jnp.concatenate([cut[:, span] for cut in cuts], 1) for span in spans])

    qkv_full, output_full = gather_weights(core_parts(core), core_parts(1 - core), places, core)

    stacked = jnp.stack([images, cotangent])
    stacked = jnp.pad(stacked, ((0, 0), (0, 0), (0, half - strip), (0, 0)))
    mine = lax.dynamic_index_in_dim(stacked, place_y, 1, keepdims=False)
    theirs = lax.dynamic_index_in_dim(stacked, 1 - place_y, 1, keepdims=False)
    arrived = exchange(theirs, far_y=1)
    whole = jnp.stack([mine, arrived], 1).reshape(2, rows, width)

    def head_columns(vector):
        table = vector.astype(jnp.float32).reshape(2, 2, 2, -1)
        table = lax.dynamic_index_in_dim(table, core, 1, keepdims=False)
        table = jnp.where(place_y == 0, table, table[::-1])
        return table.transpose(1, 0, 2).reshape(4, 1, -1)

    def spread_core(table):
        table = jnp.stack(
            [jnp.where(core == 0, table, 0.0), jnp.where(core == 1, table, 0.0)], 1
        )
        return table.reshape(-1)

    def head_spread(vector):
        table = vector.reshape(2, 2, -1).transpose(1, 0, 2)
        return spread_core(jnp.where(place_y == 0, table, table[::-1]))

    gain_one, shift_one = first_gain.astype(jnp.float32), first_shift.astype(jnp.float32)
    gain_two, shift_two = second_gain.astype(jnp.float32), second_shift.astype(jnp.float32)
    query_shift, value_shift = head_columns(query_bias), head_columns(value_bias)
    qkv_shift = jnp.concatenate(
        [query_shift, jnp.zeros_like(query_shift), value_shift], 1
    ).reshape(-1)
    up_shift = lax.dynamic_index_in_dim(
        up_bias.astype(jnp.float32).reshape(2, 2, -1), core, 1, keepdims=False
    ).reshape(-1)

    row = jnp.arange(rows)
    in_half = row % half
    spot = jnp.where(row < half, place_y, 1 - place_y) * strip + in_half
    ok = (in_half < strip) & (spot < VALID)
    live = lax.dynamic_index_in_dim(slot_live, place_y, 0, keepdims=False).astype(jnp.float32)
    row_mask = (live * ok.astype(jnp.float32))[:, None]
    key_bias = jnp.broadcast_to(
        jnp.where(ok, 0.0, NEGATIVE).astype(LOW)[:, None], (rows, LANES)
    )

    resid = whole[0].astype(jnp.float32)
    grad_top = row_mask * whole[1].astype(jnp.float32)
    fed_grad = grad_top.astype(LOW)
    fed_rows, fed_turned = pair_up(places, fed_grad)
    normed, unit_one, spread_one = flat_norm(resid, gain_one, shift_one)
    normed_rows, normed_turned = pair_up(places, normed.astype(LOW))
    qkv = (mat(normed_rows, qkv_full) + qkv_shift).astype(LOW)
    mixed, totals = attend_all(qkv, key_bias, rows)
    attended = half_sums(mixed, output_full, rows) + output_bias.astype(jnp.float32)
    middle = row_mask * (resid + attended)
    second, unit_two, spread_two = flat_norm(middle, gain_two, shift_two)
    second_rows, second_turned = pair_up(places, second.astype(LOW))
    hidden = mat(second_rows, upper_full) + up_shift
    sigma = jax.nn.sigmoid(SLOPE * hidden)
    active = (hidden * sigma).astype(LOW)
    slope = (sigma + SLOPE * hidden * sigma * (1.0 - sigma)).astype(LOW)

    def unit_cut(array):
        wide = units // 4

        def cut(part, y_far):
            start = (place_y ^ y_far) * 2 + part
            return lax.dynamic_slice_in_dim(array, start * wide, wide, 1)

        return cut

    def head_cut(array):
        wide = array.shape[1] // 4

        def cut(part, y_far):
            at = part * 2 + y_far
            return array[:, at * wide : (at + 1) * wide]

        return cut

    lower_owned = scatter_grads([(fed_turned, unit_cut(active))], core)
    hidden_grad = (mat(fed_rows, lower_full) * slope.astype(jnp.float32)).astype(LOW)
    up_bias_sums = column_flat(hidden_grad)
    upper_owned = scatter_grads([(second_turned, unit_cut(hidden_grad))], core)
    second_grad = half_sums(hidden_grad, upper_full, rows)
    fed = half_sums(active, lower_full, rows)
    layer_own = (row_mask * (middle + fed + down_bias.astype(jnp.float32))).astype(LOW)
    middle_back, gain_two_grad, shift_two_grad = flat_norm_back(
        second_grad, unit_two, spread_two, gain_two
    )
    middle_grad = row_mask * (grad_top + middle_back)
    attended_grad = middle_grad.astype(LOW)
    attended_rows, attended_turned = pair_up(places, attended_grad)
    grad_mixed = mat(attended_rows, output_full).astype(LOW)
    grad_qkv = attend_back_all(qkv, key_bias, grad_mixed, mixed, totals, rows)
    early = jnp.concatenate(
        [
            column_flat(attended_grad),
            gain_two_grad,
            shift_two_grad,
            column_flat(fed_grad),
            spread_core(up_bias_sums.reshape(2, -1)),
        ]
    )
    last_owned = scatter_grads(
        [(normed_turned, head_cut(grad_qkv)), (attended_turned, head_cut(mixed))], core
    )
    normed_grad = half_sums(grad_qkv, qkv_full, rows)
    first_back, gain_one_grad, shift_one_grad = flat_norm_back(
        normed_grad, unit_one, spread_one, gain_one
    )
    images_own = middle_grad + first_back
    qkv_sums = column_flat(grad_qkv).reshape(4, 3, -1)
    late = jnp.concatenate(
        [
            gain_one_grad,
            shift_one_grad,
            head_spread(qkv_sums[:, 0].reshape(-1)),
            head_spread(qkv_sums[:, 2].reshape(-1)),
        ]
    )

    def to_strips(own, send):
        return pick_two(place_y, own[:strip], exchange(send, far_y=1).astype(own.dtype), 0)

    layer_out = to_strips(layer_own, layer_own[half : half + strip])
    images_grad = to_strips(images_own, images_own[half : half + strip].astype(LOW))
    early = jnp.sum(lax.all_gather(early, BOTH), axis=0)
    late = vector_sum(late)

    def full_columns(owned):
        return owned.transpose(2, 0, 1, 3).reshape(depth, -1)

    def head_grad(at):
        return full_columns(last_owned[..., at * LANES : (at + 1) * LANES])

    return (
        layer_out,
        images_grad,
        late[:width],
        late[width : 2 * width],
        head_grad(0),
        late[2 * width : 3 * width],
        head_grad(1),
        head_grad(2),
        late[3 * width :],
        head_grad(3).T,
        early[:width],
        early[width : 2 * width],
        early[2 * width : 3 * width],
        full_columns(upper_owned),
        early[4 * width :],
        full_columns(lower_owned).T,
        early[3 * width : 4 * width],
    )


def pick(mesh):
    sizes = dict(mesh.shape)
    if sizes["dp"] == 16 and sizes["tensor"] == 2:
        return whole_images
    return local


def solution(mesh):
    in_specs = (
        P("dp", "tensor", None),
        P("dp", "tensor", None),
        P("dp"),
        P(),
        P(),
        P("dp", "tensor"),
        P(),
        P("dp", "tensor"),
        P("dp", "tensor"),
        P(),
        P("tensor", "dp"),
        P(),
        P(),
        P(),
        P("dp", "tensor"),
        P(),
        P("tensor", "dp"),
        P(),
    )
    out_specs = (
        P("dp", "tensor", None),
        P("dp", "tensor", None),
        P(),
        P(),
        P("dp", "tensor"),
        P(),
        P("dp", "tensor"),
        P("dp", "tensor"),
        P(),
        P("tensor", "dp"),
        P(),
        P(),
        P(),
        P("dp", "tensor"),
        P(),
        P("tensor", "dp"),
        P(),
    )
    return jax.shard_map(pick(mesh), mesh=mesh, in_specs=in_specs, out_specs=out_specs, check_vma=False)
```

```python
import jax
import jax.numpy as jnp
from jax import lax
from jax.experimental import pallas as pl
from jax.experimental.pallas import tpu as pltpu
from jax.sharding import PartitionSpec as P

HDIM = 64
VALID = 577


EPS = 1e-05
NEGATIVE = -1e30
SLOPE = 1.702


def layer_norm(values, gain, shift):
    center = values - jnp.mean(values, axis=-1, keepdims=True)
    spread = lax.rsqrt(jnp.mean(center * center, axis=-1, keepdims=True) + EPS)
    unit = center * spread
    return (unit * gain + shift, unit, spread)


def norm_back(upstream, unit, spread, gain):
    scaled = upstream * gain
    inner = (
        scaled
        - jnp.mean(scaled, axis=-1, keepdims=True)
        - unit * jnp.mean(scaled * unit, axis=-1, keepdims=True)
    )
    return (spread * inner, jnp.sum(upstream * unit, axis=(0, 1)), jnp.sum(upstream, axis=(0, 1)))


def dense(left, right):
    return jnp.einsum("spa,ab->spb", left, right, preferred_element_type=jnp.float32)


def project_back(left, right):
    return jnp.einsum("spa,ba->spb", left, right, preferred_element_type=jnp.float32)


def outer(left, right):
    return jnp.einsum("spa,spb->ab", left, right, preferred_element_type=jnp.float32)


def column_sum(values):
    return jnp.sum(values.astype(jnp.float32), axis=(0, 1))


def widen(piece, length, start):
    return lax.dynamic_update_slice_in_dim(jnp.zeros((length,), jnp.float32), piece, start, 0)


def split_heads(block):
    return block.reshape(block.shape[0], -1, HDIM)


def scores_of(query, key, key_ok):
    raw = jnp.einsum(
        "qhe,khe->hqk", split_heads(query), split_heads(key), preferred_element_type=jnp.float32
    )
    return jnp.where(key_ok[None, None, :], raw * HDIM ** (-0.5), NEGATIVE)


def attend(query, key, value, key_ok):
    scores = scores_of(query, key, key_ok)
    top = jnp.max(scores, axis=-1, keepdims=True)
    total = top + jnp.log(jnp.sum(jnp.exp(scores - top), axis=-1, keepdims=True))
    probs = jnp.exp(scores - total).astype(jnp.bfloat16)
    mixed = jnp.einsum(
        "hqk,khe->qhe", probs, split_heads(value), preferred_element_type=jnp.float32
    )
    return (mixed.reshape(query.shape[0], -1).astype(jnp.bfloat16), total)


def attend_back(query, key, value, grad_mixed, total, key_ok):
    scores = scores_of(query, key, key_ok)
    probs = jnp.exp(scores - total)
    grad_heads = split_heads(grad_mixed)
    grad_probs = jnp.einsum(
        "qhe,khe->hqk", grad_heads, split_heads(value), preferred_element_type=jnp.float32
    )
    grad_value = jnp.einsum(
        "hqk,qhe->khe", probs.astype(jnp.bfloat16), grad_heads, preferred_element_type=jnp.float32
    )
    grad_scores = (
        probs * (grad_probs - jnp.sum(probs * grad_probs, axis=-1, keepdims=True))
    ).astype(jnp.bfloat16)
    grad_query = jnp.einsum(
        "hqk,khe->qhe", grad_scores, split_heads(key), preferred_element_type=jnp.float32
    ) * HDIM ** (-0.5)
    grad_key = jnp.einsum(
        "hqk,qhe->khe", grad_scores, split_heads(query), preferred_element_type=jnp.float32
    ) * HDIM ** (-0.5)
    length = query.shape[0]
    return (
        grad_query.reshape(length, -1).astype(jnp.bfloat16),
        grad_key.reshape(length, -1).astype(jnp.bfloat16),
        grad_value.reshape(length, -1).astype(jnp.bfloat16),
    )


def local(
    images,
    cotangent,
    slot_live,
    first_gain,
    first_shift,
    query_weight,
    query_bias,
    key_weight,
    value_weight,
    value_bias,
    output_weight,
    output_bias,
    second_gain,
    second_shift,
    up_weight,
    up_bias,
    down_weight,
    down_bias,
):
    slots, strip, width = images.shape
    tensor_count = lax.axis_size("tensor")
    tensor_place = lax.axis_index("tensor")
    seq_len = strip * tensor_count
    positions = tensor_place * strip + jnp.arange(strip)
    row_mask = (
        slot_live.astype(jnp.float32)[:, None, None]
        * (positions < VALID).astype(jnp.float32)[None, :, None]
    )
    key_ok = jnp.arange(seq_len) < VALID
    query_full, key_full, value_full, upper_full, output_full, lower_full = (
        lax.all_gather(query_weight, "dp", axis=0, tiled=True),
        lax.all_gather(key_weight, "dp", axis=0, tiled=True),
        lax.all_gather(value_weight, "dp", axis=0, tiled=True),
        lax.all_gather(up_weight, "dp", axis=0, tiled=True),
        lax.all_gather(output_weight, "dp", axis=1, tiled=True),
        lax.all_gather(down_weight, "dp", axis=1, tiled=True),
    )
    head_cols = query_full.shape[1]
    head_start = tensor_place * head_cols
    gain_one = first_gain.astype(jnp.float32)
    shift_one = first_shift.astype(jnp.float32)
    gain_two = second_gain.astype(jnp.float32)
    shift_two = second_shift.astype(jnp.float32)
    query_shift = lax.dynamic_slice_in_dim(query_bias.astype(jnp.float32), head_start, head_cols)
    value_shift = lax.dynamic_slice_in_dim(value_bias.astype(jnp.float32), head_start, head_cols)
    resid = images.astype(jnp.float32)
    normed, unit_one, spread_one = layer_norm(resid, gain_one, shift_one)
    normed_rows = lax.all_gather(normed.astype(jnp.bfloat16), "tensor", axis=1, tiled=True)
    queries = (dense(normed_rows, query_full) + query_shift).astype(jnp.bfloat16)
    keys_low = dense(normed_rows, key_full).astype(jnp.bfloat16)
    values_low = (dense(normed_rows, value_full) + value_shift).astype(jnp.bfloat16)
    mixed, totals = lax.map(
        lambda items: attend(items[0], items[1], items[2], key_ok), (queries, keys_low, values_low)
    )
    attended = lax.psum_scatter(
        dense(mixed, output_full), "tensor", scatter_dimension=1, tiled=True
    ) + output_bias.astype(jnp.float32)
    middle = row_mask * (resid + attended)
    second, unit_two, spread_two = layer_norm(middle, gain_two, shift_two)
    second_low = second.astype(jnp.bfloat16)
    grad_top = row_mask * cotangent.astype(jnp.float32)
    fed_grad = grad_top.astype(jnp.bfloat16)
    down_shift = down_bias.astype(jnp.float32)
    units = upper_full.shape[1]
    second_rows = lax.all_gather(second_low, "tensor", axis=1, tiled=True)
    up_shift = lax.dynamic_slice_in_dim(up_bias.astype(jnp.float32), tensor_place * units, units)
    hidden = dense(second_rows, upper_full) + up_shift
    sigma = jax.nn.sigmoid(SLOPE * hidden)
    active = (hidden * sigma).astype(jnp.bfloat16)
    fed = (
        lax.psum_scatter(
            dense(active, lower_full).astype(jnp.bfloat16),
            "tensor",
            scatter_dimension=1,
            tiled=True,
        ).astype(jnp.float32)
        + down_shift
    )
    fed_rows = lax.all_gather(fed_grad, "tensor", axis=1, tiled=True)
    grad_active = project_back(fed_rows, lower_full)
    lower_grad = outer(active, fed_rows)
    hidden_grad = (grad_active * (sigma + SLOPE * hidden * sigma * (1.0 - sigma))).astype(
        jnp.bfloat16
    )
    upper_grad = outer(second_rows, hidden_grad)
    up_bias_grad = widen(column_sum(hidden_grad), up_bias.shape[0], tensor_place * units)
    second_grad = lax.psum_scatter(
        project_back(hidden_grad, upper_full), "tensor", scatter_dimension=1, tiled=True
    )
    layer_out = (row_mask * (middle + fed)).astype(jnp.bfloat16)
    down_bias_grad = column_sum(fed_grad)
    middle_back, gain_two_grad, shift_two_grad = norm_back(
        second_grad, unit_two, spread_two, gain_two
    )
    middle_grad = row_mask * (grad_top + middle_back)
    attended_grad = middle_grad.astype(jnp.bfloat16)
    output_bias_grad = column_sum(attended_grad)
    attended_rows = lax.all_gather(attended_grad, "tensor", axis=1, tiled=True)
    grad_mixed = project_back(attended_rows, output_full).astype(jnp.bfloat16)
    output_grad = outer(mixed, attended_rows)
    grad_query, grad_key, grad_value = lax.map(
        lambda items: attend_back(items[0], items[1], items[2], items[3], items[4], key_ok),
        (queries, keys_low, values_low, grad_mixed, totals),
    )
    query_grad = outer(normed_rows, grad_query)
    key_grad = outer(normed_rows, grad_key)
    value_grad = outer(normed_rows, grad_value)
    query_bias_grad = widen(column_sum(grad_query), width, head_start)
    value_bias_grad = widen(column_sum(grad_value), width, head_start)
    normed_terms = (
        project_back(grad_query, query_full)
        + project_back(grad_key, key_full)
        + project_back(grad_value, value_full)
    )
    normed_grad = lax.psum_scatter(
        normed_terms.astype(jnp.bfloat16), "tensor", scatter_dimension=1, tiled=True
    ).astype(jnp.float32)
    first_back, gain_one_grad, shift_one_grad = norm_back(
        normed_grad, unit_one, spread_one, gain_one
    )
    images_grad = middle_grad + first_back
    query_owned, key_owned, value_owned, upper_owned, output_owned, lower_owned = (
        lax.psum_scatter(
            query_grad.astype(jnp.bfloat16), "dp", scatter_dimension=0, tiled=True
        ).astype(jnp.float32),
        lax.psum_scatter(
            key_grad.astype(jnp.bfloat16), "dp", scatter_dimension=0, tiled=True
        ).astype(jnp.float32),
        lax.psum_scatter(
            value_grad.astype(jnp.bfloat16), "dp", scatter_dimension=0, tiled=True
        ).astype(jnp.float32),
        lax.psum_scatter(
            upper_grad.astype(jnp.bfloat16), "dp", scatter_dimension=0, tiled=True
        ).astype(jnp.float32),
        lax.psum_scatter(
            output_grad.astype(jnp.bfloat16), "dp", scatter_dimension=1, tiled=True
        ).astype(jnp.float32),
        lax.psum_scatter(
            lower_grad.astype(jnp.bfloat16), "dp", scatter_dimension=1, tiled=True
        ).astype(jnp.float32),
    )
    vector_sums = lax.psum(
        (
            gain_one_grad,
            shift_one_grad,
            query_bias_grad,
            value_bias_grad,
            output_bias_grad,
            gain_two_grad,
            shift_two_grad,
            up_bias_grad,
            down_bias_grad,
        ),
        ("dp", "tensor"),
    )
    (
        gain_one_total,
        shift_one_total,
        query_bias_total,
        value_bias_total,
        output_bias_total,
        gain_two_total,
        shift_two_total,
        up_bias_total,
        down_bias_total,
    ) = vector_sums
    return (
        layer_out,
        images_grad,
        gain_one_total,
        shift_one_total,
        query_owned,
        query_bias_total,
        key_owned,
        value_owned,
        value_bias_total,
        output_owned,
        output_bias_total,
        gain_two_total,
        shift_two_total,
        upper_owned,
        up_bias_total,
        lower_owned,
        down_bias_total,
    )


BOTH = ("dp", "tensor")
HALF_PAD = 8
LANES = 128
LOW = jnp.bfloat16
VMEM_ROOM = 56 * 2**20


def exchange(value, far_z=0, far_x=0, far_core=0, far_y=0):
    pairs = []
    for place in range(32):
        other = place ^ (far_z * 8 + far_x * 4 + far_core * 2 + far_y)
        pairs.append((place, other))
    return lax.ppermute(value, BOTH, pairs)


def pick_two(bit, own, other, axis):
    first = jnp.where(bit == 0, own, other)
    last = jnp.where(bit == 0, other, own)
    return jnp.stack([first, last], axis)


def after(value, *others):
    return lax.optimization_barrier((value, *others))[0]


def pack(places, sources, shapes, plan):
    def kernel(places_ref, *refs):
        ins, outs = refs[: len(sources)], refs[len(sources) :]
        spots = [places_ref[at] for at in range(4)]
        for at, take, to, put in plan:
            outs[to][put(*spots)] = ins[at][take(*spots)]

    return pl.pallas_call(
        kernel,
        in_specs=[pl.BlockSpec(memory_space=pltpu.SMEM)]
        + [pl.BlockSpec(memory_space=pltpu.VMEM)] * len(sources),
        out_specs=[pl.BlockSpec(memory_space=pltpu.VMEM)] * len(shapes),
        out_shape=[jax.ShapeDtypeStruct(shape, LOW) for shape in shapes],
        compiler_params=pltpu.CompilerParams(vmem_limit_bytes=VMEM_ROOM),
        cost_estimate=pl.CostEstimate(
            flops=0,
            transcendentals=0,
            bytes_accessed=sum(2 * source.size * 2 for source in sources),
        ),
    )(places, *sources)


def gather_piece(keep, send, core):
    deep, wide = keep.shape[1:]
    return pick_two(core, keep, exchange(send, far_core=1), 1).reshape(2, 2 * deep, wide)


def gather_line(piece, others, places):
    rows, wide = piece.shape[1:]
    line = [piece] + others
    plan = []
    for step in range(4):
        for part in range(2):
            plan.append(
                (
                    step,
                    lambda z, x, c, y, part=part: part,
                    part,
                    lambda z, x, c, y, step=step: z ^ step,
                )
            )
    return pack(places, line, [(4, rows, wide)] * 2, plan)


def gather_pairs(places, one, two, one_x, two_y):
    every = slice(None)
    plan = [
        (0, lambda z, x, c, y: every, 0, lambda z, x, c, y: x),
        (1, lambda z, x, c, y: every, 0, lambda z, x, c, y: 1 - x),
        (2, lambda z, x, c, y: every, 1, lambda z, x, c, y: 0),
        (3, lambda z, x, c, y: every, 1, lambda z, x, c, y: 1),
    ]
    return pack(places, [one, one_x, two, two_y], [(2,) + one.shape] * 2, plan)


def gather_all(places, one_pair, two_pair, one_y, two_x, most):
    every = slice(None)
    rows, wide = one_pair.shape[2:]
    plan = []
    for to, low, high in ((0, 0, most), (1, most, wide)):
        span = high - low
        for place_z in range(4):
            for far in range(2):
                for number in range(2):
                    plan.append(
                        (
                            number,
                            lambda z, x, c, y, a=far, p=place_z, lo=low, hi=high: (
                                a,
                                p,
                                every,
                                slice(lo, hi),
                            ),
                            to,
                            lambda z, x, c, y, a=far, p=place_z, n=number, s=span: (
                                p,
                                a,
                                every,
                                slice(n * s, n * s + s),
                            ),
                        )
                    )
                    plan.append(
                        (
                            2 + far,
                            lambda z, x, c, y, n=number, p=place_z, lo=low, hi=high: (
                                n,
                                p,
                                every,
                                slice(lo, hi),
                            ),
                            to,
                            lambda z, x, c, y, f=far, p=place_z, n=number, s=span: (
                                p,
                                x ^ f,
                                every,
                                slice((2 + n) * s, (3 + n) * s),
                            ),
                        )
                    )
    shapes = [(4, 2, rows, 4 * most), (4, 2, rows, 4 * (wide - most))]
    made = pack(places, [one_pair, one_y, two_pair, two_x], shapes, plan)
    return [array.reshape(8 * rows, -1) for array in made]


def low_add(*values):
    total = values[0].astype(jnp.float32)
    for value in values[1:]:
        total = total + value.astype(jnp.float32)
    return total


def line_kernel(one_ref, one_a, one_b, two_ref, two_a, two_b, own_ref, *send_refs):
    tall = own_ref.shape[1]
    for step in range(4):
        rows = slice(step * tall, (step + 1) * tall)
        one = low_add(one_ref[0, rows], one_a[0, rows], one_b[rows])
        two = low_add(two_ref[0, rows], two_a[0, rows], two_b[rows])
        if step == 0:
            own_ref[0] = one
            own_ref[1] = two
        else:
            send_refs[step - 1][0] = one.astype(LOW)
            send_refs[step - 1][1] = two.astype(LOW)


def scatter_first(sends):
    return exchange(sends[0], far_y=1), exchange(sends[1], far_x=1)


def scatter_second(keeps, arrived):
    one = low_add(keeps[0][1], arrived[0][1]).astype(LOW)
    two = low_add(keeps[1][1], arrived[1][1]).astype(LOW)
    return exchange(one, far_x=1), exchange(two, far_y=1)


def scatter_line(keeps, arrived, crossed):
    lines, wide = crossed[0].shape
    tall = lines // 4
    first = pl.BlockSpec((1, lines, wide), lambda i: (0, 0, 0))
    flat = pl.BlockSpec((lines, wide), lambda i: (0, 0))
    piece = pl.BlockSpec((2, tall, wide), lambda i: (0, 0, 0))
    return pl.pallas_call(
        line_kernel,
        grid=(1,),
        in_specs=[first, first, flat, first, first, flat],
        out_specs=[piece] * 4,
        out_shape=[jax.ShapeDtypeStruct((2, tall, wide), jnp.float32)]
        + [jax.ShapeDtypeStruct((2, tall, wide), LOW)] * 3,
        compiler_params=pltpu.CompilerParams(vmem_limit_bytes=VMEM_ROOM),
        cost_estimate=pl.CostEstimate(
            flops=lines * wide * 4, transcendentals=0, bytes_accessed=lines * wide * 18
        ),
    )(keeps[0], arrived[0], crossed[0], keeps[1], arrived[1], crossed[1])


def scatter_z(sends):
    return [exchange(sends[step], far_z=step) for step in (1, 2, 3)]


def scatter_last(own, others, core):
    tall, wide = own.shape[1:]
    total = low_add(own, *others).reshape(2, 2, tall // 2, wide)
    keep = lax.dynamic_index_in_dim(total, core, 1, keepdims=False)
    send = lax.dynamic_index_in_dim(total, 1 - core, 1, keepdims=False)
    far = exchange(send.astype(LOW), far_core=1).astype(jnp.float32)
    return pick_two(core, keep, far, 0)


def vector_first(vector):
    vector = vector + exchange(vector, far_core=1)
    return vector, [exchange(vector, far_z=step) for step in (1, 2, 3)]


def vector_last(vector, others):
    vector = vector + others[0] + others[1] + others[2]
    for step in ({"far_y": 1}, {"far_x": 1}):
        vector = vector + exchange(vector, **step)
    return vector


def mat_far(left, right):
    return lax.dot_general(
        left, right, (((1,), (1,)), ((), ())), preferred_element_type=jnp.float32
    )


def mat_rows(left, right):
    return lax.dot_general(
        left, right, (((0,), (0,)), ((), ())), preferred_element_type=jnp.float32
    )


def up_kernel(places_ref, left_ref, right_ref, shift_ref, active_ref, slope_ref):
    width = left_ref.shape[1]
    right = right_ref[...].reshape(width, -1)
    hidden = jnp.dot(left_ref[...], right, preferred_element_type=jnp.float32)
    hidden = hidden + shift_ref[...]
    sigma = 1.0 / (1.0 + jnp.exp(-SLOPE * hidden))
    active = hidden * sigma
    active_ref[...] = active.astype(LOW)
    slope_ref[...] = (sigma + SLOPE * active * (1.0 - sigma)).astype(LOW)


def feed_spec(gathered, start):
    lines, _, rows, wide = gathered.shape
    return pl.BlockSpec(
        (lines, 1, rows, wide // 4), lambda i, s: (0, s[3] ^ (i % 2), 0, start + i // 2)
    )


def up_call(places, left, gathered, shift):
    rows, width = left.shape
    wide = shift.shape[1] // 4
    piece = pl.BlockSpec((rows, wide), lambda i, s: (0, i))
    return pl.pallas_call(
        up_kernel,
        grid_spec=pltpu.PrefetchScalarGridSpec(
            num_scalar_prefetch=1,
            grid=(4,),
            in_specs=[
                pl.BlockSpec((rows, width), lambda i, s: (0, 0)),
                feed_spec(gathered, 0),
                pl.BlockSpec((1, wide), lambda i, s: (0, i)),
            ],
            out_specs=[piece, piece],
        ),
        out_shape=[jax.ShapeDtypeStruct((rows, 4 * wide), LOW)] * 2,
        compiler_params=pltpu.CompilerParams(vmem_limit_bytes=VMEM_ROOM),
        cost_estimate=pl.CostEstimate(
            flops=8 * rows * wide * width,
            transcendentals=8 * rows * wide,
            bytes_accessed=left.size * 2 + 8 * width * wide + 16 * rows * wide,
        ),
    )(places, left, gathered, shift)


def hidden_kernel(places_ref, left_ref, right_ref, slope_ref, out_ref, sum_ref):
    width = left_ref.shape[1]
    right = right_ref[...].reshape(width, -1)
    grad = jnp.dot(left_ref[...], right, preferred_element_type=jnp.float32)
    grad = (grad * slope_ref[...].astype(jnp.float32)).astype(LOW)
    out_ref[...] = grad
    sum_ref[...] = jnp.sum(grad.astype(jnp.float32), axis=0, keepdims=True)


def hidden_call(places, left, gathered, slope):
    rows, width = left.shape
    wide = slope.shape[1] // 4
    piece = pl.BlockSpec((rows, wide), lambda i, s: (0, i))
    return pl.pallas_call(
        hidden_kernel,
        grid_spec=pltpu.PrefetchScalarGridSpec(
            num_scalar_prefetch=1,
            grid=(4,),
            in_specs=[
                pl.BlockSpec((rows, width), lambda i, s: (0, 0)),
                feed_spec(gathered, 2),
                piece,
            ],
            out_specs=[piece, pl.BlockSpec((1, wide), lambda i, s: (0, i))],
        ),
        out_shape=[
            jax.ShapeDtypeStruct((rows, 4 * wide), LOW),
            jax.ShapeDtypeStruct((1, 4 * wide), jnp.float32),
        ],
        compiler_params=pltpu.CompilerParams(vmem_limit_bytes=VMEM_ROOM),
        cost_estimate=pl.CostEstimate(
            flops=8 * rows * wide * width,
            transcendentals=0,
            bytes_accessed=left.size * 2 + 8 * width * wide + 16 * rows * wide,
        ),
    )(places, left, gathered, slope)


def down_kernel(places_ref, left_ref, right_ref, out_ref):
    span = right_ref.shape[3] // 2
    total = None
    for far in range(2):
        right = right_ref[:, places_ref[3] ^ far].reshape(-1, 2 * span)
        for part in range(2):
            start = (part * 2 + far) * span
            one = mat_far(
                left_ref[:, start : start + span], right[:, part * span : (part + 1) * span]
            )
            total = one if total is None else total + one
    out_ref[...] = total.astype(out_ref.dtype)


def down_call(places, left, gathered, start, dtype):
    rows, deep = left.shape
    lines, _, tall, wide = gathered.shape
    return pl.pallas_call(
        down_kernel,
        grid_spec=pltpu.PrefetchScalarGridSpec(
            num_scalar_prefetch=1,
            grid=(lines // 2,),
            in_specs=[
                pl.BlockSpec((rows, deep), lambda i, s: (0, 0)),
                pl.BlockSpec((2, 2, tall, wide // 2), lambda i, s: (i, 0, 0, start)),
            ],
            out_specs=pl.BlockSpec((rows, 2 * tall), lambda i, s: (0, i)),
        ),
        out_shape=jax.ShapeDtypeStruct((rows, lines * tall), dtype),
        compiler_params=pltpu.CompilerParams(vmem_limit_bytes=VMEM_ROOM),
        cost_estimate=pl.CostEstimate(
            flops=2 * rows * deep * lines * tall,
            transcendentals=0,
            bytes_accessed=left.size * 2 + lines * tall * deep * 2 + rows * lines * tall * 4,
        ),
    )(places, left, gathered)


def owner_kernel(places_ref, left_ref, left_far, right_ref, right_far, out_ref):
    total = mat_rows(left_ref[...], right_ref[...]) + mat_rows(left_far[...], right_far[...])
    out_ref[0] = total.astype(LOW)


def owner_grads(places, left, right):
    rows, width = left[0].shape
    span = right[0].shape[1] // 4
    whole = pl.BlockSpec((rows, width), lambda i, s: (0, 0))
    piece = pl.BlockSpec((rows, span), lambda i, s: (0, i))
    return pl.pallas_call(
        owner_kernel,
        grid_spec=pltpu.PrefetchScalarGridSpec(
            num_scalar_prefetch=1,
            grid=(4,),
            in_specs=[whole, whole, piece, piece],
            out_specs=pl.BlockSpec((1, width, span), lambda i, s: (s[3] ^ (i % 2), 0, i // 2)),
        ),
        out_shape=jax.ShapeDtypeStruct((2, width, 2 * span), LOW),
        compiler_params=pltpu.CompilerParams(vmem_limit_bytes=VMEM_ROOM),
        cost_estimate=pl.CostEstimate(
            flops=16 * rows * width * span,
            transcendentals=0,
            bytes_accessed=(2 * rows * width + 8 * rows * span + 4 * width * span) * 2,
        ),
    )(places, *left, *right)


def weight_kernel(pairs, places_ref, *refs):
    ins, (one_ref, two_ref) = refs[:-2], refs[-2:]
    step = pl.program_id(0)
    parts = []
    for pair in range(pairs):
        total = None
        for image in range(2):
            group = ins[10 * pair + 5 * image : 10 * pair + 5 * image + 5]
            left = jnp.concatenate([ref[...] for ref in group[:4]], axis=1)
            one = mat_rows(left, group[4][...])
            total = one if image == 0 else total + one
        parts.append(total.astype(LOW))
    made = parts[0] if pairs == 1 else jnp.concatenate(parts, axis=1)

    @pl.when(step < 2)
    def _():
        one_ref[0] = made

    @pl.when(step >= 2)
    def _():
        two_ref[0] = made


def weight_pieces(places, operands, send):
    rows = operands[0][0][0].shape[0]
    line = 4 * LANES

    def x_far(step):
        if send:
            return jnp.where(step == 0, 0, 1)
        return jnp.where(step == 1, 1, 0)

    def y_far(step):
        if send:
            return jnp.where(step == 2, 0, 1)
        return jnp.where(step == 3, 1, 0)

    def left_map(z_far):
        return lambda i, s: (0, (s[0] ^ z_far) * 2 + (s[1] ^ x_far(i)))

    specs, arrays, wide = [], [], 0
    for left, right in operands:
        span = right[0].shape[1] // 4
        wide += span
        for image in range(2):
            for z_far in range(4):
                specs.append(pl.BlockSpec((rows, LANES), left_map(z_far)))
                arrays.append(left[image])
            specs.append(
                pl.BlockSpec((rows, span), lambda i, s: (0, jnp.where(i < 2, 0, 2) + y_far(i)))
            )
            arrays.append(right[image])

    def kernel(*refs):
        weight_kernel(len(operands), *refs)

    return pl.pallas_call(
        kernel,
        grid_spec=pltpu.PrefetchScalarGridSpec(
            num_scalar_prefetch=1,
            grid=(4,),
            in_specs=specs,
            out_specs=[
                pl.BlockSpec((1, line, wide), lambda i, s: (jnp.minimum(i, 1), 0, 0)),
                pl.BlockSpec((1, line, wide), lambda i, s: (jnp.maximum(i - 2, 0), 0, 0)),
            ],
        ),
        out_shape=[jax.ShapeDtypeStruct((2, line, wide), LOW)] * 2,
        compiler_params=pltpu.CompilerParams(vmem_limit_bytes=VMEM_ROOM),
        cost_estimate=pl.CostEstimate(
            flops=16 * rows * line * wide,
            transcendentals=0,
            bytes_accessed=rows * wide * 16 + rows * line * 16 + line * wide * 8,
        ),
    )(places, *arrays)


def lane_of(shape):
    return lax.broadcasted_iota(jnp.int32, shape, 1)


def head_views(query, key, bias, head):
    lane = lane_of(query.shape)
    mine = (lane >= HDIM) if head else (lane < HDIM)
    spot = 0 if head else HDIM
    zero = jnp.zeros_like(query)
    query_view = jnp.where(mine, query, jnp.where(lane == spot, zero + 1, zero))
    key_view = jnp.where(lane == spot, bias, key)
    return mine, query_view, key_view


def attend_kernel(qkv_ref, bias_ref, mixed_ref, total_ref):
    query = qkv_ref[:, 0:LANES] * jnp.bfloat16(HDIM ** (-0.5))
    key = qkv_ref[:, LANES : 2 * LANES]
    value = qkv_ref[:, 2 * LANES : 3 * LANES]
    bias = bias_ref[...]
    sums, tops = [], []
    for head in range(2):
        mine, query_view, key_view = head_views(query, key, bias, head)
        scores = mat_far(query_view, key_view)
        top = jnp.max(scores, axis=1, keepdims=True)
        weight = jnp.exp(scores - top).astype(LOW)
        value_view = jnp.where(mine, value, jnp.ones_like(value))
        sums.append(jnp.dot(weight, value_view, preferred_element_type=jnp.float32))
        tops.append(top)
    low = lane_of(sums[0].shape) < HDIM
    upper = jnp.where(low, sums[0], sums[1])
    lower = jnp.where(low, sums[1], sums[0])
    lower = pltpu.roll(lower, HDIM, 1)
    mixed_ref[...] = (upper / lower).astype(LOW)
    total = jnp.where(low, tops[0], tops[1]) + jnp.log(lower)
    total = jnp.transpose(total)
    total_ref[0, 0:1, :] = total[0:1]
    total_ref[0, 1:2, :] = total[HDIM : HDIM + 1]


def attend_back_kernel(qkv_ref, bias_ref, grad_ref, mixed_ref, total_ref, out_ref):
    scale = HDIM ** (-0.5)
    query = qkv_ref[:, 0:LANES] * jnp.bfloat16(scale)
    key = qkv_ref[:, LANES : 2 * LANES]
    value = qkv_ref[:, 2 * LANES : 3 * LANES]
    bias = bias_ref[...]
    grad = grad_ref[...]
    product = grad.astype(jnp.float32) * mixed_ref[...].astype(jnp.float32)
    grad_query = grad_key = grad_value = None
    for head in range(2):
        mine, query_view, key_view = head_views(query, key, bias, head)
        zero = jnp.zeros_like(query)
        scores = mat_far(key_view, query_view)
        probs = jnp.exp(scores - total_ref[0, head : head + 1, :])
        grad_view = jnp.where(mine, grad, zero)
        grad_probs = mat_far(value, grad_view)
        ones = jnp.where(mine[0:8], 1.0, 0.0)
        inner = lax.dot_general(
            ones,
            product,
            (((1,), (1,)), ((), ())),
            precision=lax.Precision.HIGHEST,
            preferred_element_type=jnp.float32,
        )
        grad_scores = (probs * (grad_probs - inner[0:1])).astype(LOW)
        one_value = jnp.dot(probs.astype(LOW), grad_view, preferred_element_type=jnp.float32)
        one_key = jnp.dot(
            grad_scores, jnp.where(mine, query, zero), preferred_element_type=jnp.float32
        )
        one_query = mat_rows(grad_scores, jnp.where(mine, key, zero))
        grad_query = one_query if head == 0 else grad_query + one_query
        grad_key = one_key if head == 0 else grad_key + one_key
        grad_value = one_value if head == 0 else grad_value + one_value
    out_ref[:, 0:LANES] = (grad_query * scale).astype(LOW)
    out_ref[:, LANES : 2 * LANES] = grad_key.astype(LOW)
    out_ref[:, 2 * LANES : 3 * LANES] = grad_value.astype(LOW)


def attend_call(qkv, bias):
    rows = qkv.shape[0]
    blocks = qkv.shape[1] // (3 * LANES)
    return pl.pallas_call(
        attend_kernel,
        grid=(blocks,),
        in_specs=[
            pl.BlockSpec((rows, 3 * LANES), lambda j: (0, j)),
            pl.BlockSpec((rows, LANES), lambda j: (0, 0)),
        ],
        out_specs=[
            pl.BlockSpec((rows, LANES), lambda j: (0, j)),
            pl.BlockSpec((1, 8, rows), lambda j: (j, 0, 0)),
        ],
        out_shape=[
            jax.ShapeDtypeStruct((rows, blocks * LANES), LOW),
            jax.ShapeDtypeStruct((blocks, 8, rows), jnp.float32),
        ],
        compiler_params=pltpu.CompilerParams(vmem_limit_bytes=VMEM_ROOM),
        cost_estimate=pl.CostEstimate(
            flops=blocks * 2 * 2 * 2 * rows * rows * LANES * 2,
            transcendentals=blocks * 2 * rows * rows,
            bytes_accessed=rows * blocks * LANES * 8,
        ),
    )(qkv, bias)


def attend_back_call(qkv, bias, grad, mixed, total):
    rows = qkv.shape[0]
    blocks = qkv.shape[1] // (3 * LANES)
    return pl.pallas_call(
        attend_back_kernel,
        grid=(blocks,),
        in_specs=[
            pl.BlockSpec((rows, 3 * LANES), lambda j: (0, j)),
            pl.BlockSpec((rows, LANES), lambda j: (0, 0)),
            pl.BlockSpec((rows, LANES), lambda j: (0, j)),
            pl.BlockSpec((rows, LANES), lambda j: (0, j)),
            pl.BlockSpec((1, 8, rows), lambda j: (j, 0, 0)),
        ],
        out_specs=pl.BlockSpec((rows, 3 * LANES), lambda j: (0, j)),
        out_shape=jax.ShapeDtypeStruct(qkv.shape, LOW),
        compiler_params=pltpu.CompilerParams(vmem_limit_bytes=VMEM_ROOM),
        cost_estimate=pl.CostEstimate(
            flops=blocks * 2 * 5 * 2 * rows * rows * LANES * 2,
            transcendentals=blocks * 2 * rows * rows,
            bytes_accessed=rows * blocks * LANES * 16,
        ),
    )(qkv, bias, grad, mixed, total)


def mat(left, right):
    return jnp.dot(left, right, preferred_element_type=jnp.float32)


def flat_norm(values, gain, shift):
    center = values - jnp.mean(values, axis=-1, keepdims=True)
    spread = lax.rsqrt(jnp.mean(center * center, axis=-1, keepdims=True) + EPS)
    unit = center * spread
    return unit * gain + shift, unit, spread


def flat_norm_back(upstream, unit, spread, gain):
    scaled = upstream * gain
    inner = (
        scaled
        - jnp.mean(scaled, axis=-1, keepdims=True)
        - unit * jnp.mean(scaled * unit, axis=-1, keepdims=True)
    )
    return spread * inner, jnp.sum(upstream * unit, axis=0), jnp.sum(upstream, axis=0)


def column_flat(values):
    return jnp.sum(values.astype(jnp.float32), axis=0)


def whole_images(
    images,
    cotangent,
    slot_live,
    first_gain,
    first_shift,
    query_weight,
    query_bias,
    key_weight,
    value_weight,
    value_bias,
    output_weight,
    output_bias,
    second_gain,
    second_shift,
    up_weight,
    up_bias,
    down_weight,
    down_bias,
):
    dp_place = lax.axis_index("dp")
    place_y = lax.axis_index("tensor")
    core, place_x, place_z = dp_place % 2, (dp_place // 2) % 2, dp_place // 4
    places = jnp.stack([place_z, place_x, core, place_y]).astype(jnp.int32)
    strip, width = images.shape[1:]
    half = -(-strip // HALF_PAD) * HALF_PAD
    rows = 2 * half
    depth, head_cols = query_weight.shape
    units = up_weight.shape[1]

    def columns_of(weights, place):
        return [
            lax.dynamic_slice_in_dim(
                weight, place * (weight.shape[1] // 2), weight.shape[1] // 2, 1
            )
            for weight in weights
        ]

    def core_parts(weights, place):
        cuts = columns_of(weights, place)
        parts = []
        for part in range(2):
            spans = [cut.shape[1] // 2 for cut in cuts]
            parts.append(
                jnp.concatenate(
                    [cut[:, part * span : (part + 1) * span] for cut, span in zip(cuts, spans)], 1
                )
            )
        return jnp.stack(parts)

    feeds = [up_weight, down_weight.T]
    feed_keep = jnp.concatenate(columns_of(feeds, core), 1)
    feed_send = jnp.concatenate(columns_of(feeds, 1 - core), 1)
    feed = pick_two(core, feed_keep, exchange(feed_send, far_core=1), 0)
    groups = [[place for place in range(32) if (place // 2) % 2 == at] for at in range(2)]
    turned_groups = [sorted(group, key=lambda place: (place % 2, place)) for group in groups]
    gathered = lax.all_gather(
        feed.reshape(2 * depth, -1),
        BOTH,
        axis=0,
        tiled=True,
        axis_index_groups=groups,
    ).reshape(8, 2, 2 * depth, -1)

    heads = [query_weight, key_weight, value_weight, output_weight.T]
    piece_one = gather_piece(core_parts(heads, core), core_parts(heads, 1 - core), core)
    line_one = gather_line(piece_one, scatter_z([None, piece_one, piece_one, piece_one]), places)

    stacked = jnp.stack([images, after(cotangent, piece_one)])
    stacked = jnp.pad(stacked, ((0, 0), (0, 0), (0, half - strip), (0, 0)))
    mine = lax.dynamic_index_in_dim(stacked, place_y, 1, keepdims=False)
    theirs = lax.dynamic_index_in_dim(stacked, 1 - place_y, 1, keepdims=False)
    arrived = after(exchange(theirs, far_y=1), *line_one)
    whole = jnp.stack([mine, arrived], 1).reshape(2, rows, width)

    def head_columns(vector):
        table = vector.astype(jnp.float32).reshape(2, 2, 2, -1)
        table = lax.dynamic_index_in_dim(table, core, 1, keepdims=False)
        table = jnp.where(place_y == 0, table, table[::-1])
        return table.transpose(1, 0, 2).reshape(4, 1, -1)

    def spread_core(table):
        table = jnp.stack(
            [jnp.where(core == 0, table, 0.0), jnp.where(core == 1, table, 0.0)], 1
        )
        return table.reshape(-1)

    def head_spread(vector):
        table = vector.reshape(2, 2, -1).transpose(1, 0, 2)
        return spread_core(jnp.where(place_y == 0, table, table[::-1]))

    gain_one, shift_one = first_gain.astype(jnp.float32), first_shift.astype(jnp.float32)
    gain_two, shift_two = second_gain.astype(jnp.float32), second_shift.astype(jnp.float32)
    query_shift, value_shift = head_columns(query_bias), head_columns(value_bias)
    qkv_shift = jnp.concatenate(
        [query_shift, jnp.zeros_like(query_shift), value_shift], 1
    ).reshape(-1)
    up_shift = head_columns(up_bias).reshape(1, -1)

    row = jnp.arange(rows)
    in_half = row % half
    spot = jnp.where(row < half, place_y, 1 - place_y) * strip + in_half
    ok = (in_half < strip) & (spot < VALID)
    live = lax.dynamic_index_in_dim(slot_live, place_y, 0, keepdims=False).astype(jnp.float32)
    row_mask = (live * ok.astype(jnp.float32))[:, None]
    key_bias = jnp.broadcast_to(
        jnp.where(ok, 0.0, NEGATIVE).astype(LOW)[:, None], (rows, LANES)
    )

    resid = whole[0].astype(jnp.float32)
    grad_top = row_mask * whole[1].astype(jnp.float32)
    fed_grad = grad_top.astype(LOW)
    def pair_of(own):
        return own, exchange(own, far_core=1)

    fed_pair = pair_of(fed_grad)
    normed, unit_one, spread_one = flat_norm(resid, gain_one, shift_one)
    normed_pair = pair_of(normed.astype(LOW))

    cross_one = exchange(line_one[0], far_x=1), exchange(line_one[1], far_y=1)
    pair_one = gather_pairs(after(places, *fed_pair, *normed_pair), *line_one, *cross_one)
    last_one = exchange(pair_one[0], far_y=1), exchange(pair_one[1], far_x=1)
    qkv_full, output_full = gather_all(places, *pair_one, *last_one, 3 * head_cols // 4)

    def heads_of(one):
        qkv = (mat(one, qkv_full) + qkv_shift).astype(LOW)
        return (qkv, *attend_call(qkv, key_bias))

    qkv_far, mixed_far, totals_far = heads_of(normed_pair[1])
    mixed_sum = exchange(mat_far(mixed_far, output_full).astype(LOW), far_core=1)
    qkv_own, mixed_own, totals_own = heads_of(normed_pair[0])
    mixed_pair = mixed_own, mixed_far
    attended = mat_far(mixed_own, output_full) + mixed_sum.astype(jnp.float32)
    attended = attended + output_bias.astype(jnp.float32)
    middle = row_mask * (resid + attended)
    second, unit_two, spread_two = flat_norm(middle, gain_two, shift_two)
    second_pair = pair_of(second.astype(LOW))
    ups = [up_call(places, one, gathered, up_shift) for one in second_pair]
    active_pair = ups[0][0], ups[1][0]

    def owner_sum(grads):
        return lax.psum_scatter(
            grads.reshape(-1, grads.shape[2]),
            BOTH,
            scatter_dimension=0,
            tiled=True,
            axis_index_groups=turned_groups,
        ).reshape(2, depth, -1)

    lower_grads = owner_grads(places, fed_pair, active_pair)
    lower_sum = owner_sum(lower_grads)
    fed_late = after(fed_pair, lower_grads)
    hiddens = [
        hidden_call(places, one, gathered, up[1]) for one, up in zip(fed_late, ups)
    ]
    hidden_pair = hiddens[0][0], hiddens[1][0]
    up_bias_sums = (hiddens[0][1] + hiddens[1][1]).reshape(-1)
    second_far = exchange(down_call(places, hidden_pair[1], gathered, 0, LOW), far_core=1)
    second_own = down_call(places, hidden_pair[0], gathered, 0, jnp.float32)
    second_grad = second_own + second_far.astype(jnp.float32)
    middle_back, gain_two_grad, shift_two_grad = flat_norm_back(
        second_grad, unit_two, spread_two, gain_two
    )
    middle_grad = row_mask * (grad_top + middle_back)
    attended_grad = middle_grad.astype(LOW)
    attended_pair = pair_of(attended_grad)
    upper_grads = owner_grads(places, second_pair, hidden_pair)
    upper_sum = owner_sum(upper_grads)

    def heads_back(one, qkv, mixed, totals):
        grad_mixed = mat(one, output_full).astype(LOW)
        return attend_back_call(qkv, key_bias, grad_mixed, mixed, totals)

    attended_late = after(attended_pair, upper_grads)
    back_own = heads_back(attended_late[0], qkv_own, mixed_own, totals_own)
    back_far = heads_back(attended_late[1], qkv_far, mixed_far, totals_far)
    back_pair = back_own, back_far
    operands = [(normed_pair, back_pair), (attended_pair, mixed_pair)]
    last_sends = weight_pieces(places, operands, True)
    last_first = scatter_first(last_sends)
    back_late = after(back_pair, last_sends)
    normed_far = exchange(mat_far(back_late[1], qkv_full).astype(LOW), far_core=1)
    normed_grad = mat_far(back_late[0], qkv_full) + normed_far.astype(jnp.float32)
    last_keeps = weight_pieces(places, operands, False)
    first_back, gain_one_grad, shift_one_grad = flat_norm_back(
        normed_grad, unit_one, spread_one, gain_one
    )
    images_own = middle_grad + first_back
    qkv_sums = (column_flat(back_own) + column_flat(back_far)).reshape(4, 3, -1)
    vector = jnp.concatenate(
        [
            column_flat(attended_grad),
            gain_two_grad,
            shift_two_grad,
            column_flat(fed_grad),
            head_spread(up_bias_sums),
            gain_one_grad,
            shift_one_grad,
            head_spread(qkv_sums[:, 0].reshape(-1)),
            head_spread(qkv_sums[:, 2].reshape(-1)),
        ]
    )
    last_first = after(last_first, last_keeps)
    last_second = scatter_second(last_keeps, last_first)
    vector, vectors = vector_first(vector)
    last_line = scatter_line(last_keeps, last_first, after(last_second, images_own, *vectors))
    last_z = scatter_z(last_line)
    fed_far = exchange(down_call(places, active_pair[1], gathered, 1, LOW), far_core=1)
    fed = down_call(places, active_pair[0], gathered, 1, jnp.float32)
    fed = fed + fed_far.astype(jnp.float32)
    layer_own = (row_mask * (middle + fed + down_bias.astype(jnp.float32))).astype(LOW)
    vector = vector_last(vector, vectors)
    last_z = after(tuple(last_z), vector)
    last_owned = scatter_last(last_line[0], last_z, core)

    def owner_last(total):
        keep = lax.dynamic_index_in_dim(total, core, 0, keepdims=False)
        send = lax.dynamic_index_in_dim(total, 1 - core, 0, keepdims=False)
        both = pick_two(core, keep, exchange(send, far_core=1), 0)
        return both.astype(jnp.float32).transpose(1, 0, 2).reshape(depth, -1)

    lower_owned, upper_owned = owner_last(lower_sum), owner_last(upper_sum)

    def to_strips(own, send):
        return pick_two(place_y, own[:strip], exchange(send, far_y=1).astype(own.dtype), 0)

    layer_out = to_strips(layer_own, layer_own[half : half + strip])
    images_grad = to_strips(images_own, images_own[half : half + strip].astype(LOW))
    def full_columns(owned):
        return owned.transpose(2, 0, 1, 3).reshape(depth, -1)

    def head_grad(at):
        return full_columns(last_owned[..., at * LANES : (at + 1) * LANES])

    early, late = vector[: 4 * width + up_bias.shape[0]], vector[4 * width + up_bias.shape[0] :]
    return (
        layer_out,
        images_grad,
        late[:width],
        late[width : 2 * width],
        head_grad(0),
        late[2 * width : 3 * width],
        head_grad(1),
        head_grad(2),
        late[3 * width :],
        head_grad(3).T,
        early[:width],
        early[width : 2 * width],
        early[2 * width : 3 * width],
        upper_owned,
        early[4 * width :],
        lower_owned.T,
        early[3 * width : 4 * width],
    )


def pick(mesh):
    sizes = dict(mesh.shape)
    if sizes["dp"] == 16 and sizes["tensor"] == 2:
        return whole_images
    return local


def solution(mesh):
    in_specs = (
        P("dp", "tensor", None),
        P("dp", "tensor", None),
        P("dp"),
        P(),
        P(),
        P("dp", "tensor"),
        P(),
        P("dp", "tensor"),
        P("dp", "tensor"),
        P(),
        P("tensor", "dp"),
        P(),
        P(),
        P(),
        P("dp", "tensor"),
        P(),
        P("tensor", "dp"),
        P(),
    )
    out_specs = (
        P("dp", "tensor", None),
        P("dp", "tensor", None),
        P(),
        P(),
        P("dp", "tensor"),
        P(),
        P("dp", "tensor"),
        P("dp", "tensor"),
        P(),
        P("tensor", "dp"),
        P(),
        P(),
        P(),
        P("dp", "tensor"),
        P(),
        P("tensor", "dp"),
        P(),
    )
    return jax.shard_map(pick(mesh), mesh=mesh, in_specs=in_specs, out_specs=out_specs, check_vma=False)
```

```python
import jax
import jax.numpy as jnp
from jax import lax
from jax.experimental import pallas as pl
from jax.experimental.pallas import tpu as pltpu
from jax.sharding import PartitionSpec as P

HDIM = 64
VALID = 577


EPS = 1e-05
NEGATIVE = -1e30
SLOPE = 1.702


def layer_norm(values, gain, shift):
    center = values - jnp.mean(values, axis=-1, keepdims=True)
    spread = lax.rsqrt(jnp.mean(center * center, axis=-1, keepdims=True) + EPS)
    unit = center * spread
    return (unit * gain + shift, unit, spread)


def norm_back(upstream, unit, spread, gain):
    scaled = upstream * gain
    inner = (
        scaled
        - jnp.mean(scaled, axis=-1, keepdims=True)
        - unit * jnp.mean(scaled * unit, axis=-1, keepdims=True)
    )
    return (spread * inner, jnp.sum(upstream * unit, axis=(0, 1)), jnp.sum(upstream, axis=(0, 1)))


def dense(left, right):
    return jnp.einsum("spa,ab->spb", left, right, preferred_element_type=jnp.float32)


def project_back(left, right):
    return jnp.einsum("spa,ba->spb", left, right, preferred_element_type=jnp.float32)


def outer(left, right):
    return jnp.einsum("spa,spb->ab", left, right, preferred_element_type=jnp.float32)


def column_sum(values):
    return jnp.sum(values.astype(jnp.float32), axis=(0, 1))


def widen(piece, length, start):
    return lax.dynamic_update_slice_in_dim(jnp.zeros((length,), jnp.float32), piece, start, 0)


def split_heads(block):
    return block.reshape(block.shape[0], -1, HDIM)


def scores_of(query, key, key_ok):
    raw = jnp.einsum(
        "qhe,khe->hqk", split_heads(query), split_heads(key), preferred_element_type=jnp.float32
    )
    return jnp.where(key_ok[None, None, :], raw * HDIM ** (-0.5), NEGATIVE)


def attend(query, key, value, key_ok):
    scores = scores_of(query, key, key_ok)
    top = jnp.max(scores, axis=-1, keepdims=True)
    total = top + jnp.log(jnp.sum(jnp.exp(scores - top), axis=-1, keepdims=True))
    probs = jnp.exp(scores - total).astype(jnp.bfloat16)
    mixed = jnp.einsum(
        "hqk,khe->qhe", probs, split_heads(value), preferred_element_type=jnp.float32
    )
    return (mixed.reshape(query.shape[0], -1).astype(jnp.bfloat16), total)


def attend_back(query, key, value, grad_mixed, total, key_ok):
    scores = scores_of(query, key, key_ok)
    probs = jnp.exp(scores - total)
    grad_heads = split_heads(grad_mixed)
    grad_probs = jnp.einsum(
        "qhe,khe->hqk", grad_heads, split_heads(value), preferred_element_type=jnp.float32
    )
    grad_value = jnp.einsum(
        "hqk,qhe->khe", probs.astype(jnp.bfloat16), grad_heads, preferred_element_type=jnp.float32
    )
    grad_scores = (
        probs * (grad_probs - jnp.sum(probs * grad_probs, axis=-1, keepdims=True))
    ).astype(jnp.bfloat16)
    grad_query = jnp.einsum(
        "hqk,khe->qhe", grad_scores, split_heads(key), preferred_element_type=jnp.float32
    ) * HDIM ** (-0.5)
    grad_key = jnp.einsum(
        "hqk,qhe->khe", grad_scores, split_heads(query), preferred_element_type=jnp.float32
    ) * HDIM ** (-0.5)
    length = query.shape[0]
    return (
        grad_query.reshape(length, -1).astype(jnp.bfloat16),
        grad_key.reshape(length, -1).astype(jnp.bfloat16),
        grad_value.reshape(length, -1).astype(jnp.bfloat16),
    )


def local(
    images,
    cotangent,
    slot_live,
    first_gain,
    first_shift,
    query_weight,
    query_bias,
    key_weight,
    value_weight,
    value_bias,
    output_weight,
    output_bias,
    second_gain,
    second_shift,
    up_weight,
    up_bias,
    down_weight,
    down_bias,
):
    slots, strip, width = images.shape
    tensor_count = lax.axis_size("tensor")
    tensor_place = lax.axis_index("tensor")
    seq_len = strip * tensor_count
    positions = tensor_place * strip + jnp.arange(strip)
    row_mask = (
        slot_live.astype(jnp.float32)[:, None, None]
        * (positions < VALID).astype(jnp.float32)[None, :, None]
    )
    key_ok = jnp.arange(seq_len) < VALID
    query_full, key_full, value_full, upper_full, output_full, lower_full = (
        lax.all_gather(query_weight, "dp", axis=0, tiled=True),
        lax.all_gather(key_weight, "dp", axis=0, tiled=True),
        lax.all_gather(value_weight, "dp", axis=0, tiled=True),
        lax.all_gather(up_weight, "dp", axis=0, tiled=True),
        lax.all_gather(output_weight, "dp", axis=1, tiled=True),
        lax.all_gather(down_weight, "dp", axis=1, tiled=True),
    )
    head_cols = query_full.shape[1]
    head_start = tensor_place * head_cols
    gain_one = first_gain.astype(jnp.float32)
    shift_one = first_shift.astype(jnp.float32)
    gain_two = second_gain.astype(jnp.float32)
    shift_two = second_shift.astype(jnp.float32)
    query_shift = lax.dynamic_slice_in_dim(query_bias.astype(jnp.float32), head_start, head_cols)
    value_shift = lax.dynamic_slice_in_dim(value_bias.astype(jnp.float32), head_start, head_cols)
    resid = images.astype(jnp.float32)
    normed, unit_one, spread_one = layer_norm(resid, gain_one, shift_one)
    normed_rows = lax.all_gather(normed.astype(jnp.bfloat16), "tensor", axis=1, tiled=True)
    queries = (dense(normed_rows, query_full) + query_shift).astype(jnp.bfloat16)
    keys_low = dense(normed_rows, key_full).astype(jnp.bfloat16)
    values_low = (dense(normed_rows, value_full) + value_shift).astype(jnp.bfloat16)
    mixed, totals = lax.map(
        lambda items: attend(items[0], items[1], items[2], key_ok), (queries, keys_low, values_low)
    )
    attended = lax.psum_scatter(
        dense(mixed, output_full), "tensor", scatter_dimension=1, tiled=True
    ) + output_bias.astype(jnp.float32)
    middle = row_mask * (resid + attended)
    second, unit_two, spread_two = layer_norm(middle, gain_two, shift_two)
    second_low = second.astype(jnp.bfloat16)
    grad_top = row_mask * cotangent.astype(jnp.float32)
    fed_grad = grad_top.astype(jnp.bfloat16)
    down_shift = down_bias.astype(jnp.float32)
    units = upper_full.shape[1]
    second_rows = lax.all_gather(second_low, "tensor", axis=1, tiled=True)
    up_shift = lax.dynamic_slice_in_dim(up_bias.astype(jnp.float32), tensor_place * units, units)
    hidden = dense(second_rows, upper_full) + up_shift
    sigma = jax.nn.sigmoid(SLOPE * hidden)
    active = (hidden * sigma).astype(jnp.bfloat16)
    fed = (
        lax.psum_scatter(
            dense(active, lower_full).astype(jnp.bfloat16),
            "tensor",
            scatter_dimension=1,
            tiled=True,
        ).astype(jnp.float32)
        + down_shift
    )
    fed_rows = lax.all_gather(fed_grad, "tensor", axis=1, tiled=True)
    grad_active = project_back(fed_rows, lower_full)
    lower_grad = outer(active, fed_rows)
    hidden_grad = (grad_active * (sigma + SLOPE * hidden * sigma * (1.0 - sigma))).astype(
        jnp.bfloat16
    )
    upper_grad = outer(second_rows, hidden_grad)
    up_bias_grad = widen(column_sum(hidden_grad), up_bias.shape[0], tensor_place * units)
    second_grad = lax.psum_scatter(
        project_back(hidden_grad, upper_full), "tensor", scatter_dimension=1, tiled=True
    )
    layer_out = (row_mask * (middle + fed)).astype(jnp.bfloat16)
    down_bias_grad = column_sum(fed_grad)
    middle_back, gain_two_grad, shift_two_grad = norm_back(
        second_grad, unit_two, spread_two, gain_two
    )
    middle_grad = row_mask * (grad_top + middle_back)
    attended_grad = middle_grad.astype(jnp.bfloat16)
    output_bias_grad = column_sum(attended_grad)
    attended_rows = lax.all_gather(attended_grad, "tensor", axis=1, tiled=True)
    grad_mixed = project_back(attended_rows, output_full).astype(jnp.bfloat16)
    output_grad = outer(mixed, attended_rows)
    grad_query, grad_key, grad_value = lax.map(
        lambda items: attend_back(items[0], items[1], items[2], items[3], items[4], key_ok),
        (queries, keys_low, values_low, grad_mixed, totals),
    )
    query_grad = outer(normed_rows, grad_query)
    key_grad = outer(normed_rows, grad_key)
    value_grad = outer(normed_rows, grad_value)
    query_bias_grad = widen(column_sum(grad_query), width, head_start)
    value_bias_grad = widen(column_sum(grad_value), width, head_start)
    normed_terms = (
        project_back(grad_query, query_full)
        + project_back(grad_key, key_full)
        + project_back(grad_value, value_full)
    )
    normed_grad = lax.psum_scatter(
        normed_terms.astype(jnp.bfloat16), "tensor", scatter_dimension=1, tiled=True
    ).astype(jnp.float32)
    first_back, gain_one_grad, shift_one_grad = norm_back(
        normed_grad, unit_one, spread_one, gain_one
    )
    images_grad = middle_grad + first_back
    query_owned, key_owned, value_owned, upper_owned, output_owned, lower_owned = (
        lax.psum_scatter(
            query_grad.astype(jnp.bfloat16), "dp", scatter_dimension=0, tiled=True
        ).astype(jnp.float32),
        lax.psum_scatter(
            key_grad.astype(jnp.bfloat16), "dp", scatter_dimension=0, tiled=True
        ).astype(jnp.float32),
        lax.psum_scatter(
            value_grad.astype(jnp.bfloat16), "dp", scatter_dimension=0, tiled=True
        ).astype(jnp.float32),
        lax.psum_scatter(
            upper_grad.astype(jnp.bfloat16), "dp", scatter_dimension=0, tiled=True
        ).astype(jnp.float32),
        lax.psum_scatter(
            output_grad.astype(jnp.bfloat16), "dp", scatter_dimension=1, tiled=True
        ).astype(jnp.float32),
        lax.psum_scatter(
            lower_grad.astype(jnp.bfloat16), "dp", scatter_dimension=1, tiled=True
        ).astype(jnp.float32),
    )
    vector_sums = lax.psum(
        (
            gain_one_grad,
            shift_one_grad,
            query_bias_grad,
            value_bias_grad,
            output_bias_grad,
            gain_two_grad,
            shift_two_grad,
            up_bias_grad,
            down_bias_grad,
        ),
        ("dp", "tensor"),
    )
    (
        gain_one_total,
        shift_one_total,
        query_bias_total,
        value_bias_total,
        output_bias_total,
        gain_two_total,
        shift_two_total,
        up_bias_total,
        down_bias_total,
    ) = vector_sums
    return (
        layer_out,
        images_grad,
        gain_one_total,
        shift_one_total,
        query_owned,
        query_bias_total,
        key_owned,
        value_owned,
        value_bias_total,
        output_owned,
        output_bias_total,
        gain_two_total,
        shift_two_total,
        upper_owned,
        up_bias_total,
        lower_owned,
        down_bias_total,
    )


BOTH = ("dp", "tensor")
HALF_PAD = 8
LANES = 128
LOW = jnp.bfloat16
VMEM_ROOM = 56 * 2**20


def exchange(value, far_z=0, far_x=0, far_core=0, far_y=0):
    pairs = []
    for place in range(32):
        other = place ^ (far_z * 8 + far_x * 4 + far_core * 2 + far_y)
        pairs.append((place, other))
    return lax.ppermute(value, BOTH, pairs)


def pick_two(bit, own, other, axis):
    first = jnp.where(bit == 0, own, other)
    last = jnp.where(bit == 0, other, own)
    return jnp.stack([first, last], axis)


def after(value, *others):
    return lax.optimization_barrier((value, *others))[0]


def pack(places, sources, shapes, plan):
    def kernel(places_ref, *refs):
        ins, outs = refs[: len(sources)], refs[len(sources) :]
        spots = [places_ref[at] for at in range(4)]
        for at, take, to, put in plan:
            outs[to][put(*spots)] = ins[at][take(*spots)]

    return pl.pallas_call(
        kernel,
        in_specs=[pl.BlockSpec(memory_space=pltpu.SMEM)]
        + [pl.BlockSpec(memory_space=pltpu.VMEM)] * len(sources),
        out_specs=[pl.BlockSpec(memory_space=pltpu.VMEM)] * len(shapes),
        out_shape=[jax.ShapeDtypeStruct(shape, LOW) for shape in shapes],
        compiler_params=pltpu.CompilerParams(vmem_limit_bytes=VMEM_ROOM),
        cost_estimate=pl.CostEstimate(
            flops=0,
            transcendentals=0,
            bytes_accessed=sum(2 * source.size * 2 for source in sources),
        ),
    )(places, *sources)


def gather_piece(keep, send, core):
    deep, wide = keep.shape[1:]
    return pick_two(core, keep, exchange(send, far_core=1), 1).reshape(2, 2 * deep, wide)


def gather_line(piece, others, places):
    rows, wide = piece.shape[1:]
    line = [piece] + others
    plan = []
    for step in range(4):
        for part in range(2):
            plan.append(
                (
                    step,
                    lambda z, x, c, y, part=part: part,
                    part,
                    lambda z, x, c, y, step=step: z ^ step,
                )
            )
    return pack(places, line, [(4, rows, wide)] * 2, plan)


def gather_pairs(places, one, two, one_x, two_y):
    every = slice(None)
    plan = [
        (0, lambda z, x, c, y: every, 0, lambda z, x, c, y: x),
        (1, lambda z, x, c, y: every, 0, lambda z, x, c, y: 1 - x),
        (2, lambda z, x, c, y: every, 1, lambda z, x, c, y: 0),
        (3, lambda z, x, c, y: every, 1, lambda z, x, c, y: 1),
    ]
    return pack(places, [one, one_x, two, two_y], [(2,) + one.shape] * 2, plan)


def gather_all(places, one_pair, two_pair, one_y, two_x, most):
    every = slice(None)
    rows, wide = one_pair.shape[2:]
    plan = []
    for to, low, high in ((0, 0, most), (1, most, wide)):
        span = high - low
        for place_z in range(4):
            for far in range(2):
                for number in range(2):
                    plan.append(
                        (
                            number,
                            lambda z, x, c, y, a=far, p=place_z, lo=low, hi=high: (
                                a,
                                p,
                                every,
                                slice(lo, hi),
                            ),
                            to,
                            lambda z, x, c, y, a=far, p=place_z, n=number, s=span: (
                                p,
                                a,
                                every,
                                slice(n * s, n * s + s),
                            ),
                        )
                    )
                    plan.append(
                        (
                            2 + far,
                            lambda z, x, c, y, n=number, p=place_z, lo=low, hi=high: (
                                n,
                                p,
                                every,
                                slice(lo, hi),
                            ),
                            to,
                            lambda z, x, c, y, f=far, p=place_z, n=number, s=span: (
                                p,
                                x ^ f,
                                every,
                                slice((2 + n) * s, (3 + n) * s),
                            ),
                        )
                    )
    shapes = [(4, 2, rows, 4 * most), (4, 2, rows, 4 * (wide - most))]
    made = pack(places, [one_pair, one_y, two_pair, two_x], shapes, plan)
    return [array.reshape(8 * rows, -1) for array in made]


def low_add(*values):
    total = values[0].astype(jnp.float32)
    for value in values[1:]:
        total = total + value.astype(jnp.float32)
    return total


def line_kernel(one_ref, one_a, one_b, two_ref, two_a, two_b, own_ref, *send_refs):
    tall = own_ref.shape[1]
    for step in range(4):
        rows = slice(step * tall, (step + 1) * tall)
        one = low_add(one_ref[0, rows], one_a[0, rows], one_b[rows])
        two = low_add(two_ref[0, rows], two_a[0, rows], two_b[rows])
        if step == 0:
            own_ref[0] = one
            own_ref[1] = two
        else:
            send_refs[step - 1][0] = one.astype(LOW)
            send_refs[step - 1][1] = two.astype(LOW)


def scatter_first(sends):
    return exchange(sends[0], far_y=1), exchange(sends[1], far_x=1)


def scatter_second(keeps, arrived):
    one = low_add(keeps[0][1], arrived[0][1]).astype(LOW)
    two = low_add(keeps[1][1], arrived[1][1]).astype(LOW)
    return exchange(one, far_x=1), exchange(two, far_y=1)


def scatter_line(keeps, arrived, crossed):
    lines, wide = crossed[0].shape
    tall = lines // 4
    first = pl.BlockSpec((1, lines, wide), lambda i: (0, 0, 0))
    flat = pl.BlockSpec((lines, wide), lambda i: (0, 0))
    piece = pl.BlockSpec((2, tall, wide), lambda i: (0, 0, 0))
    return pl.pallas_call(
        line_kernel,
        grid=(1,),
        in_specs=[first, first, flat, first, first, flat],
        out_specs=[piece] * 4,
        out_shape=[jax.ShapeDtypeStruct((2, tall, wide), jnp.float32)]
        + [jax.ShapeDtypeStruct((2, tall, wide), LOW)] * 3,
        compiler_params=pltpu.CompilerParams(vmem_limit_bytes=VMEM_ROOM),
        cost_estimate=pl.CostEstimate(
            flops=lines * wide * 4, transcendentals=0, bytes_accessed=lines * wide * 18
        ),
    )(keeps[0], arrived[0], crossed[0], keeps[1], arrived[1], crossed[1])


def scatter_z(sends):
    return [exchange(sends[step], far_z=step) for step in (1, 2, 3)]


def scatter_last(own, others, core):
    tall, wide = own.shape[1:]
    total = low_add(own, *others).reshape(2, 2, tall // 2, wide)
    keep = lax.dynamic_index_in_dim(total, core, 1, keepdims=False)
    send = lax.dynamic_index_in_dim(total, 1 - core, 1, keepdims=False)
    far = exchange(send.astype(LOW), far_core=1).astype(jnp.float32)
    return pick_two(core, keep, far, 0)


def vector_first(vector):
    vector = vector + exchange(vector, far_core=1)
    return vector, [exchange(vector, far_z=step) for step in (1, 2, 3)]


def vector_last(vector, others):
    vector = vector + others[0] + others[1] + others[2]
    for step in ({"far_y": 1}, {"far_x": 1}):
        vector = vector + exchange(vector, **step)
    return vector


def mat_far(left, right):
    return lax.dot_general(
        left, right, (((1,), (1,)), ((), ())), preferred_element_type=jnp.float32
    )


def mat_rows(left, right):
    return lax.dot_general(
        left, right, (((0,), (0,)), ((), ())), preferred_element_type=jnp.float32
    )


def fill_rows(made_ref, own_ref, far_ref):
    rows = own_ref.shape[0]

    @pl.when(pl.program_id(0) == 0)
    def _():
        made_ref[:rows] = own_ref[...]
        made_ref[rows:] = far_ref[...]


def up_kernel(
    places_ref, own_ref, far_ref, right_ref, shift_ref, active_ref, slope_ref, left_ref
):
    fill_rows(left_ref, own_ref, far_ref)
    right = right_ref[...].reshape(left_ref.shape[1], -1)
    hidden = jnp.dot(left_ref[...], right, preferred_element_type=jnp.float32)
    hidden = hidden + shift_ref[...]
    sigma = 0.5 * jnp.tanh((0.5 * SLOPE) * hidden) + 0.5
    active = hidden * sigma
    active_ref[...] = active.astype(LOW)
    slope_ref[...] = (sigma + SLOPE * active * (1.0 - sigma)).astype(LOW)


def feed_spec(gathered, start):
    lines, _, rows, wide = gathered.shape
    return pl.BlockSpec(
        (lines, 1, rows, wide // 4), lambda i, s: (0, s[3] ^ (i % 2), 0, start + i // 2)
    )


def up_call(places, pair, gathered, shift):
    rows, width = pair[0].shape
    wide = shift.shape[1] // 4
    whole = pl.BlockSpec((rows, width), lambda i, s: (0, 0))
    piece = pl.BlockSpec((2 * rows, wide), lambda i, s: (0, i))
    return pl.pallas_call(
        up_kernel,
        grid_spec=pltpu.PrefetchScalarGridSpec(
            num_scalar_prefetch=1,
            grid=(4,),
            in_specs=[
                whole,
                whole,
                feed_spec(gathered, 0),
                pl.BlockSpec((1, wide), lambda i, s: (0, i)),
            ],
            out_specs=[piece, piece],
            scratch_shapes=[pltpu.VMEM((2 * rows, width), LOW)],
        ),
        out_shape=[jax.ShapeDtypeStruct((2 * rows, 4 * wide), LOW)] * 2,
        compiler_params=pltpu.CompilerParams(vmem_limit_bytes=VMEM_ROOM),
        cost_estimate=pl.CostEstimate(
            flops=16 * rows * wide * width,
            transcendentals=8 * rows * wide,
            bytes_accessed=rows * width * 4 + 8 * width * wide + 32 * rows * wide,
        ),
    )(places, *pair, gathered, shift)


def hidden_kernel(
    places_ref, own_ref, far_ref, right_ref, slope_ref, out_ref, sum_ref, left_ref
):
    fill_rows(left_ref, own_ref, far_ref)
    right = right_ref[...].reshape(left_ref.shape[1], -1)
    grad = jnp.dot(left_ref[...], right, preferred_element_type=jnp.float32)
    grad = (grad * slope_ref[...].astype(jnp.float32)).astype(LOW)
    out_ref[...] = grad
    sum_ref[...] = jnp.sum(grad.astype(jnp.float32), axis=0, keepdims=True)


def hidden_call(places, pair, gathered, slope):
    rows, width = pair[0].shape
    wide = slope.shape[1] // 4
    whole = pl.BlockSpec((rows, width), lambda i, s: (0, 0))
    piece = pl.BlockSpec((2 * rows, wide), lambda i, s: (0, i))
    return pl.pallas_call(
        hidden_kernel,
        grid_spec=pltpu.PrefetchScalarGridSpec(
            num_scalar_prefetch=1,
            grid=(4,),
            in_specs=[whole, whole, feed_spec(gathered, 2), piece],
            out_specs=[piece, pl.BlockSpec((1, wide), lambda i, s: (0, i))],
            scratch_shapes=[pltpu.VMEM((2 * rows, width), LOW)],
        ),
        out_shape=[
            jax.ShapeDtypeStruct((2 * rows, 4 * wide), LOW),
            jax.ShapeDtypeStruct((1, 4 * wide), jnp.float32),
        ],
        compiler_params=pltpu.CompilerParams(vmem_limit_bytes=VMEM_ROOM),
        cost_estimate=pl.CostEstimate(
            flops=16 * rows * wide * width,
            transcendentals=0,
            bytes_accessed=rows * width * 4 + 8 * width * wide + 32 * rows * wide,
        ),
    )(places, *pair, gathered, slope)


def down_kernel(places_ref, left_ref, right_ref, own_ref, send_ref):
    span = right_ref.shape[3] // 2
    rows = own_ref.shape[0]
    total = None
    for far in range(2):
        right = right_ref[:, places_ref[3] ^ far].reshape(-1, 2 * span)
        for part in range(2):
            start = (part * 2 + far) * span
            one = mat_far(
                left_ref[:, start : start + span], right[:, part * span : (part + 1) * span]
            )
            total = one if total is None else total + one
    own_ref[...] = total[:rows]
    send_ref[...] = total[rows:].astype(LOW)


def down_call(places, left, gathered, start):
    both, deep = left.shape
    rows = both // 2
    lines, _, tall, wide = gathered.shape
    piece = pl.BlockSpec((rows, 2 * tall), lambda i, s: (0, i))
    own, send = pl.pallas_call(
        down_kernel,
        grid_spec=pltpu.PrefetchScalarGridSpec(
            num_scalar_prefetch=1,
            grid=(lines // 2,),
            in_specs=[
                pl.BlockSpec((both, deep), lambda i, s: (0, 0)),
                pl.BlockSpec((2, 2, tall, wide // 2), lambda i, s: (i, 0, 0, start)),
            ],
            out_specs=[piece, piece],
        ),
        out_shape=[
            jax.ShapeDtypeStruct((rows, lines * tall), jnp.float32),
            jax.ShapeDtypeStruct((rows, lines * tall), LOW),
        ],
        compiler_params=pltpu.CompilerParams(vmem_limit_bytes=VMEM_ROOM),
        cost_estimate=pl.CostEstimate(
            flops=2 * both * deep * lines * tall,
            transcendentals=0,
            bytes_accessed=left.size * 2 + lines * tall * deep * 2 + rows * lines * tall * 6,
        ),
    )(places, left, gathered)
    return own + exchange(send, far_core=1).astype(jnp.float32)


def weight_kernel(send, pairs, places_ref, *refs):
    ins, outs, lefts = refs[: 3 * pairs], refs[3 * pairs : 3 * pairs + 2], refs[3 * pairs + 2 :]
    step = pl.program_id(0)

    @pl.when(step < 2)
    def _():
        x_far = step if send else 1 - step
        for pair in range(pairs):
            rows = ins[3 * pair].shape[0]
            for block in range(4):
                at = (places_ref[0] ^ block) * 2 + (places_ref[1] ^ x_far)
                start = pl.multiple_of(at * LANES, LANES)
                for image in range(2):
                    lefts[pair][
                        image * rows : (image + 1) * rows, block * LANES : (block + 1) * LANES
                    ] = ins[3 * pair + image][:, pl.ds(start, LANES)]

    parts = [
        mat_rows(lefts[pair][...], ins[3 * pair + 2][...]).astype(LOW) for pair in range(pairs)
    ]
    made = parts[0] if pairs == 1 else jnp.concatenate(parts, axis=1)

    @pl.when(step < 2)
    def _():
        outs[0][0] = made

    @pl.when(step >= 2)
    def _():
        outs[1][0] = made


def weight_pieces(places, operands, send):
    rows, width = operands[0][0][0].shape
    line = width // 2
    first = (lambda i: jnp.minimum(i, 1)) if send else (lambda i: 1 - jnp.minimum(i, 1))

    def right_map(i, s):
        if send:
            return (0, jnp.where(i < 2, 1, i))
        return (0, jnp.where(i < 2, 0, i))

    specs, arrays, scratch, wide = [], [], [], 0
    for left, right in operands:
        span = right.shape[1] // 4
        wide += span
        for image in range(2):
            specs.append(pl.BlockSpec((rows, width), lambda i, s: (0, 0)))
            arrays.append(left[image])
        specs.append(pl.BlockSpec((2 * rows, span), right_map))
        arrays.append(right)
        scratch.append(pltpu.VMEM((2 * rows, line), LOW))

    def kernel(*refs):
        weight_kernel(send, len(operands), *refs)

    return pl.pallas_call(
        kernel,
        grid_spec=pltpu.PrefetchScalarGridSpec(
            num_scalar_prefetch=1,
            grid=(4,),
            in_specs=specs,
            out_specs=[
                pl.BlockSpec((1, line, wide), lambda i, s: (first(i), 0, 0)),
                pl.BlockSpec((1, line, wide), lambda i, s: (jnp.maximum(i - 2, 0), 0, 0)),
            ],
            scratch_shapes=scratch,
        ),
        out_shape=[jax.ShapeDtypeStruct((2, line, wide), LOW)] * 2,
        compiler_params=pltpu.CompilerParams(vmem_limit_bytes=VMEM_ROOM),
        cost_estimate=pl.CostEstimate(
            flops=16 * rows * line * wide,
            transcendentals=0,
            bytes_accessed=rows * wide * 16 + rows * line * 16 + line * wide * 8,
        ),
    )(places, *arrays)


def lane_of(shape):
    return lax.broadcasted_iota(jnp.int32, shape, 1)


def head_views(query, key, bias, head):
    lane = lane_of(query.shape)
    mine = (lane >= HDIM) if head else (lane < HDIM)
    spot = 0 if head else HDIM
    zero = jnp.zeros_like(query)
    query_view = jnp.where(mine, query, jnp.where(lane == spot, zero + 1, zero))
    key_view = jnp.where(lane == spot, bias, key)
    return mine, query_view, key_view


def attend_kernel(qkv_ref, bias_ref, mixed_ref, total_ref):
    query = qkv_ref[:, 0:LANES] * jnp.bfloat16(HDIM ** (-0.5))
    key = qkv_ref[:, LANES : 2 * LANES]
    value = qkv_ref[:, 2 * LANES : 3 * LANES]
    bias = bias_ref[...]
    sums, tops = [], []
    for head in range(2):
        mine, query_view, key_view = head_views(query, key, bias, head)
        scores = mat_far(query_view, key_view)
        top = jnp.max(scores, axis=1, keepdims=True)
        weight = jnp.exp(scores - top).astype(LOW)
        value_view = jnp.where(mine, value, jnp.ones_like(value))
        sums.append(jnp.dot(weight, value_view, preferred_element_type=jnp.float32))
        tops.append(top)
    low = lane_of(sums[0].shape) < HDIM
    upper = jnp.where(low, sums[0], sums[1])
    lower = jnp.where(low, sums[1], sums[0])
    lower = pltpu.roll(lower, HDIM, 1)
    mixed_ref[...] = (upper / lower).astype(LOW)
    total = jnp.where(low, tops[0], tops[1]) + jnp.log(lower)
    total = jnp.transpose(total)
    total_ref[0, 0:1, :] = total[0:1]
    total_ref[0, 1:2, :] = total[HDIM : HDIM + 1]


def attend_back_kernel(qkv_ref, bias_ref, grad_ref, mixed_ref, total_ref, out_ref):
    scale = HDIM ** (-0.5)
    query = qkv_ref[:, 0:LANES] * jnp.bfloat16(scale)
    key = qkv_ref[:, LANES : 2 * LANES]
    value = qkv_ref[:, 2 * LANES : 3 * LANES]
    bias = bias_ref[...]
    grad = grad_ref[...]
    product = grad.astype(jnp.float32) * mixed_ref[...].astype(jnp.float32)
    grad_query = grad_key = grad_value = None
    for head in range(2):
        mine, query_view, key_view = head_views(query, key, bias, head)
        zero = jnp.zeros_like(query)
        scores = mat_far(key_view, query_view)
        probs = jnp.exp(scores - total_ref[0, head : head + 1, :])
        grad_view = jnp.where(mine, grad, zero)
        grad_probs = mat_far(value, grad_view)
        ones = jnp.where(mine[0:8], 1.0, 0.0)
        inner = lax.dot_general(
            ones,
            product,
            (((1,), (1,)), ((), ())),
            precision=lax.Precision.HIGHEST,
            preferred_element_type=jnp.float32,
        )
        grad_scores = (probs * (grad_probs - inner[0:1])).astype(LOW)
        one_value = jnp.dot(probs.astype(LOW), grad_view, preferred_element_type=jnp.float32)
        one_key = jnp.dot(
            grad_scores, jnp.where(mine, query, zero), preferred_element_type=jnp.float32
        )
        one_query = mat_rows(grad_scores, jnp.where(mine, key, zero))
        grad_query = one_query if head == 0 else grad_query + one_query
        grad_key = one_key if head == 0 else grad_key + one_key
        grad_value = one_value if head == 0 else grad_value + one_value
    out_ref[:, 0:LANES] = (grad_query * scale).astype(LOW)
    out_ref[:, LANES : 2 * LANES] = grad_key.astype(LOW)
    out_ref[:, 2 * LANES : 3 * LANES] = grad_value.astype(LOW)


def attend_image(image, qkv, bias, given):
    both = qkv.shape[0]
    rows = both // 2
    blocks = qkv.shape[1] // (3 * LANES)

    def kernel(*refs):
        attend_kernel(*refs[:2], *refs[-2:])

    return pl.pallas_call(
        kernel,
        grid=(blocks,),
        in_specs=[
            pl.BlockSpec((rows, 3 * LANES), lambda j: (image, j)),
            pl.BlockSpec((rows, LANES), lambda j: (0, 0)),
        ]
        + [pl.BlockSpec(memory_space=pl.ANY)] * len(given),
        out_specs=[
            pl.BlockSpec((rows, LANES), lambda j: (image, j)),
            pl.BlockSpec((1, 8, rows), lambda j: (image * blocks + j, 0, 0)),
        ],
        out_shape=[
            jax.ShapeDtypeStruct((both, blocks * LANES), LOW),
            jax.ShapeDtypeStruct((2 * blocks, 8, rows), jnp.float32),
        ],
        input_output_aliases={2: 0, 3: 1} if given else {},
        compiler_params=pltpu.CompilerParams(vmem_limit_bytes=VMEM_ROOM),
        cost_estimate=pl.CostEstimate(
            flops=blocks * 2 * 2 * 2 * rows * rows * LANES * 2,
            transcendentals=blocks * 2 * rows * rows,
            bytes_accessed=rows * blocks * LANES * 8,
        ),
    )(qkv, bias, *given)


def attend_back_image(image, qkv, bias, grad, mixed, total, given):
    both = qkv.shape[0]
    rows = both // 2
    blocks = qkv.shape[1] // (3 * LANES)

    def kernel(*refs):
        attend_back_kernel(*refs[:5], refs[-1])

    return pl.pallas_call(
        kernel,
        grid=(blocks,),
        in_specs=[
            pl.BlockSpec((rows, 3 * LANES), lambda j: (image, j)),
            pl.BlockSpec((rows, LANES), lambda j: (0, 0)),
            pl.BlockSpec((rows, LANES), lambda j: (0, j)),
            pl.BlockSpec((rows, LANES), lambda j: (image, j)),
            pl.BlockSpec((1, 8, rows), lambda j: (image * blocks + j, 0, 0)),
        ]
        + [pl.BlockSpec(memory_space=pl.ANY)] * len(given),
        out_specs=pl.BlockSpec((rows, 3 * LANES), lambda j: (image, j)),
        out_shape=jax.ShapeDtypeStruct(qkv.shape, LOW),
        input_output_aliases={5: 0} if given else {},
        compiler_params=pltpu.CompilerParams(vmem_limit_bytes=VMEM_ROOM),
        cost_estimate=pl.CostEstimate(
            flops=blocks * 2 * 5 * 2 * rows * rows * LANES * 2,
            transcendentals=blocks * 2 * rows * rows,
            bytes_accessed=rows * blocks * LANES * 16,
        ),
    )(qkv, bias, grad, mixed, total, *given)


def mat(left, right):
    return jnp.dot(left, right, preferred_element_type=jnp.float32)


def flat_norm(values, gain, shift):
    center = values - jnp.mean(values, axis=-1, keepdims=True)
    spread = lax.rsqrt(jnp.mean(center * center, axis=-1, keepdims=True) + EPS)
    unit = center * spread
    return unit * gain + shift, unit, spread


def flat_norm_back(upstream, unit, spread, gain):
    scaled = upstream * gain
    inner = (
        scaled
        - jnp.mean(scaled, axis=-1, keepdims=True)
        - unit * jnp.mean(scaled * unit, axis=-1, keepdims=True)
    )
    return spread * inner, jnp.sum(upstream * unit, axis=0), jnp.sum(upstream, axis=0)


def column_flat(values):
    return jnp.sum(values.astype(jnp.float32), axis=0)


def whole_images(
    images,
    cotangent,
    slot_live,
    first_gain,
    first_shift,
    query_weight,
    query_bias,
    key_weight,
    value_weight,
    value_bias,
    output_weight,
    output_bias,
    second_gain,
    second_shift,
    up_weight,
    up_bias,
    down_weight,
    down_bias,
):
    dp_place = lax.axis_index("dp")
    place_y = lax.axis_index("tensor")
    core, place_x, place_z = dp_place % 2, (dp_place // 2) % 2, dp_place // 4
    places = jnp.stack([place_z, place_x, core, place_y]).astype(jnp.int32)
    strip, width = images.shape[1:]
    half = -(-strip // HALF_PAD) * HALF_PAD
    rows = 2 * half
    depth, head_cols = query_weight.shape
    units = up_weight.shape[1]

    def columns_of(weights, place):
        return [
            lax.dynamic_slice_in_dim(
                weight, place * (weight.shape[1] // 2), weight.shape[1] // 2, 1
            )
            for weight in weights
        ]

    def core_parts(weights, place):
        cuts = columns_of(weights, place)
        parts = []
        for part in range(2):
            spans = [cut.shape[1] // 2 for cut in cuts]
            parts.append(
                jnp.concatenate(
                    [cut[:, part * span : (part + 1) * span] for cut, span in zip(cuts, spans)], 1
                )
            )
        return jnp.stack(parts)

    feeds = [up_weight, down_weight.T]
    feed_keep = jnp.concatenate(columns_of(feeds, core), 1)
    feed_send = jnp.concatenate(columns_of(feeds, 1 - core), 1)
    feed = pick_two(core, feed_keep, exchange(feed_send, far_core=1), 0)
    groups = [[place for place in range(32) if (place // 2) % 2 == at] for at in range(2)]
    gathered = lax.all_gather(
        feed.reshape(2 * depth, -1),
        BOTH,
        axis=0,
        tiled=True,
        axis_index_groups=groups,
    ).reshape(8, 2, 2 * depth, -1)

    heads = [query_weight, key_weight, value_weight, output_weight.T]
    piece_one = gather_piece(core_parts(heads, core), core_parts(heads, 1 - core), core)
    others_one = scatter_z([None, piece_one, piece_one, piece_one])

    padding = ((0, 0), (0, half - strip), (0, 0))

    def own_and_far(slots, *waits):
        slots = jnp.pad(slots, padding)
        mine = lax.dynamic_index_in_dim(slots, place_y, 0, keepdims=False)
        theirs = lax.dynamic_index_in_dim(slots, 1 - place_y, 0, keepdims=False)
        return mine, exchange(after(theirs, *waits), far_y=1)

    image_mine, image_far = own_and_far(images, piece_one)
    line_one = gather_line(piece_one, others_one, places)
    cross_one = exchange(line_one[0], far_x=1), exchange(line_one[1], far_y=1)
    pair_one = gather_pairs(places, *line_one, *cross_one)
    image_far = after(image_far, *pair_one)
    whole = jnp.concatenate([image_mine, image_far], 0)

    def head_columns(vector):
        table = vector.astype(jnp.float32).reshape(2, 2, 2, -1)
        table = lax.dynamic_index_in_dim(table, core, 1, keepdims=False)
        table = jnp.where(place_y == 0, table, table[::-1])
        return table.transpose(1, 0, 2).reshape(4, 1, -1)

    def spread_core(table):
        table = jnp.stack(
            [jnp.where(core == 0, table, 0.0), jnp.where(core == 1, table, 0.0)], 1
        )
        return table.reshape(-1)

    def head_spread(vector):
        table = vector.reshape(2, 2, -1).transpose(1, 0, 2)
        return spread_core(jnp.where(place_y == 0, table, table[::-1]))

    gain_one, shift_one = first_gain.astype(jnp.float32), first_shift.astype(jnp.float32)
    gain_two, shift_two = second_gain.astype(jnp.float32), second_shift.astype(jnp.float32)
    query_shift, value_shift = head_columns(query_bias), head_columns(value_bias)
    qkv_shift = jnp.concatenate(
        [query_shift, jnp.zeros_like(query_shift), value_shift], 1
    ).reshape(-1)
    up_shift = head_columns(up_bias).reshape(1, -1)

    row = jnp.arange(rows)
    in_half = row % half
    spot = jnp.where(row < half, place_y, 1 - place_y) * strip + in_half
    ok = (in_half < strip) & (spot < VALID)
    live = lax.dynamic_index_in_dim(slot_live, place_y, 0, keepdims=False).astype(jnp.float32)
    row_mask = (live * ok.astype(jnp.float32))[:, None]
    key_bias = jnp.broadcast_to(
        jnp.where(ok, 0.0, NEGATIVE).astype(LOW)[:, None], (rows, LANES)
    )

    resid = whole.astype(jnp.float32)

    def full_columns(owned):
        return owned.transpose(2, 0, 1, 3).reshape(depth, -1)

    def pair_of(own):
        return own, exchange(own, far_core=1)

    normed, unit_one, spread_one = flat_norm(resid, gain_one, shift_one)
    normed_pair = pair_of(normed.astype(LOW))

    last_one = exchange(pair_one[0], far_y=1), exchange(pair_one[1], far_x=1)
    qkv_full, output_full = gather_all(after(places, *normed_pair), *pair_one, *last_one, 3 * head_cols // 4)

    grad_mine, grad_far = own_and_far(cotangent, qkv_full)
    normed_rows = jnp.concatenate(normed_pair, 0)
    qkv = (mat(normed_rows, qkv_full) + qkv_shift).astype(LOW)
    mixed_half = attend_image(1, qkv, key_bias, [])
    mixed_far = mat_far(mixed_half[0][rows:], output_full).astype(LOW)
    mixed_sum = exchange(mixed_far, far_core=1)
    mixed, totals = attend_image(0, qkv, key_bias, list(after(tuple(mixed_half), mixed_far)))
    grad_far = after(grad_far, mixed)
    grad_top = row_mask * jnp.concatenate([grad_mine, grad_far], 0).astype(jnp.float32)
    fed_grad = grad_top.astype(LOW)
    fed_pair = pair_of(fed_grad)
    attended = mat_far(mixed[:rows], output_full) + mixed_sum.astype(jnp.float32)
    attended = attended + output_bias.astype(jnp.float32)
    middle = row_mask * (resid + attended)
    second, unit_two, spread_two = flat_norm(middle, gain_two, shift_two)
    second_pair = pair_of(second.astype(LOW))
    active, slope = up_call(places, second_pair, gathered, up_shift)

    lower_sends = weight_pieces(places, [(fed_pair, active)], True)
    lower_first = scatter_first(lower_sends)
    fed_late = after(fed_pair, *lower_sends)
    hidden_grad, up_bias_sums = hidden_call(places, fed_late, gathered, slope)
    up_sends = weight_pieces(places, [(second_pair, hidden_grad)], True)
    up_first = scatter_first(up_sends)
    active_late = after(active, *up_sends)
    lower_keeps = weight_pieces(places, [(fed_pair, active_late)], False)
    lower_first = after(lower_first, *lower_keeps)
    lower_second = scatter_second(lower_keeps, lower_first)
    hidden_late = after(hidden_grad, *lower_first)
    second_grad = down_call(places, hidden_late, gathered, 0)
    middle_back, gain_two_grad, shift_two_grad = flat_norm_back(
        second_grad, unit_two, spread_two, gain_two
    )
    middle_grad = row_mask * (grad_top + middle_back)
    attended_grad = middle_grad.astype(LOW)
    attended_pair = pair_of(attended_grad)
    up_keeps = weight_pieces(places, [(second_pair, after(hidden_late, attended_grad))], False)
    lower_second = after(lower_second, *up_keeps)
    lower_line = scatter_line(lower_keeps, lower_first, lower_second)
    lower_z = scatter_z(lower_line)
    up_first = after(up_first, *up_keeps)
    up_second = scatter_second(up_keeps, up_first)
    grad_mixed = [mat(one, output_full).astype(LOW) for one in attended_pair]
    grad_mixed = after(tuple(grad_mixed), *up_first, *lower_line)
    back = attend_back_image(0, qkv, key_bias, grad_mixed[0], mixed, totals, [])
    lower_z = after(tuple(lower_z), back)
    lower_owned = full_columns(scatter_last(lower_line[0], lower_z, core))
    up_line = scatter_line(up_keeps, up_first, after(up_second, back))
    up_z = scatter_z(up_line)
    back = after(back, *up_line)
    back = attend_back_image(1, qkv, key_bias, grad_mixed[1], mixed, totals, [back])
    up_z = after(tuple(up_z), back)
    back = after(back, *up_z)
    upper_owned = full_columns(scatter_last(up_line[0], up_z, core))
    operands = [(normed_pair, back), (attended_pair, mixed)]
    last_sends = weight_pieces(places, operands, True)
    last_first = scatter_first(last_sends)
    back_late = after(back, *last_sends)
    normed_far = exchange(mat_far(back_late[rows:], qkv_full).astype(LOW), far_core=1)
    normed_grad = mat_far(back_late[:rows], qkv_full) + normed_far.astype(jnp.float32)
    last_keeps = weight_pieces(places, operands, False)
    first_back, gain_one_grad, shift_one_grad = flat_norm_back(
        normed_grad, unit_one, spread_one, gain_one
    )
    images_own = middle_grad + first_back
    qkv_sums = column_flat(back).reshape(4, 3, -1)
    vector = jnp.concatenate(
        [
            column_flat(attended_grad),
            gain_two_grad,
            shift_two_grad,
            column_flat(fed_grad),
            head_spread(up_bias_sums.reshape(-1)),
            gain_one_grad,
            shift_one_grad,
            head_spread(qkv_sums[:, 0].reshape(-1)),
            head_spread(qkv_sums[:, 2].reshape(-1)),
        ]
    )
    last_first = after(last_first, last_keeps)
    last_second = scatter_second(last_keeps, last_first)
    vector, vectors = vector_first(vector)
    last_line = scatter_line(last_keeps, last_first, after(last_second, images_own, *vectors))
    last_z = scatter_z(last_line)
    fed = down_call(places, after(active, last_keeps), gathered, 1)
    layer_own = (row_mask * (middle + fed + down_bias.astype(jnp.float32))).astype(LOW)
    vector = vector_last(vector, vectors)
    last_z = after(tuple(last_z), vector)
    last_owned = scatter_last(last_line[0], last_z, core)

    def to_strips(own, send):
        return pick_two(place_y, own[:strip], exchange(send, far_y=1).astype(own.dtype), 0)

    layer_out = to_strips(layer_own, layer_own[half : half + strip])
    images_grad = to_strips(images_own, images_own[half : half + strip].astype(LOW))
    def head_grad(at):
        return full_columns(last_owned[..., at * LANES : (at + 1) * LANES])

    early, late = vector[: 4 * width + up_bias.shape[0]], vector[4 * width + up_bias.shape[0] :]
    return (
        layer_out,
        images_grad,
        late[:width],
        late[width : 2 * width],
        head_grad(0),
        late[2 * width : 3 * width],
        head_grad(1),
        head_grad(2),
        late[3 * width :],
        head_grad(3).T,
        early[:width],
        early[width : 2 * width],
        early[2 * width : 3 * width],
        upper_owned,
        early[4 * width :],
        lower_owned.T,
        early[3 * width : 4 * width],
    )


def pick(mesh):
    sizes = dict(mesh.shape)
    if sizes["dp"] == 16 and sizes["tensor"] == 2:
        return whole_images
    return local


def solution(mesh):
    in_specs = (
        P("dp", "tensor", None),
        P("dp", "tensor", None),
        P("dp"),
        P(),
        P(),
        P("dp", "tensor"),
        P(),
        P("dp", "tensor"),
        P("dp", "tensor"),
        P(),
        P("tensor", "dp"),
        P(),
        P(),
        P(),
        P("dp", "tensor"),
        P(),
        P("tensor", "dp"),
        P(),
    )
    out_specs = (
        P("dp", "tensor", None),
        P("dp", "tensor", None),
        P(),
        P(),
        P("dp", "tensor"),
        P(),
        P("dp", "tensor"),
        P("dp", "tensor"),
        P(),
        P("tensor", "dp"),
        P(),
        P(),
        P(),
        P("dp", "tensor"),
        P(),
        P("tensor", "dp"),
        P(),
    )
    return jax.shard_map(pick(mesh), mesh=mesh, in_specs=in_specs, out_specs=out_specs, check_vma=False)
```

```python
import jax
import jax.numpy as jnp
from jax import lax
from jax.experimental import pallas as pl
from jax.experimental.pallas import tpu as pltpu
from jax.sharding import PartitionSpec as P

HDIM = 64
VALID = 577


EPS = 1e-05
NEGATIVE = -1e30
SLOPE = 1.702


def layer_norm(values, gain, shift):
    center = values - jnp.mean(values, axis=-1, keepdims=True)
    spread = lax.rsqrt(jnp.mean(center * center, axis=-1, keepdims=True) + EPS)
    unit = center * spread
    return (unit * gain + shift, unit, spread)


def norm_back(upstream, unit, spread, gain):
    scaled = upstream * gain
    inner = (
        scaled
        - jnp.mean(scaled, axis=-1, keepdims=True)
        - unit * jnp.mean(scaled * unit, axis=-1, keepdims=True)
    )
    return (spread * inner, jnp.sum(upstream * unit, axis=(0, 1)), jnp.sum(upstream, axis=(0, 1)))


def dense(left, right):
    return jnp.einsum("spa,ab->spb", left, right, preferred_element_type=jnp.float32)


def project_back(left, right):
    return jnp.einsum("spa,ba->spb", left, right, preferred_element_type=jnp.float32)


def outer(left, right):
    return jnp.einsum("spa,spb->ab", left, right, preferred_element_type=jnp.float32)


def column_sum(values):
    return jnp.sum(values.astype(jnp.float32), axis=(0, 1))


def widen(piece, length, start):
    return lax.dynamic_update_slice_in_dim(jnp.zeros((length,), jnp.float32), piece, start, 0)


def split_heads(block):
    return block.reshape(block.shape[0], -1, HDIM)


def scores_of(query, key, key_ok):
    raw = jnp.einsum(
        "qhe,khe->hqk", split_heads(query), split_heads(key), preferred_element_type=jnp.float32
    )
    return jnp.where(key_ok[None, None, :], raw * HDIM ** (-0.5), NEGATIVE)


def attend(query, key, value, key_ok):
    scores = scores_of(query, key, key_ok)
    top = jnp.max(scores, axis=-1, keepdims=True)
    total = top + jnp.log(jnp.sum(jnp.exp(scores - top), axis=-1, keepdims=True))
    probs = jnp.exp(scores - total).astype(jnp.bfloat16)
    mixed = jnp.einsum(
        "hqk,khe->qhe", probs, split_heads(value), preferred_element_type=jnp.float32
    )
    return (mixed.reshape(query.shape[0], -1).astype(jnp.bfloat16), total)


def attend_back(query, key, value, grad_mixed, total, key_ok):
    scores = scores_of(query, key, key_ok)
    probs = jnp.exp(scores - total)
    grad_heads = split_heads(grad_mixed)
    grad_probs = jnp.einsum(
        "qhe,khe->hqk", grad_heads, split_heads(value), preferred_element_type=jnp.float32
    )
    grad_value = jnp.einsum(
        "hqk,qhe->khe", probs.astype(jnp.bfloat16), grad_heads, preferred_element_type=jnp.float32
    )
    grad_scores = (
        probs * (grad_probs - jnp.sum(probs * grad_probs, axis=-1, keepdims=True))
    ).astype(jnp.bfloat16)
    grad_query = jnp.einsum(
        "hqk,khe->qhe", grad_scores, split_heads(key), preferred_element_type=jnp.float32
    ) * HDIM ** (-0.5)
    grad_key = jnp.einsum(
        "hqk,qhe->khe", grad_scores, split_heads(query), preferred_element_type=jnp.float32
    ) * HDIM ** (-0.5)
    length = query.shape[0]
    return (
        grad_query.reshape(length, -1).astype(jnp.bfloat16),
        grad_key.reshape(length, -1).astype(jnp.bfloat16),
        grad_value.reshape(length, -1).astype(jnp.bfloat16),
    )


def local(
    images,
    cotangent,
    slot_live,
    first_gain,
    first_shift,
    query_weight,
    query_bias,
    key_weight,
    value_weight,
    value_bias,
    output_weight,
    output_bias,
    second_gain,
    second_shift,
    up_weight,
    up_bias,
    down_weight,
    down_bias,
):
    slots, strip, width = images.shape
    tensor_count = lax.axis_size("tensor")
    tensor_place = lax.axis_index("tensor")
    seq_len = strip * tensor_count
    positions = tensor_place * strip + jnp.arange(strip)
    row_mask = (
        slot_live.astype(jnp.float32)[:, None, None]
        * (positions < VALID).astype(jnp.float32)[None, :, None]
    )
    key_ok = jnp.arange(seq_len) < VALID
    query_full, key_full, value_full, upper_full, output_full, lower_full = (
        lax.all_gather(query_weight, "dp", axis=0, tiled=True),
        lax.all_gather(key_weight, "dp", axis=0, tiled=True),
        lax.all_gather(value_weight, "dp", axis=0, tiled=True),
        lax.all_gather(up_weight, "dp", axis=0, tiled=True),
        lax.all_gather(output_weight, "dp", axis=1, tiled=True),
        lax.all_gather(down_weight, "dp", axis=1, tiled=True),
    )
    head_cols = query_full.shape[1]
    head_start = tensor_place * head_cols
    gain_one = first_gain.astype(jnp.float32)
    shift_one = first_shift.astype(jnp.float32)
    gain_two = second_gain.astype(jnp.float32)
    shift_two = second_shift.astype(jnp.float32)
    query_shift = lax.dynamic_slice_in_dim(query_bias.astype(jnp.float32), head_start, head_cols)
    value_shift = lax.dynamic_slice_in_dim(value_bias.astype(jnp.float32), head_start, head_cols)
    resid = images.astype(jnp.float32)
    normed, unit_one, spread_one = layer_norm(resid, gain_one, shift_one)
    normed_rows = lax.all_gather(normed.astype(jnp.bfloat16), "tensor", axis=1, tiled=True)
    queries = (dense(normed_rows, query_full) + query_shift).astype(jnp.bfloat16)
    keys_low = dense(normed_rows, key_full).astype(jnp.bfloat16)
    values_low = (dense(normed_rows, value_full) + value_shift).astype(jnp.bfloat16)
    mixed, totals = lax.map(
        lambda items: attend(items[0], items[1], items[2], key_ok), (queries, keys_low, values_low)
    )
    attended = lax.psum_scatter(
        dense(mixed, output_full), "tensor", scatter_dimension=1, tiled=True
    ) + output_bias.astype(jnp.float32)
    middle = row_mask * (resid + attended)
    second, unit_two, spread_two = layer_norm(middle, gain_two, shift_two)
    second_low = second.astype(jnp.bfloat16)
    grad_top = row_mask * cotangent.astype(jnp.float32)
    fed_grad = grad_top.astype(jnp.bfloat16)
    down_shift = down_bias.astype(jnp.float32)
    units = upper_full.shape[1]
    second_rows = lax.all_gather(second_low, "tensor", axis=1, tiled=True)
    up_shift = lax.dynamic_slice_in_dim(up_bias.astype(jnp.float32), tensor_place * units, units)
    hidden = dense(second_rows, upper_full) + up_shift
    sigma = jax.nn.sigmoid(SLOPE * hidden)
    active = (hidden * sigma).astype(jnp.bfloat16)
    fed = (
        lax.psum_scatter(
            dense(active, lower_full).astype(jnp.bfloat16),
            "tensor",
            scatter_dimension=1,
            tiled=True,
        ).astype(jnp.float32)
        + down_shift
    )
    fed_rows = lax.all_gather(fed_grad, "tensor", axis=1, tiled=True)
    grad_active = project_back(fed_rows, lower_full)
    lower_grad = outer(active, fed_rows)
    hidden_grad = (grad_active * (sigma + SLOPE * hidden * sigma * (1.0 - sigma))).astype(
        jnp.bfloat16
    )
    upper_grad = outer(second_rows, hidden_grad)
    up_bias_grad = widen(column_sum(hidden_grad), up_bias.shape[0], tensor_place * units)
    second_grad = lax.psum_scatter(
        project_back(hidden_grad, upper_full), "tensor", scatter_dimension=1, tiled=True
    )
    layer_out = (row_mask * (middle + fed)).astype(jnp.bfloat16)
    down_bias_grad = column_sum(fed_grad)
    middle_back, gain_two_grad, shift_two_grad = norm_back(
        second_grad, unit_two, spread_two, gain_two
    )
    middle_grad = row_mask * (grad_top + middle_back)
    attended_grad = middle_grad.astype(jnp.bfloat16)
    output_bias_grad = column_sum(attended_grad)
    attended_rows = lax.all_gather(attended_grad, "tensor", axis=1, tiled=True)
    grad_mixed = project_back(attended_rows, output_full).astype(jnp.bfloat16)
    output_grad = outer(mixed, attended_rows)
    grad_query, grad_key, grad_value = lax.map(
        lambda items: attend_back(items[0], items[1], items[2], items[3], items[4], key_ok),
        (queries, keys_low, values_low, grad_mixed, totals),
    )
    query_grad = outer(normed_rows, grad_query)
    key_grad = outer(normed_rows, grad_key)
    value_grad = outer(normed_rows, grad_value)
    query_bias_grad = widen(column_sum(grad_query), width, head_start)
    value_bias_grad = widen(column_sum(grad_value), width, head_start)
    normed_terms = (
        project_back(grad_query, query_full)
        + project_back(grad_key, key_full)
        + project_back(grad_value, value_full)
    )
    normed_grad = lax.psum_scatter(
        normed_terms.astype(jnp.bfloat16), "tensor", scatter_dimension=1, tiled=True
    ).astype(jnp.float32)
    first_back, gain_one_grad, shift_one_grad = norm_back(
        normed_grad, unit_one, spread_one, gain_one
    )
    images_grad = middle_grad + first_back
    query_owned, key_owned, value_owned, upper_owned, output_owned, lower_owned = (
        lax.psum_scatter(
            query_grad.astype(jnp.bfloat16), "dp", scatter_dimension=0, tiled=True
        ).astype(jnp.float32),
        lax.psum_scatter(
            key_grad.astype(jnp.bfloat16), "dp", scatter_dimension=0, tiled=True
        ).astype(jnp.float32),
        lax.psum_scatter(
            value_grad.astype(jnp.bfloat16), "dp", scatter_dimension=0, tiled=True
        ).astype(jnp.float32),
        lax.psum_scatter(
            upper_grad.astype(jnp.bfloat16), "dp", scatter_dimension=0, tiled=True
        ).astype(jnp.float32),
        lax.psum_scatter(
            output_grad.astype(jnp.bfloat16), "dp", scatter_dimension=1, tiled=True
        ).astype(jnp.float32),
        lax.psum_scatter(
            lower_grad.astype(jnp.bfloat16), "dp", scatter_dimension=1, tiled=True
        ).astype(jnp.float32),
    )
    vector_sums = lax.psum(
        (
            gain_one_grad,
            shift_one_grad,
            query_bias_grad,
            value_bias_grad,
            output_bias_grad,
            gain_two_grad,
            shift_two_grad,
            up_bias_grad,
            down_bias_grad,
        ),
        ("dp", "tensor"),
    )
    (
        gain_one_total,
        shift_one_total,
        query_bias_total,
        value_bias_total,
        output_bias_total,
        gain_two_total,
        shift_two_total,
        up_bias_total,
        down_bias_total,
    ) = vector_sums
    return (
        layer_out,
        images_grad,
        gain_one_total,
        shift_one_total,
        query_owned,
        query_bias_total,
        key_owned,
        value_owned,
        value_bias_total,
        output_owned,
        output_bias_total,
        gain_two_total,
        shift_two_total,
        upper_owned,
        up_bias_total,
        lower_owned,
        down_bias_total,
    )


BOTH = ("dp", "tensor")
HALF_PAD = 8
LANES = 128
LOW = jnp.bfloat16
VMEM_ROOM = 24 * 2**20


def exchange(value, far_z=0, far_x=0, far_core=0, far_y=0):
    pairs = []
    for place in range(32):
        other = place ^ (far_z * 8 + far_x * 4 + far_core * 2 + far_y)
        pairs.append((place, other))
    return lax.ppermute(value, BOTH, pairs)


def pick_two(bit, own, other, axis):
    first = jnp.where(bit == 0, own, other)
    last = jnp.where(bit == 0, other, own)
    return jnp.stack([first, last], axis)


def after(value, *others):
    return lax.optimization_barrier((value, *others))[0]


def pack(places, sources, shapes, plan):
    def kernel(places_ref, *refs):
        ins, outs = refs[: len(sources)], refs[len(sources) :]
        spots = [places_ref[at] for at in range(4)]
        for at, take, to, put in plan:
            outs[to][put(*spots)] = ins[at][take(*spots)]

    return pl.pallas_call(
        kernel,
        in_specs=[pl.BlockSpec(memory_space=pltpu.SMEM)]
        + [pl.BlockSpec(memory_space=pltpu.VMEM)] * len(sources),
        out_specs=[pl.BlockSpec(memory_space=pltpu.VMEM)] * len(shapes),
        out_shape=[jax.ShapeDtypeStruct(shape, LOW) for shape in shapes],
        compiler_params=pltpu.CompilerParams(vmem_limit_bytes=VMEM_ROOM),
        cost_estimate=pl.CostEstimate(
            flops=0,
            transcendentals=0,
            bytes_accessed=sum(2 * source.size * 2 for source in sources),
        ),
    )(places, *sources)


def gather_piece(keep, send, core):
    deep, wide = keep.shape[1:]
    return pick_two(core, keep, exchange(send, far_core=1), 1).reshape(2, 2 * deep, wide)


def gather_line(piece, others, places):
    rows, wide = piece.shape[1:]
    line = [piece] + others
    plan = []
    for step in range(4):
        for part in range(2):
            plan.append(
                (
                    step,
                    lambda z, x, c, y, part=part: part,
                    part,
                    lambda z, x, c, y, step=step: z ^ step,
                )
            )
    return pack(places, line, [(4, rows, wide)] * 2, plan)


def gather_pairs(places, one, two, one_x, two_y):
    every = slice(None)
    plan = [
        (0, lambda z, x, c, y: every, 0, lambda z, x, c, y: x),
        (1, lambda z, x, c, y: every, 0, lambda z, x, c, y: 1 - x),
        (2, lambda z, x, c, y: every, 1, lambda z, x, c, y: 0),
        (3, lambda z, x, c, y: every, 1, lambda z, x, c, y: 1),
    ]
    return pack(places, [one, one_x, two, two_y], [(2,) + one.shape] * 2, plan)


def gather_all(places, one_pair, two_pair, one_y, two_x, most):
    every = slice(None)
    rows, wide = one_pair.shape[2:]
    plan = []
    for to, low, high in ((0, 0, most), (1, most, wide)):
        span = high - low
        for place_z in range(4):
            for far in range(2):
                for number in range(2):
                    plan.append(
                        (
                            number,
                            lambda z, x, c, y, a=far, p=place_z, lo=low, hi=high: (
                                a,
                                p,
                                every,
                                slice(lo, hi),
                            ),
                            to,
                            lambda z, x, c, y, a=far, p=place_z, n=number, s=span: (
                                p,
                                a,
                                every,
                                slice(n * s, n * s + s),
                            ),
                        )
                    )
                    plan.append(
                        (
                            2 + far,
                            lambda z, x, c, y, n=number, p=place_z, lo=low, hi=high: (
                                n,
                                p,
                                every,
                                slice(lo, hi),
                            ),
                            to,
                            lambda z, x, c, y, f=far, p=place_z, n=number, s=span: (
                                p,
                                x ^ f,
                                every,
                                slice((2 + n) * s, (3 + n) * s),
                            ),
                        )
                    )
    shapes = [(4, 2, rows, 4 * most), (4, 2, rows, 4 * (wide - most))]
    made = pack(places, [one_pair, one_y, two_pair, two_x], shapes, plan)
    return [array.reshape(8 * rows, -1) for array in made]


def low_add(*values):
    total = values[0].astype(jnp.float32)
    for value in values[1:]:
        total = total + value.astype(jnp.float32)
    return total


def line_kernel(one_ref, one_a, one_b, two_ref, two_a, two_b, own_ref, *send_refs):
    tall = own_ref.shape[1]
    for step in range(4):
        rows = slice(step * tall, (step + 1) * tall)
        one = low_add(one_ref[0, rows], one_a[0, rows], one_b[rows])
        two = low_add(two_ref[0, rows], two_a[0, rows], two_b[rows])
        if step == 0:
            own_ref[0] = one
            own_ref[1] = two
        else:
            send_refs[step - 1][0] = one.astype(LOW)
            send_refs[step - 1][1] = two.astype(LOW)


def scatter_first(sends):
    return exchange(sends[0], far_y=1), exchange(sends[1], far_x=1)


def scatter_second(keeps, arrived):
    one = low_add(keeps[0][1], arrived[0][1]).astype(LOW)
    two = low_add(keeps[1][1], arrived[1][1]).astype(LOW)
    return exchange(one, far_x=1), exchange(two, far_y=1)


def scatter_line(keeps, arrived, crossed):
    lines, wide = crossed[0].shape
    tall = lines // 4
    first = pl.BlockSpec((1, lines, wide), lambda i: (0, 0, 0))
    flat = pl.BlockSpec((lines, wide), lambda i: (0, 0))
    piece = pl.BlockSpec((2, tall, wide), lambda i: (0, 0, 0))
    return pl.pallas_call(
        line_kernel,
        grid=(1,),
        in_specs=[first, first, flat, first, first, flat],
        out_specs=[piece] * 4,
        out_shape=[jax.ShapeDtypeStruct((2, tall, wide), jnp.float32)]
        + [jax.ShapeDtypeStruct((2, tall, wide), LOW)] * 3,
        compiler_params=pltpu.CompilerParams(vmem_limit_bytes=VMEM_ROOM),
        cost_estimate=pl.CostEstimate(
            flops=lines * wide * 4, transcendentals=0, bytes_accessed=lines * wide * 18
        ),
    )(keeps[0], arrived[0], crossed[0], keeps[1], arrived[1], crossed[1])


def scatter_z(sends):
    return [exchange(sends[step], far_z=step) for step in (1, 2, 3)]


def scatter_last(own, others, core):
    tall, wide = own.shape[1:]
    total = low_add(own, *others).reshape(2, 2, tall // 2, wide)
    keep = lax.dynamic_index_in_dim(total, core, 1, keepdims=False)
    send = lax.dynamic_index_in_dim(total, 1 - core, 1, keepdims=False)
    far = exchange(send.astype(LOW), far_core=1).astype(jnp.float32)
    return pick_two(core, keep, far, 0)


def vector_first(vector):
    vector = vector + exchange(vector, far_core=1)
    return vector, [exchange(vector, far_z=step) for step in (1, 2, 3)]


def mat_far(left, right):
    return lax.dot_general(
        left, right, (((1,), (1,)), ((), ())), preferred_element_type=jnp.float32
    )


def mat_rows(left, right):
    return lax.dot_general(
        left, right, (((0,), (0,)), ((), ())), preferred_element_type=jnp.float32
    )


def fill_rows(made_ref, own_ref, far_ref):
    rows = own_ref.shape[0]

    @pl.when(pl.program_id(0) == 0)
    def _():
        made_ref[:rows] = own_ref[...]
        made_ref[rows:] = far_ref[...]


def up_kernel(
    places_ref, own_ref, far_ref, right_ref, shift_ref, active_ref, slope_ref, left_ref
):
    fill_rows(left_ref, own_ref, far_ref)
    right = right_ref[...].reshape(left_ref.shape[1], -1)
    hidden = jnp.dot(left_ref[...], right, preferred_element_type=jnp.float32)
    hidden = hidden + shift_ref[...]
    sigma = 0.5 * jnp.tanh((0.5 * SLOPE) * hidden) + 0.5
    active = hidden * sigma
    active_ref[...] = active.astype(LOW)
    slope_ref[...] = (sigma + SLOPE * active * (1.0 - sigma)).astype(LOW)


def feed_spec(gathered, start):
    lines, _, rows, wide = gathered.shape
    return pl.BlockSpec(
        (lines, 1, rows, wide // 4), lambda i, s: (0, s[3] ^ (i % 2), 0, start + i // 2)
    )


def up_call(places, pair, gathered, shift):
    rows, width = pair[0].shape
    wide = shift.shape[1] // 4
    whole = pl.BlockSpec((rows, width), lambda i, s: (0, 0))
    piece = pl.BlockSpec((2 * rows, wide), lambda i, s: (0, i))
    return pl.pallas_call(
        up_kernel,
        grid_spec=pltpu.PrefetchScalarGridSpec(
            num_scalar_prefetch=1,
            grid=(4,),
            in_specs=[
                whole,
                whole,
                feed_spec(gathered, 0),
                pl.BlockSpec((1, wide), lambda i, s: (0, i)),
            ],
            out_specs=[piece, piece],
            scratch_shapes=[pltpu.VMEM((2 * rows, width), LOW)],
        ),
        out_shape=[jax.ShapeDtypeStruct((2 * rows, 4 * wide), LOW)] * 2,
        compiler_params=pltpu.CompilerParams(vmem_limit_bytes=VMEM_ROOM),
        cost_estimate=pl.CostEstimate(
            flops=16 * rows * wide * width,
            transcendentals=8 * rows * wide,
            bytes_accessed=rows * width * 4 + 8 * width * wide + 32 * rows * wide,
        ),
    )(places, *pair, gathered, shift)


def hidden_kernel(
    places_ref, own_ref, far_ref, right_ref, slope_ref, out_ref, sum_ref, left_ref
):
    fill_rows(left_ref, own_ref, far_ref)
    right = right_ref[...].reshape(left_ref.shape[1], -1)
    grad = jnp.dot(left_ref[...], right, preferred_element_type=jnp.float32)
    grad = (grad * slope_ref[...].astype(jnp.float32)).astype(LOW)
    out_ref[...] = grad
    sum_ref[...] = jnp.sum(grad.astype(jnp.float32), axis=0, keepdims=True)


def hidden_call(places, pair, gathered, slope):
    rows, width = pair[0].shape
    wide = slope.shape[1] // 4
    whole = pl.BlockSpec((rows, width), lambda i, s: (0, 0))
    piece = pl.BlockSpec((2 * rows, wide), lambda i, s: (0, i))
    return pl.pallas_call(
        hidden_kernel,
        grid_spec=pltpu.PrefetchScalarGridSpec(
            num_scalar_prefetch=1,
            grid=(4,),
            in_specs=[whole, whole, feed_spec(gathered, 2), piece],
            out_specs=[piece, pl.BlockSpec((1, wide), lambda i, s: (0, i))],
            scratch_shapes=[pltpu.VMEM((2 * rows, width), LOW)],
        ),
        out_shape=[
            jax.ShapeDtypeStruct((2 * rows, 4 * wide), LOW),
            jax.ShapeDtypeStruct((1, 4 * wide), jnp.float32),
        ],
        compiler_params=pltpu.CompilerParams(vmem_limit_bytes=VMEM_ROOM),
        cost_estimate=pl.CostEstimate(
            flops=16 * rows * wide * width,
            transcendentals=0,
            bytes_accessed=rows * width * 4 + 8 * width * wide + 32 * rows * wide,
        ),
    )(places, *pair, gathered, slope)


def down_kernel(places_ref, left_ref, right_ref, own_ref, send_ref):
    span = right_ref.shape[3] // 2
    rows = own_ref.shape[0]
    total = None
    for far in range(2):
        right = right_ref[:, places_ref[3] ^ far].reshape(-1, 2 * span)
        for part in range(2):
            start = (part * 2 + far) * span
            one = mat_far(
                left_ref[:, start : start + span], right[:, part * span : (part + 1) * span]
            )
            total = one if total is None else total + one
    own_ref[...] = total[:rows]
    send_ref[...] = total[rows:].astype(LOW)


def down_call(places, left, gathered, start):
    both, deep = left.shape
    rows = both // 2
    lines, _, tall, wide = gathered.shape
    piece = pl.BlockSpec((rows, 2 * tall), lambda i, s: (0, i))
    own, send = pl.pallas_call(
        down_kernel,
        grid_spec=pltpu.PrefetchScalarGridSpec(
            num_scalar_prefetch=1,
            grid=(lines // 2,),
            in_specs=[
                pl.BlockSpec((both, deep), lambda i, s: (0, 0)),
                pl.BlockSpec((2, 2, tall, wide // 2), lambda i, s: (i, 0, 0, start)),
            ],
            out_specs=[piece, piece],
        ),
        out_shape=[
            jax.ShapeDtypeStruct((rows, lines * tall), jnp.float32),
            jax.ShapeDtypeStruct((rows, lines * tall), LOW),
        ],
        compiler_params=pltpu.CompilerParams(vmem_limit_bytes=VMEM_ROOM),
        cost_estimate=pl.CostEstimate(
            flops=2 * both * deep * lines * tall,
            transcendentals=0,
            bytes_accessed=left.size * 2 + lines * tall * deep * 2 + rows * lines * tall * 6,
        ),
    )(places, left, gathered)
    return own + exchange(send, far_core=1).astype(jnp.float32)


def mat(left, right):
    return jnp.dot(left, right, preferred_element_type=jnp.float32)


def turn_kernel(places_ref, own_ref, far_ref, turned_ref, left_ref):
    rows = own_ref.shape[0]
    for block in range(4):
        at = (places_ref[0] ^ block) * 2 + (places_ref[1] ^ pl.program_id(0))
        start = pl.multiple_of(at * LANES, LANES)
        span = slice(block * LANES, (block + 1) * LANES)
        left_ref[:rows, span] = own_ref[:, pl.ds(start, LANES)]
        left_ref[rows:, span] = far_ref[:, pl.ds(start, LANES)]
    turned_ref[0] = jnp.transpose(left_ref[...])


def turn(places, pair):
    rows, width = pair[0].shape
    line = width // 2
    whole = pl.BlockSpec((rows, width), lambda i, s: (0, 0))
    return pl.pallas_call(
        turn_kernel,
        grid_spec=pltpu.PrefetchScalarGridSpec(
            num_scalar_prefetch=1,
            grid=(2,),
            in_specs=[whole, whole],
            out_specs=pl.BlockSpec((1, line, 2 * rows), lambda i, s: (i, 0, 0)),
            scratch_shapes=[pltpu.VMEM((2 * rows, line), LOW)],
        ),
        out_shape=jax.ShapeDtypeStruct((2, line, 2 * rows), LOW),
        compiler_params=pltpu.CompilerParams(vmem_limit_bytes=VMEM_ROOM),
        cost_estimate=pl.CostEstimate(
            flops=0, transcendentals=0, bytes_accessed=rows * width * 8
        ),
    )(places, *pair)


def weight_cost(operands):
    rows, line = operands[0][1].shape[0], 4 * LANES
    wide = sum(right.shape[1] for _, right in operands) // 4
    return pl.CostEstimate(
        flops=8 * rows * line * wide,
        transcendentals=0,
        bytes_accessed=rows * wide * 8 + rows * line * 8 + line * wide * 8,
    )


def piece_kernel(pairs, *refs):
    ins, outs = refs[: 2 * pairs], refs[2 * pairs :]
    step = pl.program_id(0)
    parts = [mat(ins[2 * pair][0], ins[2 * pair + 1][...]).astype(LOW) for pair in range(pairs)]
    made = parts[0] if pairs == 1 else jnp.concatenate(parts, axis=1)

    @pl.when(step < 2)
    def _():
        outs[0][0] = made

    @pl.when(step >= 2)
    def _():
        outs[1][0] = made


def weight_pieces(operands, send):
    line, rows = operands[0][0].shape[1:]
    if send:
        first = lambda i: jnp.minimum(i, 1)
        column = lambda i: jnp.maximum(i, 1)
    else:
        first = lambda i: 1 - jnp.minimum(i, 1)
        column = lambda i: jnp.where(i < 2, 0, i)
    specs, arrays, wide = [], [], 0
    for turned, right in operands:
        span = right.shape[1] // 4
        wide += span
        specs.append(pl.BlockSpec((1, line, rows), lambda i: (first(i), 0, 0)))
        specs.append(pl.BlockSpec((rows, span), lambda i: (0, column(i))))
        arrays += [turned, right]

    def kernel(*refs):
        piece_kernel(len(operands), *refs)

    return pl.pallas_call(
        kernel,
        grid=(4,),
        in_specs=specs,
        out_specs=[
            pl.BlockSpec((1, line, wide), lambda i: (first(i), 0, 0)),
            pl.BlockSpec((1, line, wide), lambda i: (jnp.maximum(i - 2, 0), 0, 0)),
        ],
        out_shape=[jax.ShapeDtypeStruct((2, line, wide), LOW)] * 2,
        compiler_params=pltpu.CompilerParams(vmem_limit_bytes=VMEM_ROOM),
        cost_estimate=weight_cost(operands),
    )(*arrays)


def lane_of(shape):
    return lax.broadcasted_iota(jnp.int32, shape, 1)


def head_views(query, key, bias, head):
    lane = lane_of(query.shape)
    mine = (lane >= HDIM) if head else (lane < HDIM)
    spot = 0 if head else HDIM
    zero = jnp.zeros_like(query)
    query_view = jnp.where(mine, query, jnp.where(lane == spot, zero + 1, zero))
    key_view = jnp.where(lane == spot, bias, key)
    return mine, query_view, key_view


def attend_kernel(qkv_ref, bias_ref, mixed_ref, total_ref):
    query = qkv_ref[:, 0:LANES] * jnp.bfloat16(HDIM ** (-0.5))
    key = qkv_ref[:, LANES : 2 * LANES]
    value = qkv_ref[:, 2 * LANES : 3 * LANES]
    bias = bias_ref[...]
    sums, tops = [], []
    for head in range(2):
        mine, query_view, key_view = head_views(query, key, bias, head)
        scores = mat_far(query_view, key_view)
        top = jnp.max(scores, axis=1, keepdims=True)
        weight = jnp.exp(scores - top).astype(LOW)
        value_view = jnp.where(mine, value, jnp.ones_like(value))
        sums.append(jnp.dot(weight, value_view, preferred_element_type=jnp.float32))
        tops.append(top)
    low = lane_of(sums[0].shape) < HDIM
    upper = jnp.where(low, sums[0], sums[1])
    lower = jnp.where(low, sums[1], sums[0])
    lower = pltpu.roll(lower, HDIM, 1)
    mixed_ref[...] = (upper / lower).astype(LOW)
    total = jnp.where(low, tops[0], tops[1]) + jnp.log(lower)
    total = jnp.transpose(total)
    total_ref[0, 0:1, :] = total[0:1]
    total_ref[0, 1:2, :] = total[HDIM : HDIM + 1]


def attend_back_kernel(qkv_ref, bias_ref, grad_ref, mixed_ref, total_ref, out_ref):
    scale = HDIM ** (-0.5)
    query = qkv_ref[:, 0:LANES] * jnp.bfloat16(scale)
    key = qkv_ref[:, LANES : 2 * LANES]
    value = qkv_ref[:, 2 * LANES : 3 * LANES]
    bias = bias_ref[...]
    grad = grad_ref[...]
    product = grad.astype(jnp.float32) * mixed_ref[...].astype(jnp.float32)
    grad_query = grad_key = grad_value = None
    for head in range(2):
        mine, query_view, key_view = head_views(query, key, bias, head)
        zero = jnp.zeros_like(query)
        scores = mat_far(key_view, query_view)
        probs = jnp.exp(scores - total_ref[0, head : head + 1, :])
        grad_view = jnp.where(mine, grad, zero)
        grad_probs = mat_far(value, grad_view)
        ones = jnp.where(mine[0:8], 1.0, 0.0)
        inner = lax.dot_general(
            ones,
            product,
            (((1,), (1,)), ((), ())),
            precision=lax.Precision.HIGHEST,
            preferred_element_type=jnp.float32,
        )
        grad_scores = (probs * (grad_probs - inner[0:1])).astype(LOW)
        one_value = jnp.dot(probs.astype(LOW), grad_view, preferred_element_type=jnp.float32)
        one_key = jnp.dot(
            grad_scores, jnp.where(mine, query, zero), preferred_element_type=jnp.float32
        )
        one_query = mat_rows(grad_scores, jnp.where(mine, key, zero))
        grad_query = one_query if head == 0 else grad_query + one_query
        grad_key = one_key if head == 0 else grad_key + one_key
        grad_value = one_value if head == 0 else grad_value + one_value
    out_ref[:, 0:LANES] = (grad_query * scale).astype(LOW)
    out_ref[:, LANES : 2 * LANES] = grad_key.astype(LOW)
    out_ref[:, 2 * LANES : 3 * LANES] = grad_value.astype(LOW)


def attend_image(image, qkv, bias, given):
    both = qkv.shape[0]
    rows = both // 2
    blocks = qkv.shape[1] // (3 * LANES)

    def kernel(*refs):
        attend_kernel(*refs[:2], *refs[-2:])

    return pl.pallas_call(
        kernel,
        grid=(blocks,),
        in_specs=[
            pl.BlockSpec((rows, 3 * LANES), lambda j: (image, j)),
            pl.BlockSpec((rows, LANES), lambda j: (0, 0)),
        ]
        + [pl.BlockSpec(memory_space=pl.ANY)] * len(given),
        out_specs=[
            pl.BlockSpec((rows, LANES), lambda j: (image, j)),
            pl.BlockSpec((1, 8, rows), lambda j: (image * blocks + j, 0, 0)),
        ],
        out_shape=[
            jax.ShapeDtypeStruct((both, blocks * LANES), LOW),
            jax.ShapeDtypeStruct((2 * blocks, 8, rows), jnp.float32),
        ],
        input_output_aliases={2: 0, 3: 1} if given else {},
        compiler_params=pltpu.CompilerParams(vmem_limit_bytes=VMEM_ROOM),
        cost_estimate=pl.CostEstimate(
            flops=blocks * 2 * 2 * 2 * rows * rows * LANES * 2,
            transcendentals=blocks * 2 * rows * rows,
            bytes_accessed=rows * blocks * LANES * 8,
        ),
    )(qkv, bias, *given)


def attend_back_image(image, qkv, bias, grad, mixed, total, given):
    both = qkv.shape[0]
    rows = both // 2
    blocks = qkv.shape[1] // (3 * LANES)

    def kernel(*refs):
        attend_back_kernel(*refs[:5], refs[-1])

    return pl.pallas_call(
        kernel,
        grid=(blocks,),
        in_specs=[
            pl.BlockSpec((rows, 3 * LANES), lambda j: (image, j)),
            pl.BlockSpec((rows, LANES), lambda j: (0, 0)),
            pl.BlockSpec((rows, LANES), lambda j: (0, j)),
            pl.BlockSpec((rows, LANES), lambda j: (image, j)),
            pl.BlockSpec((1, 8, rows), lambda j: (image * blocks + j, 0, 0)),
        ]
        + [pl.BlockSpec(memory_space=pl.ANY)] * len(given),
        out_specs=pl.BlockSpec((rows, 3 * LANES), lambda j: (image, j)),
        out_shape=jax.ShapeDtypeStruct(qkv.shape, LOW),
        input_output_aliases={5: 0} if given else {},
        compiler_params=pltpu.CompilerParams(vmem_limit_bytes=VMEM_ROOM),
        cost_estimate=pl.CostEstimate(
            flops=blocks * 2 * 5 * 2 * rows * rows * LANES * 2,
            transcendentals=blocks * 2 * rows * rows,
            bytes_accessed=rows * blocks * LANES * 16,
        ),
    )(qkv, bias, grad, mixed, total, *given)


def flat_norm(values, gain, shift):
    center = values - jnp.mean(values, axis=-1, keepdims=True)
    spread = lax.rsqrt(jnp.mean(center * center, axis=-1, keepdims=True) + EPS)
    unit = center * spread
    return unit * gain + shift, unit, spread


def flat_norm_back(upstream, unit, spread, gain):
    scaled = upstream * gain
    inner = (
        scaled
        - jnp.mean(scaled, axis=-1, keepdims=True)
        - unit * jnp.mean(scaled * unit, axis=-1, keepdims=True)
    )
    return spread * inner, jnp.sum(upstream * unit, axis=0), jnp.sum(upstream, axis=0)


def column_flat(values):
    return jnp.sum(values.astype(jnp.float32), axis=0)


def whole_images(
    images,
    cotangent,
    slot_live,
    first_gain,
    first_shift,
    query_weight,
    query_bias,
    key_weight,
    value_weight,
    value_bias,
    output_weight,
    output_bias,
    second_gain,
    second_shift,
    up_weight,
    up_bias,
    down_weight,
    down_bias,
):
    dp_place = lax.axis_index("dp")
    place_y = lax.axis_index("tensor")
    core, place_x, place_z = dp_place % 2, (dp_place // 2) % 2, dp_place // 4
    places = jnp.stack([place_z, place_x, core, place_y]).astype(jnp.int32)
    strip, width = images.shape[1:]
    half = -(-strip // HALF_PAD) * HALF_PAD
    rows = 2 * half
    depth, head_cols = query_weight.shape
    units = up_weight.shape[1]

    def columns_of(weights, place):
        return [
            lax.dynamic_slice_in_dim(
                weight, place * (weight.shape[1] // 2), weight.shape[1] // 2, 1
            )
            for weight in weights
        ]

    def core_parts(weights, place):
        cuts = columns_of(weights, place)
        parts = []
        for part in range(2):
            spans = [cut.shape[1] // 2 for cut in cuts]
            parts.append(
                jnp.concatenate(
                    [cut[:, part * span : (part + 1) * span] for cut, span in zip(cuts, spans)], 1
                )
            )
        return jnp.stack(parts)

    feeds = [up_weight, down_weight.T]
    feed_keep = jnp.concatenate(columns_of(feeds, core), 1)
    feed_send = jnp.concatenate(columns_of(feeds, 1 - core), 1)
    feed = pick_two(core, feed_keep, exchange(feed_send, far_core=1), 0)
    groups = [[place for place in range(32) if (place // 2) % 2 == at] for at in range(2)]

    gathered = lax.all_gather(
        feed.reshape(2 * depth, -1), BOTH, axis=0, tiled=True, axis_index_groups=groups
    ).reshape(8, 2, 2 * depth, -1)
    gathered = pltpu.with_memory_space_constraint(gathered, pltpu.HBM)

    heads = [query_weight, key_weight, value_weight, output_weight.T]
    piece_one = gather_piece(core_parts(heads, core), core_parts(heads, 1 - core), core)
    others_one = scatter_z([None, piece_one, piece_one, piece_one])

    padding = ((0, 0), (0, half - strip), (0, 0))

    def own_and_far(slots, *waits):
        slots = jnp.pad(slots, padding)
        mine = lax.dynamic_index_in_dim(slots, place_y, 0, keepdims=False)
        theirs = lax.dynamic_index_in_dim(slots, 1 - place_y, 0, keepdims=False)
        return mine, exchange(after(theirs, *waits), far_y=1)

    image_mine, image_far = own_and_far(images, piece_one)
    grad_mine, grad_far = own_and_far(cotangent, piece_one)
    line_one = gather_line(piece_one, others_one, places)
    cross_one = exchange(line_one[0], far_x=1), exchange(line_one[1], far_y=1)
    pair_one = gather_pairs(places, *line_one, *cross_one)
    image_far, grad_far = after((image_far, grad_far), *pair_one)
    whole = jnp.concatenate([image_mine, image_far], 0)

    def head_columns(vector):
        table = vector.astype(jnp.float32).reshape(2, 2, 2, -1)
        table = lax.dynamic_index_in_dim(table, core, 1, keepdims=False)
        table = jnp.where(place_y == 0, table, table[::-1])
        return table.transpose(1, 0, 2).reshape(4, 1, -1)

    def spread_core(table):
        table = jnp.stack(
            [jnp.where(core == 0, table, 0.0), jnp.where(core == 1, table, 0.0)], 1
        )
        return table.reshape(-1)

    def head_spread(vector):
        table = vector.reshape(2, 2, -1).transpose(1, 0, 2)
        return spread_core(jnp.where(place_y == 0, table, table[::-1]))

    gain_one, shift_one = first_gain.astype(jnp.float32), first_shift.astype(jnp.float32)
    gain_two, shift_two = second_gain.astype(jnp.float32), second_shift.astype(jnp.float32)
    query_shift, value_shift = head_columns(query_bias), head_columns(value_bias)
    qkv_shift = jnp.concatenate(
        [query_shift, jnp.zeros_like(query_shift), value_shift], 1
    ).reshape(-1)
    up_shift = head_columns(up_bias).reshape(1, -1)

    row = jnp.arange(rows)
    in_half = row % half
    spot = jnp.where(row < half, place_y, 1 - place_y) * strip + in_half
    ok = (in_half < strip) & (spot < VALID)
    live = lax.dynamic_index_in_dim(slot_live, place_y, 0, keepdims=False).astype(jnp.float32)
    row_mask = (live * ok.astype(jnp.float32))[:, None]
    key_bias = jnp.broadcast_to(
        jnp.where(ok, 0.0, NEGATIVE).astype(LOW)[:, None], (rows, LANES)
    )

    resid = whole.astype(jnp.float32)

    def full_columns(owned):
        return owned.transpose(2, 0, 1, 3).reshape(depth, -1)

    def pair_of(own):
        return own, exchange(own, far_core=1)

    normed, unit_one, spread_one = flat_norm(resid, gain_one, shift_one)
    normed_pair = pair_of(normed.astype(LOW))

    normed_turned = turn(places, normed_pair)
    grad_top = row_mask * jnp.concatenate([grad_mine, grad_far], 0).astype(jnp.float32)
    fed_grad = grad_top.astype(LOW)
    fed_pair = pair_of(fed_grad)
    fed_turned = turn(places, fed_pair)
    last_one = exchange(pair_one[0], far_y=1), exchange(pair_one[1], far_x=1)
    qkv_full, output_full = gather_all(after(places, normed_turned, fed_turned), *pair_one, *last_one, 3 * head_cols // 4)

    normed_rows = jnp.concatenate(normed_pair, 0)
    qkv = (mat(normed_rows, qkv_full) + qkv_shift).astype(LOW)
    mixed_half = attend_image(1, qkv, key_bias, [])
    mixed_far = mat_far(mixed_half[0][rows:], output_full).astype(LOW)
    mixed_sum = exchange(mixed_far, far_core=1)
    mixed, totals = attend_image(0, qkv, key_bias, list(after(tuple(mixed_half), mixed_far)))
    attended = mat_far(mixed[:rows], output_full) + mixed_sum.astype(jnp.float32)
    attended = attended + output_bias.astype(jnp.float32)
    middle = row_mask * (resid + attended)
    second, unit_two, spread_two = flat_norm(middle, gain_two, shift_two)
    second_pair = pair_of(second.astype(LOW))
    active, slope = up_call(places, second_pair, gathered, up_shift)

    lower_sends = weight_pieces([(fed_turned, active)], True)
    lower_first = scatter_first(lower_sends)
    lower_keeps = weight_pieces([(fed_turned, after(active, *lower_sends))], False)
    fed_late = after(fed_pair, *lower_keeps)
    hidden_grad, up_bias_sums = hidden_call(places, fed_late, gathered, slope)
    second_turned = turn(places, second_pair)
    up_sends = weight_pieces([(second_turned, hidden_grad)], True)
    up_first = scatter_first(up_sends)
    lower_first = after(lower_first, *up_sends)
    lower_second = scatter_second(lower_keeps, lower_first)
    hidden_late = after(hidden_grad, *lower_first)
    second_grad = down_call(places, hidden_late, gathered, 0)
    middle_back, gain_two_grad, shift_two_grad = flat_norm_back(
        second_grad, unit_two, spread_two, gain_two
    )
    middle_grad = row_mask * (grad_top + middle_back)
    attended_grad = middle_grad.astype(LOW)
    attended_pair = pair_of(attended_grad)
    up_keeps = weight_pieces([(second_turned, after(hidden_late, attended_grad))], False)
    attended_turned = turn(places, attended_pair)
    lower_second = after(lower_second, *up_keeps, attended_turned)
    lower_line = scatter_line(lower_keeps, lower_first, lower_second)
    lower_z = scatter_z(lower_line)
    up_first = after(up_first, *up_keeps)
    up_second = scatter_second(up_keeps, up_first)
    grad_mixed = [mat(one, output_full).astype(LOW) for one in attended_pair]
    grad_mixed = after(tuple(grad_mixed), *up_first, *lower_line)
    back = attend_back_image(0, qkv, key_bias, grad_mixed[0], mixed, totals, [])
    lower_z = after(tuple(lower_z), back)
    up_line = scatter_line(up_keeps, up_first, after(up_second, back))
    up_z = scatter_z(up_line)
    back = after(back, *up_line)
    back = attend_back_image(1, qkv, key_bias, grad_mixed[1], mixed, totals, [back])
    up_z = after(tuple(up_z), back)
    back = after(back, *up_z)
    last_sends = weight_pieces([(normed_turned, back), (attended_turned, mixed)], True)
    last_first = scatter_first(last_sends)
    back_late = after(back, *last_sends)
    normed_far = exchange(mat_far(back_late[rows:], qkv_full).astype(LOW), far_core=1)
    last_keeps = weight_pieces([(normed_turned, back_late), (attended_turned, mixed)], False)
    normed_grad = mat_far(back_late[:rows], qkv_full) + normed_far.astype(jnp.float32)
    first_back, gain_one_grad, shift_one_grad = flat_norm_back(
        normed_grad, unit_one, spread_one, gain_one
    )
    images_own = middle_grad + first_back
    qkv_sums = column_flat(back_late).reshape(4, 3, -1)
    vector = jnp.concatenate(
        [
            column_flat(attended_grad),
            gain_two_grad,
            shift_two_grad,
            column_flat(fed_grad),
            head_spread(up_bias_sums.reshape(-1)),
            gain_one_grad,
            shift_one_grad,
            head_spread(qkv_sums[:, 0].reshape(-1)),
            head_spread(qkv_sums[:, 2].reshape(-1)),
        ]
    )
    vector, vectors = vector_first(vector)
    last_first = after(last_first, *last_keeps, images_own, *vectors)
    last_second = scatter_second(last_keeps, last_first)
    vector = vector + vectors[0] + vectors[1] + vectors[2]
    vector_y = exchange(vector, far_y=1)
    fed = down_call(places, after(active, *last_first), gathered, 1)
    vector = vector + after(vector_y, fed)
    vector_x = exchange(vector, far_x=1)
    layer_own = (row_mask * (middle + fed + down_bias.astype(jnp.float32))).astype(LOW)
    last_line = scatter_line(last_keeps, last_first, after(last_second, layer_own))
    last_z = scatter_z(last_line)
    vector = vector + after(vector_x, *last_line)
    lower_z, up_z = after((tuple(lower_z), tuple(up_z)), *last_line)
    lower_owned = full_columns(scatter_last(lower_line[0], lower_z, core)).T
    upper_owned = full_columns(scatter_last(up_line[0], up_z, core))
    layer_late, images_late = after((layer_own, images_own), *last_line)

    def to_strips(own, send):
        far = exchange(send, far_y=1).astype(own.dtype)
        return pick_two(place_y, own[:strip], far, 1).transpose(1, 0, 2)

    layer_out = to_strips(layer_late, layer_late[half : half + strip])
    images_grad = to_strips(images_late, images_late[half : half + strip].astype(LOW))
    last_z = after(tuple(last_z), vector, layer_out, images_grad, lower_owned, upper_owned)
    last_owned = scatter_last(last_line[0], last_z, core)
    def head_grad(at):
        return full_columns(last_owned[..., at * LANES : (at + 1) * LANES])

    early, late = vector[: 4 * width + up_bias.shape[0]], vector[4 * width + up_bias.shape[0] :]
    return (
        layer_out,
        images_grad,
        late[:width],
        late[width : 2 * width],
        head_grad(0),
        late[2 * width : 3 * width],
        head_grad(1),
        head_grad(2),
        late[3 * width :],
        head_grad(3).T,
        early[:width],
        early[width : 2 * width],
        early[2 * width : 3 * width],
        upper_owned,
        early[4 * width :],
        lower_owned,
        early[3 * width : 4 * width],
    )


def pick(mesh):
    sizes = dict(mesh.shape)
    if sizes["dp"] == 16 and sizes["tensor"] == 2:
        return whole_images
    return local


def solution(mesh):
    in_specs = (
        P("dp", "tensor", None),
        P("dp", "tensor", None),
        P("dp"),
        P(),
        P(),
        P("dp", "tensor"),
        P(),
        P("dp", "tensor"),
        P("dp", "tensor"),
        P(),
        P("tensor", "dp"),
        P(),
        P(),
        P(),
        P("dp", "tensor"),
        P(),
        P("tensor", "dp"),
        P(),
    )
    out_specs = (
        P("dp", "tensor", None),
        P("dp", "tensor", None),
        P(),
        P(),
        P("dp", "tensor"),
        P(),
        P("dp", "tensor"),
        P("dp", "tensor"),
        P(),
        P("tensor", "dp"),
        P(),
        P(),
        P(),
        P("dp", "tensor"),
        P(),
        P("tensor", "dp"),
        P(),
    )
    return jax.shard_map(pick(mesh), mesh=mesh, in_specs=in_specs, out_specs=out_specs, check_vma=False)
```

```python
import jax
import jax.numpy as jnp
from jax import lax
from jax.experimental import pallas as pl
from jax.experimental.pallas import tpu as pltpu
from jax.sharding import PartitionSpec as P

HDIM = 64
VALID = 577


EPS = 1e-05
NEGATIVE = -1e30
SLOPE = 1.702


def layer_norm(values, gain, shift):
    center = values - jnp.mean(values, axis=-1, keepdims=True)
    spread = lax.rsqrt(jnp.mean(center * center, axis=-1, keepdims=True) + EPS)
    unit = center * spread
    return (unit * gain + shift, unit, spread)


def norm_back(upstream, unit, spread, gain):
    scaled = upstream * gain
    inner = (
        scaled
        - jnp.mean(scaled, axis=-1, keepdims=True)
        - unit * jnp.mean(scaled * unit, axis=-1, keepdims=True)
    )
    return (spread * inner, jnp.sum(upstream * unit, axis=(0, 1)), jnp.sum(upstream, axis=(0, 1)))


def dense(left, right):
    return jnp.einsum("spa,ab->spb", left, right, preferred_element_type=jnp.float32)


def project_back(left, right):
    return jnp.einsum("spa,ba->spb", left, right, preferred_element_type=jnp.float32)


def outer(left, right):
    return jnp.einsum("spa,spb->ab", left, right, preferred_element_type=jnp.float32)


def column_sum(values):
    return jnp.sum(values.astype(jnp.float32), axis=(0, 1))


def widen(piece, length, start):
    return lax.dynamic_update_slice_in_dim(jnp.zeros((length,), jnp.float32), piece, start, 0)


def split_heads(block):
    return block.reshape(block.shape[0], -1, HDIM)


def scores_of(query, key, key_ok):
    raw = jnp.einsum(
        "qhe,khe->hqk", split_heads(query), split_heads(key), preferred_element_type=jnp.float32
    )
    return jnp.where(key_ok[None, None, :], raw * HDIM ** (-0.5), NEGATIVE)


def attend(query, key, value, key_ok):
    scores = scores_of(query, key, key_ok)
    top = jnp.max(scores, axis=-1, keepdims=True)
    total = top + jnp.log(jnp.sum(jnp.exp(scores - top), axis=-1, keepdims=True))
    probs = jnp.exp(scores - total).astype(jnp.bfloat16)
    mixed = jnp.einsum(
        "hqk,khe->qhe", probs, split_heads(value), preferred_element_type=jnp.float32
    )
    return (mixed.reshape(query.shape[0], -1).astype(jnp.bfloat16), total)


def attend_back(query, key, value, grad_mixed, total, key_ok):
    scores = scores_of(query, key, key_ok)
    probs = jnp.exp(scores - total)
    grad_heads = split_heads(grad_mixed)
    grad_probs = jnp.einsum(
        "qhe,khe->hqk", grad_heads, split_heads(value), preferred_element_type=jnp.float32
    )
    grad_value = jnp.einsum(
        "hqk,qhe->khe", probs.astype(jnp.bfloat16), grad_heads, preferred_element_type=jnp.float32
    )
    grad_scores = (
        probs * (grad_probs - jnp.sum(probs * grad_probs, axis=-1, keepdims=True))
    ).astype(jnp.bfloat16)
    grad_query = jnp.einsum(
        "hqk,khe->qhe", grad_scores, split_heads(key), preferred_element_type=jnp.float32
    ) * HDIM ** (-0.5)
    grad_key = jnp.einsum(
        "hqk,qhe->khe", grad_scores, split_heads(query), preferred_element_type=jnp.float32
    ) * HDIM ** (-0.5)
    length = query.shape[0]
    return (
        grad_query.reshape(length, -1).astype(jnp.bfloat16),
        grad_key.reshape(length, -1).astype(jnp.bfloat16),
        grad_value.reshape(length, -1).astype(jnp.bfloat16),
    )


def local(
    images,
    cotangent,
    slot_live,
    first_gain,
    first_shift,
    query_weight,
    query_bias,
    key_weight,
    value_weight,
    value_bias,
    output_weight,
    output_bias,
    second_gain,
    second_shift,
    up_weight,
    up_bias,
    down_weight,
    down_bias,
):
    slots, strip, width = images.shape
    tensor_count = lax.axis_size("tensor")
    tensor_place = lax.axis_index("tensor")
    seq_len = strip * tensor_count
    positions = tensor_place * strip + jnp.arange(strip)
    row_mask = (
        slot_live.astype(jnp.float32)[:, None, None]
        * (positions < VALID).astype(jnp.float32)[None, :, None]
    )
    key_ok = jnp.arange(seq_len) < VALID
    query_full, key_full, value_full, upper_full, output_full, lower_full = (
        lax.all_gather(query_weight, "dp", axis=0, tiled=True),
        lax.all_gather(key_weight, "dp", axis=0, tiled=True),
        lax.all_gather(value_weight, "dp", axis=0, tiled=True),
        lax.all_gather(up_weight, "dp", axis=0, tiled=True),
        lax.all_gather(output_weight, "dp", axis=1, tiled=True),
        lax.all_gather(down_weight, "dp", axis=1, tiled=True),
    )
    head_cols = query_full.shape[1]
    head_start = tensor_place * head_cols
    gain_one = first_gain.astype(jnp.float32)
    shift_one = first_shift.astype(jnp.float32)
    gain_two = second_gain.astype(jnp.float32)
    shift_two = second_shift.astype(jnp.float32)
    query_shift = lax.dynamic_slice_in_dim(query_bias.astype(jnp.float32), head_start, head_cols)
    value_shift = lax.dynamic_slice_in_dim(value_bias.astype(jnp.float32), head_start, head_cols)
    resid = images.astype(jnp.float32)
    normed, unit_one, spread_one = layer_norm(resid, gain_one, shift_one)
    normed_rows = lax.all_gather(normed.astype(jnp.bfloat16), "tensor", axis=1, tiled=True)
    queries = (dense(normed_rows, query_full) + query_shift).astype(jnp.bfloat16)
    keys_low = dense(normed_rows, key_full).astype(jnp.bfloat16)
    values_low = (dense(normed_rows, value_full) + value_shift).astype(jnp.bfloat16)
    mixed, totals = lax.map(
        lambda items: attend(items[0], items[1], items[2], key_ok), (queries, keys_low, values_low)
    )
    attended = lax.psum_scatter(
        dense(mixed, output_full), "tensor", scatter_dimension=1, tiled=True
    ) + output_bias.astype(jnp.float32)
    middle = row_mask * (resid + attended)
    second, unit_two, spread_two = layer_norm(middle, gain_two, shift_two)
    second_low = second.astype(jnp.bfloat16)
    grad_top = row_mask * cotangent.astype(jnp.float32)
    fed_grad = grad_top.astype(jnp.bfloat16)
    down_shift = down_bias.astype(jnp.float32)
    units = upper_full.shape[1]
    second_rows = lax.all_gather(second_low, "tensor", axis=1, tiled=True)
    up_shift = lax.dynamic_slice_in_dim(up_bias.astype(jnp.float32), tensor_place * units, units)
    hidden = dense(second_rows, upper_full) + up_shift
    sigma = jax.nn.sigmoid(SLOPE * hidden)
    active = (hidden * sigma).astype(jnp.bfloat16)
    fed = (
        lax.psum_scatter(
            dense(active, lower_full).astype(jnp.bfloat16),
            "tensor",
            scatter_dimension=1,
            tiled=True,
        ).astype(jnp.float32)
        + down_shift
    )
    fed_rows = lax.all_gather(fed_grad, "tensor", axis=1, tiled=True)
    grad_active = project_back(fed_rows, lower_full)
    lower_grad = outer(active, fed_rows)
    hidden_grad = (grad_active * (sigma + SLOPE * hidden * sigma * (1.0 - sigma))).astype(
        jnp.bfloat16
    )
    upper_grad = outer(second_rows, hidden_grad)
    up_bias_grad = widen(column_sum(hidden_grad), up_bias.shape[0], tensor_place * units)
    second_grad = lax.psum_scatter(
        project_back(hidden_grad, upper_full), "tensor", scatter_dimension=1, tiled=True
    )
    layer_out = (row_mask * (middle + fed)).astype(jnp.bfloat16)
    down_bias_grad = column_sum(fed_grad)
    middle_back, gain_two_grad, shift_two_grad = norm_back(
        second_grad, unit_two, spread_two, gain_two
    )
    middle_grad = row_mask * (grad_top + middle_back)
    attended_grad = middle_grad.astype(jnp.bfloat16)
    output_bias_grad = column_sum(attended_grad)
    attended_rows = lax.all_gather(attended_grad, "tensor", axis=1, tiled=True)
    grad_mixed = project_back(attended_rows, output_full).astype(jnp.bfloat16)
    output_grad = outer(mixed, attended_rows)
    grad_query, grad_key, grad_value = lax.map(
        lambda items: attend_back(items[0], items[1], items[2], items[3], items[4], key_ok),
        (queries, keys_low, values_low, grad_mixed, totals),
    )
    query_grad = outer(normed_rows, grad_query)
    key_grad = outer(normed_rows, grad_key)
    value_grad = outer(normed_rows, grad_value)
    query_bias_grad = widen(column_sum(grad_query), width, head_start)
    value_bias_grad = widen(column_sum(grad_value), width, head_start)
    normed_terms = (
        project_back(grad_query, query_full)
        + project_back(grad_key, key_full)
        + project_back(grad_value, value_full)
    )
    normed_grad = lax.psum_scatter(
        normed_terms.astype(jnp.bfloat16), "tensor", scatter_dimension=1, tiled=True
    ).astype(jnp.float32)
    first_back, gain_one_grad, shift_one_grad = norm_back(
        normed_grad, unit_one, spread_one, gain_one
    )
    images_grad = middle_grad + first_back
    query_owned, key_owned, value_owned, upper_owned, output_owned, lower_owned = (
        lax.psum_scatter(
            query_grad.astype(jnp.bfloat16), "dp", scatter_dimension=0, tiled=True
        ).astype(jnp.float32),
        lax.psum_scatter(
            key_grad.astype(jnp.bfloat16), "dp", scatter_dimension=0, tiled=True
        ).astype(jnp.float32),
        lax.psum_scatter(
            value_grad.astype(jnp.bfloat16), "dp", scatter_dimension=0, tiled=True
        ).astype(jnp.float32),
        lax.psum_scatter(
            upper_grad.astype(jnp.bfloat16), "dp", scatter_dimension=0, tiled=True
        ).astype(jnp.float32),
        lax.psum_scatter(
            output_grad.astype(jnp.bfloat16), "dp", scatter_dimension=1, tiled=True
        ).astype(jnp.float32),
        lax.psum_scatter(
            lower_grad.astype(jnp.bfloat16), "dp", scatter_dimension=1, tiled=True
        ).astype(jnp.float32),
    )
    vector_sums = lax.psum(
        (
            gain_one_grad,
            shift_one_grad,
            query_bias_grad,
            value_bias_grad,
            output_bias_grad,
            gain_two_grad,
            shift_two_grad,
            up_bias_grad,
            down_bias_grad,
        ),
        ("dp", "tensor"),
    )
    (
        gain_one_total,
        shift_one_total,
        query_bias_total,
        value_bias_total,
        output_bias_total,
        gain_two_total,
        shift_two_total,
        up_bias_total,
        down_bias_total,
    ) = vector_sums
    return (
        layer_out,
        images_grad,
        gain_one_total,
        shift_one_total,
        query_owned,
        query_bias_total,
        key_owned,
        value_owned,
        value_bias_total,
        output_owned,
        output_bias_total,
        gain_two_total,
        shift_two_total,
        upper_owned,
        up_bias_total,
        lower_owned,
        down_bias_total,
    )


BOTH = ("dp", "tensor")
HALF_PAD = 8
LANES = 128
LOW = jnp.bfloat16
VMEM_ROOM = 24 * 2**20
SMALL = pl.CostEstimate(flops=1024, transcendentals=0, bytes_accessed=1024)


def exchange(value, far_z=0, far_x=0, far_core=0, far_y=0):
    pairs = []
    for place in range(32):
        other = place ^ (far_z * 8 + far_x * 4 + far_core * 2 + far_y)
        pairs.append((place, other))
    return lax.ppermute(value, BOTH, pairs)


def pick_two(bit, own, other, axis):
    first = jnp.where(bit == 0, own, other)
    last = jnp.where(bit == 0, other, own)
    return jnp.stack([first, last], axis)


def after(value, *others):
    return lax.optimization_barrier((value, *others))[0]


def pack(places, sources, shapes, plan):
    def kernel(places_ref, *refs):
        ins, outs = refs[: len(sources)], refs[len(sources) :]
        spots = [places_ref[at] for at in range(4)]
        for at, take, to, put in plan:
            outs[to][put(*spots)] = ins[at][take(*spots)]

    return pl.pallas_call(
        kernel,
        in_specs=[pl.BlockSpec(memory_space=pltpu.SMEM)]
        + [pl.BlockSpec(memory_space=pltpu.VMEM)] * len(sources),
        out_specs=[pl.BlockSpec(memory_space=pltpu.VMEM)] * len(shapes),
        out_shape=[jax.ShapeDtypeStruct(shape, LOW) for shape in shapes],
        compiler_params=pltpu.CompilerParams(vmem_limit_bytes=VMEM_ROOM),
        cost_estimate=pl.CostEstimate(
            flops=0,
            transcendentals=0,
            bytes_accessed=sum(2 * source.size * 2 for source in sources),
        ),
    )(places, *sources)


def gather_piece(keep, send, core):
    deep, wide = keep.shape[1:]
    return pick_two(core, keep, exchange(send, far_core=1), 1).reshape(2, 2 * deep, wide)


def gather_line(piece, others, places):
    rows, wide = piece.shape[1:]
    line = [piece] + others
    plan = []
    for step in range(4):
        for part in range(2):
            plan.append(
                (
                    step,
                    lambda z, x, c, y, part=part: part,
                    part,
                    lambda z, x, c, y, step=step: z ^ step,
                )
            )
    return pack(places, line, [(4, rows, wide)] * 2, plan)


def gather_pairs(places, one, two, one_x, two_y):
    every = slice(None)
    plan = [
        (0, lambda z, x, c, y: every, 0, lambda z, x, c, y: x),
        (1, lambda z, x, c, y: every, 0, lambda z, x, c, y: 1 - x),
        (2, lambda z, x, c, y: every, 1, lambda z, x, c, y: 0),
        (3, lambda z, x, c, y: every, 1, lambda z, x, c, y: 1),
    ]
    return pack(places, [one, one_x, two, two_y], [(2,) + one.shape] * 2, plan)


def gather_all(places, one_pair, two_pair, one_y, two_x, most):
    every = slice(None)
    rows, wide = one_pair.shape[2:]
    plan = []
    for to, low, high in ((0, 0, most), (1, most, wide)):
        span = high - low
        for place_z in range(4):
            for far in range(2):
                for number in range(2):
                    plan.append(
                        (
                            number,
                            lambda z, x, c, y, a=far, p=place_z, lo=low, hi=high: (
                                a,
                                p,
                                every,
                                slice(lo, hi),
                            ),
                            to,
                            lambda z, x, c, y, a=far, p=place_z, n=number, s=span: (
                                p,
                                a,
                                every,
                                slice(n * s, n * s + s),
                            ),
                        )
                    )
                    plan.append(
                        (
                            2 + far,
                            lambda z, x, c, y, n=number, p=place_z, lo=low, hi=high: (
                                n,
                                p,
                                every,
                                slice(lo, hi),
                            ),
                            to,
                            lambda z, x, c, y, f=far, p=place_z, n=number, s=span: (
                                p,
                                x ^ f,
                                every,
                                slice((2 + n) * s, (3 + n) * s),
                            ),
                        )
                    )
    shapes = [(4, 2, rows, 4 * most), (4, 2, rows, 4 * (wide - most))]
    made = pack(places, [one_pair, one_y, two_pair, two_x], shapes, plan)
    return [array.reshape(8 * rows, -1) for array in made]


def low_add(*values):
    total = values[0].astype(jnp.float32)
    for value in values[1:]:
        total = total + value.astype(jnp.float32)
    return total


def line_kernel(one_ref, one_a, one_b, two_ref, two_a, two_b, own_ref, *send_refs):
    tall = own_ref.shape[1]
    for step in range(4):
        rows = slice(step * tall, (step + 1) * tall)
        one = low_add(one_ref[0, rows], one_a[0, rows], one_b[rows])
        two = low_add(two_ref[0, rows], two_a[0, rows], two_b[rows])
        if step == 0:
            own_ref[0] = one
            own_ref[1] = two
        else:
            send_refs[step - 1][0] = one.astype(LOW)
            send_refs[step - 1][1] = two.astype(LOW)


def scatter_first(sends):
    return exchange(sends[0], far_y=1), exchange(sends[1], far_x=1)


def scatter_adds(keeps, arrived):
    return [low_add(keeps[at][1], arrived[at][1]).astype(LOW) for at in range(2)]


def scatter_second(adds):
    return exchange(adds[0], far_x=1), exchange(adds[1], far_y=1)


def scatter_line(keeps, arrived, crossed):
    lines, wide = crossed[0].shape
    tall = lines // 4
    first = pl.BlockSpec((1, lines, wide), lambda i: (0, 0, 0))
    flat = pl.BlockSpec((lines, wide), lambda i: (0, 0))
    piece = pl.BlockSpec((2, tall, wide), lambda i: (0, 0, 0))
    return pl.pallas_call(
        line_kernel,
        grid=(1,),
        in_specs=[first, first, flat, first, first, flat],
        out_specs=[piece] * 4,
        out_shape=[jax.ShapeDtypeStruct((2, tall, wide), jnp.float32)]
        + [jax.ShapeDtypeStruct((2, tall, wide), LOW)] * 3,
        compiler_params=pltpu.CompilerParams(vmem_limit_bytes=VMEM_ROOM),
        cost_estimate=pl.CostEstimate(
            flops=lines * wide * 4, transcendentals=0, bytes_accessed=lines * wide * 18
        ),
    )(keeps[0], arrived[0], crossed[0], keeps[1], arrived[1], crossed[1])


def scatter_z(sends):
    return [exchange(sends[step], far_z=step) for step in (1, 2, 3)]


def scatter_last(own, others, core):
    tall, wide = own.shape[1:]
    total = low_add(own, *others).reshape(2, 2, tall // 2, wide)
    keep = lax.dynamic_index_in_dim(total, core, 1, keepdims=False)
    send = lax.dynamic_index_in_dim(total, 1 - core, 1, keepdims=False)
    far = exchange(send.astype(LOW), far_core=1).astype(jnp.float32)
    return pick_two(core, keep, far, 0)


def vector_first(vector):
    vector = vector + exchange(vector, far_core=1)
    return vector, [exchange(vector, far_z=step) for step in (1, 2, 3)]


def mat_far(left, right):
    return lax.dot_general(
        left, right, (((1,), (1,)), ((), ())), preferred_element_type=jnp.float32
    )


def mat_rows(left, right):
    return lax.dot_general(
        left, right, (((0,), (0,)), ((), ())), preferred_element_type=jnp.float32
    )


def fill_rows(made_ref, own_ref, far_ref):
    rows = own_ref.shape[0]

    @pl.when(pl.program_id(0) == 0)
    def _():
        made_ref[:rows] = own_ref[...]
        made_ref[rows:] = far_ref[...]


def up_kernel(
    places_ref, own_ref, far_ref, right_ref, shift_ref, active_ref, slope_ref, left_ref
):
    fill_rows(left_ref, own_ref, far_ref)
    right = right_ref[...].reshape(left_ref.shape[1], -1)
    hidden = jnp.dot(left_ref[...], right, preferred_element_type=jnp.float32)
    hidden = hidden + shift_ref[...]
    sigma = 0.5 * jnp.tanh((0.5 * SLOPE) * hidden) + 0.5
    active = hidden * sigma
    active_ref[...] = active.astype(LOW)
    slope_ref[...] = (sigma + SLOPE * active * (1.0 - sigma)).astype(LOW)


def feed_spec(gathered, start):
    lines, _, rows, wide = gathered.shape
    return pl.BlockSpec(
        (lines, 1, rows, wide // 4), lambda i, s: (0, s[3] ^ (i % 2), 0, start + i // 2)
    )


def up_call(places, pair, gathered, shift):
    rows, width = pair[0].shape
    wide = shift.shape[1] // 4
    whole = pl.BlockSpec((rows, width), lambda i, s: (0, 0))
    piece = pl.BlockSpec((2 * rows, wide), lambda i, s: (0, i))
    return pl.pallas_call(
        up_kernel,
        grid_spec=pltpu.PrefetchScalarGridSpec(
            num_scalar_prefetch=1,
            grid=(4,),
            in_specs=[
                whole,
                whole,
                feed_spec(gathered, 0),
                pl.BlockSpec((1, wide), lambda i, s: (0, i)),
            ],
            out_specs=[piece, piece],
            scratch_shapes=[pltpu.VMEM((2 * rows, width), LOW)],
        ),
        out_shape=[jax.ShapeDtypeStruct((2 * rows, 4 * wide), LOW)] * 2,
        compiler_params=pltpu.CompilerParams(vmem_limit_bytes=VMEM_ROOM),
        cost_estimate=pl.CostEstimate(
            flops=16 * rows * wide * width,
            transcendentals=8 * rows * wide,
            bytes_accessed=rows * width * 4 + 8 * width * wide + 32 * rows * wide,
        ),
    )(places, *pair, gathered, shift)


def hidden_kernel(
    places_ref, own_ref, far_ref, right_ref, slope_ref, out_ref, sum_ref, left_ref
):
    fill_rows(left_ref, own_ref, far_ref)
    right = right_ref[...].reshape(left_ref.shape[1], -1)
    grad = jnp.dot(left_ref[...], right, preferred_element_type=jnp.float32)
    grad = (grad * slope_ref[...].astype(jnp.float32)).astype(LOW)
    out_ref[...] = grad
    sum_ref[...] = jnp.sum(grad.astype(jnp.float32), axis=0, keepdims=True)


def hidden_call(places, pair, gathered, slope):
    rows, width = pair[0].shape
    wide = slope.shape[1] // 4
    whole = pl.BlockSpec((rows, width), lambda i, s: (0, 0))
    piece = pl.BlockSpec((2 * rows, wide), lambda i, s: (0, i))
    return pl.pallas_call(
        hidden_kernel,
        grid_spec=pltpu.PrefetchScalarGridSpec(
            num_scalar_prefetch=1,
            grid=(4,),
            in_specs=[whole, whole, feed_spec(gathered, 2), piece],
            out_specs=[piece, pl.BlockSpec((1, wide), lambda i, s: (0, i))],
            scratch_shapes=[pltpu.VMEM((2 * rows, width), LOW)],
        ),
        out_shape=[
            jax.ShapeDtypeStruct((2 * rows, 4 * wide), LOW),
            jax.ShapeDtypeStruct((1, 4 * wide), jnp.float32),
        ],
        compiler_params=pltpu.CompilerParams(vmem_limit_bytes=VMEM_ROOM),
        cost_estimate=pl.CostEstimate(
            flops=16 * rows * wide * width,
            transcendentals=0,
            bytes_accessed=rows * width * 4 + 8 * width * wide + 32 * rows * wide,
        ),
    )(places, *pair, gathered, slope)


def down_kernel(places_ref, left_ref, right_ref, own_ref, send_ref):
    span = right_ref.shape[3] // 2
    rows = own_ref.shape[0]
    total = None
    for far in range(2):
        right = right_ref[:, places_ref[3] ^ far].reshape(-1, 2 * span)
        for part in range(2):
            start = (part * 2 + far) * span
            one = mat_far(
                left_ref[:, start : start + span], right[:, part * span : (part + 1) * span]
            )
            total = one if total is None else total + one
    own_ref[...] = total[:rows]
    send_ref[...] = total[rows:].astype(LOW)


def down_call(places, left, gathered, start):
    both, deep = left.shape
    rows = both // 2
    lines, _, tall, wide = gathered.shape
    piece = pl.BlockSpec((rows, 2 * tall), lambda i, s: (0, i))
    own, send = pl.pallas_call(
        down_kernel,
        grid_spec=pltpu.PrefetchScalarGridSpec(
            num_scalar_prefetch=1,
            grid=(lines // 2,),
            in_specs=[
                pl.BlockSpec((both, deep), lambda i, s: (0, 0)),
                pl.BlockSpec((2, 2, tall, wide // 2), lambda i, s: (i, 0, 0, start)),
            ],
            out_specs=[piece, piece],
        ),
        out_shape=[
            jax.ShapeDtypeStruct((rows, lines * tall), jnp.float32),
            jax.ShapeDtypeStruct((rows, lines * tall), LOW),
        ],
        compiler_params=pltpu.CompilerParams(vmem_limit_bytes=VMEM_ROOM),
        cost_estimate=SMALL,
    )(places, left, gathered)
    return own + exchange(send, far_core=1).astype(jnp.float32)


def mat(left, right):
    return jnp.dot(left, right, preferred_element_type=jnp.float32)


def turn_kernel(places_ref, own_ref, far_ref, turned_ref, left_ref):
    rows = own_ref.shape[0]
    for block in range(4):
        at = (places_ref[0] ^ block) * 2 + (places_ref[1] ^ pl.program_id(0))
        start = pl.multiple_of(at * LANES, LANES)
        span = slice(block * LANES, (block + 1) * LANES)
        left_ref[:rows, span] = own_ref[:, pl.ds(start, LANES)]
        left_ref[rows:, span] = far_ref[:, pl.ds(start, LANES)]
    turned_ref[0] = jnp.transpose(left_ref[...])


def turn(places, pair):
    rows, width = pair[0].shape
    line = width // 2
    whole = pl.BlockSpec((rows, width), lambda i, s: (0, 0))
    return pl.pallas_call(
        turn_kernel,
        grid_spec=pltpu.PrefetchScalarGridSpec(
            num_scalar_prefetch=1,
            grid=(2,),
            in_specs=[whole, whole],
            out_specs=pl.BlockSpec((1, line, 2 * rows), lambda i, s: (i, 0, 0)),
            scratch_shapes=[pltpu.VMEM((2 * rows, line), LOW)],
        ),
        out_shape=jax.ShapeDtypeStruct((2, line, 2 * rows), LOW),
        compiler_params=pltpu.CompilerParams(vmem_limit_bytes=VMEM_ROOM),
        cost_estimate=pl.CostEstimate(
            flops=0, transcendentals=0, bytes_accessed=rows * width * 8
        ),
    )(places, *pair)


def weight_cost(operands):
    rows, line = operands[0][1].shape[0], 4 * LANES
    wide = sum(right.shape[1] for _, right in operands) // 4
    return pl.CostEstimate(
        flops=8 * rows * line * wide,
        transcendentals=0,
        bytes_accessed=rows * wide * 8 + rows * line * 8 + line * wide * 8,
    )


def piece_kernel(pairs, *refs):
    ins, outs = refs[: 2 * pairs], refs[2 * pairs :]
    step = pl.program_id(0)
    parts = [mat(ins[2 * pair][0], ins[2 * pair + 1][...]).astype(LOW) for pair in range(pairs)]
    made = parts[0] if pairs == 1 else jnp.concatenate(parts, axis=1)

    @pl.when(step < 2)
    def _():
        outs[0][0] = made

    @pl.when(step >= 2)
    def _():
        outs[1][0] = made


def weight_pieces(operands, send):
    line, rows = operands[0][0].shape[1:]
    if send:
        first = lambda i: jnp.minimum(i, 1)
        column = lambda i: jnp.maximum(i, 1)
    else:
        first = lambda i: 1 - jnp.minimum(i, 1)
        column = lambda i: jnp.where(i < 2, 0, i)
    specs, arrays, wide = [], [], 0
    for turned, right in operands:
        span = right.shape[1] // 4
        wide += span
        specs.append(pl.BlockSpec((1, line, rows), lambda i: (first(i), 0, 0)))
        specs.append(pl.BlockSpec((rows, span), lambda i: (0, column(i))))
        arrays += [turned, right]

    def kernel(*refs):
        piece_kernel(len(operands), *refs)

    return pl.pallas_call(
        kernel,
        grid=(4,),
        in_specs=specs,
        out_specs=[
            pl.BlockSpec((1, line, wide), lambda i: (first(i), 0, 0)),
            pl.BlockSpec((1, line, wide), lambda i: (jnp.maximum(i - 2, 0), 0, 0)),
        ],
        out_shape=[jax.ShapeDtypeStruct((2, line, wide), LOW)] * 2,
        compiler_params=pltpu.CompilerParams(vmem_limit_bytes=VMEM_ROOM),
        cost_estimate=weight_cost(operands),
    )(*arrays)


def lane_of(shape):
    return lax.broadcasted_iota(jnp.int32, shape, 1)


def head_views(query, key, bias, head):
    lane = lane_of(query.shape)
    mine = (lane >= HDIM) if head else (lane < HDIM)
    spot = 0 if head else HDIM
    zero = jnp.zeros_like(query)
    query_view = jnp.where(mine, query, jnp.where(lane == spot, zero + 1, zero))
    key_view = jnp.where(lane == spot, bias, key)
    return mine, query_view, key_view


def attend_kernel(qkv_ref, bias_ref, mixed_ref, total_ref):
    query = qkv_ref[:, 0:LANES] * jnp.bfloat16(HDIM ** (-0.5))
    key = qkv_ref[:, LANES : 2 * LANES]
    value = qkv_ref[:, 2 * LANES : 3 * LANES]
    bias = bias_ref[...]
    sums, tops = [], []
    for head in range(2):
        mine, query_view, key_view = head_views(query, key, bias, head)
        scores = mat_far(query_view, key_view)
        top = jnp.max(scores, axis=1, keepdims=True)
        weight = jnp.exp(scores - top).astype(LOW)
        value_view = jnp.where(mine, value, jnp.ones_like(value))
        sums.append(jnp.dot(weight, value_view, preferred_element_type=jnp.float32))
        tops.append(top)
    low = lane_of(sums[0].shape) < HDIM
    upper = jnp.where(low, sums[0], sums[1])
    lower = jnp.where(low, sums[1], sums[0])
    lower = pltpu.roll(lower, HDIM, 1)
    mixed_ref[...] = (upper / lower).astype(LOW)
    total = jnp.where(low, tops[0], tops[1]) + jnp.log(lower)
    total = jnp.transpose(total)
    total_ref[0, 0:1, :] = total[0:1]
    total_ref[0, 1:2, :] = total[HDIM : HDIM + 1]


def attend_back_kernel(qkv_ref, bias_ref, grad_ref, mixed_ref, total_ref, out_ref):
    scale = HDIM ** (-0.5)
    query = qkv_ref[:, 0:LANES] * jnp.bfloat16(scale)
    key = qkv_ref[:, LANES : 2 * LANES]
    value = qkv_ref[:, 2 * LANES : 3 * LANES]
    bias = bias_ref[...]
    grad = grad_ref[...]
    product = grad.astype(jnp.float32) * mixed_ref[...].astype(jnp.float32)
    grad_query = grad_key = grad_value = None
    for head in range(2):
        mine, query_view, key_view = head_views(query, key, bias, head)
        zero = jnp.zeros_like(query)
        scores = mat_far(key_view, query_view)
        probs = jnp.exp(scores - total_ref[0, head : head + 1, :])
        grad_view = jnp.where(mine, grad, zero)
        grad_probs = mat_far(value, grad_view)
        ones = jnp.where(mine[0:8], 1.0, 0.0)
        inner = lax.dot_general(
            ones,
            product,
            (((1,), (1,)), ((), ())),
            precision=lax.Precision.HIGHEST,
            preferred_element_type=jnp.float32,
        )
        grad_scores = (probs * (grad_probs - inner[0:1])).astype(LOW)
        one_value = jnp.dot(probs.astype(LOW), grad_view, preferred_element_type=jnp.float32)
        one_key = jnp.dot(
            grad_scores, jnp.where(mine, query, zero), preferred_element_type=jnp.float32
        )
        one_query = mat_rows(grad_scores, jnp.where(mine, key, zero))
        grad_query = one_query if head == 0 else grad_query + one_query
        grad_key = one_key if head == 0 else grad_key + one_key
        grad_value = one_value if head == 0 else grad_value + one_value
    out_ref[:, 0:LANES] = (grad_query * scale).astype(LOW)
    out_ref[:, LANES : 2 * LANES] = grad_key.astype(LOW)
    out_ref[:, 2 * LANES : 3 * LANES] = grad_value.astype(LOW)


def attend_image(image, qkv, bias, given):
    both = qkv.shape[0]
    rows = both // 2
    blocks = qkv.shape[1] // (3 * LANES)

    def kernel(*refs):
        attend_kernel(*refs[:2], *refs[-2:])

    return pl.pallas_call(
        kernel,
        grid=(blocks,),
        in_specs=[
            pl.BlockSpec((rows, 3 * LANES), lambda j: (image, j)),
            pl.BlockSpec((rows, LANES), lambda j: (0, 0)),
        ]
        + [pl.BlockSpec(memory_space=pl.ANY)] * len(given),
        out_specs=[
            pl.BlockSpec((rows, LANES), lambda j: (image, j)),
            pl.BlockSpec((1, 8, rows), lambda j: (image * blocks + j, 0, 0)),
        ],
        out_shape=[
            jax.ShapeDtypeStruct((both, blocks * LANES), LOW),
            jax.ShapeDtypeStruct((2 * blocks, 8, rows), jnp.float32),
        ],
        input_output_aliases={2: 0, 3: 1} if given else {},
        compiler_params=pltpu.CompilerParams(vmem_limit_bytes=VMEM_ROOM),
        cost_estimate=pl.CostEstimate(
            flops=blocks * 2 * 2 * 2 * rows * rows * LANES * 2,
            transcendentals=blocks * 2 * rows * rows,
            bytes_accessed=rows * blocks * LANES * 8,
        ),
    )(qkv, bias, *given)


def attend_back_image(image, qkv, bias, grad, mixed, total, given):
    both = qkv.shape[0]
    rows = both // 2
    blocks = qkv.shape[1] // (3 * LANES)

    def kernel(*refs):
        attend_back_kernel(*refs[:5], refs[-1])

    return pl.pallas_call(
        kernel,
        grid=(blocks,),
        in_specs=[
            pl.BlockSpec((rows, 3 * LANES), lambda j: (image, j)),
            pl.BlockSpec((rows, LANES), lambda j: (0, 0)),
            pl.BlockSpec((rows, LANES), lambda j: (0, j)),
            pl.BlockSpec((rows, LANES), lambda j: (image, j)),
            pl.BlockSpec((1, 8, rows), lambda j: (image * blocks + j, 0, 0)),
        ]
        + [pl.BlockSpec(memory_space=pl.ANY)] * len(given),
        out_specs=pl.BlockSpec((rows, 3 * LANES), lambda j: (image, j)),
        out_shape=jax.ShapeDtypeStruct(qkv.shape, LOW),
        input_output_aliases={5: 0} if given else {},
        compiler_params=pltpu.CompilerParams(vmem_limit_bytes=VMEM_ROOM),
        cost_estimate=pl.CostEstimate(
            flops=blocks * 2 * 5 * 2 * rows * rows * LANES * 2,
            transcendentals=blocks * 2 * rows * rows,
            bytes_accessed=rows * blocks * LANES * 16,
        ),
    )(qkv, bias, grad, mixed, total, *given)


def flat_norm(values, gain, shift):
    center = values - jnp.mean(values, axis=-1, keepdims=True)
    spread = lax.rsqrt(jnp.mean(center * center, axis=-1, keepdims=True) + EPS)
    unit = center * spread
    return unit * gain + shift, unit, spread


def flat_norm_back(upstream, unit, spread, gain):
    scaled = upstream * gain
    inner = (
        scaled
        - jnp.mean(scaled, axis=-1, keepdims=True)
        - unit * jnp.mean(scaled * unit, axis=-1, keepdims=True)
    )
    return spread * inner, jnp.sum(upstream * unit, axis=0), jnp.sum(upstream, axis=0)


def column_flat(values):
    return jnp.sum(values.astype(jnp.float32), axis=0)


def whole_images(
    images,
    cotangent,
    slot_live,
    first_gain,
    first_shift,
    query_weight,
    query_bias,
    key_weight,
    value_weight,
    value_bias,
    output_weight,
    output_bias,
    second_gain,
    second_shift,
    up_weight,
    up_bias,
    down_weight,
    down_bias,
):
    dp_place = lax.axis_index("dp")
    place_y = lax.axis_index("tensor")
    core, place_x, place_z = dp_place % 2, (dp_place // 2) % 2, dp_place // 4
    places = jnp.stack([place_z, place_x, core, place_y]).astype(jnp.int32)
    strip, width = images.shape[1:]
    half = -(-strip // HALF_PAD) * HALF_PAD
    rows = 2 * half
    depth, head_cols = query_weight.shape
    units = up_weight.shape[1]

    def columns_of(weights, place):
        return [
            lax.dynamic_slice_in_dim(
                weight, place * (weight.shape[1] // 2), weight.shape[1] // 2, 1
            )
            for weight in weights
        ]

    def core_parts(weights, place):
        cuts = columns_of(weights, place)
        parts = []
        for part in range(2):
            spans = [cut.shape[1] // 2 for cut in cuts]
            parts.append(
                jnp.concatenate(
                    [cut[:, part * span : (part + 1) * span] for cut, span in zip(cuts, spans)], 1
                )
            )
        return jnp.stack(parts)

    feeds = [up_weight, down_weight.T]
    feed_keep = jnp.concatenate(columns_of(feeds, core), 1)
    feed_send = jnp.concatenate(columns_of(feeds, 1 - core), 1)
    feed = pick_two(core, feed_keep, exchange(feed_send, far_core=1), 0)
    groups = [[place for place in range(32) if (place // 2) % 2 == at] for at in range(2)]

    gathered = lax.all_gather(
        feed.reshape(2 * depth, -1), BOTH, axis=0, tiled=True, axis_index_groups=groups
    ).reshape(8, 2, 2 * depth, -1)
    gathered = pltpu.with_memory_space_constraint(gathered, pltpu.HBM)

    heads = [query_weight, key_weight, value_weight, output_weight.T]
    piece_one = gather_piece(core_parts(heads, core), core_parts(heads, 1 - core), core)
    others_one = scatter_z([None, piece_one, piece_one, piece_one])

    padding = ((0, 0), (0, half - strip), (0, 0))

    def own_and_far(slots, *waits):
        slots = jnp.pad(slots, padding)
        mine = lax.dynamic_index_in_dim(slots, place_y, 0, keepdims=False)
        theirs = lax.dynamic_index_in_dim(slots, 1 - place_y, 0, keepdims=False)
        return mine, exchange(after(theirs, *waits), far_y=1)

    image_mine, image_far = own_and_far(images, piece_one)
    grad_mine, grad_far = own_and_far(cotangent, piece_one)
    line_one = gather_line(piece_one, others_one, places)
    cross_one = exchange(line_one[0], far_x=1), exchange(line_one[1], far_y=1)
    pair_one = gather_pairs(places, *line_one, *cross_one)
    image_far, grad_far = after((image_far, grad_far), *pair_one)
    whole = jnp.concatenate([image_mine, image_far], 0)

    def head_columns(vector):
        table = vector.astype(jnp.float32).reshape(2, 2, 2, -1)
        table = lax.dynamic_index_in_dim(table, core, 1, keepdims=False)
        table = jnp.where(place_y == 0, table, table[::-1])
        return table.transpose(1, 0, 2).reshape(4, 1, -1)

    def spread_core(table):
        table = jnp.stack(
            [jnp.where(core == 0, table, 0.0), jnp.where(core == 1, table, 0.0)], 1
        )
        return table.reshape(-1)

    def head_spread(vector):
        table = vector.reshape(2, 2, -1).transpose(1, 0, 2)
        return spread_core(jnp.where(place_y == 0, table, table[::-1]))

    gain_one, shift_one = first_gain.astype(jnp.float32), first_shift.astype(jnp.float32)
    gain_two, shift_two = second_gain.astype(jnp.float32), second_shift.astype(jnp.float32)
    query_shift, value_shift = head_columns(query_bias), head_columns(value_bias)
    qkv_shift = jnp.concatenate(
        [query_shift, jnp.zeros_like(query_shift), value_shift], 1
    ).reshape(-1)
    up_shift = head_columns(up_bias).reshape(1, -1)

    row = jnp.arange(rows)
    in_half = row % half
    spot = jnp.where(row < half, place_y, 1 - place_y) * strip + in_half
    ok = (in_half < strip) & (spot < VALID)
    live = lax.dynamic_index_in_dim(slot_live, place_y, 0, keepdims=False).astype(jnp.float32)
    row_mask = (live * ok.astype(jnp.float32))[:, None]
    key_bias = jnp.broadcast_to(
        jnp.where(ok, 0.0, NEGATIVE).astype(LOW)[:, None], (rows, LANES)
    )

    resid = whole.astype(jnp.float32)

    def full_columns(owned):
        return owned.transpose(2, 0, 1, 3).reshape(depth, -1)

    def pair_of(own):
        return own, exchange(own, far_core=1)

    normed, unit_one, spread_one = flat_norm(resid, gain_one, shift_one)
    normed_pair = pair_of(normed.astype(LOW))

    normed_turned = turn(places, normed_pair)
    grad_top = row_mask * jnp.concatenate([grad_mine, grad_far], 0).astype(jnp.float32)
    fed_grad = grad_top.astype(LOW)
    fed_pair = pair_of(fed_grad)
    fed_turned = turn(places, fed_pair)
    last_one = exchange(pair_one[0], far_y=1), exchange(pair_one[1], far_x=1)
    qkv_full, output_full = gather_all(after(places, normed_turned, fed_turned), *pair_one, *last_one, 3 * head_cols // 4)

    normed_rows = jnp.concatenate(normed_pair, 0)
    qkv = (mat(normed_rows, qkv_full) + qkv_shift).astype(LOW)
    mixed_half = attend_image(1, qkv, key_bias, [])
    mixed_far = mat_far(mixed_half[0][rows:], output_full).astype(LOW)
    mixed_sum = exchange(mixed_far, far_core=1)
    mixed, totals = attend_image(0, qkv, key_bias, list(after(tuple(mixed_half), mixed_far)))
    attended = mat_far(mixed[:rows], output_full) + mixed_sum.astype(jnp.float32)
    attended = attended + output_bias.astype(jnp.float32)
    middle = row_mask * (resid + attended)
    second, unit_two, spread_two = flat_norm(middle, gain_two, shift_two)
    second_pair = pair_of(second.astype(LOW))
    active, slope = up_call(places, second_pair, gathered, up_shift)

    lower_sends = weight_pieces([(fed_turned, active)], True)
    lower_first = scatter_first(lower_sends)
    lower_keeps = weight_pieces([(fed_turned, after(active, *lower_sends))], False)
    fed_late = after(fed_pair, *lower_keeps)
    hidden_grad, up_bias_sums = hidden_call(places, fed_late, gathered, slope)
    second_turned = turn(places, second_pair)
    up_sends = weight_pieces([(second_turned, hidden_grad)], True)
    up_first = scatter_first(up_sends)
    lower_first = after(lower_first, *up_sends)
    lower_second = scatter_second(scatter_adds(lower_keeps, lower_first))
    hidden_late = after(hidden_grad, *lower_first)
    second_grad = down_call(places, hidden_late, gathered, 0)
    middle_back, gain_two_grad, shift_two_grad = flat_norm_back(
        second_grad, unit_two, spread_two, gain_two
    )
    middle_grad = row_mask * (grad_top + middle_back)
    attended_grad = middle_grad.astype(LOW)
    attended_pair = pair_of(attended_grad)
    grad_mixed = mat(attended_pair[0], output_full).astype(LOW)
    back = attend_back_image(0, qkv, key_bias, grad_mixed, mixed, totals, [])
    up_keeps = weight_pieces([(second_turned, after(hidden_late, back))], False)
    up_first = after(up_first, back)
    up_adds = scatter_adds(up_keeps, up_first)
    up_second = scatter_second(up_adds)
    lower_second = after(lower_second, back, *up_keeps)
    lower_line = scatter_line(lower_keeps, lower_first, lower_second)
    lower_z = scatter_z(lower_line)
    attended_turned = turn(places, attended_pair)
    grad_mixed = mat(attended_pair[1], output_full).astype(LOW)
    grad_mixed = after(grad_mixed, *up_adds, *lower_line, attended_turned)
    back = attend_back_image(1, qkv, key_bias, grad_mixed, mixed, totals, [back])
    up_second, lower_z = after((up_second, tuple(lower_z)), back)
    up_line = scatter_line(up_keeps, up_first, up_second)
    up_z = scatter_z(up_line)
    back = after(back, *up_line)
    last_sends = weight_pieces([(normed_turned, back), (attended_turned, mixed)], True)
    last_first = scatter_first(last_sends)
    back_late = after(back, *last_sends)
    last_keeps = weight_pieces([(normed_turned, back_late), (attended_turned, mixed)], False)
    back_late = after(back_late, *last_keeps)
    normed_far = exchange(mat_far(back_late[rows:], qkv_full).astype(LOW), far_core=1)
    normed_grad = mat_far(back_late[:rows], qkv_full) + normed_far.astype(jnp.float32)
    first_back, gain_one_grad, shift_one_grad = flat_norm_back(
        normed_grad, unit_one, spread_one, gain_one
    )
    images_own = middle_grad + first_back
    qkv_sums = column_flat(back_late).reshape(4, 3, -1)
    vector = jnp.concatenate(
        [
            column_flat(attended_grad),
            gain_two_grad,
            shift_two_grad,
            column_flat(fed_grad),
            head_spread(up_bias_sums.reshape(-1)),
            gain_one_grad,
            shift_one_grad,
            head_spread(qkv_sums[:, 0].reshape(-1)),
            head_spread(qkv_sums[:, 2].reshape(-1)),
        ]
    )
    vector, vectors = vector_first(vector)
    last_first = after(last_first, *last_keeps, images_own, *vectors)
    last_adds = scatter_adds(last_keeps, last_first)
    last_second = scatter_second(last_adds)
    fed = down_call(places, after(active, *last_adds), gathered, 1)
    layer_own = (row_mask * (middle + fed + down_bias.astype(jnp.float32))).astype(LOW)
    vector = after(vector, *last_adds) + vectors[0] + vectors[1] + vectors[2]
    vector = vector + after(exchange(vector, far_y=1), layer_own)
    vector_x = exchange(vector, far_x=1)
    last_line = scatter_line(last_keeps, last_first, after(last_second, layer_own, *up_z))
    last_z = scatter_z(last_line)
    images_far = exchange(after(images_own, *last_adds)[half : half + strip].astype(LOW), far_y=1)
    layer_far = exchange(after(layer_own, *last_second)[half : half + strip], far_y=1)
    vector = vector + after(vector_x, *last_line, images_far, layer_far)
    lower_z, up_z = after((tuple(lower_z), tuple(up_z)), *last_line)
    lower_owned = full_columns(scatter_last(lower_line[0], lower_z, core)).T
    upper_owned = full_columns(scatter_last(up_line[0], up_z, core))

    def to_strips(own, far):
        return pick_two(place_y, own[:strip], far, 1).transpose(1, 0, 2)

    layer_out = to_strips(layer_own, layer_far)
    images_grad = to_strips(after(images_own, *last_line), images_far.astype(jnp.float32))
    last_z = after(tuple(last_z), vector, layer_out, images_grad, lower_owned, upper_owned)
    last_owned = scatter_last(last_line[0], last_z, core)
    def head_grad(at):
        return full_columns(last_owned[..., at * LANES : (at + 1) * LANES])

    early, late = vector[: 4 * width + up_bias.shape[0]], vector[4 * width + up_bias.shape[0] :]
    return (
        layer_out,
        images_grad,
        late[:width],
        late[width : 2 * width],
        head_grad(0),
        late[2 * width : 3 * width],
        head_grad(1),
        head_grad(2),
        late[3 * width :],
        head_grad(3).T,
        early[:width],
        early[width : 2 * width],
        early[2 * width : 3 * width],
        upper_owned,
        early[4 * width :],
        lower_owned,
        early[3 * width : 4 * width],
    )


def pick(mesh):
    sizes = dict(mesh.shape)
    if sizes["dp"] == 16 and sizes["tensor"] == 2:
        return whole_images
    return local


def solution(mesh):
    in_specs = (
        P("dp", "tensor", None),
        P("dp", "tensor", None),
        P("dp"),
        P(),
        P(),
        P("dp", "tensor"),
        P(),
        P("dp", "tensor"),
        P("dp", "tensor"),
        P(),
        P("tensor", "dp"),
        P(),
        P(),
        P(),
        P("dp", "tensor"),
        P(),
        P("tensor", "dp"),
        P(),
    )
    out_specs = (
        P("dp", "tensor", None),
        P("dp", "tensor", None),
        P(),
        P(),
        P("dp", "tensor"),
        P(),
        P("dp", "tensor"),
        P("dp", "tensor"),
        P(),
        P("tensor", "dp"),
        P(),
        P(),
        P(),
        P("dp", "tensor"),
        P(),
        P("tensor", "dp"),
        P(),
    )
    return jax.shard_map(pick(mesh), mesh=mesh, in_specs=in_specs, out_specs=out_specs, check_vma=False)
```

```python
import jax
import jax.numpy as jnp
from jax import lax
from jax.experimental import pallas as pl
from jax.experimental.pallas import tpu as pltpu
from jax.sharding import PartitionSpec as P

HDIM = 64
VALID = 577


EPS = 1e-05
NEGATIVE = -1e30
SLOPE = 1.702


def layer_norm(values, gain, shift):
    center = values - jnp.mean(values, axis=-1, keepdims=True)
    spread = lax.rsqrt(jnp.mean(center * center, axis=-1, keepdims=True) + EPS)
    unit = center * spread
    return (unit * gain + shift, unit, spread)


def norm_back(upstream, unit, spread, gain):
    scaled = upstream * gain
    inner = (
        scaled
        - jnp.mean(scaled, axis=-1, keepdims=True)
        - unit * jnp.mean(scaled * unit, axis=-1, keepdims=True)
    )
    return (spread * inner, jnp.sum(upstream * unit, axis=(0, 1)), jnp.sum(upstream, axis=(0, 1)))


def dense(left, right):
    return jnp.einsum("spa,ab->spb", left, right, preferred_element_type=jnp.float32)


def project_back(left, right):
    return jnp.einsum("spa,ba->spb", left, right, preferred_element_type=jnp.float32)


def outer(left, right):
    return jnp.einsum("spa,spb->ab", left, right, preferred_element_type=jnp.float32)


def column_sum(values):
    return jnp.sum(values.astype(jnp.float32), axis=(0, 1))


def widen(piece, length, start):
    return lax.dynamic_update_slice_in_dim(jnp.zeros((length,), jnp.float32), piece, start, 0)


def split_heads(block):
    return block.reshape(block.shape[0], -1, HDIM)


def scores_of(query, key, key_ok):
    raw = jnp.einsum(
        "qhe,khe->hqk", split_heads(query), split_heads(key), preferred_element_type=jnp.float32
    )
    return jnp.where(key_ok[None, None, :], raw * HDIM ** (-0.5), NEGATIVE)


def attend(query, key, value, key_ok):
    scores = scores_of(query, key, key_ok)
    top = jnp.max(scores, axis=-1, keepdims=True)
    total = top + jnp.log(jnp.sum(jnp.exp(scores - top), axis=-1, keepdims=True))
    probs = jnp.exp(scores - total).astype(jnp.bfloat16)
    mixed = jnp.einsum(
        "hqk,khe->qhe", probs, split_heads(value), preferred_element_type=jnp.float32
    )
    return (mixed.reshape(query.shape[0], -1).astype(jnp.bfloat16), total)


def attend_back(query, key, value, grad_mixed, total, key_ok):
    scores = scores_of(query, key, key_ok)
    probs = jnp.exp(scores - total)
    grad_heads = split_heads(grad_mixed)
    grad_probs = jnp.einsum(
        "qhe,khe->hqk", grad_heads, split_heads(value), preferred_element_type=jnp.float32
    )
    grad_value = jnp.einsum(
        "hqk,qhe->khe", probs.astype(jnp.bfloat16), grad_heads, preferred_element_type=jnp.float32
    )
    grad_scores = (
        probs * (grad_probs - jnp.sum(probs * grad_probs, axis=-1, keepdims=True))
    ).astype(jnp.bfloat16)
    grad_query = jnp.einsum(
        "hqk,khe->qhe", grad_scores, split_heads(key), preferred_element_type=jnp.float32
    ) * HDIM ** (-0.5)
    grad_key = jnp.einsum(
        "hqk,qhe->khe", grad_scores, split_heads(query), preferred_element_type=jnp.float32
    ) * HDIM ** (-0.5)
    length = query.shape[0]
    return (
        grad_query.reshape(length, -1).astype(jnp.bfloat16),
        grad_key.reshape(length, -1).astype(jnp.bfloat16),
        grad_value.reshape(length, -1).astype(jnp.bfloat16),
    )


def local(
    images,
    cotangent,
    slot_live,
    first_gain,
    first_shift,
    query_weight,
    query_bias,
    key_weight,
    value_weight,
    value_bias,
    output_weight,
    output_bias,
    second_gain,
    second_shift,
    up_weight,
    up_bias,
    down_weight,
    down_bias,
):
    slots, strip, width = images.shape
    tensor_count = lax.axis_size("tensor")
    tensor_place = lax.axis_index("tensor")
    seq_len = strip * tensor_count
    positions = tensor_place * strip + jnp.arange(strip)
    row_mask = (
        slot_live.astype(jnp.float32)[:, None, None]
        * (positions < VALID).astype(jnp.float32)[None, :, None]
    )
    key_ok = jnp.arange(seq_len) < VALID
    query_full, key_full, value_full, upper_full, output_full, lower_full = (
        lax.all_gather(query_weight, "dp", axis=0, tiled=True),
        lax.all_gather(key_weight, "dp", axis=0, tiled=True),
        lax.all_gather(value_weight, "dp", axis=0, tiled=True),
        lax.all_gather(up_weight, "dp", axis=0, tiled=True),
        lax.all_gather(output_weight, "dp", axis=1, tiled=True),
        lax.all_gather(down_weight, "dp", axis=1, tiled=True),
    )
    head_cols = query_full.shape[1]
    head_start = tensor_place * head_cols
    gain_one = first_gain.astype(jnp.float32)
    shift_one = first_shift.astype(jnp.float32)
    gain_two = second_gain.astype(jnp.float32)
    shift_two = second_shift.astype(jnp.float32)
    query_shift = lax.dynamic_slice_in_dim(query_bias.astype(jnp.float32), head_start, head_cols)
    value_shift = lax.dynamic_slice_in_dim(value_bias.astype(jnp.float32), head_start, head_cols)
    resid = images.astype(jnp.float32)
    normed, unit_one, spread_one = layer_norm(resid, gain_one, shift_one)
    normed_rows = lax.all_gather(normed.astype(jnp.bfloat16), "tensor", axis=1, tiled=True)
    queries = (dense(normed_rows, query_full) + query_shift).astype(jnp.bfloat16)
    keys_low = dense(normed_rows, key_full).astype(jnp.bfloat16)
    values_low = (dense(normed_rows, value_full) + value_shift).astype(jnp.bfloat16)
    mixed, totals = lax.map(
        lambda items: attend(items[0], items[1], items[2], key_ok), (queries, keys_low, values_low)
    )
    attended = lax.psum_scatter(
        dense(mixed, output_full), "tensor", scatter_dimension=1, tiled=True
    ) + output_bias.astype(jnp.float32)
    middle = row_mask * (resid + attended)
    second, unit_two, spread_two = layer_norm(middle, gain_two, shift_two)
    second_low = second.astype(jnp.bfloat16)
    grad_top = row_mask * cotangent.astype(jnp.float32)
    fed_grad = grad_top.astype(jnp.bfloat16)
    down_shift = down_bias.astype(jnp.float32)
    units = upper_full.shape[1]
    second_rows = lax.all_gather(second_low, "tensor", axis=1, tiled=True)
    up_shift = lax.dynamic_slice_in_dim(up_bias.astype(jnp.float32), tensor_place * units, units)
    hidden = dense(second_rows, upper_full) + up_shift
    sigma = jax.nn.sigmoid(SLOPE * hidden)
    active = (hidden * sigma).astype(jnp.bfloat16)
    fed = (
        lax.psum_scatter(
            dense(active, lower_full).astype(jnp.bfloat16),
            "tensor",
            scatter_dimension=1,
            tiled=True,
        ).astype(jnp.float32)
        + down_shift
    )
    fed_rows = lax.all_gather(fed_grad, "tensor", axis=1, tiled=True)
    grad_active = project_back(fed_rows, lower_full)
    lower_grad = outer(active, fed_rows)
    hidden_grad = (grad_active * (sigma + SLOPE * hidden * sigma * (1.0 - sigma))).astype(
        jnp.bfloat16
    )
    upper_grad = outer(second_rows, hidden_grad)
    up_bias_grad = widen(column_sum(hidden_grad), up_bias.shape[0], tensor_place * units)
    second_grad = lax.psum_scatter(
        project_back(hidden_grad, upper_full), "tensor", scatter_dimension=1, tiled=True
    )
    layer_out = (row_mask * (middle + fed)).astype(jnp.bfloat16)
    down_bias_grad = column_sum(fed_grad)
    middle_back, gain_two_grad, shift_two_grad = norm_back(
        second_grad, unit_two, spread_two, gain_two
    )
    middle_grad = row_mask * (grad_top + middle_back)
    attended_grad = middle_grad.astype(jnp.bfloat16)
    output_bias_grad = column_sum(attended_grad)
    attended_rows = lax.all_gather(attended_grad, "tensor", axis=1, tiled=True)
    grad_mixed = project_back(attended_rows, output_full).astype(jnp.bfloat16)
    output_grad = outer(mixed, attended_rows)
    grad_query, grad_key, grad_value = lax.map(
        lambda items: attend_back(items[0], items[1], items[2], items[3], items[4], key_ok),
        (queries, keys_low, values_low, grad_mixed, totals),
    )
    query_grad = outer(normed_rows, grad_query)
    key_grad = outer(normed_rows, grad_key)
    value_grad = outer(normed_rows, grad_value)
    query_bias_grad = widen(column_sum(grad_query), width, head_start)
    value_bias_grad = widen(column_sum(grad_value), width, head_start)
    normed_terms = (
        project_back(grad_query, query_full)
        + project_back(grad_key, key_full)
        + project_back(grad_value, value_full)
    )
    normed_grad = lax.psum_scatter(
        normed_terms.astype(jnp.bfloat16), "tensor", scatter_dimension=1, tiled=True
    ).astype(jnp.float32)
    first_back, gain_one_grad, shift_one_grad = norm_back(
        normed_grad, unit_one, spread_one, gain_one
    )
    images_grad = middle_grad + first_back
    query_owned, key_owned, value_owned, upper_owned, output_owned, lower_owned = (
        lax.psum_scatter(
            query_grad.astype(jnp.bfloat16), "dp", scatter_dimension=0, tiled=True
        ).astype(jnp.float32),
        lax.psum_scatter(
            key_grad.astype(jnp.bfloat16), "dp", scatter_dimension=0, tiled=True
        ).astype(jnp.float32),
        lax.psum_scatter(
            value_grad.astype(jnp.bfloat16), "dp", scatter_dimension=0, tiled=True
        ).astype(jnp.float32),
        lax.psum_scatter(
            upper_grad.astype(jnp.bfloat16), "dp", scatter_dimension=0, tiled=True
        ).astype(jnp.float32),
        lax.psum_scatter(
            output_grad.astype(jnp.bfloat16), "dp", scatter_dimension=1, tiled=True
        ).astype(jnp.float32),
        lax.psum_scatter(
            lower_grad.astype(jnp.bfloat16), "dp", scatter_dimension=1, tiled=True
        ).astype(jnp.float32),
    )
    vector_sums = lax.psum(
        (
            gain_one_grad,
            shift_one_grad,
            query_bias_grad,
            value_bias_grad,
            output_bias_grad,
            gain_two_grad,
            shift_two_grad,
            up_bias_grad,
            down_bias_grad,
        ),
        ("dp", "tensor"),
    )
    (
        gain_one_total,
        shift_one_total,
        query_bias_total,
        value_bias_total,
        output_bias_total,
        gain_two_total,
        shift_two_total,
        up_bias_total,
        down_bias_total,
    ) = vector_sums
    return (
        layer_out,
        images_grad,
        gain_one_total,
        shift_one_total,
        query_owned,
        query_bias_total,
        key_owned,
        value_owned,
        value_bias_total,
        output_owned,
        output_bias_total,
        gain_two_total,
        shift_two_total,
        upper_owned,
        up_bias_total,
        lower_owned,
        down_bias_total,
    )


BOTH = ("dp", "tensor")
HALF_PAD = 8
LANES = 128
LOW = jnp.bfloat16
VMEM_ROOM = 24 * 2**20
SMALL = pl.CostEstimate(flops=1024, transcendentals=0, bytes_accessed=1024)


def exchange(value, far_z=0, far_x=0, far_core=0, far_y=0):
    pairs = []
    for place in range(32):
        other = place ^ (far_z * 8 + far_x * 4 + far_core * 2 + far_y)
        pairs.append((place, other))
    return lax.ppermute(value, BOTH, pairs)


def pick_two(bit, own, other, axis):
    first = jnp.where(bit == 0, own, other)
    last = jnp.where(bit == 0, other, own)
    return jnp.stack([first, last], axis)


def after(value, *others):
    return lax.optimization_barrier((value, *others))[0]


def pack(places, sources, shapes, plan):
    def kernel(places_ref, *refs):
        ins, outs = refs[: len(sources)], refs[len(sources) :]
        spots = [places_ref[at] for at in range(4)]
        for at, take, to, put in plan:
            outs[to][put(*spots)] = ins[at][take(*spots)]

    return pl.pallas_call(
        kernel,
        in_specs=[pl.BlockSpec(memory_space=pltpu.SMEM)]
        + [pl.BlockSpec(memory_space=pltpu.VMEM)] * len(sources),
        out_specs=[pl.BlockSpec(memory_space=pltpu.VMEM)] * len(shapes),
        out_shape=[jax.ShapeDtypeStruct(shape, LOW) for shape in shapes],
        compiler_params=pltpu.CompilerParams(vmem_limit_bytes=VMEM_ROOM),
        cost_estimate=pl.CostEstimate(
            flops=0,
            transcendentals=0,
            bytes_accessed=sum(2 * source.size * 2 for source in sources),
        ),
    )(places, *sources)


def gather_piece(keep, send, core):
    deep, wide = keep.shape[1:]
    return pick_two(core, keep, exchange(send, far_core=1), 1).reshape(2, 2 * deep, wide)


def gather_line(piece, others, places):
    rows, wide = piece.shape[1:]
    line = [piece] + others
    plan = []
    for step in range(4):
        for part in range(2):
            plan.append(
                (
                    step,
                    lambda z, x, c, y, part=part: part,
                    part,
                    lambda z, x, c, y, step=step: z ^ step,
                )
            )
    return pack(places, line, [(4, rows, wide)] * 2, plan)


def gather_pairs(places, one, two, one_x, two_y):
    every = slice(None)
    plan = [
        (0, lambda z, x, c, y: every, 0, lambda z, x, c, y: x),
        (1, lambda z, x, c, y: every, 0, lambda z, x, c, y: 1 - x),
        (2, lambda z, x, c, y: every, 1, lambda z, x, c, y: 0),
        (3, lambda z, x, c, y: every, 1, lambda z, x, c, y: 1),
    ]
    return pack(places, [one, one_x, two, two_y], [(2,) + one.shape] * 2, plan)


def gather_all(places, one_pair, two_pair, one_y, two_x, most):
    every = slice(None)
    rows, wide = one_pair.shape[2:]
    plan = []
    for to, low, high in ((0, 0, most), (1, most, wide)):
        span = high - low
        for place_z in range(4):
            for far in range(2):
                for number in range(2):
                    plan.append(
                        (
                            number,
                            lambda z, x, c, y, a=far, p=place_z, lo=low, hi=high: (
                                a,
                                p,
                                every,
                                slice(lo, hi),
                            ),
                            to,
                            lambda z, x, c, y, a=far, p=place_z, n=number, s=span: (
                                p,
                                a,
                                every,
                                slice(n * s, n * s + s),
                            ),
                        )
                    )
                    plan.append(
                        (
                            2 + far,
                            lambda z, x, c, y, n=number, p=place_z, lo=low, hi=high: (
                                n,
                                p,
                                every,
                                slice(lo, hi),
                            ),
                            to,
                            lambda z, x, c, y, f=far, p=place_z, n=number, s=span: (
                                p,
                                x ^ f,
                                every,
                                slice((2 + n) * s, (3 + n) * s),
                            ),
                        )
                    )
    shapes = [(4, 2, rows, 4 * most), (4, 2, rows, 4 * (wide - most))]
    made = pack(places, [one_pair, one_y, two_pair, two_x], shapes, plan)
    return [array.reshape(8 * rows, -1) for array in made]


def low_add(*values):
    total = values[0].astype(jnp.float32)
    for value in values[1:]:
        total = total + value.astype(jnp.float32)
    return total


def line_kernel(one_ref, one_a, one_b, two_ref, two_a, two_b, own_ref, *send_refs):
    tall = own_ref.shape[1]
    for step in range(4):
        rows = slice(step * tall, (step + 1) * tall)
        one = low_add(one_ref[0, rows], one_a[0, rows], one_b[rows])
        two = low_add(two_ref[0, rows], two_a[0, rows], two_b[rows])
        if step == 0:
            own_ref[0] = one
            own_ref[1] = two
        else:
            send_refs[step - 1][0] = one.astype(LOW)
            send_refs[step - 1][1] = two.astype(LOW)


def scatter_first(sends):
    return exchange(sends[0], far_y=1), exchange(sends[1], far_x=1)


def scatter_adds(keeps, arrived):
    return [low_add(keeps[at][1], arrived[at][1]).astype(LOW) for at in range(2)]


def scatter_second(adds):
    return exchange(adds[0], far_x=1), exchange(adds[1], far_y=1)


def scatter_line(keeps, arrived, crossed):
    lines, wide = crossed[0].shape
    tall = lines // 4
    first = pl.BlockSpec((1, lines, wide), lambda i: (0, 0, 0))
    flat = pl.BlockSpec((lines, wide), lambda i: (0, 0))
    piece = pl.BlockSpec((2, tall, wide), lambda i: (0, 0, 0))
    return pl.pallas_call(
        line_kernel,
        grid=(1,),
        in_specs=[first, first, flat, first, first, flat],
        out_specs=[piece] * 4,
        out_shape=[jax.ShapeDtypeStruct((2, tall, wide), jnp.float32)]
        + [jax.ShapeDtypeStruct((2, tall, wide), LOW)] * 3,
        compiler_params=pltpu.CompilerParams(vmem_limit_bytes=VMEM_ROOM),
        cost_estimate=pl.CostEstimate(
            flops=lines * wide * 4, transcendentals=0, bytes_accessed=lines * wide * 18
        ),
    )(keeps[0], arrived[0], crossed[0], keeps[1], arrived[1], crossed[1])


def scatter_z(sends):
    return [exchange(sends[step], far_z=step) for step in (1, 2, 3)]


def scatter_last(own, others, core):
    tall, wide = own.shape[1:]
    total = low_add(own, *others).reshape(2, 2, tall // 2, wide)
    keep = lax.dynamic_index_in_dim(total, core, 1, keepdims=False)
    send = lax.dynamic_index_in_dim(total, 1 - core, 1, keepdims=False)
    far = exchange(send.astype(LOW), far_core=1).astype(jnp.float32)
    return pick_two(core, keep, far, 0)


def vector_first(vector):
    vector = vector + exchange(vector, far_core=1)
    return vector, [exchange(vector, far_z=step) for step in (1, 2, 3)]


def mat_far(left, right):
    return lax.dot_general(
        left, right, (((1,), (1,)), ((), ())), preferred_element_type=jnp.float32
    )


def mat_rows(left, right):
    return lax.dot_general(
        left, right, (((0,), (0,)), ((), ())), preferred_element_type=jnp.float32
    )


def fill_rows(made_ref, own_ref, far_ref):
    rows = own_ref.shape[0]

    @pl.when(pl.program_id(0) == 0)
    def _():
        made_ref[:rows] = own_ref[...]
        made_ref[rows:] = far_ref[...]


def up_kernel(
    places_ref, own_ref, far_ref, right_ref, shift_ref, active_ref, slope_ref, left_ref
):
    fill_rows(left_ref, own_ref, far_ref)
    right = right_ref[...].reshape(left_ref.shape[1], -1)
    hidden = jnp.dot(left_ref[...], right, preferred_element_type=jnp.float32)
    hidden = hidden + shift_ref[...]
    sigma = 0.5 * jnp.tanh((0.5 * SLOPE) * hidden) + 0.5
    active = hidden * sigma
    active_ref[...] = active.astype(LOW)
    slope_ref[...] = (sigma + SLOPE * active * (1.0 - sigma)).astype(LOW)


def feed_spec(gathered, start):
    lines, _, rows, wide = gathered.shape
    return pl.BlockSpec(
        (lines, 1, rows, wide // 4), lambda i, s: (0, s[3] ^ (i % 2), 0, start + i // 2)
    )


def up_call(places, pair, gathered, shift):
    rows, width = pair[0].shape
    wide = shift.shape[1] // 4
    whole = pl.BlockSpec((rows, width), lambda i, s: (0, 0))
    piece = pl.BlockSpec((2 * rows, wide), lambda i, s: (0, i))
    return pl.pallas_call(
        up_kernel,
        grid_spec=pltpu.PrefetchScalarGridSpec(
            num_scalar_prefetch=1,
            grid=(4,),
            in_specs=[
                whole,
                whole,
                feed_spec(gathered, 0),
                pl.BlockSpec((1, wide), lambda i, s: (0, i)),
            ],
            out_specs=[piece, piece],
            scratch_shapes=[pltpu.VMEM((2 * rows, width), LOW)],
        ),
        out_shape=[jax.ShapeDtypeStruct((2 * rows, 4 * wide), LOW)] * 2,
        compiler_params=pltpu.CompilerParams(vmem_limit_bytes=VMEM_ROOM),
        cost_estimate=pl.CostEstimate(
            flops=16 * rows * wide * width,
            transcendentals=8 * rows * wide,
            bytes_accessed=rows * width * 4 + 8 * width * wide + 32 * rows * wide,
        ),
    )(places, *pair, gathered, shift)


def hidden_kernel(
    places_ref, own_ref, far_ref, right_ref, slope_ref, out_ref, sum_ref, left_ref
):
    fill_rows(left_ref, own_ref, far_ref)
    right = right_ref[...].reshape(left_ref.shape[1], -1)
    grad = jnp.dot(left_ref[...], right, preferred_element_type=jnp.float32)
    grad = (grad * slope_ref[...].astype(jnp.float32)).astype(LOW)
    out_ref[...] = grad
    sum_ref[...] = jnp.sum(grad.astype(jnp.float32), axis=0, keepdims=True)


def hidden_call(places, pair, gathered, slope):
    rows, width = pair[0].shape
    wide = slope.shape[1] // 4
    whole = pl.BlockSpec((rows, width), lambda i, s: (0, 0))
    piece = pl.BlockSpec((2 * rows, wide), lambda i, s: (0, i))
    return pl.pallas_call(
        hidden_kernel,
        grid_spec=pltpu.PrefetchScalarGridSpec(
            num_scalar_prefetch=1,
            grid=(4,),
            in_specs=[whole, whole, feed_spec(gathered, 2), piece],
            out_specs=[piece, pl.BlockSpec((1, wide), lambda i, s: (0, i))],
            scratch_shapes=[pltpu.VMEM((2 * rows, width), LOW)],
        ),
        out_shape=[
            jax.ShapeDtypeStruct((2 * rows, 4 * wide), LOW),
            jax.ShapeDtypeStruct((1, 4 * wide), jnp.float32),
        ],
        compiler_params=pltpu.CompilerParams(vmem_limit_bytes=VMEM_ROOM),
        cost_estimate=pl.CostEstimate(
            flops=16 * rows * wide * width,
            transcendentals=0,
            bytes_accessed=rows * width * 4 + 8 * width * wide + 32 * rows * wide,
        ),
    )(places, *pair, gathered, slope)


def down_kernel(places_ref, left_ref, right_ref, own_ref, send_ref):
    span = right_ref.shape[3] // 2
    rows = own_ref.shape[0]
    total = None
    for far in range(2):
        right = right_ref[:, places_ref[3] ^ far].reshape(-1, 2 * span)
        for part in range(2):
            start = (part * 2 + far) * span
            one = mat_far(
                left_ref[:, start : start + span], right[:, part * span : (part + 1) * span]
            )
            total = one if total is None else total + one
    own_ref[...] = total[:rows]
    send_ref[...] = total[rows:].astype(LOW)


def down_call(places, left, gathered, start):
    both, deep = left.shape
    rows = both // 2
    lines, _, tall, wide = gathered.shape
    piece = pl.BlockSpec((rows, 2 * tall), lambda i, s: (0, i))
    own, send = pl.pallas_call(
        down_kernel,
        grid_spec=pltpu.PrefetchScalarGridSpec(
            num_scalar_prefetch=1,
            grid=(lines // 2,),
            in_specs=[
                pl.BlockSpec((both, deep), lambda i, s: (0, 0)),
                pl.BlockSpec((2, 2, tall, wide // 2), lambda i, s: (i, 0, 0, start)),
            ],
            out_specs=[piece, piece],
        ),
        out_shape=[
            jax.ShapeDtypeStruct((rows, lines * tall), jnp.float32),
            jax.ShapeDtypeStruct((rows, lines * tall), LOW),
        ],
        compiler_params=pltpu.CompilerParams(vmem_limit_bytes=VMEM_ROOM),
        cost_estimate=SMALL,
    )(places, left, gathered)
    return own, send


def mat(left, right):
    return jnp.dot(left, right, preferred_element_type=jnp.float32)


def turn_kernel(places_ref, own_ref, far_ref, turned_ref, left_ref):
    rows = own_ref.shape[0]
    for block in range(4):
        at = (places_ref[0] ^ block) * 2 + (places_ref[1] ^ pl.program_id(0))
        start = pl.multiple_of(at * LANES, LANES)
        span = slice(block * LANES, (block + 1) * LANES)
        left_ref[:rows, span] = own_ref[:, pl.ds(start, LANES)]
        left_ref[rows:, span] = far_ref[:, pl.ds(start, LANES)]
    turned_ref[0] = jnp.transpose(left_ref[...])


def turn(places, pair):
    rows, width = pair[0].shape
    line = width // 2
    whole = pl.BlockSpec((rows, width), lambda i, s: (0, 0))
    return pl.pallas_call(
        turn_kernel,
        grid_spec=pltpu.PrefetchScalarGridSpec(
            num_scalar_prefetch=1,
            grid=(2,),
            in_specs=[whole, whole],
            out_specs=pl.BlockSpec((1, line, 2 * rows), lambda i, s: (i, 0, 0)),
            scratch_shapes=[pltpu.VMEM((2 * rows, line), LOW)],
        ),
        out_shape=jax.ShapeDtypeStruct((2, line, 2 * rows), LOW),
        compiler_params=pltpu.CompilerParams(vmem_limit_bytes=VMEM_ROOM),
        cost_estimate=pl.CostEstimate(
            flops=0, transcendentals=0, bytes_accessed=rows * width * 8
        ),
    )(places, *pair)


def weight_cost(operands):
    rows, line = operands[0][1].shape[0], 4 * LANES
    wide = sum(right.shape[1] for _, right in operands) // 4
    return pl.CostEstimate(
        flops=8 * rows * line * wide,
        transcendentals=0,
        bytes_accessed=rows * wide * 8 + rows * line * 8 + line * wide * 8,
    )


def piece_kernel(pairs, *refs):
    ins, outs = refs[: 2 * pairs], refs[2 * pairs :]
    step = pl.program_id(0)
    parts = [mat(ins[2 * pair][0], ins[2 * pair + 1][...]).astype(LOW) for pair in range(pairs)]
    made = parts[0] if pairs == 1 else jnp.concatenate(parts, axis=1)

    @pl.when(step < 2)
    def _():
        outs[0][0] = made

    @pl.when(step >= 2)
    def _():
        outs[1][0] = made


def weight_pieces(operands, send, cost=None):
    line, rows = operands[0][0].shape[1:]
    if send:
        first = lambda i: jnp.minimum(i, 1)
        column = lambda i: jnp.maximum(i, 1)
    else:
        first = lambda i: 1 - jnp.minimum(i, 1)
        column = lambda i: jnp.where(i < 2, 0, i)
    specs, arrays, wide = [], [], 0
    for turned, right in operands:
        span = right.shape[1] // 4
        wide += span
        specs.append(pl.BlockSpec((1, line, rows), lambda i: (first(i), 0, 0)))
        specs.append(pl.BlockSpec((rows, span), lambda i: (0, column(i))))
        arrays += [turned, right]

    def kernel(*refs):
        piece_kernel(len(operands), *refs)

    return pl.pallas_call(
        kernel,
        grid=(4,),
        in_specs=specs,
        out_specs=[
            pl.BlockSpec((1, line, wide), lambda i: (first(i), 0, 0)),
            pl.BlockSpec((1, line, wide), lambda i: (jnp.maximum(i - 2, 0), 0, 0)),
        ],
        out_shape=[jax.ShapeDtypeStruct((2, line, wide), LOW)] * 2,
        compiler_params=pltpu.CompilerParams(vmem_limit_bytes=VMEM_ROOM),
        cost_estimate=cost or weight_cost(operands),
    )(*arrays)


def lane_of(shape):
    return lax.broadcasted_iota(jnp.int32, shape, 1)


def head_views(query, key, bias, head):
    lane = lane_of(query.shape)
    mine = (lane >= HDIM) if head else (lane < HDIM)
    spot = 0 if head else HDIM
    zero = jnp.zeros_like(query)
    query_view = jnp.where(mine, query, jnp.where(lane == spot, zero + 1, zero))
    key_view = jnp.where(lane == spot, bias, key)
    return mine, query_view, key_view


def attend_kernel(qkv_ref, bias_ref, mixed_ref, total_ref):
    query = qkv_ref[:, 0:LANES] * jnp.bfloat16(HDIM ** (-0.5))
    key = qkv_ref[:, LANES : 2 * LANES]
    value = qkv_ref[:, 2 * LANES : 3 * LANES]
    bias = bias_ref[...]
    sums, tops = [], []
    for head in range(2):
        mine, query_view, key_view = head_views(query, key, bias, head)
        scores = mat_far(query_view, key_view)
        top = jnp.max(scores, axis=1, keepdims=True)
        weight = jnp.exp(scores - top).astype(LOW)
        value_view = jnp.where(mine, value, jnp.ones_like(value))
        sums.append(jnp.dot(weight, value_view, preferred_element_type=jnp.float32))
        tops.append(top)
    low = lane_of(sums[0].shape) < HDIM
    upper = jnp.where(low, sums[0], sums[1])
    lower = jnp.where(low, sums[1], sums[0])
    lower = pltpu.roll(lower, HDIM, 1)
    mixed_ref[...] = (upper / lower).astype(LOW)
    total = jnp.where(low, tops[0], tops[1]) + jnp.log(lower)
    total = jnp.transpose(total)
    total_ref[0, 0:1, :] = total[0:1]
    total_ref[0, 1:2, :] = total[HDIM : HDIM + 1]


def attend_back_kernel(qkv_ref, bias_ref, grad_ref, mixed_ref, total_ref, out_ref):
    scale = HDIM ** (-0.5)
    query = qkv_ref[:, 0:LANES] * jnp.bfloat16(scale)
    key = qkv_ref[:, LANES : 2 * LANES]
    value = qkv_ref[:, 2 * LANES : 3 * LANES]
    bias = bias_ref[...]
    grad = grad_ref[...]
    product = grad.astype(jnp.float32) * mixed_ref[...].astype(jnp.float32)
    grad_query = grad_key = grad_value = None
    for head in range(2):
        mine, query_view, key_view = head_views(query, key, bias, head)
        zero = jnp.zeros_like(query)
        scores = mat_far(key_view, query_view)
        probs = jnp.exp(scores - total_ref[0, head : head + 1, :])
        grad_view = jnp.where(mine, grad, zero)
        grad_probs = mat_far(value, grad_view)
        ones = jnp.where(mine[0:8], 1.0, 0.0)
        inner = lax.dot_general(
            ones,
            product,
            (((1,), (1,)), ((), ())),
            precision=lax.Precision.HIGHEST,
            preferred_element_type=jnp.float32,
        )
        grad_scores = (probs * (grad_probs - inner[0:1])).astype(LOW)
        one_value = jnp.dot(probs.astype(LOW), grad_view, preferred_element_type=jnp.float32)
        one_key = jnp.dot(
            grad_scores, jnp.where(mine, query, zero), preferred_element_type=jnp.float32
        )
        one_query = mat_rows(grad_scores, jnp.where(mine, key, zero))
        grad_query = one_query if head == 0 else grad_query + one_query
        grad_key = one_key if head == 0 else grad_key + one_key
        grad_value = one_value if head == 0 else grad_value + one_value
    out_ref[:, 0:LANES] = (grad_query * scale).astype(LOW)
    out_ref[:, LANES : 2 * LANES] = grad_key.astype(LOW)
    out_ref[:, 2 * LANES : 3 * LANES] = grad_value.astype(LOW)


def attend_image(image, qkv, bias, given):
    both = qkv.shape[0]
    rows = both // 2
    blocks = qkv.shape[1] // (3 * LANES)

    def kernel(*refs):
        attend_kernel(*refs[:2], *refs[-2:])

    return pl.pallas_call(
        kernel,
        grid=(blocks,),
        in_specs=[
            pl.BlockSpec((rows, 3 * LANES), lambda j: (image, j)),
            pl.BlockSpec((rows, LANES), lambda j: (0, 0)),
        ]
        + [pl.BlockSpec(memory_space=pl.ANY)] * len(given),
        out_specs=[
            pl.BlockSpec((rows, LANES), lambda j: (image, j)),
            pl.BlockSpec((1, 8, rows), lambda j: (image * blocks + j, 0, 0)),
        ],
        out_shape=[
            jax.ShapeDtypeStruct((both, blocks * LANES), LOW),
            jax.ShapeDtypeStruct((2 * blocks, 8, rows), jnp.float32),
        ],
        input_output_aliases={2: 0, 3: 1} if given else {},
        compiler_params=pltpu.CompilerParams(vmem_limit_bytes=VMEM_ROOM),
        cost_estimate=pl.CostEstimate(
            flops=blocks * 2 * 2 * 2 * rows * rows * LANES * 2,
            transcendentals=blocks * 2 * rows * rows,
            bytes_accessed=rows * blocks * LANES * 8,
        ),
    )(qkv, bias, *given)


def attend_back_image(image, qkv, bias, grad, mixed, total, given):
    both = qkv.shape[0]
    rows = both // 2
    blocks = qkv.shape[1] // (3 * LANES)

    def kernel(*refs):
        attend_back_kernel(*refs[:5], refs[-1])

    return pl.pallas_call(
        kernel,
        grid=(blocks,),
        in_specs=[
            pl.BlockSpec((rows, 3 * LANES), lambda j: (image, j)),
            pl.BlockSpec((rows, LANES), lambda j: (0, 0)),
            pl.BlockSpec((rows, LANES), lambda j: (0, j)),
            pl.BlockSpec((rows, LANES), lambda j: (image, j)),
            pl.BlockSpec((1, 8, rows), lambda j: (image * blocks + j, 0, 0)),
        ]
        + [pl.BlockSpec(memory_space=pl.ANY)] * len(given),
        out_specs=pl.BlockSpec((rows, 3 * LANES), lambda j: (image, j)),
        out_shape=jax.ShapeDtypeStruct(qkv.shape, LOW),
        input_output_aliases={5: 0} if given else {},
        compiler_params=pltpu.CompilerParams(vmem_limit_bytes=VMEM_ROOM),
        cost_estimate=pl.CostEstimate(
            flops=blocks * 2 * 5 * 2 * rows * rows * LANES * 2,
            transcendentals=blocks * 2 * rows * rows,
            bytes_accessed=rows * blocks * LANES * 16,
        ),
    )(qkv, bias, grad, mixed, total, *given)


def flat_norm(values, gain, shift):
    center = values - jnp.mean(values, axis=-1, keepdims=True)
    spread = lax.rsqrt(jnp.mean(center * center, axis=-1, keepdims=True) + EPS)
    unit = center * spread
    return unit * gain + shift, unit, spread


def flat_norm_back(upstream, unit, spread, gain):
    scaled = upstream * gain
    inner = (
        scaled
        - jnp.mean(scaled, axis=-1, keepdims=True)
        - unit * jnp.mean(scaled * unit, axis=-1, keepdims=True)
    )
    return spread * inner, jnp.sum(upstream * unit, axis=0), jnp.sum(upstream, axis=0)


def column_flat(values):
    return jnp.sum(values.astype(jnp.float32), axis=0)


def whole_images(
    images,
    cotangent,
    slot_live,
    first_gain,
    first_shift,
    query_weight,
    query_bias,
    key_weight,
    value_weight,
    value_bias,
    output_weight,
    output_bias,
    second_gain,
    second_shift,
    up_weight,
    up_bias,
    down_weight,
    down_bias,
):
    dp_place = lax.axis_index("dp")
    place_y = lax.axis_index("tensor")
    core, place_x, place_z = dp_place % 2, (dp_place // 2) % 2, dp_place // 4
    places = jnp.stack([place_z, place_x, core, place_y]).astype(jnp.int32)
    strip, width = images.shape[1:]
    half = -(-strip // HALF_PAD) * HALF_PAD
    rows = 2 * half
    depth, head_cols = query_weight.shape
    units = up_weight.shape[1]

    def columns_of(weights, place):
        return [
            lax.dynamic_slice_in_dim(
                weight, place * (weight.shape[1] // 2), weight.shape[1] // 2, 1
            )
            for weight in weights
        ]

    def core_parts(weights, place):
        cuts = columns_of(weights, place)
        parts = []
        for part in range(2):
            spans = [cut.shape[1] // 2 for cut in cuts]
            parts.append(
                jnp.concatenate(
                    [cut[:, part * span : (part + 1) * span] for cut, span in zip(cuts, spans)], 1
                )
            )
        return jnp.stack(parts)

    feeds = [up_weight, down_weight.T]
    feed_keep = jnp.concatenate(columns_of(feeds, core), 1)
    feed_send = jnp.concatenate(columns_of(feeds, 1 - core), 1)
    feed = pick_two(core, feed_keep, exchange(feed_send, far_core=1), 0)
    groups = [[place for place in range(32) if (place // 2) % 2 == at] for at in range(2)]

    gathered = lax.all_gather(
        feed.reshape(2 * depth, -1), BOTH, axis=0, tiled=True, axis_index_groups=groups
    ).reshape(8, 2, 2 * depth, -1)
    gathered = pltpu.with_memory_space_constraint(gathered, pltpu.HBM)

    heads = [query_weight, key_weight, value_weight, output_weight.T]
    piece_one = gather_piece(core_parts(heads, core), core_parts(heads, 1 - core), core)
    others_one = scatter_z([None, piece_one, piece_one, piece_one])

    padding = ((0, 0), (0, half - strip), (0, 0))

    def own_and_far(slots, *waits):
        slots = jnp.pad(slots, padding)
        mine = lax.dynamic_index_in_dim(slots, place_y, 0, keepdims=False)
        theirs = lax.dynamic_index_in_dim(slots, 1 - place_y, 0, keepdims=False)
        return mine, exchange(after(theirs, *waits), far_y=1)

    image_mine, image_far = own_and_far(images, piece_one)
    grad_mine, grad_far = own_and_far(cotangent, piece_one)
    line_one = gather_line(piece_one, others_one, places)
    cross_one = exchange(line_one[0], far_x=1), exchange(line_one[1], far_y=1)
    pair_one = gather_pairs(places, *line_one, *cross_one)
    image_far, grad_far = after((image_far, grad_far), *pair_one)
    whole = jnp.concatenate([image_mine, image_far], 0)

    def head_columns(vector):
        table = vector.astype(jnp.float32).reshape(2, 2, 2, -1)
        table = lax.dynamic_index_in_dim(table, core, 1, keepdims=False)
        table = jnp.where(place_y == 0, table, table[::-1])
        return table.transpose(1, 0, 2).reshape(4, 1, -1)

    def spread_core(table):
        table = jnp.stack(
            [jnp.where(core == 0, table, 0.0), jnp.where(core == 1, table, 0.0)], 1
        )
        return table.reshape(-1)

    def head_spread(vector):
        table = vector.reshape(2, 2, -1).transpose(1, 0, 2)
        return spread_core(jnp.where(place_y == 0, table, table[::-1]))

    gain_one, shift_one = first_gain.astype(jnp.float32), first_shift.astype(jnp.float32)
    gain_two, shift_two = second_gain.astype(jnp.float32), second_shift.astype(jnp.float32)
    query_shift, value_shift = head_columns(query_bias), head_columns(value_bias)
    qkv_shift = jnp.concatenate(
        [query_shift, jnp.zeros_like(query_shift), value_shift], 1
    ).reshape(-1)
    up_shift = head_columns(up_bias).reshape(1, -1)

    row = jnp.arange(rows)
    in_half = row % half
    spot = jnp.where(row < half, place_y, 1 - place_y) * strip + in_half
    ok = (in_half < strip) & (spot < VALID)
    live = lax.dynamic_index_in_dim(slot_live, place_y, 0, keepdims=False).astype(jnp.float32)
    row_mask = (live * ok.astype(jnp.float32))[:, None]
    key_bias = jnp.broadcast_to(
        jnp.where(ok, 0.0, NEGATIVE).astype(LOW)[:, None], (rows, LANES)
    )

    resid = whole.astype(jnp.float32)

    def full_columns(owned):
        return owned.transpose(2, 0, 1, 3).reshape(depth, -1)

    def pair_of(own):
        return own, exchange(own, far_core=1)

    normed, unit_one, spread_one = flat_norm(resid, gain_one, shift_one)
    normed_pair = pair_of(normed.astype(LOW))

    normed_turned = turn(places, normed_pair)
    grad_top = row_mask * jnp.concatenate([grad_mine, grad_far], 0).astype(jnp.float32)
    fed_grad = grad_top.astype(LOW)
    fed_pair = pair_of(fed_grad)
    fed_turned = turn(places, fed_pair)
    last_one = exchange(pair_one[0], far_y=1), exchange(pair_one[1], far_x=1)
    qkv_full, output_full = gather_all(after(places, normed_turned, fed_turned), *pair_one, *last_one, 3 * head_cols // 4)

    normed_rows = jnp.concatenate(normed_pair, 0)
    qkv = (mat(normed_rows, qkv_full) + qkv_shift).astype(LOW)
    mixed_half = attend_image(1, qkv, key_bias, [])
    mixed_far = mat_far(mixed_half[0][rows:], output_full).astype(LOW)
    mixed_sum = exchange(mixed_far, far_core=1)
    mixed, totals = attend_image(0, qkv, key_bias, list(after(tuple(mixed_half), mixed_far)))
    attended = mat_far(mixed[:rows], output_full) + mixed_sum.astype(jnp.float32)
    attended = attended + output_bias.astype(jnp.float32)
    middle = row_mask * (resid + attended)
    second, unit_two, spread_two = flat_norm(middle, gain_two, shift_two)
    second_pair = pair_of(second.astype(LOW))
    second_turned = turn(places, second_pair)
    up_pair = after(second_pair, second_turned)
    active, slope = up_call(places, up_pair, gathered, up_shift)

    lower_sends = weight_pieces([(fed_turned, active)], True)
    lower_first = scatter_first(lower_sends)
    lower_keeps = weight_pieces([(fed_turned, after(active, *lower_sends))], False)
    fed_late = after(fed_pair, *lower_keeps)
    hidden_grad, up_bias_sums = hidden_call(places, fed_late, gathered, slope)
    up_sends = weight_pieces([(second_turned, hidden_grad)], True)
    up_first = scatter_first(up_sends)
    lower_first = after(lower_first, *up_sends)
    lower_second = scatter_second(scatter_adds(lower_keeps, lower_first))
    hidden_late = after(hidden_grad, *lower_first)
    second_grad, second_send = down_call(places, hidden_late, gathered, 0)
    second_grad = second_grad + exchange(second_send, far_core=1).astype(jnp.float32)
    middle_back, gain_two_grad, shift_two_grad = flat_norm_back(
        second_grad, unit_two, spread_two, gain_two
    )
    middle_grad = row_mask * (grad_top + middle_back)
    attended_grad = middle_grad.astype(LOW)
    attended_pair = pair_of(attended_grad)
    grad_mixed = mat(attended_pair[0], output_full).astype(LOW)
    back = attend_back_image(0, qkv, key_bias, grad_mixed, mixed, totals, [])
    up_keeps = weight_pieces([(second_turned, after(hidden_late, back))], False)
    up_first = after(up_first, back)
    up_adds = scatter_adds(up_keeps, up_first)
    up_second = scatter_second(up_adds)
    lower_second = after(lower_second, back, *up_keeps)
    lower_line = scatter_line(lower_keeps, lower_first, lower_second)
    lower_z = scatter_z(lower_line)
    attended_turned = turn(places, attended_pair)
    grad_mixed = mat(attended_pair[1], output_full).astype(LOW)
    grad_mixed = after(grad_mixed, *up_adds, *lower_line, attended_turned)
    back = attend_back_image(1, qkv, key_bias, grad_mixed, mixed, totals, [back])
    up_second, lower_z = after((up_second, tuple(lower_z)), back)
    up_line = scatter_line(up_keeps, up_first, up_second)
    up_z = scatter_z(up_line)
    back = after(back, *up_line)
    last_sends = weight_pieces(
        [(normed_turned, back), (attended_turned, mixed)], True, SMALL
    )
    last_first = scatter_first(last_sends)
    back_late = after(back, *last_sends)
    last_keeps = weight_pieces(
        [(normed_turned, back_late), (attended_turned, mixed)], False, SMALL
    )
    fed, fed_send = down_call(places, after(active, *last_keeps), gathered, 1)
    back_late = after(back_late, fed, fed_send, *up_z)
    normed_send = mat_far(back_late[rows:], qkv_full).astype(LOW)
    last_first = after(last_first, normed_send)
    last_adds = scatter_adds(last_keeps, last_first)
    last_second = scatter_second(last_adds)
    back_late = after(back_late, *last_adds)
    normed_far = exchange(normed_send, far_core=1)
    fed = fed + exchange(fed_send, far_core=1).astype(jnp.float32)
    layer_own = (row_mask * (middle + fed + down_bias.astype(jnp.float32))).astype(LOW)
    normed_grad = mat_far(back_late[:rows], qkv_full) + normed_far.astype(jnp.float32)
    first_back, gain_one_grad, shift_one_grad = flat_norm_back(
        normed_grad, unit_one, spread_one, gain_one
    )
    images_own = middle_grad + first_back
    qkv_sums = column_flat(back_late).reshape(4, 3, -1)
    vector = jnp.concatenate(
        [
            column_flat(attended_grad),
            gain_two_grad,
            shift_two_grad,
            column_flat(fed_grad),
            head_spread(up_bias_sums.reshape(-1)),
            gain_one_grad,
            shift_one_grad,
            head_spread(qkv_sums[:, 0].reshape(-1)),
            head_spread(qkv_sums[:, 2].reshape(-1)),
        ]
    )
    vector, vectors = vector_first(vector)
    last_line = scatter_line(last_keeps, last_first, after(last_second, images_own))
    last_z = scatter_z(last_line)
    images_far = exchange(
        after(images_own, *last_second)[half : half + strip].astype(LOW), far_y=1
    )
    layer_far = exchange(after(layer_own, *last_adds)[half : half + strip], far_y=1)
    vector = vector + vectors[0] + vectors[1] + vectors[2]
    vector = vector + after(exchange(vector, far_x=1), images_far, *last_line)
    vector = vector + after(exchange(vector, far_y=1), layer_far)
    lower_z, up_z = after((tuple(lower_z), tuple(up_z)), *last_line, images_far)
    lower_owned = full_columns(scatter_last(lower_line[0], lower_z, core)).T
    upper_owned = full_columns(scatter_last(up_line[0], up_z, core))

    def to_strips(own, far):
        return pick_two(place_y, own[:strip], far, 1).transpose(1, 0, 2)

    layer_out = to_strips(layer_own, layer_far)
    images_grad = to_strips(after(images_own, *last_line), images_far.astype(jnp.float32))
    last_z = after(tuple(last_z), vector, layer_out, images_grad, lower_owned, upper_owned)
    last_owned = scatter_last(last_line[0], last_z, core)
    def head_grad(at):
        return full_columns(last_owned[..., at * LANES : (at + 1) * LANES])

    early, late = vector[: 4 * width + up_bias.shape[0]], vector[4 * width + up_bias.shape[0] :]
    return (
        layer_out,
        images_grad,
        late[:width],
        late[width : 2 * width],
        head_grad(0),
        late[2 * width : 3 * width],
        head_grad(1),
        head_grad(2),
        late[3 * width :],
        head_grad(3).T,
        early[:width],
        early[width : 2 * width],
        early[2 * width : 3 * width],
        upper_owned,
        early[4 * width :],
        lower_owned,
        early[3 * width : 4 * width],
    )


def pick(mesh):
    sizes = dict(mesh.shape)
    if sizes["dp"] == 16 and sizes["tensor"] == 2:
        return whole_images
    return local


def solution(mesh):
    in_specs = (
        P("dp", "tensor", None),
        P("dp", "tensor", None),
        P("dp"),
        P(),
        P(),
        P("dp", "tensor"),
        P(),
        P("dp", "tensor"),
        P("dp", "tensor"),
        P(),
        P("tensor", "dp"),
        P(),
        P(),
        P(),
        P("dp", "tensor"),
        P(),
        P("tensor", "dp"),
        P(),
    )
    out_specs = (
        P("dp", "tensor", None),
        P("dp", "tensor", None),
        P(),
        P(),
        P("dp", "tensor"),
        P(),
        P("dp", "tensor"),
        P("dp", "tensor"),
        P(),
        P("tensor", "dp"),
        P(),
        P(),
        P(),
        P("dp", "tensor"),
        P(),
        P("tensor", "dp"),
        P(),
    )
    return jax.shard_map(pick(mesh), mesh=mesh, in_specs=in_specs, out_specs=out_specs, check_vma=False)
```

```python
import jax
import jax.numpy as jnp
from jax import lax
from jax.experimental import pallas as pl
from jax.experimental.pallas import tpu as pltpu
from jax.sharding import PartitionSpec as P

HDIM = 64
VALID = 577


EPS = 1e-05
NEGATIVE = -1e30
SLOPE = 1.702


def layer_norm(values, gain, shift):
    center = values - jnp.mean(values, axis=-1, keepdims=True)
    spread = lax.rsqrt(jnp.mean(center * center, axis=-1, keepdims=True) + EPS)
    unit = center * spread
    return (unit * gain + shift, unit, spread)


def norm_back(upstream, unit, spread, gain):
    scaled = upstream * gain
    inner = (
        scaled
        - jnp.mean(scaled, axis=-1, keepdims=True)
        - unit * jnp.mean(scaled * unit, axis=-1, keepdims=True)
    )
    return (spread * inner, jnp.sum(upstream * unit, axis=(0, 1)), jnp.sum(upstream, axis=(0, 1)))


def dense(left, right):
    return jnp.einsum("spa,ab->spb", left, right, preferred_element_type=jnp.float32)


def project_back(left, right):
    return jnp.einsum("spa,ba->spb", left, right, preferred_element_type=jnp.float32)


def outer(left, right):
    return jnp.einsum("spa,spb->ab", left, right, preferred_element_type=jnp.float32)


def column_sum(values):
    return jnp.sum(values.astype(jnp.float32), axis=(0, 1))


def widen(piece, length, start):
    return lax.dynamic_update_slice_in_dim(jnp.zeros((length,), jnp.float32), piece, start, 0)


def split_heads(block):
    return block.reshape(block.shape[0], -1, HDIM)


def scores_of(query, key, key_ok):
    raw = jnp.einsum(
        "qhe,khe->hqk", split_heads(query), split_heads(key), preferred_element_type=jnp.float32
    )
    return jnp.where(key_ok[None, None, :], raw * HDIM ** (-0.5), NEGATIVE)


def attend(query, key, value, key_ok):
    scores = scores_of(query, key, key_ok)
    top = jnp.max(scores, axis=-1, keepdims=True)
    total = top + jnp.log(jnp.sum(jnp.exp(scores - top), axis=-1, keepdims=True))
    probs = jnp.exp(scores - total).astype(jnp.bfloat16)
    mixed = jnp.einsum(
        "hqk,khe->qhe", probs, split_heads(value), preferred_element_type=jnp.float32
    )
    return (mixed.reshape(query.shape[0], -1).astype(jnp.bfloat16), total)


def attend_back(query, key, value, grad_mixed, total, key_ok):
    scores = scores_of(query, key, key_ok)
    probs = jnp.exp(scores - total)
    grad_heads = split_heads(grad_mixed)
    grad_probs = jnp.einsum(
        "qhe,khe->hqk", grad_heads, split_heads(value), preferred_element_type=jnp.float32
    )
    grad_value = jnp.einsum(
        "hqk,qhe->khe", probs.astype(jnp.bfloat16), grad_heads, preferred_element_type=jnp.float32
    )
    grad_scores = (
        probs * (grad_probs - jnp.sum(probs * grad_probs, axis=-1, keepdims=True))
    ).astype(jnp.bfloat16)
    grad_query = jnp.einsum(
        "hqk,khe->qhe", grad_scores, split_heads(key), preferred_element_type=jnp.float32
    ) * HDIM ** (-0.5)
    grad_key = jnp.einsum(
        "hqk,qhe->khe", grad_scores, split_heads(query), preferred_element_type=jnp.float32
    ) * HDIM ** (-0.5)
    length = query.shape[0]
    return (
        grad_query.reshape(length, -1).astype(jnp.bfloat16),
        grad_key.reshape(length, -1).astype(jnp.bfloat16),
        grad_value.reshape(length, -1).astype(jnp.bfloat16),
    )


def local(
    images,
    cotangent,
    slot_live,
    first_gain,
    first_shift,
    query_weight,
    query_bias,
    key_weight,
    value_weight,
    value_bias,
    output_weight,
    output_bias,
    second_gain,
    second_shift,
    up_weight,
    up_bias,
    down_weight,
    down_bias,
):
    slots, strip, width = images.shape
    tensor_count = lax.axis_size("tensor")
    tensor_place = lax.axis_index("tensor")
    seq_len = strip * tensor_count
    positions = tensor_place * strip + jnp.arange(strip)
    row_mask = (
        slot_live.astype(jnp.float32)[:, None, None]
        * (positions < VALID).astype(jnp.float32)[None, :, None]
    )
    key_ok = jnp.arange(seq_len) < VALID
    query_full, key_full, value_full, upper_full, output_full, lower_full = (
        lax.all_gather(query_weight, "dp", axis=0, tiled=True),
        lax.all_gather(key_weight, "dp", axis=0, tiled=True),
        lax.all_gather(value_weight, "dp", axis=0, tiled=True),
        lax.all_gather(up_weight, "dp", axis=0, tiled=True),
        lax.all_gather(output_weight, "dp", axis=1, tiled=True),
        lax.all_gather(down_weight, "dp", axis=1, tiled=True),
    )
    head_cols = query_full.shape[1]
    head_start = tensor_place * head_cols
    gain_one = first_gain.astype(jnp.float32)
    shift_one = first_shift.astype(jnp.float32)
    gain_two = second_gain.astype(jnp.float32)
    shift_two = second_shift.astype(jnp.float32)
    query_shift = lax.dynamic_slice_in_dim(query_bias.astype(jnp.float32), head_start, head_cols)
    value_shift = lax.dynamic_slice_in_dim(value_bias.astype(jnp.float32), head_start, head_cols)
    resid = images.astype(jnp.float32)
    normed, unit_one, spread_one = layer_norm(resid, gain_one, shift_one)
    normed_rows = lax.all_gather(normed.astype(jnp.bfloat16), "tensor", axis=1, tiled=True)
    queries = (dense(normed_rows, query_full) + query_shift).astype(jnp.bfloat16)
    keys_low = dense(normed_rows, key_full).astype(jnp.bfloat16)
    values_low = (dense(normed_rows, value_full) + value_shift).astype(jnp.bfloat16)
    mixed, totals = lax.map(
        lambda items: attend(items[0], items[1], items[2], key_ok), (queries, keys_low, values_low)
    )
    attended = lax.psum_scatter(
        dense(mixed, output_full), "tensor", scatter_dimension=1, tiled=True
    ) + output_bias.astype(jnp.float32)
    middle = row_mask * (resid + attended)
    second, unit_two, spread_two = layer_norm(middle, gain_two, shift_two)
    second_low = second.astype(jnp.bfloat16)
    grad_top = row_mask * cotangent.astype(jnp.float32)
    fed_grad = grad_top.astype(jnp.bfloat16)
    down_shift = down_bias.astype(jnp.float32)
    units = upper_full.shape[1]
    second_rows = lax.all_gather(second_low, "tensor", axis=1, tiled=True)
    up_shift = lax.dynamic_slice_in_dim(up_bias.astype(jnp.float32), tensor_place * units, units)
    hidden = dense(second_rows, upper_full) + up_shift
    sigma = jax.nn.sigmoid(SLOPE * hidden)
    active = (hidden * sigma).astype(jnp.bfloat16)
    fed = (
        lax.psum_scatter(
            dense(active, lower_full).astype(jnp.bfloat16),
            "tensor",
            scatter_dimension=1,
            tiled=True,
        ).astype(jnp.float32)
        + down_shift
    )
    fed_rows = lax.all_gather(fed_grad, "tensor", axis=1, tiled=True)
    grad_active = project_back(fed_rows, lower_full)
    lower_grad = outer(active, fed_rows)
    hidden_grad = (grad_active * (sigma + SLOPE * hidden * sigma * (1.0 - sigma))).astype(
        jnp.bfloat16
    )
    upper_grad = outer(second_rows, hidden_grad)
    up_bias_grad = widen(column_sum(hidden_grad), up_bias.shape[0], tensor_place * units)
    second_grad = lax.psum_scatter(
        project_back(hidden_grad, upper_full), "tensor", scatter_dimension=1, tiled=True
    )
    layer_out = (row_mask * (middle + fed)).astype(jnp.bfloat16)
    down_bias_grad = column_sum(fed_grad)
    middle_back, gain_two_grad, shift_two_grad = norm_back(
        second_grad, unit_two, spread_two, gain_two
    )
    middle_grad = row_mask * (grad_top + middle_back)
    attended_grad = middle_grad.astype(jnp.bfloat16)
    output_bias_grad = column_sum(attended_grad)
    attended_rows = lax.all_gather(attended_grad, "tensor", axis=1, tiled=True)
    grad_mixed = project_back(attended_rows, output_full).astype(jnp.bfloat16)
    output_grad = outer(mixed, attended_rows)
    grad_query, grad_key, grad_value = lax.map(
        lambda items: attend_back(items[0], items[1], items[2], items[3], items[4], key_ok),
        (queries, keys_low, values_low, grad_mixed, totals),
    )
    query_grad = outer(normed_rows, grad_query)
    key_grad = outer(normed_rows, grad_key)
    value_grad = outer(normed_rows, grad_value)
    query_bias_grad = widen(column_sum(grad_query), width, head_start)
    value_bias_grad = widen(column_sum(grad_value), width, head_start)
    normed_terms = (
        project_back(grad_query, query_full)
        + project_back(grad_key, key_full)
        + project_back(grad_value, value_full)
    )
    normed_grad = lax.psum_scatter(
        normed_terms.astype(jnp.bfloat16), "tensor", scatter_dimension=1, tiled=True
    ).astype(jnp.float32)
    first_back, gain_one_grad, shift_one_grad = norm_back(
        normed_grad, unit_one, spread_one, gain_one
    )
    images_grad = middle_grad + first_back
    query_owned, key_owned, value_owned, upper_owned, output_owned, lower_owned = (
        lax.psum_scatter(
            query_grad.astype(jnp.bfloat16), "dp", scatter_dimension=0, tiled=True
        ).astype(jnp.float32),
        lax.psum_scatter(
            key_grad.astype(jnp.bfloat16), "dp", scatter_dimension=0, tiled=True
        ).astype(jnp.float32),
        lax.psum_scatter(
            value_grad.astype(jnp.bfloat16), "dp", scatter_dimension=0, tiled=True
        ).astype(jnp.float32),
        lax.psum_scatter(
            upper_grad.astype(jnp.bfloat16), "dp", scatter_dimension=0, tiled=True
        ).astype(jnp.float32),
        lax.psum_scatter(
            output_grad.astype(jnp.bfloat16), "dp", scatter_dimension=1, tiled=True
        ).astype(jnp.float32),
        lax.psum_scatter(
            lower_grad.astype(jnp.bfloat16), "dp", scatter_dimension=1, tiled=True
        ).astype(jnp.float32),
    )
    vector_sums = lax.psum(
        (
            gain_one_grad,
            shift_one_grad,
            query_bias_grad,
            value_bias_grad,
            output_bias_grad,
            gain_two_grad,
            shift_two_grad,
            up_bias_grad,
            down_bias_grad,
        ),
        ("dp", "tensor"),
    )
    (
        gain_one_total,
        shift_one_total,
        query_bias_total,
        value_bias_total,
        output_bias_total,
        gain_two_total,
        shift_two_total,
        up_bias_total,
        down_bias_total,
    ) = vector_sums
    return (
        layer_out,
        images_grad,
        gain_one_total,
        shift_one_total,
        query_owned,
        query_bias_total,
        key_owned,
        value_owned,
        value_bias_total,
        output_owned,
        output_bias_total,
        gain_two_total,
        shift_two_total,
        upper_owned,
        up_bias_total,
        lower_owned,
        down_bias_total,
    )


BOTH = ("dp", "tensor")
HALF_PAD = 8
LANES = 128
LOW = jnp.bfloat16
VMEM_ROOM = 24 * 2**20
SMALL = pl.CostEstimate(flops=1024, transcendentals=0, bytes_accessed=1024)


def exchange(value, far_z=0, far_x=0, far_core=0, far_y=0):
    pairs = []
    for place in range(32):
        other = place ^ (far_z * 8 + far_x * 4 + far_core * 2 + far_y)
        pairs.append((place, other))
    return lax.ppermute(value, BOTH, pairs)


def pick_two(bit, own, other, axis):
    first = jnp.where(bit == 0, own, other)
    last = jnp.where(bit == 0, other, own)
    return jnp.stack([first, last], axis)


def after(value, *others):
    return lax.optimization_barrier((value, *others))[0]


def pack(places, sources, shapes, plan):
    def kernel(places_ref, *refs):
        ins, outs = refs[: len(sources)], refs[len(sources) :]
        spots = [places_ref[at] for at in range(4)]
        for at, take, to, put in plan:
            outs[to][put(*spots)] = ins[at][take(*spots)]

    return pl.pallas_call(
        kernel,
        in_specs=[pl.BlockSpec(memory_space=pltpu.SMEM)]
        + [pl.BlockSpec(memory_space=pltpu.VMEM)] * len(sources),
        out_specs=[pl.BlockSpec(memory_space=pltpu.VMEM)] * len(shapes),
        out_shape=[jax.ShapeDtypeStruct(shape, LOW) for shape in shapes],
        compiler_params=pltpu.CompilerParams(vmem_limit_bytes=VMEM_ROOM),
        cost_estimate=pl.CostEstimate(
            flops=0,
            transcendentals=0,
            bytes_accessed=sum(2 * source.size * 2 for source in sources),
        ),
    )(places, *sources)


def gather_piece(keep, send, core):
    deep, wide = keep.shape[1:]
    return pick_two(core, keep, exchange(send, far_core=1), 1).reshape(2, 2 * deep, wide)


def gather_line(piece, others, places):
    rows, wide = piece.shape[1:]
    line = [piece] + others
    plan = []
    for step in range(4):
        for part in range(2):
            plan.append(
                (
                    step,
                    lambda z, x, c, y, part=part: part,
                    part,
                    lambda z, x, c, y, step=step: z ^ step,
                )
            )
    return pack(places, line, [(4, rows, wide)] * 2, plan)


def gather_pairs(places, one, two, one_x, two_y):
    every = slice(None)
    plan = [
        (0, lambda z, x, c, y: every, 0, lambda z, x, c, y: x),
        (1, lambda z, x, c, y: every, 0, lambda z, x, c, y: 1 - x),
        (2, lambda z, x, c, y: every, 1, lambda z, x, c, y: 0),
        (3, lambda z, x, c, y: every, 1, lambda z, x, c, y: 1),
    ]
    return pack(places, [one, one_x, two, two_y], [(2,) + one.shape] * 2, plan)


def gather_all(places, one_pair, two_pair, one_y, two_x, most):
    every = slice(None)
    rows, wide = one_pair.shape[2:]
    plan = []
    for to, low, high in ((0, 0, most), (1, most, wide)):
        span = high - low
        for place_z in range(4):
            for far in range(2):
                for number in range(2):
                    plan.append(
                        (
                            number,
                            lambda z, x, c, y, a=far, p=place_z, lo=low, hi=high: (
                                a,
                                p,
                                every,
                                slice(lo, hi),
                            ),
                            to,
                            lambda z, x, c, y, a=far, p=place_z, n=number, s=span: (
                                p,
                                a,
                                every,
                                slice(n * s, n * s + s),
                            ),
                        )
                    )
                    plan.append(
                        (
                            2 + far,
                            lambda z, x, c, y, n=number, p=place_z, lo=low, hi=high: (
                                n,
                                p,
                                every,
                                slice(lo, hi),
                            ),
                            to,
                            lambda z, x, c, y, f=far, p=place_z, n=number, s=span: (
                                p,
                                x ^ f,
                                every,
                                slice((2 + n) * s, (3 + n) * s),
                            ),
                        )
                    )
    shapes = [(4, 2, rows, 4 * most), (4, 2, rows, 4 * (wide - most))]
    made = pack(places, [one_pair, one_y, two_pair, two_x], shapes, plan)
    return [array.reshape(8 * rows, -1) for array in made]


def low_add(*values):
    total = values[0].astype(jnp.float32)
    for value in values[1:]:
        total = total + value.astype(jnp.float32)
    return total


def line_kernel(one_ref, one_a, one_b, two_ref, two_a, two_b, own_ref, *send_refs):
    tall = own_ref.shape[1]
    for step in range(4):
        rows = slice(step * tall, (step + 1) * tall)
        one = low_add(one_ref[0, rows], one_a[0, rows], one_b[rows])
        two = low_add(two_ref[0, rows], two_a[0, rows], two_b[rows])
        if step == 0:
            own_ref[0] = one
            own_ref[1] = two
        else:
            send_refs[step - 1][0] = one.astype(LOW)
            send_refs[step - 1][1] = two.astype(LOW)


def scatter_first(sends):
    return exchange(sends[0], far_y=1), exchange(sends[1], far_x=1)


def scatter_adds(keeps, arrived):
    return [low_add(keeps[at][1], arrived[at][1]).astype(LOW) for at in range(2)]


def scatter_second(adds):
    return exchange(adds[0], far_x=1), exchange(adds[1], far_y=1)


def scatter_line(keeps, arrived, crossed):
    lines, wide = crossed[0].shape
    tall = lines // 4
    first = pl.BlockSpec((1, lines, wide), lambda i: (0, 0, 0))
    flat = pl.BlockSpec((lines, wide), lambda i: (0, 0))
    piece = pl.BlockSpec((2, tall, wide), lambda i: (0, 0, 0))
    return pl.pallas_call(
        line_kernel,
        grid=(1,),
        in_specs=[first, first, flat, first, first, flat],
        out_specs=[piece] * 4,
        out_shape=[jax.ShapeDtypeStruct((2, tall, wide), jnp.float32)]
        + [jax.ShapeDtypeStruct((2, tall, wide), LOW)] * 3,
        compiler_params=pltpu.CompilerParams(vmem_limit_bytes=VMEM_ROOM),
        cost_estimate=pl.CostEstimate(
            flops=lines * wide * 4, transcendentals=0, bytes_accessed=lines * wide * 18
        ),
    )(keeps[0], arrived[0], crossed[0], keeps[1], arrived[1], crossed[1])


def scatter_z(sends):
    return [exchange(sends[step], far_z=step) for step in (1, 2, 3)]


def scatter_last(own, others, core):
    tall, wide = own.shape[1:]
    total = low_add(own, *others).reshape(2, 2, tall // 2, wide)
    keep = lax.dynamic_index_in_dim(total, core, 1, keepdims=False)
    send = lax.dynamic_index_in_dim(total, 1 - core, 1, keepdims=False)
    far = exchange(send.astype(LOW), far_core=1).astype(jnp.float32)
    return pick_two(core, keep, far, 0)


def vector_first(vector):
    vector = vector + exchange(vector, far_core=1)
    return vector, [exchange(vector, far_z=step) for step in (1, 2, 3)]


def mat_far(left, right):
    return lax.dot_general(
        left, right, (((1,), (1,)), ((), ())), preferred_element_type=jnp.float32
    )


def mat_rows(left, right):
    return lax.dot_general(
        left, right, (((0,), (0,)), ((), ())), preferred_element_type=jnp.float32
    )


def fill_rows(made_ref, own_ref, far_ref):
    rows = own_ref.shape[0]

    @pl.when(pl.program_id(0) == 0)
    def _():
        made_ref[:rows] = own_ref[...]
        made_ref[rows:] = far_ref[...]


def up_kernel(
    places_ref, own_ref, far_ref, right_ref, shift_ref, active_ref, slope_ref, left_ref
):
    fill_rows(left_ref, own_ref, far_ref)
    right = right_ref[...].reshape(left_ref.shape[1], -1)
    hidden = jnp.dot(left_ref[...], right, preferred_element_type=jnp.float32)
    hidden = hidden + shift_ref[...]
    sigma = 0.5 * jnp.tanh((0.5 * SLOPE) * hidden) + 0.5
    active = hidden * sigma
    active_ref[...] = active.astype(LOW)
    slope_ref[...] = (sigma + SLOPE * active * (1.0 - sigma)).astype(LOW)


def feed_spec(gathered, start):
    lines, _, rows, wide = gathered.shape
    return pl.BlockSpec(
        (lines, 1, rows, wide // 4), lambda i, s: (0, s[3] ^ (i % 2), 0, start + i // 2)
    )


def up_call(places, pair, gathered, shift):
    rows, width = pair[0].shape
    wide = shift.shape[1] // 4
    whole = pl.BlockSpec((rows, width), lambda i, s: (0, 0))
    piece = pl.BlockSpec((2 * rows, wide), lambda i, s: (0, i))
    return pl.pallas_call(
        up_kernel,
        grid_spec=pltpu.PrefetchScalarGridSpec(
            num_scalar_prefetch=1,
            grid=(4,),
            in_specs=[
                whole,
                whole,
                feed_spec(gathered, 0),
                pl.BlockSpec((1, wide), lambda i, s: (0, i)),
            ],
            out_specs=[piece, piece],
            scratch_shapes=[pltpu.VMEM((2 * rows, width), LOW)],
        ),
        out_shape=[jax.ShapeDtypeStruct((2 * rows, 4 * wide), LOW)] * 2,
        compiler_params=pltpu.CompilerParams(vmem_limit_bytes=VMEM_ROOM),
        cost_estimate=pl.CostEstimate(
            flops=16 * rows * wide * width,
            transcendentals=8 * rows * wide,
            bytes_accessed=rows * width * 4 + 8 * width * wide + 32 * rows * wide,
        ),
    )(places, *pair, gathered, shift)


def hidden_kernel(
    places_ref, own_ref, far_ref, right_ref, slope_ref, out_ref, sum_ref, left_ref
):
    fill_rows(left_ref, own_ref, far_ref)
    right = right_ref[...].reshape(left_ref.shape[1], -1)
    grad = jnp.dot(left_ref[...], right, preferred_element_type=jnp.float32)
    grad = (grad * slope_ref[...].astype(jnp.float32)).astype(LOW)
    out_ref[...] = grad
    sum_ref[...] = jnp.sum(grad.astype(jnp.float32), axis=0, keepdims=True)


def hidden_call(places, pair, gathered, slope):
    rows, width = pair[0].shape
    wide = slope.shape[1] // 4
    whole = pl.BlockSpec((rows, width), lambda i, s: (0, 0))
    piece = pl.BlockSpec((2 * rows, wide), lambda i, s: (0, i))
    return pl.pallas_call(
        hidden_kernel,
        grid_spec=pltpu.PrefetchScalarGridSpec(
            num_scalar_prefetch=1,
            grid=(4,),
            in_specs=[whole, whole, feed_spec(gathered, 2), piece],
            out_specs=[piece, pl.BlockSpec((1, wide), lambda i, s: (0, i))],
            scratch_shapes=[pltpu.VMEM((2 * rows, width), LOW)],
        ),
        out_shape=[
            jax.ShapeDtypeStruct((2 * rows, 4 * wide), LOW),
            jax.ShapeDtypeStruct((1, 4 * wide), jnp.float32),
        ],
        compiler_params=pltpu.CompilerParams(vmem_limit_bytes=VMEM_ROOM),
        cost_estimate=pl.CostEstimate(
            flops=16 * rows * wide * width,
            transcendentals=0,
            bytes_accessed=rows * width * 4 + 8 * width * wide + 32 * rows * wide,
        ),
    )(places, *pair, gathered, slope)


def down_kernel(places_ref, left_ref, right_ref, own_ref, send_ref):
    span = right_ref.shape[3] // 2
    rows = own_ref.shape[0]
    total = None
    for far in range(2):
        right = right_ref[:, places_ref[3] ^ far].reshape(-1, 2 * span)
        for part in range(2):
            start = (part * 2 + far) * span
            one = mat_far(
                left_ref[:, start : start + span], right[:, part * span : (part + 1) * span]
            )
            total = one if total is None else total + one
    own_ref[...] = total[:rows]
    send_ref[...] = total[rows:].astype(LOW)


def down_call(places, left, gathered, start):
    both, deep = left.shape
    rows = both // 2
    lines, _, tall, wide = gathered.shape
    piece = pl.BlockSpec((rows, 2 * tall), lambda i, s: (0, i))
    own, send = pl.pallas_call(
        down_kernel,
        grid_spec=pltpu.PrefetchScalarGridSpec(
            num_scalar_prefetch=1,
            grid=(lines // 2,),
            in_specs=[
                pl.BlockSpec((both, deep), lambda i, s: (0, 0)),
                pl.BlockSpec((2, 2, tall, wide // 2), lambda i, s: (i, 0, 0, start)),
            ],
            out_specs=[piece, piece],
        ),
        out_shape=[
            jax.ShapeDtypeStruct((rows, lines * tall), jnp.float32),
            jax.ShapeDtypeStruct((rows, lines * tall), LOW),
        ],
        compiler_params=pltpu.CompilerParams(vmem_limit_bytes=VMEM_ROOM),
        cost_estimate=SMALL,
    )(places, left, gathered)
    return own, send


def mat(left, right):
    return jnp.dot(left, right, preferred_element_type=jnp.float32)


def turn_kernel(places_ref, own_ref, far_ref, turned_ref, left_ref):
    rows = own_ref.shape[0]
    for block in range(4):
        at = (places_ref[0] ^ block) * 2 + (places_ref[1] ^ pl.program_id(0))
        start = pl.multiple_of(at * LANES, LANES)
        span = slice(block * LANES, (block + 1) * LANES)
        left_ref[:rows, span] = own_ref[:, pl.ds(start, LANES)]
        left_ref[rows:, span] = far_ref[:, pl.ds(start, LANES)]
    turned_ref[0] = jnp.transpose(left_ref[...])


def turn(places, pair):
    rows, width = pair[0].shape
    line = width // 2
    whole = pl.BlockSpec((rows, width), lambda i, s: (0, 0))
    return pl.pallas_call(
        turn_kernel,
        grid_spec=pltpu.PrefetchScalarGridSpec(
            num_scalar_prefetch=1,
            grid=(2,),
            in_specs=[whole, whole],
            out_specs=pl.BlockSpec((1, line, 2 * rows), lambda i, s: (i, 0, 0)),
            scratch_shapes=[pltpu.VMEM((2 * rows, line), LOW)],
        ),
        out_shape=jax.ShapeDtypeStruct((2, line, 2 * rows), LOW),
        compiler_params=pltpu.CompilerParams(vmem_limit_bytes=VMEM_ROOM),
        cost_estimate=pl.CostEstimate(
            flops=0, transcendentals=0, bytes_accessed=rows * width * 8
        ),
    )(places, *pair)


def weight_cost(operands):
    rows, line = operands[0][1].shape[0], 4 * LANES
    wide = sum(right.shape[1] for _, right in operands) // 4
    return pl.CostEstimate(
        flops=8 * rows * line * wide,
        transcendentals=0,
        bytes_accessed=rows * wide * 8 + rows * line * 8 + line * wide * 8,
    )


def piece_kernel(pairs, *refs):
    ins, outs = refs[: 2 * pairs], refs[2 * pairs :]
    step = pl.program_id(0)
    parts = [mat(ins[2 * pair][0], ins[2 * pair + 1][...]).astype(LOW) for pair in range(pairs)]
    made = parts[0] if pairs == 1 else jnp.concatenate(parts, axis=1)

    @pl.when(step < 2)
    def _():
        outs[0][0] = made

    @pl.when(step >= 2)
    def _():
        outs[1][0] = made


def weight_pieces(operands, send, cost=None):
    line, rows = operands[0][0].shape[1:]
    if send:
        first = lambda i: jnp.minimum(i, 1)
        column = lambda i: jnp.maximum(i, 1)
    else:
        first = lambda i: 1 - jnp.minimum(i, 1)
        column = lambda i: jnp.where(i < 2, 0, i)
    specs, arrays, wide = [], [], 0
    for turned, right in operands:
        span = right.shape[1] // 4
        wide += span
        specs.append(pl.BlockSpec((1, line, rows), lambda i: (first(i), 0, 0)))
        specs.append(pl.BlockSpec((rows, span), lambda i: (0, column(i))))
        arrays += [turned, right]

    def kernel(*refs):
        piece_kernel(len(operands), *refs)

    return pl.pallas_call(
        kernel,
        grid=(4,),
        in_specs=specs,
        out_specs=[
            pl.BlockSpec((1, line, wide), lambda i: (first(i), 0, 0)),
            pl.BlockSpec((1, line, wide), lambda i: (jnp.maximum(i - 2, 0), 0, 0)),
        ],
        out_shape=[jax.ShapeDtypeStruct((2, line, wide), LOW)] * 2,
        compiler_params=pltpu.CompilerParams(vmem_limit_bytes=VMEM_ROOM),
        cost_estimate=cost or weight_cost(operands),
    )(*arrays)


def lane_of(shape):
    return lax.broadcasted_iota(jnp.int32, shape, 1)


def head_views(query, key, bias, head):
    lane = lane_of(query.shape)
    mine = (lane >= HDIM) if head else (lane < HDIM)
    spot = 0 if head else HDIM
    zero = jnp.zeros_like(query)
    query_view = jnp.where(mine, query, jnp.where(lane == spot, zero + 1, zero))
    key_view = jnp.where(lane == spot, bias, key)
    return mine, query_view, key_view


def attend_kernel(qkv_ref, bias_ref, mixed_ref, total_ref):
    query = qkv_ref[:, 0:LANES] * jnp.bfloat16(HDIM ** (-0.5))
    key = qkv_ref[:, LANES : 2 * LANES]
    value = qkv_ref[:, 2 * LANES : 3 * LANES]
    bias = bias_ref[...]
    sums, tops = [], []
    for head in range(2):
        mine, query_view, key_view = head_views(query, key, bias, head)
        scores = mat_far(query_view, key_view)
        top = jnp.max(scores, axis=1, keepdims=True)
        weight = jnp.exp(scores - top).astype(LOW)
        value_view = jnp.where(mine, value, jnp.ones_like(value))
        sums.append(jnp.dot(weight, value_view, preferred_element_type=jnp.float32))
        tops.append(top)
    low = lane_of(sums[0].shape) < HDIM
    upper = jnp.where(low, sums[0], sums[1])
    lower = jnp.where(low, sums[1], sums[0])
    lower = pltpu.roll(lower, HDIM, 1)
    mixed_ref[...] = (upper / lower).astype(LOW)
    total = jnp.where(low, tops[0], tops[1]) + jnp.log(lower)
    total = jnp.transpose(total)
    total_ref[0, 0:1, :] = total[0:1]
    total_ref[0, 1:2, :] = total[HDIM : HDIM + 1]


def attend_back_kernel(qkv_ref, bias_ref, grad_ref, mixed_ref, total_ref, out_ref):
    scale = HDIM ** (-0.5)
    query = qkv_ref[:, 0:LANES] * jnp.bfloat16(scale)
    key = qkv_ref[:, LANES : 2 * LANES]
    value = qkv_ref[:, 2 * LANES : 3 * LANES]
    bias = bias_ref[...]
    grad = grad_ref[...]
    product = grad.astype(jnp.float32) * mixed_ref[...].astype(jnp.float32)
    grad_query = grad_key = grad_value = None
    for head in range(2):
        mine, query_view, key_view = head_views(query, key, bias, head)
        zero = jnp.zeros_like(query)
        scores = mat_far(key_view, query_view)
        probs = jnp.exp(scores - total_ref[0, head : head + 1, :])
        grad_view = jnp.where(mine, grad, zero)
        grad_probs = mat_far(value, grad_view)
        ones = jnp.where(mine[0:8], 1.0, 0.0)
        inner = lax.dot_general(
            ones,
            product,
            (((1,), (1,)), ((), ())),
            precision=lax.Precision.HIGHEST,
            preferred_element_type=jnp.float32,
        )
        grad_scores = (probs * (grad_probs - inner[0:1])).astype(LOW)
        one_value = jnp.dot(probs.astype(LOW), grad_view, preferred_element_type=jnp.float32)
        one_key = jnp.dot(
            grad_scores, jnp.where(mine, query, zero), preferred_element_type=jnp.float32
        )
        one_query = mat_rows(grad_scores, jnp.where(mine, key, zero))
        grad_query = one_query if head == 0 else grad_query + one_query
        grad_key = one_key if head == 0 else grad_key + one_key
        grad_value = one_value if head == 0 else grad_value + one_value
    out_ref[:, 0:LANES] = (grad_query * scale).astype(LOW)
    out_ref[:, LANES : 2 * LANES] = grad_key.astype(LOW)
    out_ref[:, 2 * LANES : 3 * LANES] = grad_value.astype(LOW)


def attend_image(image, qkv, bias, given):
    both = qkv.shape[0]
    rows = both // 2
    blocks = qkv.shape[1] // (3 * LANES)

    def kernel(*refs):
        attend_kernel(*refs[:2], *refs[-2:])

    return pl.pallas_call(
        kernel,
        grid=(blocks,),
        in_specs=[
            pl.BlockSpec((rows, 3 * LANES), lambda j: (image, j)),
            pl.BlockSpec((rows, LANES), lambda j: (0, 0)),
        ]
        + [pl.BlockSpec(memory_space=pl.ANY)] * len(given),
        out_specs=[
            pl.BlockSpec((rows, LANES), lambda j: (image, j)),
            pl.BlockSpec((1, 8, rows), lambda j: (image * blocks + j, 0, 0)),
        ],
        out_shape=[
            jax.ShapeDtypeStruct((both, blocks * LANES), LOW),
            jax.ShapeDtypeStruct((2 * blocks, 8, rows), jnp.float32),
        ],
        input_output_aliases={2: 0, 3: 1} if given else {},
        compiler_params=pltpu.CompilerParams(vmem_limit_bytes=VMEM_ROOM),
        cost_estimate=pl.CostEstimate(
            flops=blocks * 2 * 2 * 2 * rows * rows * LANES * 2,
            transcendentals=blocks * 2 * rows * rows,
            bytes_accessed=rows * blocks * LANES * 8,
        ),
    )(qkv, bias, *given)


def attend_back_image(image, qkv, bias, grad, mixed, total, given):
    both = qkv.shape[0]
    rows = both // 2
    blocks = qkv.shape[1] // (3 * LANES)

    def kernel(*refs):
        attend_back_kernel(*refs[:5], refs[-1])

    return pl.pallas_call(
        kernel,
        grid=(blocks,),
        in_specs=[
            pl.BlockSpec((rows, 3 * LANES), lambda j: (image, j)),
            pl.BlockSpec((rows, LANES), lambda j: (0, 0)),
            pl.BlockSpec((rows, LANES), lambda j: (0, j)),
            pl.BlockSpec((rows, LANES), lambda j: (image, j)),
            pl.BlockSpec((1, 8, rows), lambda j: (image * blocks + j, 0, 0)),
        ]
        + [pl.BlockSpec(memory_space=pl.ANY)] * len(given),
        out_specs=pl.BlockSpec((rows, 3 * LANES), lambda j: (image, j)),
        out_shape=jax.ShapeDtypeStruct(qkv.shape, LOW),
        input_output_aliases={5: 0} if given else {},
        compiler_params=pltpu.CompilerParams(vmem_limit_bytes=VMEM_ROOM),
        cost_estimate=pl.CostEstimate(
            flops=blocks * 2 * 5 * 2 * rows * rows * LANES * 2,
            transcendentals=blocks * 2 * rows * rows,
            bytes_accessed=rows * blocks * LANES * 16,
        ),
    )(qkv, bias, grad, mixed, total, *given)


def flat_norm(values, gain, shift):
    center = values - jnp.mean(values, axis=-1, keepdims=True)
    spread = lax.rsqrt(jnp.mean(center * center, axis=-1, keepdims=True) + EPS)
    unit = center * spread
    return unit * gain + shift, unit, spread


def flat_norm_back(upstream, unit, spread, gain):
    scaled = upstream * gain
    inner = (
        scaled
        - jnp.mean(scaled, axis=-1, keepdims=True)
        - unit * jnp.mean(scaled * unit, axis=-1, keepdims=True)
    )
    return spread * inner, jnp.sum(upstream * unit, axis=0), jnp.sum(upstream, axis=0)


def column_flat(values):
    return jnp.sum(values.astype(jnp.float32), axis=0)


def whole_images(
    images,
    cotangent,
    slot_live,
    first_gain,
    first_shift,
    query_weight,
    query_bias,
    key_weight,
    value_weight,
    value_bias,
    output_weight,
    output_bias,
    second_gain,
    second_shift,
    up_weight,
    up_bias,
    down_weight,
    down_bias,
):
    dp_place = lax.axis_index("dp")
    place_y = lax.axis_index("tensor")
    core, place_x, place_z = dp_place % 2, (dp_place // 2) % 2, dp_place // 4
    places = jnp.stack([place_z, place_x, core, place_y]).astype(jnp.int32)
    strip, width = images.shape[1:]
    half = -(-strip // HALF_PAD) * HALF_PAD
    rows = 2 * half
    depth, head_cols = query_weight.shape
    units = up_weight.shape[1]

    def columns_of(weights, place):
        return [
            lax.dynamic_slice_in_dim(
                weight, place * (weight.shape[1] // 2), weight.shape[1] // 2, 1
            )
            for weight in weights
        ]

    def core_parts(weights, place):
        cuts = columns_of(weights, place)
        parts = []
        for part in range(2):
            spans = [cut.shape[1] // 2 for cut in cuts]
            parts.append(
                jnp.concatenate(
                    [cut[:, part * span : (part + 1) * span] for cut, span in zip(cuts, spans)], 1
                )
            )
        return jnp.stack(parts)

    feeds = [up_weight, down_weight.T]
    feed_keep = jnp.concatenate(columns_of(feeds, core), 1)
    feed_send = jnp.concatenate(columns_of(feeds, 1 - core), 1)
    feed = pick_two(core, feed_keep, exchange(feed_send, far_core=1), 0)
    groups = [[place for place in range(32) if (place // 2) % 2 == at] for at in range(2)]

    gathered = lax.all_gather(
        feed.reshape(2 * depth, -1), BOTH, axis=0, tiled=True, axis_index_groups=groups
    ).reshape(8, 2, 2 * depth, -1)
    gathered = pltpu.with_memory_space_constraint(gathered, pltpu.HBM)

    heads = [query_weight, key_weight, value_weight, output_weight.T]
    piece_one = gather_piece(core_parts(heads, core), core_parts(heads, 1 - core), core)
    others_one = scatter_z([None, piece_one, piece_one, piece_one])

    padding = ((0, 0), (0, half - strip), (0, 0))

    def own_and_far(slots, *waits):
        slots = jnp.pad(slots, padding)
        mine = lax.dynamic_index_in_dim(slots, place_y, 0, keepdims=False)
        theirs = lax.dynamic_index_in_dim(slots, 1 - place_y, 0, keepdims=False)
        return mine, exchange(after(theirs, *waits), far_y=1)

    image_mine, image_far = own_and_far(images, piece_one)
    grad_mine, grad_far = own_and_far(cotangent, piece_one)
    line_one = gather_line(piece_one, others_one, places)
    cross_one = exchange(line_one[0], far_x=1), exchange(line_one[1], far_y=1)
    pair_one = gather_pairs(places, *line_one, *cross_one)
    image_far, grad_far = after((image_far, grad_far), *pair_one)
    whole = jnp.concatenate([image_mine, image_far], 0)

    def head_columns(vector):
        table = vector.astype(jnp.float32).reshape(2, 2, 2, -1)
        table = lax.dynamic_index_in_dim(table, core, 1, keepdims=False)
        table = jnp.where(place_y == 0, table, table[::-1])
        return table.transpose(1, 0, 2).reshape(4, 1, -1)

    def spread_core(table):
        table = jnp.stack(
            [jnp.where(core == 0, table, 0.0), jnp.where(core == 1, table, 0.0)], 1
        )
        return table.reshape(-1)

    def head_spread(vector):
        table = vector.reshape(2, 2, -1).transpose(1, 0, 2)
        return spread_core(jnp.where(place_y == 0, table, table[::-1]))

    gain_one, shift_one = first_gain.astype(jnp.float32), first_shift.astype(jnp.float32)
    gain_two, shift_two = second_gain.astype(jnp.float32), second_shift.astype(jnp.float32)
    query_shift, value_shift = head_columns(query_bias), head_columns(value_bias)
    qkv_shift = jnp.concatenate(
        [query_shift, jnp.zeros_like(query_shift), value_shift], 1
    ).reshape(-1)
    up_shift = head_columns(up_bias).reshape(1, -1)

    row = jnp.arange(rows)
    in_half = row % half
    spot = jnp.where(row < half, place_y, 1 - place_y) * strip + in_half
    ok = (in_half < strip) & (spot < VALID)
    live = lax.dynamic_index_in_dim(slot_live, place_y, 0, keepdims=False).astype(jnp.float32)
    row_mask = (live * ok.astype(jnp.float32))[:, None]
    key_bias = jnp.broadcast_to(
        jnp.where(ok, 0.0, NEGATIVE).astype(LOW)[:, None], (rows, LANES)
    )

    resid = whole.astype(jnp.float32)

    def full_columns(owned):
        return owned.transpose(2, 0, 1, 3).reshape(depth, -1)

    def pair_of(own):
        return own, exchange(own, far_core=1)

    normed, unit_one, spread_one = flat_norm(resid, gain_one, shift_one)
    normed_pair = pair_of(normed.astype(LOW))

    normed_turned = turn(places, normed_pair)
    grad_top = row_mask * jnp.concatenate([grad_mine, grad_far], 0).astype(jnp.float32)
    fed_grad = grad_top.astype(LOW)
    fed_pair = pair_of(fed_grad)
    fed_turned = turn(places, fed_pair)
    last_one = exchange(pair_one[0], far_y=1), exchange(pair_one[1], far_x=1)
    qkv_full, output_full = gather_all(after(places, normed_turned, fed_turned), *pair_one, *last_one, 3 * head_cols // 4)

    normed_rows = jnp.concatenate(normed_pair, 0)
    qkv = (mat(normed_rows, qkv_full) + qkv_shift).astype(LOW)
    mixed_half = attend_image(1, qkv, key_bias, [])
    mixed_far = mat_far(mixed_half[0][rows:], output_full).astype(LOW)
    mixed_sum = exchange(mixed_far, far_core=1)
    mixed, totals = attend_image(0, qkv, key_bias, list(after(tuple(mixed_half), mixed_far)))
    attended = mat_far(mixed[:rows], output_full) + mixed_sum.astype(jnp.float32)
    attended = attended + output_bias.astype(jnp.float32)
    middle = row_mask * (resid + attended)
    second, unit_two, spread_two = flat_norm(middle, gain_two, shift_two)
    second_pair = pair_of(second.astype(LOW))
    second_turned = turn(places, second_pair)
    up_pair = after(second_pair, second_turned)
    active, slope = up_call(places, up_pair, gathered, up_shift)

    lower_sends = weight_pieces([(fed_turned, active)], True)
    lower_first = scatter_first(lower_sends)
    lower_keeps = weight_pieces([(fed_turned, after(active, *lower_sends))], False)
    fed_late = after(fed_pair, *lower_keeps)
    hidden_grad, up_bias_sums = hidden_call(places, fed_late, gathered, slope)
    up_sends = weight_pieces([(second_turned, hidden_grad)], True)
    up_first = scatter_first(up_sends)
    lower_first = after(lower_first, *up_sends)
    lower_second = scatter_second(scatter_adds(lower_keeps, lower_first))
    hidden_late = after(hidden_grad, *lower_first)
    second_grad, second_send = down_call(places, hidden_late, gathered, 0)
    second_grad = second_grad + exchange(second_send, far_core=1).astype(jnp.float32)
    middle_back, gain_two_grad, shift_two_grad = flat_norm_back(
        second_grad, unit_two, spread_two, gain_two
    )
    middle_grad = row_mask * (grad_top + middle_back)
    attended_grad = middle_grad.astype(LOW)
    attended_pair = pair_of(attended_grad)
    grad_mixed = mat(attended_pair[0], output_full).astype(LOW)
    back = attend_back_image(0, qkv, key_bias, grad_mixed, mixed, totals, [])
    up_keeps = weight_pieces([(second_turned, after(hidden_late, back))], False)
    up_first = after(up_first, back)
    up_adds = scatter_adds(up_keeps, up_first)
    up_second = scatter_second(up_adds)
    lower_second = after(lower_second, back, *up_keeps)
    lower_line = scatter_line(lower_keeps, lower_first, lower_second)
    lower_z = scatter_z(lower_line)
    attended_turned = turn(places, attended_pair)
    grad_mixed = mat(attended_pair[1], output_full).astype(LOW)
    grad_mixed = after(grad_mixed, *up_adds, *lower_line, attended_turned)
    back = attend_back_image(1, qkv, key_bias, grad_mixed, mixed, totals, [back])
    up_second, lower_z = after((up_second, tuple(lower_z)), back)
    up_line = scatter_line(up_keeps, up_first, up_second)
    up_z = scatter_z(up_line)
    back = after(back, *up_line)
    last_sends = weight_pieces(
        [(normed_turned, back), (attended_turned, mixed)], True, SMALL
    )
    last_first = scatter_first(last_sends)
    back_late = after(back, *last_sends)
    last_keeps = weight_pieces(
        [(normed_turned, back_late), (attended_turned, mixed)], False, SMALL
    )
    fed, fed_send = down_call(places, after(active, *last_keeps), gathered, 1)
    back_late = after(back_late, fed, fed_send, *up_z)
    normed_send = mat_far(back_late[rows:], qkv_full).astype(LOW)
    last_first = after(last_first, normed_send)
    last_adds = scatter_adds(last_keeps, last_first)
    last_second = scatter_second(last_adds)
    back_late = after(back_late, *last_adds)
    normed_far = exchange(normed_send, far_core=1)
    fed = fed + exchange(fed_send, far_core=1).astype(jnp.float32)
    layer_own = (row_mask * (middle + fed + down_bias.astype(jnp.float32))).astype(LOW)
    normed_grad = mat_far(back_late[:rows], qkv_full) + normed_far.astype(jnp.float32)
    first_back, gain_one_grad, shift_one_grad = flat_norm_back(
        normed_grad, unit_one, spread_one, gain_one
    )
    images_own = middle_grad + first_back
    qkv_sums = column_flat(back_late).reshape(4, 3, -1)
    vector = jnp.concatenate(
        [
            column_flat(attended_grad),
            gain_two_grad,
            shift_two_grad,
            column_flat(fed_grad),
            head_spread(up_bias_sums.reshape(-1)),
            gain_one_grad,
            shift_one_grad,
            head_spread(qkv_sums[:, 0].reshape(-1)),
            head_spread(qkv_sums[:, 2].reshape(-1)),
        ]
    )
    vector, vectors = vector_first(vector)
    last_line = scatter_line(last_keeps, last_first, after(last_second, images_own))
    last_z = scatter_z(last_line)
    images_far = exchange(
        after(images_own, *last_second)[half : half + strip].astype(LOW), far_y=1
    )
    layer_far = exchange(after(layer_own, *last_adds)[half : half + strip], far_y=1)
    vector = vector + vectors[0] + vectors[1] + vectors[2]
    vector = vector + after(exchange(vector, far_x=1), images_far, *last_line)
    vector = vector + after(exchange(vector, far_y=1), layer_far)
    lower_z, up_z = after((tuple(lower_z), tuple(up_z)), *last_line, layer_far)
    lower_owned = full_columns(scatter_last(lower_line[0], lower_z, core)).T
    upper_owned = full_columns(scatter_last(up_line[0], up_z, core))

    def to_strips(own, far):
        return pick_two(place_y, own[:strip], far, 1).transpose(1, 0, 2)

    layer_out = to_strips(layer_own, layer_far)
    images_grad = to_strips(after(images_own, *last_line), images_far.astype(jnp.float32))
    last_z = after(tuple(last_z), vector, layer_out, images_grad, lower_owned, upper_owned)
    last_owned = scatter_last(last_line[0], last_z, core)
    def head_grad(at):
        return full_columns(last_owned[..., at * LANES : (at + 1) * LANES])

    early, late = vector[: 4 * width + up_bias.shape[0]], vector[4 * width + up_bias.shape[0] :]
    return (
        layer_out,
        images_grad,
        late[:width],
        late[width : 2 * width],
        head_grad(0),
        late[2 * width : 3 * width],
        head_grad(1),
        head_grad(2),
        late[3 * width :],
        head_grad(3).T,
        early[:width],
        early[width : 2 * width],
        early[2 * width : 3 * width],
        upper_owned,
        early[4 * width :],
        lower_owned,
        early[3 * width : 4 * width],
    )


def pick(mesh):
    sizes = dict(mesh.shape)
    if sizes["dp"] == 16 and sizes["tensor"] == 2:
        return whole_images
    return local


def solution(mesh):
    in_specs = (
        P("dp", "tensor", None),
        P("dp", "tensor", None),
        P("dp"),
        P(),
        P(),
        P("dp", "tensor"),
        P(),
        P("dp", "tensor"),
        P("dp", "tensor"),
        P(),
        P("tensor", "dp"),
        P(),
        P(),
        P(),
        P("dp", "tensor"),
        P(),
        P("tensor", "dp"),
        P(),
    )
    out_specs = (
        P("dp", "tensor", None),
        P("dp", "tensor", None),
        P(),
        P(),
        P("dp", "tensor"),
        P(),
        P("dp", "tensor"),
        P("dp", "tensor"),
        P(),
        P("tensor", "dp"),
        P(),
        P(),
        P(),
        P("dp", "tensor"),
        P(),
        P("tensor", "dp"),
        P(),
    )
    return jax.shard_map(pick(mesh), mesh=mesh, in_specs=in_specs, out_specs=out_specs, check_vma=False)
```

```python
import jax
import jax.numpy as jnp
from jax import lax
from jax.experimental import pallas as pl
from jax.experimental.pallas import tpu as pltpu
from jax.sharding import PartitionSpec as P

HDIM = 64
VALID = 577


EPS = 1e-05
NEGATIVE = -1e30
SLOPE = 1.702


def layer_norm(values, gain, shift):
    center = values - jnp.mean(values, axis=-1, keepdims=True)
    spread = lax.rsqrt(jnp.mean(center * center, axis=-1, keepdims=True) + EPS)
    unit = center * spread
    return (unit * gain + shift, unit, spread)


def norm_back(upstream, unit, spread, gain):
    scaled = upstream * gain
    inner = (
        scaled
        - jnp.mean(scaled, axis=-1, keepdims=True)
        - unit * jnp.mean(scaled * unit, axis=-1, keepdims=True)
    )
    return (spread * inner, jnp.sum(upstream * unit, axis=(0, 1)), jnp.sum(upstream, axis=(0, 1)))


def dense(left, right):
    return jnp.einsum("spa,ab->spb", left, right, preferred_element_type=jnp.float32)


def project_back(left, right):
    return jnp.einsum("spa,ba->spb", left, right, preferred_element_type=jnp.float32)


def outer(left, right):
    return jnp.einsum("spa,spb->ab", left, right, preferred_element_type=jnp.float32)


def column_sum(values):
    return jnp.sum(values.astype(jnp.float32), axis=(0, 1))


def widen(piece, length, start):
    return lax.dynamic_update_slice_in_dim(jnp.zeros((length,), jnp.float32), piece, start, 0)


def split_heads(block):
    return block.reshape(block.shape[0], -1, HDIM)


def scores_of(query, key, key_ok):
    raw = jnp.einsum(
        "qhe,khe->hqk", split_heads(query), split_heads(key), preferred_element_type=jnp.float32
    )
    return jnp.where(key_ok[None, None, :], raw * HDIM ** (-0.5), NEGATIVE)


def attend(query, key, value, key_ok):
    scores = scores_of(query, key, key_ok)
    top = jnp.max(scores, axis=-1, keepdims=True)
    total = top + jnp.log(jnp.sum(jnp.exp(scores - top), axis=-1, keepdims=True))
    probs = jnp.exp(scores - total).astype(jnp.bfloat16)
    mixed = jnp.einsum(
        "hqk,khe->qhe", probs, split_heads(value), preferred_element_type=jnp.float32
    )
    return (mixed.reshape(query.shape[0], -1).astype(jnp.bfloat16), total)


def attend_back(query, key, value, grad_mixed, total, key_ok):
    scores = scores_of(query, key, key_ok)
    probs = jnp.exp(scores - total)
    grad_heads = split_heads(grad_mixed)
    grad_probs = jnp.einsum(
        "qhe,khe->hqk", grad_heads, split_heads(value), preferred_element_type=jnp.float32
    )
    grad_value = jnp.einsum(
        "hqk,qhe->khe", probs.astype(jnp.bfloat16), grad_heads, preferred_element_type=jnp.float32
    )
    grad_scores = (
        probs * (grad_probs - jnp.sum(probs * grad_probs, axis=-1, keepdims=True))
    ).astype(jnp.bfloat16)
    grad_query = jnp.einsum(
        "hqk,khe->qhe", grad_scores, split_heads(key), preferred_element_type=jnp.float32
    ) * HDIM ** (-0.5)
    grad_key = jnp.einsum(
        "hqk,qhe->khe", grad_scores, split_heads(query), preferred_element_type=jnp.float32
    ) * HDIM ** (-0.5)
    length = query.shape[0]
    return (
        grad_query.reshape(length, -1).astype(jnp.bfloat16),
        grad_key.reshape(length, -1).astype(jnp.bfloat16),
        grad_value.reshape(length, -1).astype(jnp.bfloat16),
    )


def local(
    images,
    cotangent,
    slot_live,
    first_gain,
    first_shift,
    query_weight,
    query_bias,
    key_weight,
    value_weight,
    value_bias,
    output_weight,
    output_bias,
    second_gain,
    second_shift,
    up_weight,
    up_bias,
    down_weight,
    down_bias,
):
    slots, strip, width = images.shape
    tensor_count = lax.axis_size("tensor")
    tensor_place = lax.axis_index("tensor")
    seq_len = strip * tensor_count
    positions = tensor_place * strip + jnp.arange(strip)
    row_mask = (
        slot_live.astype(jnp.float32)[:, None, None]
        * (positions < VALID).astype(jnp.float32)[None, :, None]
    )
    key_ok = jnp.arange(seq_len) < VALID
    query_full, key_full, value_full, upper_full, output_full, lower_full = (
        lax.all_gather(query_weight, "dp", axis=0, tiled=True),
        lax.all_gather(key_weight, "dp", axis=0, tiled=True),
        lax.all_gather(value_weight, "dp", axis=0, tiled=True),
        lax.all_gather(up_weight, "dp", axis=0, tiled=True),
        lax.all_gather(output_weight, "dp", axis=1, tiled=True),
        lax.all_gather(down_weight, "dp", axis=1, tiled=True),
    )
    head_cols = query_full.shape[1]
    head_start = tensor_place * head_cols
    gain_one = first_gain.astype(jnp.float32)
    shift_one = first_shift.astype(jnp.float32)
    gain_two = second_gain.astype(jnp.float32)
    shift_two = second_shift.astype(jnp.float32)
    query_shift = lax.dynamic_slice_in_dim(query_bias.astype(jnp.float32), head_start, head_cols)
    value_shift = lax.dynamic_slice_in_dim(value_bias.astype(jnp.float32), head_start, head_cols)
    resid = images.astype(jnp.float32)
    normed, unit_one, spread_one = layer_norm(resid, gain_one, shift_one)
    normed_rows = lax.all_gather(normed.astype(jnp.bfloat16), "tensor", axis=1, tiled=True)
    queries = (dense(normed_rows, query_full) + query_shift).astype(jnp.bfloat16)
    keys_low = dense(normed_rows, key_full).astype(jnp.bfloat16)
    values_low = (dense(normed_rows, value_full) + value_shift).astype(jnp.bfloat16)
    mixed, totals = lax.map(
        lambda items: attend(items[0], items[1], items[2], key_ok), (queries, keys_low, values_low)
    )
    attended = lax.psum_scatter(
        dense(mixed, output_full), "tensor", scatter_dimension=1, tiled=True
    ) + output_bias.astype(jnp.float32)
    middle = row_mask * (resid + attended)
    second, unit_two, spread_two = layer_norm(middle, gain_two, shift_two)
    second_low = second.astype(jnp.bfloat16)
    grad_top = row_mask * cotangent.astype(jnp.float32)
    fed_grad = grad_top.astype(jnp.bfloat16)
    down_shift = down_bias.astype(jnp.float32)
    units = upper_full.shape[1]
    second_rows = lax.all_gather(second_low, "tensor", axis=1, tiled=True)
    up_shift = lax.dynamic_slice_in_dim(up_bias.astype(jnp.float32), tensor_place * units, units)
    hidden = dense(second_rows, upper_full) + up_shift
    sigma = jax.nn.sigmoid(SLOPE * hidden)
    active = (hidden * sigma).astype(jnp.bfloat16)
    fed = (
        lax.psum_scatter(
            dense(active, lower_full).astype(jnp.bfloat16),
            "tensor",
            scatter_dimension=1,
            tiled=True,
        ).astype(jnp.float32)
        + down_shift
    )
    fed_rows = lax.all_gather(fed_grad, "tensor", axis=1, tiled=True)
    grad_active = project_back(fed_rows, lower_full)
    lower_grad = outer(active, fed_rows)
    hidden_grad = (grad_active * (sigma + SLOPE * hidden * sigma * (1.0 - sigma))).astype(
        jnp.bfloat16
    )
    upper_grad = outer(second_rows, hidden_grad)
    up_bias_grad = widen(column_sum(hidden_grad), up_bias.shape[0], tensor_place * units)
    second_grad = lax.psum_scatter(
        project_back(hidden_grad, upper_full), "tensor", scatter_dimension=1, tiled=True
    )
    layer_out = (row_mask * (middle + fed)).astype(jnp.bfloat16)
    down_bias_grad = column_sum(fed_grad)
    middle_back, gain_two_grad, shift_two_grad = norm_back(
        second_grad, unit_two, spread_two, gain_two
    )
    middle_grad = row_mask * (grad_top + middle_back)
    attended_grad = middle_grad.astype(jnp.bfloat16)
    output_bias_grad = column_sum(attended_grad)
    attended_rows = lax.all_gather(attended_grad, "tensor", axis=1, tiled=True)
    grad_mixed = project_back(attended_rows, output_full).astype(jnp.bfloat16)
    output_grad = outer(mixed, attended_rows)
    grad_query, grad_key, grad_value = lax.map(
        lambda items: attend_back(items[0], items[1], items[2], items[3], items[4], key_ok),
        (queries, keys_low, values_low, grad_mixed, totals),
    )
    query_grad = outer(normed_rows, grad_query)
    key_grad = outer(normed_rows, grad_key)
    value_grad = outer(normed_rows, grad_value)
    query_bias_grad = widen(column_sum(grad_query), width, head_start)
    value_bias_grad = widen(column_sum(grad_value), width, head_start)
    normed_terms = (
        project_back(grad_query, query_full)
        + project_back(grad_key, key_full)
        + project_back(grad_value, value_full)
    )
    normed_grad = lax.psum_scatter(
        normed_terms.astype(jnp.bfloat16), "tensor", scatter_dimension=1, tiled=True
    ).astype(jnp.float32)
    first_back, gain_one_grad, shift_one_grad = norm_back(
        normed_grad, unit_one, spread_one, gain_one
    )
    images_grad = middle_grad + first_back
    query_owned, key_owned, value_owned, upper_owned, output_owned, lower_owned = (
        lax.psum_scatter(
            query_grad.astype(jnp.bfloat16), "dp", scatter_dimension=0, tiled=True
        ).astype(jnp.float32),
        lax.psum_scatter(
            key_grad.astype(jnp.bfloat16), "dp", scatter_dimension=0, tiled=True
        ).astype(jnp.float32),
        lax.psum_scatter(
            value_grad.astype(jnp.bfloat16), "dp", scatter_dimension=0, tiled=True
        ).astype(jnp.float32),
        lax.psum_scatter(
            upper_grad.astype(jnp.bfloat16), "dp", scatter_dimension=0, tiled=True
        ).astype(jnp.float32),
        lax.psum_scatter(
            output_grad.astype(jnp.bfloat16), "dp", scatter_dimension=1, tiled=True
        ).astype(jnp.float32),
        lax.psum_scatter(
            lower_grad.astype(jnp.bfloat16), "dp", scatter_dimension=1, tiled=True
        ).astype(jnp.float32),
    )
    vector_sums = lax.psum(
        (
            gain_one_grad,
            shift_one_grad,
            query_bias_grad,
            value_bias_grad,
            output_bias_grad,
            gain_two_grad,
            shift_two_grad,
            up_bias_grad,
            down_bias_grad,
        ),
        ("dp", "tensor"),
    )
    (
        gain_one_total,
        shift_one_total,
        query_bias_total,
        value_bias_total,
        output_bias_total,
        gain_two_total,
        shift_two_total,
        up_bias_total,
        down_bias_total,
    ) = vector_sums
    return (
        layer_out,
        images_grad,
        gain_one_total,
        shift_one_total,
        query_owned,
        query_bias_total,
        key_owned,
        value_owned,
        value_bias_total,
        output_owned,
        output_bias_total,
        gain_two_total,
        shift_two_total,
        upper_owned,
        up_bias_total,
        lower_owned,
        down_bias_total,
    )


BOTH = ("dp", "tensor")
HALF_PAD = 8
LANES = 128
LOW = jnp.bfloat16
VMEM_ROOM = 24 * 2**20
SMALL = pl.CostEstimate(flops=1024, transcendentals=0, bytes_accessed=1024)


def exchange(value, far_z=0, far_x=0, far_core=0, far_y=0):
    pairs = []
    for place in range(32):
        other = place ^ (far_z * 8 + far_x * 4 + far_core * 2 + far_y)
        pairs.append((place, other))
    return lax.ppermute(value, BOTH, pairs)


def pick_two(bit, own, other, axis):
    first = jnp.where(bit == 0, own, other)
    last = jnp.where(bit == 0, other, own)
    return jnp.stack([first, last], axis)


def after(value, *others):
    return lax.optimization_barrier((value, *others))[0]


def pack(places, sources, shapes, plan):
    def kernel(places_ref, *refs):
        ins, outs = refs[: len(sources)], refs[len(sources) :]
        spots = [places_ref[at] for at in range(4)]
        for at, take, to, put in plan:
            outs[to][put(*spots)] = ins[at][take(*spots)]

    return pl.pallas_call(
        kernel,
        in_specs=[pl.BlockSpec(memory_space=pltpu.SMEM)]
        + [pl.BlockSpec(memory_space=pltpu.VMEM)] * len(sources),
        out_specs=[pl.BlockSpec(memory_space=pltpu.VMEM)] * len(shapes),
        out_shape=[jax.ShapeDtypeStruct(shape, LOW) for shape in shapes],
        compiler_params=pltpu.CompilerParams(vmem_limit_bytes=VMEM_ROOM),
        cost_estimate=pl.CostEstimate(
            flops=0,
            transcendentals=0,
            bytes_accessed=sum(2 * source.size * 2 for source in sources),
        ),
    )(places, *sources)


def gather_piece(keep, send, core):
    deep, wide = keep.shape[1:]
    return pick_two(core, keep, exchange(send, far_core=1), 1).reshape(2, 2 * deep, wide)


def gather_line(piece, others, places):
    rows, wide = piece.shape[1:]
    line = [piece] + others
    plan = []
    for step in range(4):
        for part in range(2):
            plan.append(
                (
                    step,
                    lambda z, x, c, y, part=part: part,
                    part,
                    lambda z, x, c, y, step=step: z ^ step,
                )
            )
    return pack(places, line, [(4, rows, wide)] * 2, plan)


def gather_pairs(places, one, two, one_x, two_y):
    every = slice(None)
    plan = [
        (0, lambda z, x, c, y: every, 0, lambda z, x, c, y: x),
        (1, lambda z, x, c, y: every, 0, lambda z, x, c, y: 1 - x),
        (2, lambda z, x, c, y: every, 1, lambda z, x, c, y: 0),
        (3, lambda z, x, c, y: every, 1, lambda z, x, c, y: 1),
    ]
    return pack(places, [one, one_x, two, two_y], [(2,) + one.shape] * 2, plan)


def gather_all(places, one_pair, two_pair, one_y, two_x, most):
    every = slice(None)
    rows, wide = one_pair.shape[2:]
    plan = []
    for to, low, high in ((0, 0, most), (1, most, wide)):
        span = high - low
        for place_z in range(4):
            for far in range(2):
                for number in range(2):
                    plan.append(
                        (
                            number,
                            lambda z, x, c, y, a=far, p=place_z, lo=low, hi=high: (
                                a,
                                p,
                                every,
                                slice(lo, hi),
                            ),
                            to,
                            lambda z, x, c, y, a=far, p=place_z, n=number, s=span: (
                                p,
                                a,
                                every,
                                slice(n * s, n * s + s),
                            ),
                        )
                    )
                    plan.append(
                        (
                            2 + far,
                            lambda z, x, c, y, n=number, p=place_z, lo=low, hi=high: (
                                n,
                                p,
                                every,
                                slice(lo, hi),
                            ),
                            to,
                            lambda z, x, c, y, f=far, p=place_z, n=number, s=span: (
                                p,
                                x ^ f,
                                every,
                                slice((2 + n) * s, (3 + n) * s),
                            ),
                        )
                    )
    shapes = [(4, 2, rows, 4 * most), (4, 2, rows, 4 * (wide - most))]
    made = pack(places, [one_pair, one_y, two_pair, two_x], shapes, plan)
    return [array.reshape(8 * rows, -1) for array in made]


def low_add(*values):
    total = values[0].astype(jnp.float32)
    for value in values[1:]:
        total = total + value.astype(jnp.float32)
    return total


def line_kernel(one_ref, one_a, one_b, two_ref, two_a, two_b, own_ref, *send_refs):
    tall = own_ref.shape[1]
    for step in range(4):
        rows = slice(step * tall, (step + 1) * tall)
        one = low_add(one_ref[0, rows], one_a[0, rows], one_b[rows])
        two = low_add(two_ref[0, rows], two_a[0, rows], two_b[rows])
        if step == 0:
            own_ref[0] = one
            own_ref[1] = two
        else:
            send_refs[step - 1][0] = one.astype(LOW)
            send_refs[step - 1][1] = two.astype(LOW)


def scatter_first(sends):
    return exchange(sends[0], far_y=1), exchange(sends[1], far_x=1)


def scatter_adds(keeps, arrived):
    return [low_add(keeps[at][1], arrived[at][1]).astype(LOW) for at in range(2)]


def scatter_second(adds):
    return exchange(adds[0], far_x=1), exchange(adds[1], far_y=1)


def scatter_line(keeps, arrived, crossed):
    lines, wide = crossed[0].shape
    tall = lines // 4
    first = pl.BlockSpec((1, lines, wide), lambda i: (0, 0, 0))
    flat = pl.BlockSpec((lines, wide), lambda i: (0, 0))
    piece = pl.BlockSpec((2, tall, wide), lambda i: (0, 0, 0))
    return pl.pallas_call(
        line_kernel,
        grid=(1,),
        in_specs=[first, first, flat, first, first, flat],
        out_specs=[piece] * 4,
        out_shape=[jax.ShapeDtypeStruct((2, tall, wide), jnp.float32)]
        + [jax.ShapeDtypeStruct((2, tall, wide), LOW)] * 3,
        compiler_params=pltpu.CompilerParams(vmem_limit_bytes=VMEM_ROOM),
        cost_estimate=pl.CostEstimate(
            flops=lines * wide * 4, transcendentals=0, bytes_accessed=lines * wide * 18
        ),
    )(keeps[0], arrived[0], crossed[0], keeps[1], arrived[1], crossed[1])


def scatter_z(sends):
    return [exchange(sends[step], far_z=step) for step in (1, 2, 3)]


def scatter_last(own, others, core):
    tall, wide = own.shape[1:]
    total = low_add(own, *others).reshape(2, 2, tall // 2, wide)
    keep = lax.dynamic_index_in_dim(total, core, 1, keepdims=False)
    send = lax.dynamic_index_in_dim(total, 1 - core, 1, keepdims=False)
    far = exchange(send.astype(LOW), far_core=1).astype(jnp.float32)
    return pick_two(core, keep, far, 0)


def vector_first(vector):
    vector = vector + exchange(vector, far_core=1)
    return vector, [exchange(vector, far_z=step) for step in (1, 2, 3)]


def mat_far(left, right):
    return lax.dot_general(
        left, right, (((1,), (1,)), ((), ())), preferred_element_type=jnp.float32
    )


def mat_rows(left, right):
    return lax.dot_general(
        left, right, (((0,), (0,)), ((), ())), preferred_element_type=jnp.float32
    )


def fill_rows(made_ref, own_ref, far_ref):
    rows = own_ref.shape[0]

    @pl.when(pl.program_id(0) == 0)
    def _():
        made_ref[:rows] = own_ref[...]
        made_ref[rows:] = far_ref[...]


def up_kernel(
    places_ref, own_ref, far_ref, right_ref, shift_ref, active_ref, slope_ref, left_ref
):
    fill_rows(left_ref, own_ref, far_ref)
    right = right_ref[...].reshape(left_ref.shape[1], -1)
    hidden = jnp.dot(left_ref[...], right, preferred_element_type=jnp.float32)
    hidden = hidden + shift_ref[...]
    sigma = 0.5 * jnp.tanh((0.5 * SLOPE) * hidden) + 0.5
    active = hidden * sigma
    active_ref[...] = active.astype(LOW)
    slope_ref[...] = (sigma + SLOPE * active * (1.0 - sigma)).astype(LOW)


def feed_spec(gathered, start):
    lines, _, rows, wide = gathered.shape
    return pl.BlockSpec(
        (lines, 1, rows, wide // 4), lambda i, s: (0, s[3] ^ (i % 2), 0, start + i // 2)
    )


def up_call(places, pair, gathered, shift):
    rows, width = pair[0].shape
    wide = shift.shape[1] // 4
    whole = pl.BlockSpec((rows, width), lambda i, s: (0, 0))
    piece = pl.BlockSpec((2 * rows, wide), lambda i, s: (0, i))
    return pl.pallas_call(
        up_kernel,
        grid_spec=pltpu.PrefetchScalarGridSpec(
            num_scalar_prefetch=1,
            grid=(4,),
            in_specs=[
                whole,
                whole,
                feed_spec(gathered, 0),
                pl.BlockSpec((1, wide), lambda i, s: (0, i)),
            ],
            out_specs=[piece, piece],
            scratch_shapes=[pltpu.VMEM((2 * rows, width), LOW)],
        ),
        out_shape=[jax.ShapeDtypeStruct((2 * rows, 4 * wide), LOW)] * 2,
        compiler_params=pltpu.CompilerParams(vmem_limit_bytes=VMEM_ROOM),
        cost_estimate=pl.CostEstimate(
            flops=16 * rows * wide * width,
            transcendentals=8 * rows * wide,
            bytes_accessed=rows * width * 4 + 8 * width * wide + 32 * rows * wide,
        ),
    )(places, *pair, gathered, shift)


def hidden_kernel(
    places_ref, own_ref, far_ref, right_ref, slope_ref, out_ref, sum_ref, left_ref
):
    fill_rows(left_ref, own_ref, far_ref)
    right = right_ref[...].reshape(left_ref.shape[1], -1)
    grad = jnp.dot(left_ref[...], right, preferred_element_type=jnp.float32)
    grad = (grad * slope_ref[...].astype(jnp.float32)).astype(LOW)
    out_ref[...] = grad
    sum_ref[...] = jnp.sum(grad.astype(jnp.float32), axis=0, keepdims=True)


def hidden_call(places, pair, gathered, slope):
    rows, width = pair[0].shape
    wide = slope.shape[1] // 4
    whole = pl.BlockSpec((rows, width), lambda i, s: (0, 0))
    piece = pl.BlockSpec((2 * rows, wide), lambda i, s: (0, i))
    return pl.pallas_call(
        hidden_kernel,
        grid_spec=pltpu.PrefetchScalarGridSpec(
            num_scalar_prefetch=1,
            grid=(4,),
            in_specs=[whole, whole, feed_spec(gathered, 2), piece],
            out_specs=[piece, pl.BlockSpec((1, wide), lambda i, s: (0, i))],
            scratch_shapes=[pltpu.VMEM((2 * rows, width), LOW)],
        ),
        out_shape=[
            jax.ShapeDtypeStruct((2 * rows, 4 * wide), LOW),
            jax.ShapeDtypeStruct((1, 4 * wide), jnp.float32),
        ],
        compiler_params=pltpu.CompilerParams(vmem_limit_bytes=VMEM_ROOM),
        cost_estimate=pl.CostEstimate(
            flops=16 * rows * wide * width,
            transcendentals=0,
            bytes_accessed=rows * width * 4 + 8 * width * wide + 32 * rows * wide,
        ),
    )(places, *pair, gathered, slope)


def down_kernel(places_ref, left_ref, right_ref, own_ref, send_ref):
    span = right_ref.shape[3] // 2
    rows = own_ref.shape[0]
    total = None
    for far in range(2):
        right = right_ref[:, places_ref[3] ^ far].reshape(-1, 2 * span)
        for part in range(2):
            start = (part * 2 + far) * span
            one = mat_far(
                left_ref[:, start : start + span], right[:, part * span : (part + 1) * span]
            )
            total = one if total is None else total + one
    own_ref[...] = total[:rows]
    send_ref[...] = total[rows:].astype(LOW)


def down_call(places, left, gathered, start):
    both, deep = left.shape
    rows = both // 2
    lines, _, tall, wide = gathered.shape
    piece = pl.BlockSpec((rows, 2 * tall), lambda i, s: (0, i))
    own, send = pl.pallas_call(
        down_kernel,
        grid_spec=pltpu.PrefetchScalarGridSpec(
            num_scalar_prefetch=1,
            grid=(lines // 2,),
            in_specs=[
                pl.BlockSpec((both, deep), lambda i, s: (0, 0)),
                pl.BlockSpec((2, 2, tall, wide // 2), lambda i, s: (i, 0, 0, start)),
            ],
            out_specs=[piece, piece],
        ),
        out_shape=[
            jax.ShapeDtypeStruct((rows, lines * tall), jnp.float32),
            jax.ShapeDtypeStruct((rows, lines * tall), LOW),
        ],
        compiler_params=pltpu.CompilerParams(vmem_limit_bytes=VMEM_ROOM),
        cost_estimate=SMALL,
    )(places, left, gathered)
    return own, send


def mat(left, right):
    return jnp.dot(left, right, preferred_element_type=jnp.float32)


def turn_kernel(places_ref, own_ref, far_ref, turned_ref, left_ref):
    rows = own_ref.shape[0]
    for block in range(4):
        at = (places_ref[0] ^ block) * 2 + (places_ref[1] ^ pl.program_id(0))
        start = pl.multiple_of(at * LANES, LANES)
        span = slice(block * LANES, (block + 1) * LANES)
        left_ref[:rows, span] = own_ref[:, pl.ds(start, LANES)]
        left_ref[rows:, span] = far_ref[:, pl.ds(start, LANES)]
    turned_ref[0] = jnp.transpose(left_ref[...])


def turn(places, pair):
    rows, width = pair[0].shape
    line = width // 2
    whole = pl.BlockSpec((rows, width), lambda i, s: (0, 0))
    return pl.pallas_call(
        turn_kernel,
        grid_spec=pltpu.PrefetchScalarGridSpec(
            num_scalar_prefetch=1,
            grid=(2,),
            in_specs=[whole, whole],
            out_specs=pl.BlockSpec((1, line, 2 * rows), lambda i, s: (i, 0, 0)),
            scratch_shapes=[pltpu.VMEM((2 * rows, line), LOW)],
        ),
        out_shape=jax.ShapeDtypeStruct((2, line, 2 * rows), LOW),
        compiler_params=pltpu.CompilerParams(vmem_limit_bytes=VMEM_ROOM),
        cost_estimate=pl.CostEstimate(
            flops=0, transcendentals=0, bytes_accessed=rows * width * 8
        ),
    )(places, *pair)


def weight_cost(operands):
    rows, line = operands[0][1].shape[0], 4 * LANES
    wide = sum(right.shape[1] for _, right in operands) // 4
    return pl.CostEstimate(
        flops=8 * rows * line * wide,
        transcendentals=0,
        bytes_accessed=rows * wide * 8 + rows * line * 8 + line * wide * 8,
    )


def piece_kernel(pairs, *refs):
    ins, outs = refs[: 2 * pairs], refs[2 * pairs :]
    step = pl.program_id(0)
    parts = [mat(ins[2 * pair][0], ins[2 * pair + 1][...]).astype(LOW) for pair in range(pairs)]
    made = parts[0] if pairs == 1 else jnp.concatenate(parts, axis=1)

    @pl.when(step < 2)
    def _():
        outs[0][0] = made

    @pl.when(step >= 2)
    def _():
        outs[1][0] = made


def weight_pieces(operands, send, cost=None):
    line, rows = operands[0][0].shape[1:]
    if send:
        first = lambda i: jnp.minimum(i, 1)
        column = lambda i: jnp.maximum(i, 1)
    else:
        first = lambda i: 1 - jnp.minimum(i, 1)
        column = lambda i: jnp.where(i < 2, 0, i)
    specs, arrays, wide = [], [], 0
    for turned, right in operands:
        span = right.shape[1] // 4
        wide += span
        specs.append(pl.BlockSpec((1, line, rows), lambda i: (first(i), 0, 0)))
        specs.append(pl.BlockSpec((rows, span), lambda i: (0, column(i))))
        arrays += [turned, right]

    def kernel(*refs):
        piece_kernel(len(operands), *refs)

    return pl.pallas_call(
        kernel,
        grid=(4,),
        in_specs=specs,
        out_specs=[
            pl.BlockSpec((1, line, wide), lambda i: (first(i), 0, 0)),
            pl.BlockSpec((1, line, wide), lambda i: (jnp.maximum(i - 2, 0), 0, 0)),
        ],
        out_shape=[jax.ShapeDtypeStruct((2, line, wide), LOW)] * 2,
        compiler_params=pltpu.CompilerParams(vmem_limit_bytes=VMEM_ROOM),
        cost_estimate=cost or weight_cost(operands),
    )(*arrays)


def lane_of(shape):
    return lax.broadcasted_iota(jnp.int32, shape, 1)


def head_views(query, key, bias, head):
    lane = lane_of(query.shape)
    mine = (lane >= HDIM) if head else (lane < HDIM)
    spot = 0 if head else HDIM
    zero = jnp.zeros_like(query)
    query_view = jnp.where(mine, query, jnp.where(lane == spot, zero + 1, zero))
    key_view = jnp.where(lane == spot, bias, key)
    return mine, query_view, key_view


def attend_kernel(qkv_ref, bias_ref, mixed_ref, total_ref):
    query = qkv_ref[:, 0:LANES] * jnp.bfloat16(HDIM ** (-0.5))
    key = qkv_ref[:, LANES : 2 * LANES]
    value = qkv_ref[:, 2 * LANES : 3 * LANES]
    bias = bias_ref[...]
    sums, tops = [], []
    for head in range(2):
        mine, query_view, key_view = head_views(query, key, bias, head)
        scores = mat_far(query_view, key_view)
        top = jnp.max(scores, axis=1, keepdims=True)
        weight = jnp.exp(scores - top).astype(LOW)
        value_view = jnp.where(mine, value, jnp.ones_like(value))
        sums.append(jnp.dot(weight, value_view, preferred_element_type=jnp.float32))
        tops.append(top)
    low = lane_of(sums[0].shape) < HDIM
    upper = jnp.where(low, sums[0], sums[1])
    lower = jnp.where(low, sums[1], sums[0])
    lower = pltpu.roll(lower, HDIM, 1)
    mixed_ref[...] = (upper / lower).astype(LOW)
    total = jnp.where(low, tops[0], tops[1]) + jnp.log(lower)
    total = jnp.transpose(total)
    total_ref[0, 0:1, :] = total[0:1]
    total_ref[0, 1:2, :] = total[HDIM : HDIM + 1]


def attend_back_kernel(qkv_ref, bias_ref, grad_ref, mixed_ref, total_ref, out_ref):
    scale = HDIM ** (-0.5)
    query = qkv_ref[:, 0:LANES] * jnp.bfloat16(scale)
    key = qkv_ref[:, LANES : 2 * LANES]
    value = qkv_ref[:, 2 * LANES : 3 * LANES]
    bias = bias_ref[...]
    grad = grad_ref[...]
    product = grad.astype(jnp.float32) * mixed_ref[...].astype(jnp.float32)
    shape = (8, LANES)
    head_of = lane_of(shape) // HDIM
    ones = jnp.where(head_of == lax.broadcasted_iota(jnp.int32, shape, 0), 1.0, 0.0)
    inner = lax.dot_general(
        ones,
        product,
        (((1,), (1,)), ((), ())),
        precision=lax.Precision.HIGHEST,
        preferred_element_type=jnp.float32,
    )
    grad_query = grad_key = grad_value = None
    for head in range(2):
        mine, query_view, key_view = head_views(query, key, bias, head)
        zero = jnp.zeros_like(query)
        scores = mat_far(key_view, query_view)
        probs = jnp.exp(scores - total_ref[0, head : head + 1, :])
        grad_view = jnp.where(mine, grad, zero)
        grad_probs = mat_far(value, grad_view)
        grad_scores = (probs * (grad_probs - inner[head : head + 1])).astype(LOW)
        one_value = jnp.dot(probs.astype(LOW), grad_view, preferred_element_type=jnp.float32)
        one_key = jnp.dot(
            grad_scores, jnp.where(mine, query, zero), preferred_element_type=jnp.float32
        )
        one_query = mat_rows(grad_scores, jnp.where(mine, key, zero))
        grad_query = one_query if head == 0 else grad_query + one_query
        grad_key = one_key if head == 0 else grad_key + one_key
        grad_value = one_value if head == 0 else grad_value + one_value
    out_ref[:, 0:LANES] = (grad_query * scale).astype(LOW)
    out_ref[:, LANES : 2 * LANES] = grad_key.astype(LOW)
    out_ref[:, 2 * LANES : 3 * LANES] = grad_value.astype(LOW)


def attend_image(image, qkv, bias, given):
    both = qkv.shape[0]
    rows = both // 2
    blocks = qkv.shape[1] // (3 * LANES)

    def kernel(*refs):
        attend_kernel(*refs[:2], *refs[-2:])

    return pl.pallas_call(
        kernel,
        grid=(blocks,),
        in_specs=[
            pl.BlockSpec((rows, 3 * LANES), lambda j: (image, j)),
            pl.BlockSpec((rows, LANES), lambda j: (0, 0)),
        ]
        + [pl.BlockSpec(memory_space=pl.ANY)] * len(given),
        out_specs=[
            pl.BlockSpec((rows, LANES), lambda j: (image, j)),
            pl.BlockSpec((1, 8, rows), lambda j: (image * blocks + j, 0, 0)),
        ],
        out_shape=[
            jax.ShapeDtypeStruct((both, blocks * LANES), LOW),
            jax.ShapeDtypeStruct((2 * blocks, 8, rows), jnp.float32),
        ],
        input_output_aliases={2: 0, 3: 1} if given else {},
        compiler_params=pltpu.CompilerParams(vmem_limit_bytes=VMEM_ROOM),
        cost_estimate=pl.CostEstimate(
            flops=blocks * 2 * 2 * 2 * rows * rows * LANES * 2,
            transcendentals=blocks * 2 * rows * rows,
            bytes_accessed=rows * blocks * LANES * 8,
        ),
    )(qkv, bias, *given)


def attend_back_image(image, qkv, bias, grad, mixed, total, given):
    both = qkv.shape[0]
    rows = both // 2
    blocks = qkv.shape[1] // (3 * LANES)

    def kernel(*refs):
        attend_back_kernel(*refs[:5], refs[-1])

    return pl.pallas_call(
        kernel,
        grid=(blocks,),
        in_specs=[
            pl.BlockSpec((rows, 3 * LANES), lambda j: (image, j)),
            pl.BlockSpec((rows, LANES), lambda j: (0, 0)),
            pl.BlockSpec((rows, LANES), lambda j: (0, j)),
            pl.BlockSpec((rows, LANES), lambda j: (image, j)),
            pl.BlockSpec((1, 8, rows), lambda j: (image * blocks + j, 0, 0)),
        ]
        + [pl.BlockSpec(memory_space=pl.ANY)] * len(given),
        out_specs=pl.BlockSpec((rows, 3 * LANES), lambda j: (image, j)),
        out_shape=jax.ShapeDtypeStruct(qkv.shape, LOW),
        input_output_aliases={5: 0} if given else {},
        compiler_params=pltpu.CompilerParams(vmem_limit_bytes=VMEM_ROOM),
        cost_estimate=pl.CostEstimate(
            flops=blocks * 2 * 5 * 2 * rows * rows * LANES * 2,
            transcendentals=blocks * 2 * rows * rows,
            bytes_accessed=rows * blocks * LANES * 16,
        ),
    )(qkv, bias, grad, mixed, total, *given)


def flat_norm(values, gain, shift):
    center = values - jnp.mean(values, axis=-1, keepdims=True)
    spread = lax.rsqrt(jnp.mean(center * center, axis=-1, keepdims=True) + EPS)
    unit = center * spread
    return unit * gain + shift, unit, spread


def flat_norm_back(upstream, unit, spread, gain):
    scaled = upstream * gain
    inner = (
        scaled
        - jnp.mean(scaled, axis=-1, keepdims=True)
        - unit * jnp.mean(scaled * unit, axis=-1, keepdims=True)
    )
    return spread * inner, jnp.sum(upstream * unit, axis=0), jnp.sum(upstream, axis=0)


def column_flat(values):
    return jnp.sum(values.astype(jnp.float32), axis=0)


def whole_images(
    images,
    cotangent,
    slot_live,
    first_gain,
    first_shift,
    query_weight,
    query_bias,
    key_weight,
    value_weight,
    value_bias,
    output_weight,
    output_bias,
    second_gain,
    second_shift,
    up_weight,
    up_bias,
    down_weight,
    down_bias,
):
    dp_place = lax.axis_index("dp")
    place_y = lax.axis_index("tensor")
    core, place_x, place_z = dp_place % 2, (dp_place // 2) % 2, dp_place // 4
    places = jnp.stack([place_z, place_x, core, place_y]).astype(jnp.int32)
    strip, width = images.shape[1:]
    half = -(-strip // HALF_PAD) * HALF_PAD
    rows = 2 * half
    depth, head_cols = query_weight.shape
    units = up_weight.shape[1]

    def columns_of(weights, place):
        return [
            lax.dynamic_slice_in_dim(
                weight, place * (weight.shape[1] // 2), weight.shape[1] // 2, 1
            )
            for weight in weights
        ]

    def core_parts(weights, place):
        cuts = columns_of(weights, place)
        parts = []
        for part in range(2):
            spans = [cut.shape[1] // 2 for cut in cuts]
            parts.append(
                jnp.concatenate(
                    [cut[:, part * span : (part + 1) * span] for cut, span in zip(cuts, spans)], 1
                )
            )
        return jnp.stack(parts)

    feeds = [up_weight, down_weight.T]
    feed_keep = jnp.concatenate(columns_of(feeds, core), 1)
    feed_send = jnp.concatenate(columns_of(feeds, 1 - core), 1)
    feed = pick_two(core, feed_keep, exchange(feed_send, far_core=1), 0)
    groups = [[place for place in range(32) if (place // 2) % 2 == at] for at in range(2)]

    gathered = lax.all_gather(
        feed.reshape(2 * depth, -1), BOTH, axis=0, tiled=True, axis_index_groups=groups
    ).reshape(8, 2, 2 * depth, -1)
    gathered = pltpu.with_memory_space_constraint(gathered, pltpu.HBM)

    heads = [query_weight, key_weight, value_weight, output_weight.T]
    piece_one = gather_piece(core_parts(heads, core), core_parts(heads, 1 - core), core)
    others_one = scatter_z([None, piece_one, piece_one, piece_one])

    padding = ((0, 0), (0, half - strip), (0, 0))

    def own_and_far(slots, *waits):
        slots = jnp.pad(slots, padding)
        mine = lax.dynamic_index_in_dim(slots, place_y, 0, keepdims=False)
        theirs = lax.dynamic_index_in_dim(slots, 1 - place_y, 0, keepdims=False)
        return mine, exchange(after(theirs, *waits), far_y=1)

    image_mine, image_far = own_and_far(images, piece_one)
    grad_mine, grad_far = own_and_far(cotangent, piece_one)
    line_one = gather_line(piece_one, others_one, places)
    cross_one = exchange(line_one[0], far_x=1), exchange(line_one[1], far_y=1)
    pair_one = gather_pairs(places, *line_one, *cross_one)
    image_far, grad_far = after((image_far, grad_far), *pair_one)
    whole = jnp.concatenate([image_mine, image_far], 0)

    def head_columns(vector):
        table = vector.astype(jnp.float32).reshape(2, 2, 2, -1)
        table = lax.dynamic_index_in_dim(table, core, 1, keepdims=False)
        table = jnp.where(place_y == 0, table, table[::-1])
        return table.transpose(1, 0, 2).reshape(4, 1, -1)

    def spread_core(table):
        table = jnp.stack(
            [jnp.where(core == 0, table, 0.0), jnp.where(core == 1, table, 0.0)], 1
        )
        return table.reshape(-1)

    def head_spread(vector):
        table = vector.reshape(2, 2, -1).transpose(1, 0, 2)
        return spread_core(jnp.where(place_y == 0, table, table[::-1]))

    gain_one, shift_one = first_gain.astype(jnp.float32), first_shift.astype(jnp.float32)
    gain_two, shift_two = second_gain.astype(jnp.float32), second_shift.astype(jnp.float32)
    query_shift, value_shift = head_columns(query_bias), head_columns(value_bias)
    qkv_shift = jnp.concatenate(
        [query_shift, jnp.zeros_like(query_shift), value_shift], 1
    ).reshape(-1)
    up_shift = head_columns(up_bias).reshape(1, -1)

    row = jnp.arange(rows)
    in_half = row % half
    spot = jnp.where(row < half, place_y, 1 - place_y) * strip + in_half
    ok = (in_half < strip) & (spot < VALID)
    live = lax.dynamic_index_in_dim(slot_live, place_y, 0, keepdims=False).astype(jnp.float32)
    row_mask = (live * ok.astype(jnp.float32))[:, None]
    key_bias = jnp.broadcast_to(
        jnp.where(ok, 0.0, NEGATIVE).astype(LOW)[:, None], (rows, LANES)
    )

    resid = whole.astype(jnp.float32)

    def full_columns(owned):
        return owned.transpose(2, 0, 1, 3).reshape(depth, -1)

    def pair_of(own):
        return own, exchange(own, far_core=1)

    normed, unit_one, spread_one = flat_norm(resid, gain_one, shift_one)
    normed_pair = pair_of(normed.astype(LOW))

    normed_turned = turn(places, normed_pair)
    grad_top = row_mask * jnp.concatenate([grad_mine, grad_far], 0).astype(jnp.float32)
    fed_grad = grad_top.astype(LOW)
    fed_pair = pair_of(fed_grad)
    fed_turned = turn(places, fed_pair)
    last_one = exchange(pair_one[0], far_y=1), exchange(pair_one[1], far_x=1)
    qkv_full, output_full = gather_all(after(places, normed_turned, fed_turned), *pair_one, *last_one, 3 * head_cols // 4)

    normed_rows = jnp.concatenate(normed_pair, 0)
    qkv = (mat(normed_rows, qkv_full) + qkv_shift).astype(LOW)
    mixed_half = attend_image(1, qkv, key_bias, [])
    mixed_far = mat_far(mixed_half[0][rows:], output_full).astype(LOW)
    mixed_sum = exchange(mixed_far, far_core=1)
    mixed, totals = attend_image(0, qkv, key_bias, list(after(tuple(mixed_half), mixed_far)))
    attended = mat_far(mixed[:rows], output_full) + mixed_sum.astype(jnp.float32)
    attended = attended + output_bias.astype(jnp.float32)
    middle = row_mask * (resid + attended)
    second, unit_two, spread_two = flat_norm(middle, gain_two, shift_two)
    second_pair = pair_of(second.astype(LOW))
    second_turned = turn(places, second_pair)
    up_pair = after(second_pair, second_turned)
    active, slope = up_call(places, up_pair, gathered, up_shift)

    lower_sends = weight_pieces([(fed_turned, active)], True)
    lower_first = scatter_first(lower_sends)
    lower_keeps = weight_pieces([(fed_turned, after(active, *lower_sends))], False)
    fed_late = after(fed_pair, *lower_keeps)
    hidden_grad, up_bias_sums = hidden_call(places, fed_late, gathered, slope)
    up_sends = weight_pieces([(second_turned, hidden_grad)], True)
    up_first = scatter_first(up_sends)
    lower_first = after(lower_first, *up_sends)
    lower_second = scatter_second(scatter_adds(lower_keeps, lower_first))
    hidden_late = after(hidden_grad, *lower_first)
    second_grad, second_send = down_call(places, hidden_late, gathered, 0)
    second_grad = second_grad + exchange(second_send, far_core=1).astype(jnp.float32)
    middle_back, gain_two_grad, shift_two_grad = flat_norm_back(
        second_grad, unit_two, spread_two, gain_two
    )
    middle_grad = row_mask * (grad_top + middle_back)
    attended_grad = middle_grad.astype(LOW)
    attended_pair = pair_of(attended_grad)
    grad_mixed = mat(attended_pair[0], output_full).astype(LOW)
    back = attend_back_image(0, qkv, key_bias, grad_mixed, mixed, totals, [])
    up_keeps = weight_pieces([(second_turned, after(hidden_late, back))], False)
    up_first = after(up_first, back)
    up_adds = scatter_adds(up_keeps, up_first)
    up_second = scatter_second(up_adds)
    lower_second = after(lower_second, back, *up_keeps)
    lower_line = scatter_line(lower_keeps, lower_first, lower_second)
    lower_z = scatter_z(lower_line)
    attended_turned = turn(places, attended_pair)
    grad_mixed = mat(attended_pair[1], output_full).astype(LOW)
    grad_mixed = after(grad_mixed, *up_adds, *lower_line, attended_turned)
    back = attend_back_image(1, qkv, key_bias, grad_mixed, mixed, totals, [back])
    up_second, lower_z = after((up_second, tuple(lower_z)), back)
    up_line = scatter_line(up_keeps, up_first, up_second)
    up_z = scatter_z(up_line)
    back = after(back, *up_line)
    last_sends = weight_pieces(
        [(normed_turned, back), (attended_turned, mixed)], True, SMALL
    )
    last_first = scatter_first(last_sends)
    back_late = after(back, *last_sends)
    last_keeps = weight_pieces(
        [(normed_turned, back_late), (attended_turned, mixed)], False, SMALL
    )
    fed, fed_send = down_call(places, after(active, *last_keeps), gathered, 1)
    back_late = after(back_late, fed, fed_send, *up_z)
    normed_send = mat_far(back_late[rows:], qkv_full).astype(LOW)
    last_first = after(last_first, normed_send)
    last_adds = scatter_adds(last_keeps, last_first)
    last_second = scatter_second(last_adds)
    back_late = after(back_late, *last_adds)
    normed_far = exchange(normed_send, far_core=1)
    fed = fed + exchange(fed_send, far_core=1).astype(jnp.float32)
    layer_own = (row_mask * (middle + fed + down_bias.astype(jnp.float32))).astype(LOW)
    normed_grad = mat_far(back_late[:rows], qkv_full) + normed_far.astype(jnp.float32)
    first_back, gain_one_grad, shift_one_grad = flat_norm_back(
        normed_grad, unit_one, spread_one, gain_one
    )
    images_own = middle_grad + first_back
    qkv_sums = column_flat(back_late).reshape(4, 3, -1)
    vector = jnp.concatenate(
        [
            column_flat(attended_grad),
            gain_two_grad,
            shift_two_grad,
            column_flat(fed_grad),
            head_spread(up_bias_sums.reshape(-1)),
            gain_one_grad,
            shift_one_grad,
            head_spread(qkv_sums[:, 0].reshape(-1)),
            head_spread(qkv_sums[:, 2].reshape(-1)),
        ]
    )
    vector, vectors = vector_first(vector)
    last_line = scatter_line(last_keeps, last_first, after(last_second, images_own))
    last_z = scatter_z(last_line)
    images_far = exchange(
        after(images_own, *last_second)[half : half + strip].astype(LOW), far_y=1
    )
    layer_far = exchange(after(layer_own, *last_adds)[half : half + strip], far_y=1)
    vector = vector + vectors[0] + vectors[1] + vectors[2]
    vector = vector + after(exchange(vector, far_x=1), images_far, *last_line)
    vector = vector + after(exchange(vector, far_y=1), layer_far)
    lower_z, up_z = after((tuple(lower_z), tuple(up_z)), *last_line, layer_far)
    lower_owned = full_columns(scatter_last(lower_line[0], lower_z, core)).T
    upper_owned = full_columns(scatter_last(up_line[0], up_z, core))

    def to_strips(own, far):
        return pick_two(place_y, own[:strip], far, 1).transpose(1, 0, 2)

    layer_out = to_strips(layer_own, layer_far)
    images_grad = to_strips(after(images_own, *last_line), images_far.astype(jnp.float32))
    last_z = after(tuple(last_z), vector, layer_out, images_grad, lower_owned, upper_owned)
    last_owned = scatter_last(last_line[0], last_z, core)
    def head_grad(at):
        return full_columns(last_owned[..., at * LANES : (at + 1) * LANES])

    early, late = vector[: 4 * width + up_bias.shape[0]], vector[4 * width + up_bias.shape[0] :]
    return (
        layer_out,
        images_grad,
        late[:width],
        late[width : 2 * width],
        head_grad(0),
        late[2 * width : 3 * width],
        head_grad(1),
        head_grad(2),
        late[3 * width :],
        head_grad(3).T,
        early[:width],
        early[width : 2 * width],
        early[2 * width : 3 * width],
        upper_owned,
        early[4 * width :],
        lower_owned,
        early[3 * width : 4 * width],
    )


def pick(mesh):
    sizes = dict(mesh.shape)
    if sizes["dp"] == 16 and sizes["tensor"] == 2:
        return whole_images
    return local


def solution(mesh):
    in_specs = (
        P("dp", "tensor", None),
        P("dp", "tensor", None),
        P("dp"),
        P(),
        P(),
        P("dp", "tensor"),
        P(),
        P("dp", "tensor"),
        P("dp", "tensor"),
        P(),
        P("tensor", "dp"),
        P(),
        P(),
        P(),
        P("dp", "tensor"),
        P(),
        P("tensor", "dp"),
        P(),
    )
    out_specs = (
        P("dp", "tensor", None),
        P("dp", "tensor", None),
        P(),
        P(),
        P("dp", "tensor"),
        P(),
        P("dp", "tensor"),
        P("dp", "tensor"),
        P(),
        P("tensor", "dp"),
        P(),
        P(),
        P(),
        P("dp", "tensor"),
        P(),
        P("tensor", "dp"),
        P(),
    )
    return jax.shard_map(pick(mesh), mesh=mesh, in_specs=in_specs, out_specs=out_specs, check_vma=False)
```
